32 devices in a mesh: section: 2 (over core), seq: 4 (over y, x), head: 4 (over z).
Axes of the slice: x: 2, y: 2, z: 4, core: 2. Of those that a mesh axis runs over, the one named last changes fastest.
Arguments:
- incoming: bfloat16 [2, 4, 512, 1536], P('section', None, 'seq'), may hold values from -6 to 6
- segment_ids: int32 [4, 512], replicated, may hold values from 0 to 5, as said below
- positions: int32 [4, 512], P(None, 'seq'), may hold values from 0 to 6142, as said below
- conv_gains: float32 [2, 1536], replicated, may hold values from 0.5 to 1.5
- conv_in: bfloat16 [1536, 3, 1536], P(None, None, 'head'), may hold values from -0.15625 to 0.15625
- conv_kernel: float32 [3, 1536], P(None, 'head'), may hold values from -3 to 3
- conv_out: bfloat16 [1536, 1536], P('head'), may hold values from -0.15625 to 0.15625
- conv_gate_up: bfloat16 [1536, 2, 6912], P(None, None, 'head'), may hold values from -0.15625 to 0.15625
- conv_down: bfloat16 [6912, 1536], P('head'), may hold values from -0.078125 to 0.078125
- attn_gains: float32 [2, 1536], replicated, may hold values from 0.5 to 1.5
- w_query: bfloat16 [1536, 1536], P(None, 'head'), may hold values from -0.15625 to 0.15625
- w_keyval: bfloat16 [1536, 2, 512], P(None, None, 'head'), may hold values from -0.15625 to 0.15625
- qk_gains: float32 [2, 64], replicated, may hold values from 0.5 to 1.5
- attn_out: bfloat16 [1536, 1536], P('head'), may hold values from -1.25 to 1.25
- attn_gate_up: bfloat16 [1536, 2, 6912], P(None, None, 'head'), may hold values from -0.15625 to 0.15625
- attn_down: bfloat16 [6912, 1536], P('head'), may hold values from -0.078125 to 0.078125
Outputs:
- section_edges: bfloat16 [2, 4, 512, 1536], P('section', None, 'seq')
- grad_conv_gains: float32 [2, 1536], P(None, ('section', 'seq'))
- grad_conv_in: float32 [1536, 3, 1536], P(('section', 'seq'), None, 'head')
- grad_conv_kernel: float32 [3, 1536], P(None, 'head')
- grad_conv_out: float32 [1536, 1536], P('head', ('section', 'seq'))
- grad_conv_gate_up: float32 [1536, 2, 6912], P(('section', 'seq'), None, 'head')
- grad_conv_down: float32 [6912, 1536], P('head', ('section', 'seq'))
- grad_attn_gains: float32 [2, 1536], P(None, ('section', 'seq'))
- grad_query: float32 [1536, 1536], P(('section', 'seq'), 'head')
- grad_keyval: float32 [1536, 2, 512], P(('section', 'seq'), None, 'head')
- grad_qk_gains: float32 [2, 64], replicated
- grad_attn_out: float32 [1536, 1536], P('head', ('section', 'seq'))
- grad_attn_gate_up: float32 [1536, 2, 6912], P(('section', 'seq'), None, 'head')
- grad_attn_down: float32 [6912, 1536], P('head', ('section', 'seq'))
The draws below stay inside these ranges and needn't reach their ends.
Inputs may be any that keep to these rules, and one draw needn't show every extreme that they name: `segment_ids`: 0 at the first token; along the sequence (micro-batches in order) each token's number equals the previous one or exceeds it by one; six documents. Within a document the positions rise by one from token to token; a document's first position is below 6144.
All inputs are finite; a program needn't handle non-finite values.
Results may differ from the reference program's by a relative error of at most 0.04.
Values may be sent and summed in bfloat16 or wider, within the bound.
A program may use at most 320 MiB of HBM per device.

```python
import jax
import jax.numpy as jnp
from jax import lax

D = 1536
FF = 6912
HEADS = 24
KV = 8
HD = 64
KERNEL = 3
MICRO = 4
MB_TOK = 512
SEQ_LEN = 2048


def document_layout(key):
    picked = jax.random.permutation(jax.random.fold_in(key, 11), SEQ_LEN - 1)[:5] + 1
    starts = jnp.zeros((SEQ_LEN,), jnp.int32).at[picked].set(1).at[0].set(1)
    numbers = jnp.cumsum(starts) - 1
    order = jnp.arange(SEQ_LEN, dtype=jnp.int32)
    begins = lax.cummax(jnp.where(starts == 1, order, 0), axis=0)
    offsets = jax.random.randint(jax.random.fold_in(key, 12), (6,), 0, 4096)
    offsets = offsets.at[0].set(0).at[5].set(4095 + begins[SEQ_LEN - 1])
    return (numbers, order - begins + offsets[numbers])


def draw_segment_ids(key, part):
    return document_layout(key)[0].reshape(MICRO, MB_TOK).astype(jnp.int32)


def draw_positions(key, part):
    return document_layout(key)[1].reshape(MICRO, MB_TOK).astype(jnp.int32)


def block_scale(rng, shape, split, low, largest):
    factor_of = 1.0
    for axis_at, parts in split:
        steps = jax.random.uniform(jax.random.fold_in(jax.random.fold_in(rng, 6), axis_at), (parts,), jnp.float32, low / len(split), largest / len(split))
        factor_of = factor_of * jnp.repeat(jnp.exp(steps), shape[axis_at] // parts).reshape((-1,) + (1,) * (len(shape) - 1 - axis_at))
    return factor_of


def noise(own_key, dims, spread, bound, pieces=(), kind=jnp.bfloat16):
    level = block_scale(own_key, dims, pieces, -0.22, 0.18) if pieces else 1.0
    array = jax.random.normal(own_key, dims, jnp.float32) * spread * level
    return jnp.minimum(jnp.maximum(array, -bound), bound).astype(kind)


def setup_inputs(seed: int = 0) -> dict:
    key_of = jax.random.split(jax.random.key(seed), 17)
    return {
        "incoming": noise(key_of[0], (2, MICRO, MB_TOK, D), 1.0, 6.0, ((0, 2), (2, 4))),
        "segment_ids": draw_segment_ids(jax.random.fold_in(key_of[16], 71), 0),
        "positions": draw_positions(jax.random.fold_in(key_of[16], 71), 0),
        "conv_gains": jnp.clip(1.0 + 0.1 * jax.random.normal(key_of[3], (2, D), jnp.float32), 0.5, 1.5),
        "conv_in": noise(key_of[4], (D, 3, D), D ** -0.5, 0.15625, ((2, 4),)),
        "conv_kernel": noise(key_of[5], (KERNEL, D), 0.6, 3.0, ((1, 4),), jnp.float32),
        "conv_out": noise(key_of[6], (D, D), D ** -0.5, 0.15625, ((0, 4),)),
        "conv_gate_up": noise(key_of[7], (D, 2, FF), D ** -0.5, 0.15625, ((2, 4),)),
        "conv_down": noise(key_of[8], (FF, D), FF ** -0.5, 0.078125, ((0, 4),)),
        "attn_gains": jnp.clip(1.0 + 0.1 * jax.random.normal(key_of[9], (2, D), jnp.float32), 0.5, 1.5),
        "w_query": noise(key_of[10], (D, HEADS * HD), D ** -0.5, 0.15625, ((1, 4),)),
        "w_keyval": noise(key_of[11], (D, 2, KV * HD), D ** -0.5, 0.15625, ((2, 4),)),
        "qk_gains": jnp.clip(1.0 + 0.1 * jax.random.normal(key_of[12], (2, HD), jnp.float32), 0.5, 1.5),
        "attn_out": noise(key_of[13], (HEADS * HD, D), (D // 64) ** -0.5, 1.25, ((0, 4),)),
        "attn_gate_up": noise(key_of[14], (D, 2, FF), D ** -0.5, 0.15625, ((2, 4),)),
        "attn_down": noise(key_of[15], (FF, D), FF ** -0.5, 0.078125, ((0, 4),)),
    }


EPS = 1e-05
THETA = 1000000.0
HIGH = lax.Precision.HIGHEST

@jax.custom_vjp
def low(v):
    return lax.optimization_barrier(v.astype(jnp.bfloat16)).astype(jnp.float32)

@jax.custom_vjp
def low_back(v):
    return v

def low_keep(v):
    return (low(v), None)

def low_pass(kept, grad):
    return (grad,)

def back_keep(v):
    return (v, None)

def back_low(kept, grad):
    return (low(grad),)
low.defvjp(low_keep, low_pass)
low_back.defvjp(back_keep, back_low)

def matmul(former, latter):
    return jnp.dot(former, latter, precision=HIGH)

def norm_apply(values, gain):
    return values * lax.rsqrt(lax.optimization_barrier(jnp.mean(values * values, -1, keepdims=True)) + EPS) * gain

def rotate(values, cosine, sine_table):
    half_width = values.shape[-1] // 2
    turned = jnp.concatenate([-values[..., half_width:], values[..., :half_width]], -1)
    return values * cosine + turned * sine_table

def tables(places, head_width):
    angle_rates = THETA ** (-jnp.arange(0, head_width, 2).astype(jnp.float32) / head_width)
    angles = places.astype(jnp.float32)[:, None] * angle_rates[None, :]
    angles = jnp.concatenate([angles, angles], -1)
    return (jnp.cos(angles), jnp.sin(angles))

def feed_forward(hidden, gain, gate_up, down_proj):
    normed = low(norm_apply(hidden, gain))
    joined = low_back(matmul(normed, gate_up.reshape(gate_up.shape[0], -1)))
    half_width = down_proj.shape[0]
    active = low(jax.nn.silu(joined[:, :half_width]) * joined[:, half_width:])
    return hidden + low_back(matmul(active, down_proj))

def conv_section(entry_rows, segments, gain_pair, w_in, kernel, w_out, gate_up, down_proj):
    model_width = entry_rows.shape[1]
    normed = low(norm_apply(entry_rows, gain_pair[0]))
    projected = low_back(matmul(normed, w_in.reshape(model_width, -1))).reshape(-1, 3, model_width)
    gated = projected[:, 0] * projected[:, 2]
    mixed = kernel[2] * gated
    for offset in (1, 2):
        earlier = jnp.concatenate([jnp.zeros((offset, model_width), gated.dtype), gated[:-offset]], 0)
        matches = jnp.concatenate([jnp.zeros((offset,), jnp.bool_), segments[offset:] == segments[:-offset]], 0)
        mixed = mixed + kernel[2 - offset] * jnp.where(matches[:, None], earlier, 0.0)
    mixed = low(projected[:, 1] * mixed)
    hidden = entry_rows + low_back(matmul(mixed, w_out))
    return feed_forward(hidden, gain_pair[1], gate_up, down_proj)

def attend_block(block_in, key_rows, values, segments, key_order, score_scale):
    queries, query_segments, query_order = block_in
    scores = jnp.einsum('bgrd,kgd->grbk', queries, key_rows, precision=HIGH) * score_scale
    scores = low_back(scores)
    allowed = (query_segments[:, None] == segments[None, :]) & (key_order[None, :] <= query_order[:, None])
    scores = jnp.where(allowed, scores, -1e+30)
    summit = lax.optimization_barrier(jnp.max(scores, -1, keepdims=True))
    raised = jnp.exp(scores - summit)
    weights = low(raised / lax.optimization_barrier(jnp.sum(raised, -1, keepdims=True)))
    return jnp.einsum('grbk,kgd->bgrd', weights, values, precision=HIGH)

def attention_section(entry_rows, segments, places, gain_pair, w_q, w_kv, qk_pair, w_o, gate_up, down_proj):
    length, model_width = entry_rows.shape
    group_size = HEADS // KV
    normed = low(norm_apply(entry_rows, gain_pair[0]))
    queries = low_back(matmul(normed, w_q)).reshape(length, KV, group_size, HD)
    pairs = low_back(matmul(normed, w_kv.reshape(model_width, -1))).reshape(length, 2, KV, HD)
    cosine, sine_table = tables(places, HD)
    queries = low(rotate(norm_apply(queries, qk_pair[0]), cosine[:, None, None], sine_table[:, None, None]))
    key_rows = low(rotate(norm_apply(pairs[:, 0], qk_pair[1]), cosine[:, None], sine_table[:, None]))
    values = low(pairs[:, 1])
    block_len = min(256, length)
    key_order = jnp.arange(length, dtype=jnp.int32)

    def one_block(block_in):
        return attend_block(block_in, key_rows, values, segments, key_order, HD ** (-0.5))
    attended = lax.map(jax.checkpoint(one_block), (queries.reshape(length // block_len, block_len, KV, group_size, HD), segments.reshape(-1, block_len), key_order.reshape(-1, block_len)))
    attended = low_back(low(attended.reshape(length, HEADS * HD)))
    hidden = entry_rows + low_back(matmul(attended, w_o))
    return feed_forward(hidden, gain_pair[1], gate_up, down_proj)

def reference(incoming, segment_ids, positions, conv_gains, conv_in, conv_kernel, conv_out, conv_gate_up, conv_down, attn_gains, w_query, w_keyval, qk_gains, attn_out, attn_gate_up, attn_down):
    segments = segment_ids.reshape(-1).astype(jnp.int32)
    places = positions.reshape(-1).astype(jnp.int32)
    start = incoming[0].astype(jnp.float32).reshape(SEQ_LEN, D)
    cotangent = incoming[1].astype(jnp.float32).reshape(SEQ_LEN, D)
    weights = tuple((weight.astype(jnp.float32) for weight in (conv_gains, conv_in, conv_kernel, conv_out, conv_gate_up, conv_down, attn_gains, w_query, w_keyval, qk_gains, attn_out, attn_gate_up, attn_down)))

    def forward(entry_rows, *params):
        middle = conv_section(entry_rows, segments, params[0], params[1], params[2], params[3], params[4], params[5])
        middle = low_back(low(middle))
        return attention_section(middle, segments, places, params[6], params[7], params[8], params[9], params[10], params[11], params[12])
    result, pull_back = jax.vjp(forward, start, *weights)
    grads = pull_back(cotangent)
    section_edges = jnp.stack([grads[0], result]).reshape(2, MICRO, MB_TOK, D).astype(jnp.bfloat16)
    return (section_edges, grads[1], grads[2], grads[3], grads[4], grads[5], grads[6], grads[7], grads[8], grads[9], grads[10], grads[11], grads[12], grads[13])
```

```python
import functools

import jax
import jax.numpy as jnp
from jax import lax
from jax.experimental import pallas as pl
from jax.experimental.pallas import tpu as pltpu
from jax.sharding import PartitionSpec as P

EPS = 1e-05
THETA = 1000000.0
FLOAT = jnp.float32
HALF = jnp.bfloat16
MESH = pl.DeviceIdType.MESH
VMEM = pl.BlockSpec(memory_space=pltpu.VMEM)


def product(former, latter):
    return jnp.dot(former, latter, preferred_element_type=FLOAT)


def outer_sum(former, latter):
    return lax.dot_general(former, latter, (((0,), (0,)), ((), ())), preferred_element_type=FLOAT)


def back_product(former, latter):
    return lax.dot_general(former, latter, (((1,), (1,)), ((), ())), preferred_element_type=FLOAT)


def swiglu(joined):
    half_width = joined.shape[1] // 2
    return jax.nn.silu(joined[:, :half_width]) * joined[:, half_width:]


def norm_apply(values, gain):
    return values * lax.rsqrt(jnp.mean(values * values, -1, keepdims=True) + EPS) * gain


def norm_back(values, gain, grad):
    scale = lax.rsqrt(jnp.mean(values * values, -1, keepdims=True) + EPS)
    weighted = grad * gain
    inner = jnp.mean(weighted * values, -1, keepdims=True)
    grad_values = scale * weighted - values * (scale * scale * scale * inner)
    return grad_values, jnp.sum(grad * values * scale, 0, keepdims=True)


def place():
    return lax.axis_index("section"), lax.axis_index("seq"), lax.axis_index("head")


def greet(peers):
    barrier = pltpu.get_barrier_semaphore()
    for peer in peers:
        pl.semaphore_signal(barrier, inc=1, device_id=peer, device_id_type=MESH)
    pl.semaphore_wait(barrier, len(peers))


def head_peers(where, size):
    section, seq, head = where
    return [(section, seq, lax.rem(head + k, size)) for k in range(1, size)]


def remote(source, target, send, recv, peer):
    return pltpu.make_async_remote_copy(
        src_ref=source,
        dst_ref=target,
        send_sem=send,
        recv_sem=recv,
        device_id=peer,
        device_id_type=MESH,
    )


def rows_of(index, count):
    return pl.ds(pl.multiple_of(index * count, count), count)


def scatter_start(part, slots, send, recv, where, size, count):
    copies = []
    for k, peer in enumerate(head_peers(where, size)):
        copy = remote(part.at[rows_of(peer[2], count)], slots.at[k], send.at[k], recv.at[k], peer)
        copy.start()
        copies.append(copy)
    return copies


def scatter_sum(copies, part, slots, where, count):
    total = part[rows_of(where[2], count), :].astype(FLOAT)
    for copy in copies:
        copy.wait()
    for k in range(len(copies)):
        total = total + slots[k].astype(FLOAT)
    return total


def gather_start(full, send, recv, where, size, count):
    mine = full.at[rows_of(where[2], count)]
    copies = []
    for k, peer in enumerate(head_peers(where, size)):
        copy = remote(mine, mine, send.at[k], recv.at[k], peer)
        copy.start()
        copies.append(copy)
    return copies


def wait_all(copies):
    for copy in copies:
        copy.wait()


def turned(values):
    width = values.shape[-1]
    if width == 128:
        lane = lax.broadcasted_iota(jnp.int32, values.shape, 1)
        low = lax.rem(lane, 64) < 32
        return jnp.where(low, -pltpu.roll(values, 96, 1), pltpu.roll(values, 32, 1))
    parts = []
    for start in range(0, width, 64):
        parts += [-values[:, start + 32 : start + 64], values[:, start : start + 32]]
    return jnp.concatenate(parts, -1)


def head_mean(values):
    width = values.shape[-1]
    if width == 64:
        return jnp.mean(values, -1, keepdims=True)
    lane = lax.broadcasted_iota(jnp.int32, values.shape, 1)
    first = jnp.sum(jnp.where(lane < 64, values, 0.0), -1, keepdims=True)
    second = jnp.sum(jnp.where(lane < 64, 0.0, values), -1, keepdims=True)
    return jnp.where(lane < 64, first, second) * (1.0 / 64.0)


def chunks_of(width):
    return [(start, min(128, width - start)) for start in range(0, width, 128)]


def rotary(raw, gain, cosine, sine):
    width = raw.shape[-1]
    normed = raw * lax.rsqrt(head_mean(raw * raw) + EPS) * gain[:, :width]
    return normed * cosine[:, :width] + turned(normed) * sine[:, :width]


def rotary_back(raw, gain, cosine, sine, grad):
    width = raw.shape[-1]
    back = grad * cosine[:, :width] - turned(grad) * sine[:, :width]
    scale = lax.rsqrt(head_mean(raw * raw) + EPS)
    weighted = back * gain[:, :width]
    grad_raw = scale * weighted - raw * (scale * scale * scale * head_mean(weighted * raw))
    return grad_raw, jnp.sum(back * raw * scale, 0, keepdims=True)


def call(body, name, collective, outs, scratch, args, flops=0, moved=0):
    params = dict(vmem_limit_bytes=56 << 20)
    if collective is not None:
        params.update(collective_id=collective, has_side_effects=True)
    return pl.pallas_call(
        body,
        name=name,
        out_shape=[jax.ShapeDtypeStruct(shape, kind) for shape, kind in outs],
        in_specs=[VMEM] * len(args),
        out_specs=[VMEM] * len(outs),
        scratch_shapes=scratch,
        compiler_params=pltpu.CompilerParams(**params),
        cost_estimate=pl.CostEstimate(flops=flops, bytes_accessed=moved, transcendentals=0),
    )(*args)


def dma(count):
    return pltpu.SemaphoreType.DMA((count,))


def per_device(
    incoming,
    segment_ids,
    positions,
    conv_gains,
    conv_in,
    conv_kernel,
    conv_out,
    conv_gate_up,
    conv_down,
    attn_gains,
    w_query,
    w_keyval,
    qk_gains,
    attn_out,
    attn_gate_up,
    attn_down,
):
    sections = lax.axis_size("section")
    seqs = lax.axis_size("seq")
    heads = lax.axis_size("head")
    section, seq, head = place()
    micro, local_rows, width = incoming.shape[1:]
    rows = local_rows // sections
    tokens = micro * rows
    own = tokens // heads
    block_tok = segment_ids.shape[1]
    length = micro * block_tok
    slots = sections * seqs
    channels = conv_in.shape[2]
    hidden_units = conv_down.shape[0]
    head_width = qk_gains.shape[1]
    query_width = w_query.shape[1]
    pair_width = 2 * w_keyval.shape[2]
    kv_local = w_keyval.shape[2] // head_width
    group = query_width // (kv_local * head_width)
    score_scale = head_width ** (-0.5)
    half_model = width // sections

    local_order = (
        jnp.arange(micro, dtype=jnp.int32)[:, None] * block_tok
        + seq * local_rows
        + section * rows
        + jnp.arange(rows, dtype=jnp.int32)[None, :]
    ).reshape(tokens)
    segments = segment_ids.reshape(length)
    padded = jnp.concatenate([jnp.full((2,), -1, jnp.int32), segments])
    local_segments = segments[local_order]
    same = jnp.stack(
        [
            (local_segments == padded[local_order + 1]).astype(FLOAT),
            (local_segments == padded[local_order]).astype(FLOAT),
        ],
        1,
    )
    local_segments = local_segments[:, None]
    angle_rates = THETA ** (-jnp.arange(0, head_width, 2).astype(FLOAT) / head_width)
    local_positions = lax.dynamic_slice_in_dim(positions, section * rows, rows, 1).reshape(tokens)
    angles = local_positions.astype(FLOAT)[:, None] * angle_rates[None, :]
    cosine = jnp.tile(jnp.cos(angles), (1, 4))
    sine = jnp.tile(jnp.sin(angles), (1, 4))
    query_gain = jnp.tile(qk_gains[0:1], (1, 2))
    key_gain = jnp.tile(qk_gains[1:2], (1, 2))
    w_in = conv_in.transpose(1, 0, 2)
    w_pair = w_keyval.reshape(width, pair_width)
    first_up = conv_gate_up.transpose(1, 2, 0).reshape(2 * hidden_units, width)
    second_up = attn_gate_up.transpose(1, 2, 0).reshape(2 * hidden_units, width)

    def shifted_rows(ext, micro_at, back):
        return ext[micro_at, 8 - back : 8 - back + rows, :]

    def conv_forward(
        in_ref, same_ref, gain_ref, win_ref, kernel_ref, wout_ref,
        x_ref, g_ref, n1_ref, pc_ref, edge_ref, y_ref, h1_ref, n2_ref,
        other, edges, normed_edges, ext, part, zslots,
        swap_send, swap_recv, edge_send, edge_recv, zs, zr, gs, gr,
    ):
        where = place()
        s, q, h = where
        partner = (1 - s, q, h)
        following = (s, lax.rem(q + 1, seqs), h)
        preceding = (s, lax.rem(q + seqs - 1, seqs), h)
        greet([partner, following, preceding] + head_peers(where, heads))
        give = pl.multiple_of((1 - s) * rows, rows)
        swap = remote(in_ref.at[0, :, pl.ds(give, rows)], other, swap_send.at[0], swap_recv.at[0], partner)
        swap.start()
        near = remote(in_ref.at[0, :, rows - 16 : rows], edges.at[0], edge_send.at[0], edge_recv.at[0], partner)
        near.start()
        far = remote(
            in_ref.at[0, :, local_rows - 16 : local_rows], edges.at[1], edge_send.at[1], edge_recv.at[1], following
        )
        far.start()
        keep = pl.multiple_of(s * rows, rows)
        swap.wait()
        mine = in_ref[0, :, pl.ds(keep, rows), :].reshape(tokens, width)
        theirs = other[...].reshape(tokens, width)
        first = s == 0
        x = jnp.where(first, mine, theirs)
        x_ref[...] = x
        g_ref[...] = jnp.where(first, theirs, mine)
        n1_ref[...] = norm_apply(x.astype(FLOAT), gain_ref[0:1, :]).astype(HALF)
        near.wait()
        far.wait()
        for m in range(micro):
            before = edges[1, max(m - 1, 0)]
            far_edge = jnp.where(q == 0, before, edges[1, m])
            edge = jnp.where(first, far_edge, edges[0, m]).astype(FLOAT)
            normed_edges[m * 16 : (m + 1) * 16, :] = norm_apply(edge, gain_ref[0:1, :]).astype(HALF)
        for k in range(3):
            pc_ref[k] = product(n1_ref[...], win_ref[k])
        edge_b = product(normed_edges[...], win_ref[0])
        edge_u = product(normed_edges[...], win_ref[2])
        edge_gated = edge_b * edge_u
        gated = pc_ref[0] * pc_ref[2]
        for m in range(micro):
            ext[m, 0:8, :] = edge_gated[m * 16 + 8 : m * 16 + 16, :]
            edge_ref[m] = edge_gated[m * 16 + 8 : m * 16 + 16, :]
            ext[m, 8 : 8 + rows, :] = gated[m * rows : (m + 1) * rows, :]
        for m in range(micro):
            span = slice(m * rows, (m + 1) * rows)
            mixed = (
                kernel_ref[2:3, :] * gated[span]
                + kernel_ref[1:2, :] * jnp.where(same_ref[span, 0:1] > 0, shifted_rows(ext, m, 1), 0.0)
                + kernel_ref[0:1, :] * jnp.where(same_ref[span, 1:2] > 0, shifted_rows(ext, m, 2), 0.0)
            )
            y_ref[span, :] = (pc_ref[1, span, :] * mixed).astype(HALF)
        part[...] = product(y_ref[...], wout_ref[...]).astype(HALF)
        copies = scatter_start(part, zslots, zs, zr, where, heads, own)
        start = x_ref[rows_of(h, own), :].astype(FLOAT)
        hidden = start + scatter_sum(copies, part, zslots, where, own)
        h1_ref[...] = hidden
        n2_ref[rows_of(h, own), :] = norm_apply(hidden, gain_ref[1:2, :]).astype(HALF)
        wait_all(gather_start(n2_ref, gs, gr, where, heads, own))

    zscratch = [pltpu.VMEM((heads - 1, own, width), HALF)]
    zsems = [dma(heads - 1)] * 4
    x, g, n1, projected, edge_gated, mixed, h1, n2 = call(
        conv_forward,
        "conv_forward",
        0,
        [
            ((tokens, width), HALF),
            ((tokens, width), HALF),
            ((tokens, width), HALF),
            ((3, tokens, channels), FLOAT),
            ((micro, 8, channels), FLOAT),
            ((tokens, channels), HALF),
            ((own, width), FLOAT),
            ((tokens, width), HALF),
        ],
        [
            pltpu.VMEM((micro, rows, width), HALF),
            pltpu.VMEM((2, micro, 16, width), HALF),
            pltpu.VMEM((micro * 16, width), HALF),
            pltpu.VMEM((micro, 8 + rows, channels), FLOAT),
            pltpu.VMEM((tokens, width), HALF),
        ]
        + zscratch
        + [dma(1), dma(1), dma(2), dma(2)]
        + zsems,
        [incoming, same, conv_gains, w_in, conv_kernel, conv_out],
        flops=10**9,
        moved=80 << 20,
    )

    def ffn_forward(normed, up, down):
        joined = back_product(normed, up)
        active = swiglu(joined).astype(HALF)
        return joined, active, product(active, down).astype(HALF)

    def ffn_backward(grad_low, joined, up, down):
        grad_active = back_product(grad_low, down)
        grad_joined = jax.vjp(swiglu, joined)[1](grad_active)[0].astype(HALF)
        return grad_joined, product(grad_joined, up).astype(HALF)

    f1, a1, part = ffn_forward(n2, first_up, conv_down)

    def enter_attention(part_ref, h1_ref, gain_ref, m_ref, n3_ref, zslots, zs, zr, gs, gr):
        where = place()
        greet(head_peers(where, heads))
        copies = scatter_start(part_ref, zslots, zs, zr, where, heads, own)
        middle = (h1_ref[...] + scatter_sum(copies, part_ref, zslots, where, own)).astype(HALF).astype(FLOAT)
        m_ref[...] = middle
        n3_ref[rows_of(where[2], own), :] = norm_apply(middle, gain_ref[0:1, :]).astype(HALF)
        wait_all(gather_start(n3_ref, gs, gr, where, heads, own))

    middle, n3 = call(
        enter_attention,
        "enter_attention",
        1,
        [((own, width), FLOAT), ((tokens, width), HALF)],
        zscratch + zsems,
        [part, h1, attn_gains],
        moved=60 << 20,
    )

    def slot_peer(me, j, h):
        other = lax.rem(me + j, slots)
        return (lax.rem(other, sections), lax.div(other, sections), h)

    def query_key(n3_ref, wq_ref, wp_ref, cos_ref, sin_ref, qg_ref, kg_ref, qr_ref, r_ref, q_ref, all_ref, send, recv):
        s, q, h = place()
        me = q * sections + s
        peers = [slot_peer(me, j, h) for j in range(1, slots)]
        greet(peers)
        cos, sin = cos_ref[...], sin_ref[...]
        r_ref[...] = product(n3_ref[...], wp_ref[...])
        half_pair = pair_width // 2
        for start, size in chunks_of(half_pair):
            span = slice(start, start + size)
            all_ref[me, :, span] = rotary(r_ref[:, span], kg_ref[...], cos, sin).astype(HALF)
        all_ref[me, :, half_pair:] = r_ref[:, half_pair:].astype(HALF)
        copies = []
        for j, peer in enumerate(peers):
            copy = remote(all_ref.at[me], all_ref.at[me], send.at[j], recv.at[j], peer)
            copy.start()
            copies.append(copy)
        qr_ref[...] = product(n3_ref[...], wq_ref[...])
        for start, size in chunks_of(query_width):
            span = slice(start, start + size)
            q_ref[:, span] = rotary(qr_ref[:, span], qg_ref[...], cos, sin).astype(HALF)
        wait_all(copies)

    query_raw, pair_raw, queries, all_pairs = call(
        query_key,
        "query_key",
        2,
        [
            ((tokens, query_width), FLOAT),
            ((tokens, pair_width), FLOAT),
            ((tokens, query_width), HALF),
            ((slots, tokens, pair_width), HALF),
        ],
        [dma(slots - 1), dma(slots - 1)],
        [n3, w_query, w_pair, cosine, sine, query_gain, key_gain],
        flops=5 * 10**8,
        moved=40 << 20,
    )

    def query_rows(ref, m, c):
        block = ref[m * rows : (m + 1) * rows, :]
        base = c * group * head_width
        return jnp.concatenate(
            [block[:, base + r * head_width : base + (r + 1) * head_width] for r in range(group)], 0
        )

    def keys_of(all_ref, at, c, kind):
        block = all_ref[:, at * rows : (at + 1) * rows, :].reshape(block_tok, pair_width)
        base = kind * kv_local * head_width + c * head_width
        return block[:, base : base + head_width]

    def allowed_pairs(segq_ref, seg_ref, m, at, s, q):
        own_segments = segq_ref[m * rows : (m + 1) * rows, :]
        allowed = own_segments == seg_ref[at : at + 1, :]
        if at == m:
            base = q * local_rows + s * rows
            order = base + lax.broadcasted_iota(jnp.int32, (rows, block_tok), 0)
            allowed = allowed & (lax.broadcasted_iota(jnp.int32, (rows, block_tok), 1) <= order)
        bias = jnp.where(allowed, 0.0, -1e30)
        return jnp.concatenate([bias] * group, 0)

    def probabilities(rows_in, keys, biases):
        scores = [
            jnp.where(bias < 0, -1e30, back_product(rows_in, key) * score_scale)
            for key, bias in zip(keys, biases)
        ]
        summit = functools.reduce(jnp.maximum, [jnp.max(part, -1, keepdims=True) for part in scores])
        raised = [jnp.exp(part - summit) for part in scores]
        total = functools.reduce(jnp.add, [jnp.sum(part, -1, keepdims=True) for part in raised])
        inverse = 1.0 / total
        return [part * inverse for part in raised]

    def attend(q_ref, all_ref, segq_ref, seg_ref, o_ref):
        s, q, _ = place()
        for m in range(micro):
            biases = [allowed_pairs(segq_ref, seg_ref, m, at, s, q) for at in range(m + 1)]
            results = []
            for c in range(kv_local):
                keys = [keys_of(all_ref, at, c, 0) for at in range(m + 1)]
                weights = probabilities(query_rows(q_ref, m, c), keys, biases)
                total = functools.reduce(
                    jnp.add,
                    [product(weights[at].astype(HALF), keys_of(all_ref, at, c, 1)) for at in range(m + 1)],
                )
                results += [total[r * rows : (r + 1) * rows] for r in range(group)]
            o_ref[m * rows : (m + 1) * rows, :] = jnp.concatenate(results, -1).astype(HALF)

    (attended,) = call(
        attend,
        "attend",
        None,
        [((tokens, query_width), HALF)],
        [],
        [queries, all_pairs, local_segments, segment_ids],
        flops=2 * 10**9,
        moved=30 << 20,
    )

    def leave_attention(o_ref, wo_ref, m_ref, gain_ref, h2_ref, n4_ref, part, zslots, zs, zr, gs, gr):
        where = place()
        greet(head_peers(where, heads))
        part[...] = product(o_ref[...], wo_ref[...]).astype(HALF)
        copies = scatter_start(part, zslots, zs, zr, where, heads, own)
        hidden = m_ref[...] + scatter_sum(copies, part, zslots, where, own)
        h2_ref[...] = hidden
        n4_ref[rows_of(where[2], own), :] = norm_apply(hidden, gain_ref[1:2, :]).astype(HALF)
        wait_all(gather_start(n4_ref, gs, gr, where, heads, own))

    part_scratch = [pltpu.VMEM((tokens, width), HALF)]
    h2, n4 = call(
        leave_attention,
        "leave_attention",
        3,
        [((own, width), FLOAT), ((tokens, width), HALF)],
        part_scratch + zscratch + zsems,
        [attended, attn_out, middle, attn_gains],
        moved=60 << 20,
    )

    f2, a2, part_y = ffn_forward(n4, second_up, attn_down)
    gf2, part_g = ffn_backward(g, f2, second_up, attn_down)

    def turn_back(
        py_ref, pg_ref, h2_ref, g_ref, gain_ref, yout_ref, gh2_ref, low_ref, gg_ref,
        yslots, zslots, ys, yr, zs, zr, gs, gr, hs, hr,
    ):
        where = place()
        mine = rows_of(where[2], own)
        greet(head_peers(where, heads))
        copies = scatter_start(pg_ref, zslots, zs, zr, where, heads, own)
        later = scatter_start(py_ref, yslots, ys, yr, where, heads, own)
        hidden = h2_ref[...]
        grad_normed = scatter_sum(copies, pg_ref, zslots, where, own)
        grad_hidden, grad_gain = norm_back(hidden, gain_ref[1:2, :], grad_normed)
        grad = g_ref[mine, :].astype(FLOAT) + grad_hidden
        gh2_ref[...] = grad
        gg_ref[...] = grad_gain
        low_ref[mine, :] = grad.astype(HALF)
        gathers = gather_start(low_ref, gs, gr, where, heads, own)
        yout_ref[mine, :] = (hidden + scatter_sum(later, py_ref, yslots, where, own)).astype(HALF)
        gathers += gather_start(yout_ref, hs, hr, where, heads, own)
        wait_all(gathers)

    yout, gh2, gh2_low, grad_gain_attn1 = call(
        turn_back,
        "turn_back",
        4,
        [((tokens, width), HALF), ((own, width), FLOAT), ((tokens, width), HALF), ((1, width), FLOAT)],
        zscratch * 2 + zsems * 2,
        [part_y, part_g, h2, g, attn_gains],
        moved=90 << 20,
    )

    def attend_back(low_ref, wo_ref, q_ref, all_ref, segq_ref, seg_ref, gq_ref, gp_ref, grads, totals):
        s, q, _ = place()
        grads[...] = back_product(low_ref[...], wo_ref[...]).astype(HALF)
        for m in range(micro):
            biases = [allowed_pairs(segq_ref, seg_ref, m, at, s, q) for at in range(m + 1)]
            results = []
            for c in range(kv_local):
                keys = [keys_of(all_ref, at, c, 0) for at in range(m + 1)]
                values = [keys_of(all_ref, at, c, 1) for at in range(m + 1)]
                rows_in = query_rows(q_ref, m, c)
                grad_rows = query_rows(grads, m, c)
                chances = probabilities(rows_in, keys, biases)
                grad_chances = [back_product(grad_rows, value) for value in values]
                inner = functools.reduce(
                    jnp.add,
                    [jnp.sum(a * b, -1, keepdims=True) for a, b in zip(grad_chances, chances)],
                )
                total = None
                for at in range(m + 1):
                    grad_scores = (chances[at] * (grad_chances[at] - inner)).astype(HALF)
                    term = product(grad_scores, keys[at])
                    total = term if total is None else total + term
                    grad_key = outer_sum(grad_scores, rows_in) * score_scale
                    grad_value = outer_sum(chances[at].astype(HALF), grad_rows)
                    if at == m:
                        totals[at, c] = grad_key
                        totals[at, kv_local + c] = grad_value
                    else:
                        totals[at, c] += grad_key
                        totals[at, kv_local + c] += grad_value
                total = total * score_scale
                results += [total[r * rows : (r + 1) * rows] for r in range(group)]
            gq_ref[m * rows : (m + 1) * rows, :] = jnp.concatenate(results, -1)
        for at in range(micro):
            joined = jnp.concatenate([totals[at, k] for k in range(2 * kv_local)], -1).astype(HALF)
            gp_ref[:, at * rows : (at + 1) * rows, :] = joined.reshape(slots, rows, pair_width)

    grad_queries, grad_pairs = call(
        attend_back,
        "attend_back",
        None,
        [((tokens, query_width), FLOAT), ((slots, tokens, pair_width), HALF)],
        [
            pltpu.VMEM((tokens, query_width), HALF),
            pltpu.VMEM((micro, 2 * kv_local, block_tok, head_width), FLOAT),
        ],
        [gh2_low, attn_out, queries, all_pairs, local_segments, segment_ids],
        flops=5 * 10**9,
        moved=50 << 20,
    )

    def back_through_entry(
        gp_ref, gq_ref, qr_ref, r_ref, cos_ref, sin_ref, qg_ref, kg_ref, wq_ref, wp_ref, m_ref, gh2_ref, gain_ref,
        bq_ref, br_ref, low_ref, gg_ref, gqk_ref,
        pair_slots, part, zslots, ps, pr, zs, zr, gs, gr,
    ):
        where = place()
        s, q, h = where
        mine = rows_of(h, own)
        me = q * sections + s
        peers = [slot_peer(me, j, h) for j in range(1, slots)]
        greet(peers + head_peers(where, heads))
        copies = []
        for j, peer in enumerate(peers):
            slot = peer[1] * sections + peer[0]
            copy = remote(gp_ref.at[slot], pair_slots.at[j], ps.at[j], pr.at[j], peer)
            copy.start()
            copies.append(copy)
        cos, sin = cos_ref[...], sin_ref[...]
        gqk_ref[...] = jnp.zeros_like(gqk_ref)
        for start, size in chunks_of(query_width):
            span = slice(start, start + size)
            grad_raw, grad_gain = rotary_back(qr_ref[:, span], qg_ref[...], cos, sin, gq_ref[:, span])
            bq_ref[:, span] = grad_raw.astype(HALF)
            gqk_ref[0:1, :size] += grad_gain
        partial = back_product(bq_ref[...], wq_ref[...])
        wait_all(copies)
        grad_pair = gp_ref[me].astype(FLOAT)
        for j in range(slots - 1):
            grad_pair = grad_pair + pair_slots[j].astype(FLOAT)
        half_pair = pair_width // 2
        for start, size in chunks_of(half_pair):
            span = slice(start, start + size)
            grad_raw, grad_gain = rotary_back(r_ref[:, span], kg_ref[...], cos, sin, grad_pair[:, span])
            br_ref[:, span] = grad_raw.astype(HALF)
            gqk_ref[1:2, :size] += grad_gain
        br_ref[:, half_pair:] = grad_pair[:, half_pair:].astype(HALF)
        part[...] = (partial + back_product(br_ref[...], wp_ref[...])).astype(HALF)
        zcopies = scatter_start(part, zslots, zs, zr, where, heads, own)
        grad_normed = scatter_sum(zcopies, part, zslots, where, own)
        grad_entry, grad_gain = norm_back(m_ref[...], gain_ref[0:1, :], grad_normed)
        gg_ref[...] = grad_gain
        low_ref[mine, :] = (gh2_ref[...] + grad_entry).astype(HALF)
        wait_all(gather_start(low_ref, gs, gr, where, heads, own))

    bq, br, gm_low, grad_gain_attn0, grad_qk = call(
        back_through_entry,
        "back_through_entry",
        5,
        [
            ((tokens, query_width), HALF),
            ((tokens, pair_width), HALF),
            ((tokens, width), HALF),
            ((1, width), FLOAT),
            ((8, 128), FLOAT),
        ],
        [pltpu.VMEM((slots - 1, tokens, pair_width), HALF)]
        + part_scratch
        + zscratch
        + [dma(slots - 1), dma(slots - 1)]
        + zsems,
        [
            grad_pairs, grad_queries, query_raw, pair_raw, cosine, sine, query_gain, key_gain,
            w_query, w_pair, middle, gh2, attn_gains,
        ],
        flops=10**9,
        moved=90 << 20,
    )

    gf1, part = ffn_backward(gm_low, f1, first_up, conv_down)

    def back_through_ffn(part_ref, h1_ref, gm_ref, gain_ref, gh1_ref, low_ref, gg_ref, zslots, zs, zr, gs, gr):
        where = place()
        mine = rows_of(where[2], own)
        greet(head_peers(where, heads))
        copies = scatter_start(part_ref, zslots, zs, zr, where, heads, own)
        grad_normed = scatter_sum(copies, part_ref, zslots, where, own)
        grad_hidden, grad_gain = norm_back(h1_ref[...], gain_ref[1:2, :], grad_normed)
        gg_ref[...] = grad_gain
        grad = gm_ref[mine, :].astype(FLOAT) + grad_hidden
        gh1_ref[...] = grad
        low_ref[mine, :] = grad.astype(HALF)
        wait_all(gather_start(low_ref, gs, gr, where, heads, own))

    gh1, gh1_low, grad_gain_conv1 = call(
        back_through_ffn,
        "back_through_ffn",
        6,
        [((own, width), FLOAT), ((tokens, width), HALF), ((1, width), FLOAT)],
        zscratch + zsems,
        [part, h1, gm_low, conv_gains],
        moved=60 << 20,
    )

    def conv_backward(
        low_ref, gh1_ref, pc_ref, edge_ref, same_ref, kernel_ref, wout_ref, win_ref, x_ref, gain_ref, yout_ref,
        bp_ref, gk_ref, gg_ref, edges_ref,
        ext, spread, gz_ext, outgoing, arrived, full, part, zslots,
        edge_send, edge_recv, swap_send, swap_recv, zs, zr, gs, gr,
    ):
        where = place()
        s, q, h = where
        mine = rows_of(h, own)
        first = s == 0
        partner = (1 - s, q, h)
        preceding = (1 - s, jnp.where(first, lax.rem(q + seqs - 1, seqs), q), h)
        following = (1 - s, jnp.where(first, q, lax.rem(q + 1, seqs)), h)
        greet([partner, preceding, following] + head_peers(where, heads))
        gated = pc_ref[0] * pc_ref[2]
        grad_y = back_product(low_ref[...], wout_ref[...])
        gz = grad_y * pc_ref[1]
        zero = jnp.zeros((8, channels), FLOAT)
        for m in range(micro):
            span = slice(m * rows, (m + 1) * rows)
            one = jnp.where(same_ref[span, 0:1] > 0, gz[span], 0.0) * kernel_ref[1:2, :]
            two = jnp.where(same_ref[span, 1:2] > 0, gz[span], 0.0) * kernel_ref[0:1, :]
            gz_ext[0, m, 0:rows, :] = one
            gz_ext[0, m, rows : rows + 8, :] = zero
            gz_ext[1, m, 0:rows, :] = two
            gz_ext[1, m, rows : rows + 8, :] = zero
            outgoing[m] = zero
            outgoing[m, 0:1, :] = two[0:1]
            outgoing[m, 1:2, :] = one[0:1] + two[1:2]
        edge = remote(outgoing, arrived, edge_send.at[0], edge_recv.at[0], preceding)
        edge.start()
        taps = [None, None, None]
        for m in range(micro):
            span = slice(m * rows, (m + 1) * rows)
            ext[m, 0:8, :] = edge_ref[m]
            ext[m, 8 : 8 + rows, :] = gated[span]
            back_one = jnp.where(same_ref[span, 0:1] > 0, shifted_rows(ext, m, 1), 0.0)
            back_two = jnp.where(same_ref[span, 1:2] > 0, shifted_rows(ext, m, 2), 0.0)
            mixed = (
                kernel_ref[2:3, :] * gated[span]
                + kernel_ref[1:2, :] * back_one
                + kernel_ref[0:1, :] * back_two
            )
            bp_ref[span, channels : 2 * channels] = (grad_y[span] * mixed).astype(HALF)
            for k, value in enumerate((back_two, back_one, gated[span])):
                term = jnp.sum(value * gz[span], 0, keepdims=True)
                taps[k] = term if taps[k] is None else taps[k] + term
        gk_ref[...] = jnp.concatenate(taps + [jnp.zeros((5, channels), FLOAT)], 0)
        for m in range(micro):
            span = slice(m * rows, (m + 1) * rows)
            spread[m] = (
                kernel_ref[2:3, :] * gz[span]
                + gz_ext[0, m, 1 : rows + 1, :]
                + gz_ext[1, m, 2 : rows + 2, :]
            )
        edge.wait()
        wrap = (s == sections - 1) & (q == seqs - 1)
        for m in range(micro):
            follow = arrived[m + 1, 0:2, :] if m + 1 < micro else jnp.zeros((2, channels), FLOAT)
            spread[m, rows - 2 : rows, :] += jnp.where(wrap, follow, arrived[m, 0:2, :])
        for m in range(micro):
            span = slice(m * rows, (m + 1) * rows)
            bp_ref[span, 0:channels] = (spread[m] * pc_ref[2, span, :]).astype(HALF)
            bp_ref[span, 2 * channels :] = (spread[m] * pc_ref[0, span, :]).astype(HALF)
        total = back_product(bp_ref[:, 0:channels], win_ref[0])
        total = total + back_product(bp_ref[:, channels : 2 * channels], win_ref[1])
        total = total + back_product(bp_ref[:, 2 * channels :], win_ref[2])
        part[...] = total.astype(HALF)
        copies = scatter_start(part, zslots, zs, zr, where, heads, own)
        start = x_ref[mine, :].astype(FLOAT)
        grad_normed = scatter_sum(copies, part, zslots, where, own)
        grad_start, grad_gain = norm_back(start, gain_ref[0:1, :], grad_normed)
        gg_ref[...] = grad_gain
        full[mine, :] = (gh1_ref[...] + grad_start).astype(HALF)
        wait_all(gather_start(full, gs, gr, where, heads, own))
        keep = pl.ds(pl.multiple_of(s * rows, rows), rows)
        edges_ref[0, :, keep, :] = jnp.where(first, full[...], yout_ref[...]).reshape(micro, rows, width)
        part[...] = jnp.where(first, yout_ref[...], full[...])
        swaps = []
        for m in range(micro):
            copy = remote(
                part.at[m * rows : (m + 1) * rows], edges_ref.at[0, m, keep], swap_send.at[m], swap_recv.at[m], partner
            )
            copy.start()
            swaps.append(copy)
        wait_all(swaps)

    bp, grad_taps, grad_gain_conv0, section_edges = call(
        conv_backward,
        "conv_backward",
        7,
        [
            ((tokens, 3 * channels), HALF),
            ((8, channels), FLOAT),
            ((1, width), FLOAT),
            ((1, micro, local_rows, width), HALF),
        ],
        [
            pltpu.VMEM((micro, 8 + rows, channels), FLOAT),
            pltpu.VMEM((micro, rows, channels), FLOAT),
            pltpu.VMEM((2, micro, rows + 8, channels), FLOAT),
            pltpu.VMEM((micro, 8, channels), FLOAT),
            pltpu.VMEM((micro, 8, channels), FLOAT),
            pltpu.VMEM((tokens, width), HALF),
            pltpu.VMEM((tokens, width), HALF),
        ]
        + zscratch
        + [dma(1), dma(1), dma(micro), dma(micro)]
        + zsems,
        [gh1_low, gh1, projected, edge_gated, same, conv_kernel, conv_out, w_in, x, conv_gains, yout],
        flops=10**9,
        moved=80 << 20,
    )

    swap_pairs = [(i, sections - 1 - i) for i in range(sections)]

    def both_tokens(array):
        return jnp.concatenate([array, lax.ppermute(array, "section", swap_pairs)], 0)

    def half_of(array):
        low, high = array[:, :half_model], array[:, half_model:]
        kept = jnp.where(section == 0, low, high)
        given = jnp.where(section == 0, high, low)
        return jnp.concatenate([kept, lax.ppermute(given, "section", swap_pairs)], 0)

    def weight_grad(former_half, latter_all):
        summed = outer_sum(former_half, latter_all).astype(HALF)
        return lax.psum_scatter(summed, "seq", scatter_dimension=0, tiled=True).astype(FLOAT)

    n4_half, g_half = half_of(n4), half_of(g)
    grad_attn_down = weight_grad(g_half, both_tokens(a2)).T
    grad_attn_up = weight_grad(n4_half, both_tokens(gf2)).reshape(-1, 2, hidden_units)
    grad_attn_out = weight_grad(half_of(gh2_low), both_tokens(attended)).T
    n3_half = half_of(n3)
    grad_mixers = weight_grad(n3_half, both_tokens(jnp.concatenate([bq, br], 1)))
    grad_query = grad_mixers[:, :query_width]
    grad_keyval = grad_mixers[:, query_width:].reshape(-1, 2, pair_width // 2)
    grad_conv_down = weight_grad(half_of(gm_low), both_tokens(a1)).T
    grad_conv_up = weight_grad(half_of(n2), both_tokens(gf1)).reshape(-1, 2, hidden_units)
    grad_conv_out = weight_grad(half_of(gh1_low), both_tokens(mixed)).T
    grad_conv_in = weight_grad(half_of(n1), both_tokens(bp)).reshape(-1, 3, channels)

    folded = grad_qk[0:2, :head_width] + grad_qk[0:2, head_width : 2 * head_width]
    gain_rows = jnp.concatenate([grad_gain_conv0, grad_gain_conv1, grad_gain_attn0, grad_gain_attn1], 0)
    gain_rows, folded = lax.psum((gain_rows, folded), ("section", "seq", "head"))
    grad_taps = lax.psum(grad_taps[0:3], ("section", "seq"))
    share = width // (sections * seqs)
    gain_share = lax.dynamic_slice_in_dim(gain_rows, (section * seqs + seq) * share, share, 1)
    return (
        section_edges,
        gain_share[0:2],
        grad_conv_in,
        grad_taps,
        grad_conv_out,
        grad_conv_up,
        grad_conv_down,
        gain_share[2:4],
        grad_query,
        grad_keyval,
        folded,
        grad_attn_out,
        grad_attn_up,
        grad_attn_down,
    )


def solution(mesh):
    return jax.shard_map(
        per_device,
        mesh=mesh,
        in_specs=(
            P("section", None, "seq", None),
            P(),
            P(None, "seq"),
            P(),
            P(None, None, "head"),
            P(None, "head"),
            P("head", None),
            P(None, None, "head"),
            P("head", None),
            P(),
            P(None, "head"),
            P(None, None, "head"),
            P(),
            P("head", None),
            P(None, None, "head"),
            P("head", None),
        ),
        out_specs=(
            P("section", None, "seq", None),
            P(None, ("section", "seq")),
            P(("section", "seq"), None, "head"),
            P(None, "head"),
            P("head", ("section", "seq")),
            P(("section", "seq"), None, "head"),
            P("head", ("section", "seq")),
            P(None, ("section", "seq")),
            P(("section", "seq"), "head"),
            P(("section", "seq"), None, "head"),
            P(),
            P("head", ("section", "seq")),
            P(("section", "seq"), None, "head"),
            P("head", ("section", "seq")),
        ),
        check_vma=False,
    )
```

```python
import functools

import jax
import jax.numpy as jnp
from jax import lax
from jax.experimental import pallas as pl
from jax.experimental.pallas import tpu as pltpu
from jax.sharding import PartitionSpec as P

EPS = 1e-05
THETA = 1000000.0
FLOAT = jnp.float32
HALF = jnp.bfloat16
MESH = pl.DeviceIdType.MESH
VMEM = pl.BlockSpec(memory_space=pltpu.VMEM)
ANY = pl.BlockSpec(memory_space=pl.ANY)


def product(former, latter):
    return jnp.dot(former, latter, preferred_element_type=FLOAT)


def outer_sum(former, latter):
    return lax.dot_general(former, latter, (((0,), (0,)), ((), ())), preferred_element_type=FLOAT)


def back_product(former, latter):
    return lax.dot_general(former, latter, (((1,), (1,)), ((), ())), preferred_element_type=FLOAT)


def norm_apply(values, gain):
    return values * lax.rsqrt(jnp.mean(values * values, -1, keepdims=True) + EPS) * gain


def norm_back(values, gain, grad):
    scale = lax.rsqrt(jnp.mean(values * values, -1, keepdims=True) + EPS)
    weighted = grad * gain
    inner = jnp.mean(weighted * values, -1, keepdims=True)
    grad_values = scale * weighted - values * (scale * scale * scale * inner)
    return grad_values, jnp.sum(grad * values * scale, 0, keepdims=True)


BLOCKS = 8
LAG = 3


def place():
    return lax.axis_index("section"), lax.axis_index("seq"), lax.axis_index("head")


def remote(source, target, send, recv, peer):
    return pltpu.make_async_remote_copy(
        src_ref=source,
        dst_ref=target,
        send_sem=send,
        recv_sem=recv,
        device_id=peer,
        device_id_type=MESH,
    )


def signal(peer):
    pl.semaphore_signal(pltpu.get_barrier_semaphore(), inc=1, device_id=peer, device_id_type=MESH)


def wait_greetings(count):
    pl.semaphore_wait(pltpu.get_barrier_semaphore(), count)


def greet(others, where=None, size=0):
    for peer in others:
        signal(peer)
    if where is None:
        wait_greetings(len(others))
        return
    section, seq, head = where
    end = (head == 0) | (head == size - 1)

    @pl.when(end)
    def _():
        signal((section, seq, jnp.where(head == 0, 1, size - 2)))
        wait_greetings(len(others) + 1)

    @pl.when(jnp.logical_not(end))
    def _():
        signal((section, seq, jnp.minimum(head + 1, size - 1)))
        signal((section, seq, jnp.maximum(head - 1, 0)))
        wait_greetings(len(others) + 2)


def seq_peers(where, seqs):
    section, seq, head = where
    return [(section, lax.rem(seq + k, seqs), head) for k in range(1, seqs)]


def rows_of(index, count):
    return pl.ds(pl.multiple_of(index * count, count), count)


def wait_all(copies):
    for copy in copies:
        copy.wait()


def start_all(copies):
    for copy in copies:
        copy.start()


def loop(count, step):
    def body(i, carried):
        step(i)
        return carried

    lax.fori_loop(0, count, body, 0)


def head_total(part, full, inbox, reduce_send, reduce_recv, gather_send, gather_recv, where, size, finish, filler=None, fillers=0):
    section, seq, head = where
    count = part.shape[0] // (2 * BLOCKS)
    last = size - 1
    end = (head == 0) | (head == last)

    def rows(flow, i):
        return rows_of(flow * BLOCKS + i, count)

    def fill(t):
        if filler is not None:

            @pl.when(t < fillers)
            def _():
                filler(t)

    def fill_rest(start):
        if fillers > start:
            loop(fillers - start, lambda i: filler(start + i))

    def reduced(flow, i, peer):
        return remote(part.at[rows(flow, i)], inbox.at[flow, i], reduce_send.at[flow, i], reduce_recv.at[flow, i], peer)

    def gathered(flow, i, peer):
        span = full.at[rows(flow, i)]
        return remote(span, span, gather_send.at[flow, i], gather_recv.at[flow, i], peer)

    @pl.when(end)
    def _():
        flow = jnp.where(head == 0, 0, 1)
        inner = (section, seq, jnp.where(head == 0, 1, last - 1))
        loop(BLOCKS, lambda i: reduced(1 - flow, i, inner).start())

        def own(i):
            reduced(flow, i, inner).wait_recv()
            total = part[rows(flow, i), :].astype(FLOAT) + inbox[flow, i].astype(FLOAT)
            full[rows(flow, i), :] = finish(flow, i, total)
            gathered(flow, i, inner).start()
            fill(i)

        loop(BLOCKS, own)
        fill_rest(BLOCKS)

        def drain(i):
            gathered(1 - flow, i, inner).wait_recv()
            reduced(1 - flow, i, inner).wait_send()
            gathered(flow, i, inner).wait_send()

        loop(BLOCKS, drain)

    @pl.when(jnp.logical_not(end))
    def _():
        low = head < size // 2
        near = jnp.where(low, 1, 0)
        ahead = (section, seq, jnp.where(low, head + 1, head - 1))
        behind = (section, seq, jnp.where(low, head - 1, head + 1))

        def add(flow, i, peer):
            reduced(flow, i, peer).wait_recv()
            span = rows(flow, i)
            part[span, :] = (part[span, :].astype(FLOAT) + inbox[flow, i].astype(FLOAT)).astype(HALF)
            reduced(flow, i, peer).start()

        def forward(flow, i, peer):
            gathered(flow, i, peer).wait_recv()
            gathered(flow, i, peer).start()

        def lagged(act, first, second, at):
            def step(i):
                fill(at + i)

                @pl.when(i < BLOCKS)
                def _():
                    act(first, i, ahead)

                @pl.when(i >= LAG)
                def _():
                    act(second, i - LAG, behind)

            loop(BLOCKS + LAG, step)

        lagged(add, near, 1 - near, 0)
        lagged(forward, 1 - near, near, BLOCKS + LAG)
        fill_rest(2 * (BLOCKS + LAG))

        def drain(i):
            reduced(near, i, ahead).wait_send()
            reduced(1 - near, i, behind).wait_send()
            gathered(1 - near, i, ahead).wait_send()
            gathered(near, i, behind).wait_send()

        loop(BLOCKS, drain)


class Carried:
    def __init__(self, sources, pieces, targets, sems):
        self.sources, self.pieces, self.targets, self.sems = sources, pieces, targets, sems
        self.copies = []

    def peers(self, where, seqs):
        return seq_peers(where, seqs) if self.pieces else []

    def start(self, where, seqs, chosen=None):
        for at, (array, kind, first, count) in enumerate(self.pieces):
            if chosen is not None and at not in chosen:
                continue
            for k, peer in enumerate(seq_peers(where, seqs)):
                source = self.sources[array].at[kind, peer[1], first : first + count]
                copy = remote(source, self.targets[at].at[k], self.sems[0].at[at, k], self.sems[1].at[at, k], peer)
                copy.start()
                self.copies.append(copy)

    def wait(self):
        wait_all(self.copies)


def turned(values):
    width = values.shape[-1]
    if width == 128:
        lane = lax.broadcasted_iota(jnp.int32, values.shape, 1)
        low = lax.rem(lane, 64) < 32
        return jnp.where(low, -pltpu.roll(values, 96, 1), pltpu.roll(values, 32, 1))
    parts = []
    for start in range(0, width, 64):
        parts += [-values[:, start + 32 : start + 64], values[:, start : start + 32]]
    return jnp.concatenate(parts, -1)


def head_mean(values):
    width = values.shape[-1]
    if width == 64:
        return jnp.mean(values, -1, keepdims=True)
    lane = lax.broadcasted_iota(jnp.int32, values.shape, 1)
    first = jnp.sum(jnp.where(lane < 64, values, 0.0), -1, keepdims=True)
    second = jnp.sum(jnp.where(lane < 64, 0.0, values), -1, keepdims=True)
    return jnp.where(lane < 64, first, second) * (1.0 / 64.0)


def chunks_of(width):
    return [(start, min(128, width - start)) for start in range(0, width, 128)]


def rotary(raw, gain, cosine, sine):
    width = raw.shape[-1]
    normed = raw * lax.rsqrt(head_mean(raw * raw) + EPS) * gain[:, :width]
    return normed * cosine[:, :width] + turned(normed) * sine[:, :width]


def rotary_back(raw, gain, cosine, sine, grad):
    width = raw.shape[-1]
    back = grad * cosine[:, :width] - turned(grad) * sine[:, :width]
    scale = lax.rsqrt(head_mean(raw * raw) + EPS)
    weighted = back * gain[:, :width]
    grad_raw = scale * weighted - raw * (scale * scale * scale * head_mean(weighted * raw))
    return grad_raw, jnp.sum(back * raw * scale, 0, keepdims=True)


def call(body, name, collective, outs, scratch, args, carried=(), flops=0, moved=0):
    params = dict(vmem_limit_bytes=60 << 20)
    if collective is not None:
        params.update(collective_id=collective, has_side_effects=True)
    arrays = []
    pieces = []
    for array, kind, first, count in carried:
        known = [i for i, other in enumerate(arrays) if other is array]
        if not known:
            arrays.append(array)
        pieces.append((known[0] if known else len(arrays) - 1, kind, first, count))
    n_in, n_out, n_arrays, n_pieces = len(args), len(outs), len(arrays), len(pieces)
    seqs = arrays[0].shape[1] if arrays else 0

    def whole(*refs):
        ins, refs = refs[:n_in], refs[n_in:]
        sources, refs = refs[:n_arrays], refs[n_arrays:]
        results, refs = refs[:n_out], refs[n_out:]
        targets, refs = refs[:n_pieces], refs[n_pieces:]
        own, sems = refs[: len(scratch)], refs[len(scratch) :]
        extra = [Carried(sources, pieces, targets, sems)] if collective is not None else []
        body(*ins, *results, *own, *extra)

    sems = [pltpu.SemaphoreType.DMA((n_pieces, seqs - 1))] * 2 if pieces else []
    shapes = [jax.ShapeDtypeStruct(out[0], out[1]) for out in outs]
    for at, _, _, count in pieces:
        shapes.append(jax.ShapeDtypeStruct((seqs - 1, count, arrays[at].shape[3]), arrays[at].dtype))
    results = pl.pallas_call(
        whole,
        name=name,
        out_shape=shapes,
        in_specs=[arg[1] if isinstance(arg, tuple) else VMEM for arg in args] + [ANY] * n_arrays,
        out_specs=[out[2] if len(out) > 2 else VMEM for out in outs] + [ANY] * n_pieces,
        scratch_shapes=list(scratch) + sems,
        compiler_params=pltpu.CompilerParams(**params),
        cost_estimate=pl.CostEstimate(flops=flops, bytes_accessed=moved, transcendentals=0),
    )(*[arg[0] if isinstance(arg, tuple) else arg for arg in args], *arrays)
    return list(results[:n_out]), list(results[n_out:])


def dma(count):
    return pltpu.SemaphoreType.DMA((count,))


def per_device(
    incoming,
    segment_ids,
    positions,
    conv_gains,
    conv_in,
    conv_kernel,
    conv_out,
    conv_gate_up,
    conv_down,
    attn_gains,
    w_query,
    w_keyval,
    qk_gains,
    attn_out,
    attn_gate_up,
    attn_down,
):
    sections = lax.axis_size("section")
    seqs = lax.axis_size("seq")
    heads = lax.axis_size("head")
    section, seq, head = place()
    micro, local_rows, width = incoming.shape[1:]
    rows = local_rows // sections
    tokens = micro * rows
    half_tokens = tokens // 2
    step_rows = half_tokens // BLOCKS
    block_tok = segment_ids.shape[1]
    length = micro * block_tok
    slots = sections * seqs
    channels = conv_in.shape[2]
    hidden_units = conv_down.shape[0]
    head_width = qk_gains.shape[1]
    query_width = w_query.shape[1]
    pair_width = 2 * w_keyval.shape[2]
    kv_local = w_keyval.shape[2] // head_width
    group = query_width // (kv_local * head_width)
    score_scale = head_width ** (-0.5)
    half_model = width // sections
    share = width // (sections * seqs)

    segments = segment_ids.reshape(length)

    def own_tokens(per_token):
        start = seq * local_rows + section * rows
        return lax.dynamic_slice_in_dim(per_token.reshape(micro, block_tok), start, rows, 1).reshape(tokens)

    def moved_back(by):
        return jnp.concatenate([jnp.full((by,), -1, jnp.int32), segments[:-by]])

    local_segments = own_tokens(segments)
    same = jnp.stack([(local_segments == own_tokens(moved_back(by))).astype(FLOAT) for by in (1, 2)], 1)
    local_segments = local_segments[:, None]
    pair_index = lax.broadcasted_iota(jnp.int32, (1, 2 * head_width), 1) % (head_width // 2)
    angle_rates = THETA ** (-2.0 * pair_index.astype(FLOAT) / head_width)
    local_positions = lax.dynamic_slice_in_dim(positions, section * rows, rows, 1).reshape(tokens)
    angles = local_positions.astype(FLOAT)[:, None] * angle_rates
    cosine, sine = jnp.cos(angles), jnp.sin(angles)
    query_gain = jnp.tile(qk_gains[0:1], (1, 2))
    key_gain = jnp.tile(qk_gains[1:2], (1, 2))
    w_in = conv_in.transpose(1, 0, 2)
    w_pair = w_keyval.reshape(width, pair_width)
    first_up = conv_gate_up.transpose(1, 2, 0)
    second_up = attn_gate_up.transpose(1, 2, 0)
    slabs = [(start, min(512, hidden_units - start)) for start in range(0, hidden_units, 512)]
    tile_width = 256
    tiles = -(-hidden_units // tile_width)
    padded_units = tiles * tile_width

    def shifted_rows(ext, micro_at, back):
        return ext[micro_at, 8 - back : 8 - back + rows, :]

    def own_rows(flow, i):
        return rows_of(flow * BLOCKS + i, step_rows)

    def kept_rows(i):
        return rows_of(i, step_rows)

    total_scratch = [pltpu.VMEM((2, BLOCKS, step_rows, width), HALF)] + [
        pltpu.SemaphoreType.DMA((2, BLOCKS)) for _ in range(4)
    ]
    part_scratch = [pltpu.VMEM((tokens, width), HALF)]

    weight_scratch = [
        pltpu.VMEM((2, hidden_units, width), HALF),
        pltpu.VMEM((hidden_units, width), HALF),
        dma(3 * len(slabs)),
    ]

    def weight_loads(up_hbm, down_hbm, up_ref, down_ref, sems):
        copies = []
        for j, (start, count) in enumerate(slabs):
            span = slice(start, start + count)
            pairs = [(up_hbm.at[0, span], up_ref.at[0, span]), (up_hbm.at[1, span], up_ref.at[1, span])]
            pairs.append((down_hbm.at[span], down_ref.at[span]))
            for k, (source, target) in enumerate(pairs):
                copies.append(pltpu.make_async_copy(source, target, sems.at[3 * j + k]))
        return copies

    def conv_forward(
        in_ref, same_ref, gain_ref, win_ref, kernel_ref, wout_ref, attn_gain_ref, up_hbm, down_hbm,
        x_ref, g_ref, n1_ref, pc_ref, edge_ref, y_ref, h1_ref, n2_ref, f1_ref, a1_ref, m_ref, n3_ref,
        other, edges, normed_edges, ext, swap_send, swap_recv, edge_send, edge_recv, up_ref, down_ref, weight_sems, acc,
        part, inbox, rs, rr, gs, gr, inbox2, rs2, rr2, gs2, gr2, carry,
    ):
        where = place()
        s, q, h = where
        partner = (1 - s, q, h)
        following = (s, lax.rem(q + 1, seqs), h)
        preceding = (s, lax.rem(q + seqs - 1, seqs), h)
        weights = weight_loads(up_hbm, down_hbm, up_ref, down_ref, weight_sems)
        start_all(weights)
        greet([partner, following, preceding], where, heads)
        give = pl.multiple_of((1 - s) * rows, rows)
        swap = remote(in_ref.at[0, :, pl.ds(give, rows)], other, swap_send.at[0], swap_recv.at[0], partner)
        swap.start()
        near = remote(in_ref.at[0, :, rows - 16 : rows], edges.at[0], edge_send.at[0], edge_recv.at[0], partner)
        near.start()
        far = remote(
            in_ref.at[0, :, local_rows - 16 : local_rows], edges.at[1], edge_send.at[1], edge_recv.at[1], following
        )
        far.start()
        keep = pl.multiple_of(s * rows, rows)
        swap.wait()
        mine = in_ref[0, :, pl.ds(keep, rows), :].reshape(tokens, width)
        theirs = other[...].reshape(tokens, width)
        first = s == 0
        x = jnp.where(first, mine, theirs)
        x_ref[...] = x
        g_ref[...] = jnp.where(first, theirs, mine)
        n1_ref[...] = norm_apply(x.astype(FLOAT), gain_ref[0:1, :]).astype(HALF)
        near.wait()
        far.wait()
        for m in range(micro):
            before = edges[1, max(m - 1, 0)]
            far_edge = jnp.where(q == 0, before, edges[1, m])
            edge = jnp.where(first, far_edge, edges[0, m]).astype(FLOAT)
            normed_edges[m * 16 : (m + 1) * 16, :] = norm_apply(edge, gain_ref[0:1, :]).astype(HALF)
        for k in range(3):
            pc_ref[k] = product(n1_ref[...], win_ref[k])
        edge_b = product(normed_edges[...], win_ref[0])
        edge_u = product(normed_edges[...], win_ref[2])
        edge_gated = edge_b * edge_u
        gated = pc_ref[0] * pc_ref[2]
        for m in range(micro):
            ext[m, 0:8, :] = edge_gated[m * 16 + 8 : m * 16 + 16, :]
            edge_ref[m] = edge_gated[m * 16 + 8 : m * 16 + 16, :]
            ext[m, 8 : 8 + rows, :] = gated[m * rows : (m + 1) * rows, :]
        for m in range(micro):
            span = slice(m * rows, (m + 1) * rows)
            mixed = (
                kernel_ref[2:3, :] * gated[span]
                + kernel_ref[1:2, :] * jnp.where(same_ref[span, 0:1] > 0, shifted_rows(ext, m, 1), 0.0)
                + kernel_ref[0:1, :] * jnp.where(same_ref[span, 1:2] > 0, shifted_rows(ext, m, 2), 0.0)
            )
            y_ref[span, :] = (pc_ref[1, span, :] * mixed).astype(HALF)
        part[...] = product(y_ref[...], wout_ref[...]).astype(HALF)

        def finish(flow, i, total):
            hidden = x_ref[own_rows(flow, i), :].astype(FLOAT) + total
            h1_ref[kept_rows(i), :] = hidden
            return norm_apply(hidden, gain_ref[1:2, :]).astype(HALF)

        head_total(part, n2_ref, inbox, rs, rr, gs, gr, where, heads, finish)
        for j, (start, count) in enumerate(slabs):
            wait_all(weights[3 * j : 3 * j + 3])
            span = slice(start, start + count)
            gate = back_product(n2_ref[...], up_ref[0, span, :])
            rise = back_product(n2_ref[...], up_ref[1, span, :])
            f1_ref[0, :, span] = gate
            f1_ref[1, :, span] = rise
            active = (gate / (1.0 + jnp.exp(-gate)) * rise).astype(HALF)
            a1_ref[:, span] = active
            term = product(active, down_ref[span, :])
            if j == 0:
                acc[...] = term
            else:
                acc[...] += term
        part[...] = acc[...].astype(HALF)

        def finish_middle(flow, i, total):
            middle = (h1_ref[kept_rows(i), :] + total).astype(HALF).astype(FLOAT)
            m_ref[kept_rows(i), :] = middle
            return norm_apply(middle, attn_gain_ref[0:1, :]).astype(HALF)

        head_total(part, n3_ref, inbox2, rs2, rr2, gs2, gr2, where, heads, finish_middle)

    (x, g, n1, projected, edge_gated, mixed, h1, n2, f1, a1, middle, n3), _ = call(
        conv_forward,
        "conv_forward",
        0,
        [
            ((tokens, width), HALF),
            ((tokens, width), HALF),
            ((tokens, width), HALF),
            ((3, tokens, channels), FLOAT),
            ((micro, 8, channels), FLOAT),
            ((tokens, channels), HALF),
            ((half_tokens, width), FLOAT),
            ((tokens, width), HALF),
            ((2, tokens, hidden_units), FLOAT),
            ((tokens, hidden_units), HALF),
            ((half_tokens, width), FLOAT),
            ((tokens, width), HALF),
        ],
        [
            pltpu.VMEM((micro, rows, width), HALF),
            pltpu.VMEM((2, micro, 16, width), HALF),
            pltpu.VMEM((micro * 16, width), HALF),
            pltpu.VMEM((micro, 8 + rows, channels), FLOAT),
            dma(1),
            dma(1),
            dma(2),
            dma(2),
        ]
        + weight_scratch
        + [pltpu.VMEM((tokens, width), FLOAT)]
        + part_scratch
        + total_scratch
        + total_scratch,
        [incoming, same, conv_gains, w_in, conv_kernel, conv_out, attn_gains, (first_up, ANY), (conv_down, ANY)],
        flops=5 * 10**9,
        moved=200 << 20,
    )

    swap_pairs = [(i, sections - 1 - i) for i in range(sections)]

    def both_tokens(array):
        return jnp.concatenate([array, lax.ppermute(array, "section", swap_pairs)], 0)

    def half_of(array):
        low, high = array[:, :half_model], array[:, half_model:]
        kept = jnp.where(section == 0, low, high)
        given = jnp.where(section == 0, high, low)
        return jnp.concatenate([kept, lax.ppermute(given, "section", swap_pairs)], 0)

    def weight_partial(former, latter):
        return outer_sum(half_of(former), both_tokens(latter)).astype(HALF).reshape(1, seqs, share, -1)

    def weight_total(piece, arrived):
        partial_sums, kind, first, count = piece
        total = lax.dynamic_index_in_dim(partial_sums[kind], seq, 0, False)[first : first + count].astype(FLOAT)
        for k in range(seqs - 1):
            total = total + arrived[k].astype(FLOAT)
        return total

    def transposed(array_ref, given_ref):
        start = pl.multiple_of(lax.axis_index("section") * half_model, 128)
        own = array_ref[:, pl.ds(start, half_model)]
        both = jnp.concatenate([own, given_ref[...]], 0)
        return both.astype(FLOAT).T.astype(HALF)

    def half_swaps(arrays, targets, send, recv, where):
        s, q, h = where
        copies = []
        for k, (array_ref, target) in enumerate(zip(arrays, targets)):
            start = pl.multiple_of((1 - s) * half_model, 128)
            copies.append(remote(array_ref.at[:, pl.ds(start, half_model)], target, send.at[k], recv.at[k], (1 - s, q, h)))
        return copies

    def latter_swap(latter, kind, start, count, send, recv, where):
        s, q, h = where
        return remote(
            latter.at[kind, 0:tokens, start : start + count],
            latter.at[kind, tokens : 2 * tokens, start : start + count],
            send,
            recv,
            (1 - s, q, h),
        )

    def gradient_tiles(former, latter, stage, partial_hbm, first_in, local_sems, send, recv, where):
        peers = seq_peers(where, seqs)

        def split(t):
            kind = lax.div(t, tiles)
            at = lax.rem(t, tiles)
            return kind, pl.ds(pl.multiple_of(at * tile_width, tile_width), tile_width)

        def stored(t, dest):
            kind, columns = split(t)
            return pltpu.make_async_copy(
                stage.at[kind, dest, :, columns], partial_hbm.at[kind, dest, :, columns], local_sems.at[t, dest]
            )

        def sent(t, k):
            kind, columns = split(t)
            return remote(
                stage.at[kind, peers[k][1], :, columns], first_in.at[k, :, columns], send.at[t, k], recv.at[t, k], peers[k]
            )

        def tile(t):
            kind, columns = split(t)
            use = jnp.where(kind == 0, 0, 1)
            result = product(former[use], latter[kind, :, columns]).astype(HALF)
            stage[kind, :, :, columns] = result.reshape(seqs, share, tile_width)
            for dest in range(seqs):
                stored(t, dest).start()

            @pl.when(kind == 0)
            def _():
                for k in range(seqs - 1):
                    sent(t, k).start()

        def finish():
            def stored_all(t):
                for dest in range(seqs):
                    stored(t, dest).wait()

            def sent_all(t):
                for k in range(seqs - 1):
                    sent(t, k).wait()

            loop(3 * tiles, stored_all)
            loop(tiles, sent_all)

        return tile, finish

    ffn_scratch = weight_scratch + [
        pltpu.VMEM((tokens, width), FLOAT),
        pltpu.VMEM((2, tokens, half_model), HALF),
        pltpu.VMEM((2, half_model, 2 * tokens), HALF),
        pltpu.VMEM((3, 2 * tokens, padded_units), HALF),
        pltpu.VMEM((3, seqs, share, padded_units), HALF),
        dma(2),
        dma(2),
        pltpu.SemaphoreType.DMA((3, len(slabs))),
        pltpu.SemaphoreType.DMA((3, len(slabs))),
        pltpu.SemaphoreType.DMA((3 * tiles, seqs)),
        pltpu.SemaphoreType.DMA((tiles, seqs - 1)),
        pltpu.SemaphoreType.DMA((tiles, seqs - 1)),
    ]
    partial_outs = [
        ((3, seqs, share, padded_units), HALF, ANY),
        ((seqs - 1, share, padded_units), HALF, ANY),
    ]

    def slot_peer(me, j, h):
        other = lax.rem(me + j, slots)
        return (lax.rem(other, sections), lax.div(other, sections), h)

    def query_key(
        n3_ref, wq_ref, wp_ref, cos_ref, sin_ref, qg_ref, kg_ref, qr_ref, r_ref, q_ref, all_ref, send, recv, carry
    ):
        s, q, h = place()
        me = q * sections + s
        peers = [slot_peer(me, j, h) for j in range(1, slots)]
        greet(peers)
        cos, sin = cos_ref[...], sin_ref[...]
        r_ref[...] = product(n3_ref[...], wp_ref[...])
        half_pair = pair_width // 2
        for start, size in chunks_of(half_pair):
            span = slice(start, start + size)
            all_ref[me, :, span] = rotary(r_ref[:, span], kg_ref[...], cos, sin).astype(HALF)
        all_ref[me, :, half_pair:] = r_ref[:, half_pair:].astype(HALF)
        copies = []
        for j, peer in enumerate(peers):
            copy = remote(all_ref.at[me], all_ref.at[me], send.at[j], recv.at[j], peer)
            copy.start()
            copies.append(copy)
        qr_ref[...] = product(n3_ref[...], wq_ref[...])
        for start, size in chunks_of(query_width):
            span = slice(start, start + size)
            q_ref[:, span] = rotary(qr_ref[:, span], qg_ref[...], cos, sin).astype(HALF)
        wait_all(copies)

    (query_raw, pair_raw, queries, all_pairs), _ = call(
        query_key,
        "query_key",
        2,
        [
            ((tokens, query_width), FLOAT),
            ((tokens, pair_width), FLOAT),
            ((tokens, query_width), HALF),
            ((slots, tokens, pair_width), HALF),
        ],
        [dma(slots - 1), dma(slots - 1)],
        [n3, w_query, w_pair, cosine, sine, query_gain, key_gain],
        flops=5 * 10**8,
        moved=40 << 20,
    )

    def query_rows(ref, m, c):
        block = ref[m * rows : (m + 1) * rows, :]
        base = c * group * head_width
        return jnp.concatenate(
            [block[:, base + r * head_width : base + (r + 1) * head_width] for r in range(group)], 0
        )

    def keys_of(all_ref, at, c, kind):
        block = all_ref[:, at * rows : (at + 1) * rows, :].reshape(block_tok, pair_width)
        base = kind * kv_local * head_width + c * head_width
        return block[:, base : base + head_width]

    def allowed_pairs(segq_ref, seg_ref, m, at, s, q):
        own_segments = segq_ref[m * rows : (m + 1) * rows, :]
        allowed = own_segments == seg_ref[at : at + 1, :]
        if at == m:
            base = q * local_rows + s * rows
            order = base + lax.broadcasted_iota(jnp.int32, (rows, block_tok), 0)
            allowed = allowed & (lax.broadcasted_iota(jnp.int32, (rows, block_tok), 1) <= order)
        bias = jnp.where(allowed, 0.0, -1e30)
        return jnp.concatenate([bias] * group, 0)

    def probabilities(rows_in, keys, biases):
        scores = [
            jnp.where(bias < 0, -1e30, back_product(rows_in, key) * score_scale)
            for key, bias in zip(keys, biases)
        ]
        summit = functools.reduce(jnp.maximum, [jnp.max(part, -1, keepdims=True) for part in scores])
        raised = [jnp.exp(part - summit) for part in scores]
        total = functools.reduce(jnp.add, [jnp.sum(part, -1, keepdims=True) for part in raised])
        inverse = 1.0 / total
        return [part * inverse for part in raised]

    def attend(q_ref, all_ref, segq_ref, seg_ref, o_ref):
        s, q, _ = place()
        for m in range(micro):
            biases = [allowed_pairs(segq_ref, seg_ref, m, at, s, q) for at in range(m + 1)]
            results = []
            for c in range(kv_local):
                keys = [keys_of(all_ref, at, c, 0) for at in range(m + 1)]
                weights = probabilities(query_rows(q_ref, m, c), keys, biases)
                total = functools.reduce(
                    jnp.add,
                    [product(weights[at].astype(HALF), keys_of(all_ref, at, c, 1)) for at in range(m + 1)],
                )
                results += [total[r * rows : (r + 1) * rows] for r in range(group)]
            o_ref[m * rows : (m + 1) * rows, :] = jnp.concatenate(results, -1).astype(HALF)

    (attended,), _ = call(
        attend,
        "attend",
        None,
        [((tokens, query_width), HALF)],
        [],
        [queries, all_pairs, local_segments, segment_ids],
        flops=2 * 10**9,
        moved=30 << 20,
    )

    def leave_attention(o_ref, wo_ref, m_ref, gain_ref, h2_ref, n4_ref, part, inbox, rs, rr, gs, gr, carry):
        where = place()
        greet([], where, heads)
        part[...] = product(o_ref[...], wo_ref[...]).astype(HALF)

        def finish(flow, i, total):
            hidden = m_ref[kept_rows(i), :] + total
            h2_ref[kept_rows(i), :] = hidden
            return norm_apply(hidden, gain_ref[1:2, :]).astype(HALF)

        head_total(part, n4_ref, inbox, rs, rr, gs, gr, where, heads, finish)

    (h2, n4), _ = call(
        leave_attention,
        "leave_attention",
        3,
        [((half_tokens, width), FLOAT), ((tokens, width), HALF)],
        part_scratch + total_scratch,
        [attended, attn_out, middle, attn_gains],
        moved=60 << 20,
    )

    def slab_width(start, count):
        return min(-(-count // tile_width) * tile_width, padded_units - start)

    def clear_padding(latter):
        if padded_units > hidden_units:
            latter[:, :, hidden_units:] = jnp.zeros((3, 2 * tokens, padded_units - hidden_units), HALF)

    def second_ffn(
        n4_ref, g_ref, h2_ref, gain_ref, up_hbm, down_hbm,
        py_ref, gh2_ref, low_ref, gg_ref, partial_hbm, first_in,
        acc_y, up_ref, down_ref, weight_sems, acc, given, former, latter, stage, hs, hr, ls, lr, local_sems, ts, tr,
        part, inbox, rs, rr, gs, gr, carry,
    ):
        where = place()
        s, q, h = where
        weights = weight_loads(up_hbm, down_hbm, up_ref, down_ref, weight_sems)
        start_all(weights)
        clear_padding(latter)
        greet([(1 - s, q, h)] + seq_peers(where, seqs), where, heads)
        halves = half_swaps([g_ref, n4_ref], [given.at[0], given.at[1]], hs, hr, where)
        start_all(halves)
        gg_ref[...] = jnp.zeros_like(gg_ref)
        swaps = []
        for j, (start, count) in enumerate(slabs):
            wait_all(weights[3 * j : 3 * j + 3])
            span = slice(start, start + count)
            gate = back_product(n4_ref[...], up_ref[0, span, :])
            rise = back_product(n4_ref[...], up_ref[1, span, :])
            grad_active = back_product(g_ref[...], down_ref[span, :])
            chance = 1.0 / (1.0 + jnp.exp(-gate))
            silu = gate * chance
            active = (silu * rise).astype(HALF)
            grad_gate = (grad_active * rise * (chance * (1.0 + gate * (1.0 - chance)))).astype(HALF)
            grad_rise = (grad_active * silu).astype(HALF)
            latter[0, 0:tokens, span] = active
            latter[1, 0:tokens, span] = grad_gate
            latter[2, 0:tokens, span] = grad_rise
            for kind in range(3):
                swap = latter_swap(
                    latter, kind, start, slab_width(start, count), ls.at[kind, j], lr.at[kind, j], where
                )
                swap.start()
                swaps.append(swap)
            term = product(grad_gate, up_ref[0, span, :]) + product(grad_rise, up_ref[1, span, :])
            term_y = product(active, down_ref[span, :])
            if j == 0:
                acc[...] = term
                acc_y[...] = term_y
            else:
                acc[...] += term
                acc_y[...] += term_y
        part[...] = acc[...].astype(HALF)

        for flow, holder in ((0, 0), (1, heads - 1)):

            @pl.when(h == holder)
            def _(flow=flow):
                acc_y[flow * half_tokens : (flow + 1) * half_tokens, :] += h2_ref[...]

        py_ref[...] = acc_y[...].astype(HALF)
        wait_all(halves)
        former[0] = transposed(g_ref, given.at[0])
        former[1] = transposed(n4_ref, given.at[1])
        wait_all(swaps)
        tile, tiles_done = gradient_tiles(
            former, latter, stage, partial_hbm, first_in, local_sems, ts, tr, where
        )

        def finish(flow, i, total):
            grad_hidden, grad_gain = norm_back(h2_ref[kept_rows(i), :], gain_ref[1:2, :], total)
            grad = g_ref[own_rows(flow, i), :].astype(FLOAT) + grad_hidden
            gh2_ref[kept_rows(i), :] = grad
            gg_ref[...] += grad_gain
            return grad.astype(HALF)

        head_total(part, low_ref, inbox, rs, rr, gs, gr, where, heads, finish, tile, 3 * tiles)
        tiles_done()

    (part_y, gh2, gh2_low, grad_gain_attn1, partial2, down2_in), _ = call(
        second_ffn,
        "second_ffn",
        4,
        [
            ((tokens, width), HALF),
            ((half_tokens, width), FLOAT),
            ((tokens, width), HALF),
            ((1, width), FLOAT),
        ]
        + partial_outs,
        [pltpu.VMEM((tokens, width), FLOAT)] + ffn_scratch + part_scratch + total_scratch,
        [n4, g, h2, attn_gains, (second_up, ANY), (attn_down, ANY)],
        flops=12 * 10**9,
        moved=150 << 20,
    )
    yout = lax.psum(part_y, "head")
    quarter = share // 4
    up2_pieces = [
        (partial2, 1, 0, 2 * quarter),
        (partial2, 1, 2 * quarter, 2 * quarter),
        (partial2, 2, 0, 2 * quarter),
        (partial2, 2, 2 * quarter, 2 * quarter),
    ]
    out2 = weight_partial(gh2_low, attended)

    def attention_backward(
        glow_ref, wo_ref, q_ref, all_ref, segq_ref, seg_ref,
        qr_ref, r_ref, cos_ref, sin_ref, qg_ref, kg_ref, wq_ref, wp_ref, m_ref, gh2_ref, gain_ref,
        bq_ref, br_ref, low_ref, gg_ref, gqk_ref,
        grads, totals, gq_ref, gp_ref, pair_slots, ps, pr,
        part, inbox, rs, rr, gs, gr, carry,
    ):
        where = place()
        s, q, h = where
        me = q * sections + s
        peers = [slot_peer(me, j, h) for j in range(1, slots)]
        greet(peers, where, heads)
        carry.start(where, seqs, [0])
        gg_ref[...] = jnp.zeros_like(gg_ref)
        gqk_ref[...] = jnp.zeros_like(gqk_ref)
        grads[...] = back_product(glow_ref[...], wo_ref[...]).astype(HALF)
        for m in range(micro):
            biases = [allowed_pairs(segq_ref, seg_ref, m, at, s, q) for at in range(m + 1)]
            results = []
            for c in range(kv_local):
                keys = [keys_of(all_ref, at, c, 0) for at in range(m + 1)]
                values = [keys_of(all_ref, at, c, 1) for at in range(m + 1)]
                rows_in = query_rows(q_ref, m, c)
                grad_rows = query_rows(grads, m, c)
                chances = probabilities(rows_in, keys, biases)
                grad_chances = [back_product(grad_rows, value) for value in values]
                inner = functools.reduce(
                    jnp.add,
                    [jnp.sum(a * b, -1, keepdims=True) for a, b in zip(grad_chances, chances)],
                )
                total = None
                for at in range(m + 1):
                    grad_scores = (chances[at] * (grad_chances[at] - inner)).astype(HALF)
                    term = product(grad_scores, keys[at])
                    total = term if total is None else total + term
                    grad_key = outer_sum(grad_scores, rows_in) * score_scale
                    grad_value = outer_sum(chances[at].astype(HALF), grad_rows)
                    if at == m:
                        totals[at, c] = grad_key
                        totals[at, kv_local + c] = grad_value
                    else:
                        totals[at, c] += grad_key
                        totals[at, kv_local + c] += grad_value
                total = total * score_scale
                results += [total[r * rows : (r + 1) * rows] for r in range(group)]
            gq_ref[m * rows : (m + 1) * rows, :] = jnp.concatenate(results, -1)
        for at in range(micro):
            joined = jnp.concatenate([totals[at, k] for k in range(2 * kv_local)], -1).astype(HALF)
            gp_ref[:, at * rows : (at + 1) * rows, :] = joined.reshape(slots, rows, pair_width)
        copies = []
        for j, peer in enumerate(peers):
            slot = peer[1] * sections + peer[0]
            copy = remote(gp_ref.at[slot], pair_slots.at[j], ps.at[j], pr.at[j], peer)
            copy.start()
            copies.append(copy)
        carry.start(where, seqs, [1, 2])
        cos, sin = cos_ref[...], sin_ref[...]
        for start, size in chunks_of(query_width):
            span = slice(start, start + size)
            grad_raw, grad_gain = rotary_back(qr_ref[:, span], qg_ref[...], cos, sin, gq_ref[:, span])
            bq_ref[:, span] = grad_raw.astype(HALF)
            gqk_ref[0:1, :size] += grad_gain
        partial = back_product(bq_ref[...], wq_ref[...])
        wait_all(copies)
        grad_pair = gp_ref[me].astype(FLOAT)
        for j in range(slots - 1):
            grad_pair = grad_pair + pair_slots[j].astype(FLOAT)
        half_pair = pair_width // 2
        for start, size in chunks_of(half_pair):
            span = slice(start, start + size)
            grad_raw, grad_gain = rotary_back(r_ref[:, span], kg_ref[...], cos, sin, grad_pair[:, span])
            br_ref[:, span] = grad_raw.astype(HALF)
            gqk_ref[1:2, :size] += grad_gain
        br_ref[:, half_pair:] = grad_pair[:, half_pair:].astype(HALF)
        part[...] = (partial + back_product(br_ref[...], wp_ref[...])).astype(HALF)

        def finish(flow, i, total):
            grad_entry, grad_gain = norm_back(m_ref[kept_rows(i), :], gain_ref[0:1, :], total)
            gg_ref[...] += grad_gain
            return (gh2_ref[kept_rows(i), :] + grad_entry).astype(HALF)

        head_total(part, low_ref, inbox, rs, rr, gs, gr, where, heads, finish)
        carry.wait()

    (bq, br, gm_low, grad_gain_attn0, grad_qk), up2_in = call(
        attention_backward,
        "attention_backward",
        5,
        [
            ((tokens, query_width), HALF),
            ((tokens, pair_width), HALF),
            ((tokens, width), HALF),
            ((1, width), FLOAT),
            ((8, 128), FLOAT),
        ],
        [
            pltpu.VMEM((tokens, query_width), HALF),
            pltpu.VMEM((micro, 2 * kv_local, block_tok, head_width), FLOAT),
            pltpu.VMEM((tokens, query_width), FLOAT),
            pltpu.VMEM((slots, tokens, pair_width), HALF),
            pltpu.VMEM((slots - 1, tokens, pair_width), HALF),
            dma(slots - 1),
            dma(slots - 1),
        ]
        + part_scratch
        + total_scratch,
        [
            gh2_low, attn_out, queries, all_pairs, local_segments, segment_ids,
            query_raw, pair_raw, cosine, sine, query_gain, key_gain, w_query, w_pair, middle, gh2, attn_gains,
        ],
        up2_pieces[:3],
        flops=6 * 10**9,
        moved=130 << 20,
    )

    def first_ffn_back(
        gm_ref, n2_ref, f1_ref, a1_ref, h1_ref, gain_ref, up_hbm, down_hbm,
        gh1_ref, low_ref, gg_ref, partial_hbm, first_in,
        up_ref, down_ref, weight_sems, acc, given, former, latter, stage, hs, hr, ls, lr, local_sems, ts, tr,
        part, inbox, rs, rr, gs, gr, carry,
    ):
        where = place()
        s, q, h = where
        weights = weight_loads(up_hbm, down_hbm, up_ref, down_ref, weight_sems)
        start_all(weights)
        clear_padding(latter)
        latter[0, 0:tokens, 0:hidden_units] = a1_ref[...]
        greet([(1 - s, q, h)] + seq_peers(where, seqs), where, heads)
        halves = half_swaps([gm_ref, n2_ref], [given.at[0], given.at[1]], hs, hr, where)
        start_all(halves)
        gg_ref[...] = jnp.zeros_like(gg_ref)
        swaps = []
        for j, (start, count) in enumerate(slabs):
            wait_all(weights[3 * j : 3 * j + 3])
            span = slice(start, start + count)
            gate = f1_ref[0, :, span]
            rise = f1_ref[1, :, span]
            grad_active = back_product(gm_ref[...], down_ref[span, :])
            chance = 1.0 / (1.0 + jnp.exp(-gate))
            grad_gate = (grad_active * rise * (chance * (1.0 + gate * (1.0 - chance)))).astype(HALF)
            grad_rise = (grad_active * (gate * chance)).astype(HALF)
            latter[1, 0:tokens, span] = grad_gate
            latter[2, 0:tokens, span] = grad_rise
            for kind in range(3):
                swap = latter_swap(
                    latter, kind, start, slab_width(start, count), ls.at[kind, j], lr.at[kind, j], where
                )
                swap.start()
                swaps.append(swap)
            term = product(grad_gate, up_ref[0, span, :]) + product(grad_rise, up_ref[1, span, :])
            if j == 0:
                acc[...] = term
            else:
                acc[...] += term
        part[...] = acc[...].astype(HALF)
        wait_all(halves)
        former[0] = transposed(gm_ref, given.at[0])
        former[1] = transposed(n2_ref, given.at[1])
        wait_all(swaps)
        tile, tiles_done = gradient_tiles(
            former, latter, stage, partial_hbm, first_in, local_sems, ts, tr, where
        )

        def finish(flow, i, total):
            grad_hidden, grad_gain = norm_back(h1_ref[kept_rows(i), :], gain_ref[1:2, :], total)
            gg_ref[...] += grad_gain
            grad = gm_ref[own_rows(flow, i), :].astype(FLOAT) + grad_hidden
            gh1_ref[kept_rows(i), :] = grad
            return grad.astype(HALF)

        head_total(part, low_ref, inbox, rs, rr, gs, gr, where, heads, finish, tile, 3 * tiles)
        tiles_done()

    (gh1, gh1_low, grad_gain_conv1, partial1, down1_in), _ = call(
        first_ffn_back,
        "first_ffn_back",
        6,
        [((half_tokens, width), FLOAT), ((tokens, width), HALF), ((1, width), FLOAT)] + partial_outs,
        ffn_scratch + part_scratch + total_scratch,
        [gm_low, n2, f1, a1, h1, conv_gains, (first_up, ANY), (conv_down, ANY)],
        flops=9 * 10**9,
        moved=150 << 20,
    )
    mixers = weight_partial(n3, jnp.concatenate([bq, br], 1))
    out2_piece, mixers_piece = (out2, 0, 0, share), (mixers, 0, 0, share)

    def conv_backward(
        low_ref, gh1_ref, pc_ref, edge_ref, same_ref, kernel_ref, wout_ref, win_ref, x_ref, gain_ref, yout_ref,
        bp_ref, gk_ref, gg_ref, edges_ref,
        ext, spread, gz_ext, outgoing, arrived, full, edge_send, edge_recv, swap_send, swap_recv,
        part, inbox, rs, rr, gs, gr, carry,
    ):
        where = place()
        s, q, h = where
        first = s == 0
        partner = (1 - s, q, h)
        preceding = (1 - s, jnp.where(first, lax.rem(q + seqs - 1, seqs), q), h)
        following = (1 - s, jnp.where(first, q, lax.rem(q + 1, seqs)), h)
        greet([partner, preceding, following] + carry.peers(where, seqs), where, heads)
        gg_ref[...] = jnp.zeros_like(gg_ref)
        gated = pc_ref[0] * pc_ref[2]
        grad_y = back_product(low_ref[...], wout_ref[...])
        gz = grad_y * pc_ref[1]
        zero = jnp.zeros((8, channels), FLOAT)
        for m in range(micro):
            span = slice(m * rows, (m + 1) * rows)
            one = jnp.where(same_ref[span, 0:1] > 0, gz[span], 0.0) * kernel_ref[1:2, :]
            two = jnp.where(same_ref[span, 1:2] > 0, gz[span], 0.0) * kernel_ref[0:1, :]
            gz_ext[0, m, 0:rows, :] = one
            gz_ext[0, m, rows : rows + 8, :] = zero
            gz_ext[1, m, 0:rows, :] = two
            gz_ext[1, m, rows : rows + 8, :] = zero
            outgoing[m] = zero
            outgoing[m, 0:1, :] = two[0:1]
            outgoing[m, 1:2, :] = one[0:1] + two[1:2]
        edge = remote(outgoing, arrived, edge_send.at[0], edge_recv.at[0], preceding)
        edge.start()
        carry.start(where, seqs)
        taps = [None, None, None]
        for m in range(micro):
            span = slice(m * rows, (m + 1) * rows)
            ext[m, 0:8, :] = edge_ref[m]
            ext[m, 8 : 8 + rows, :] = gated[span]
            back_one = jnp.where(same_ref[span, 0:1] > 0, shifted_rows(ext, m, 1), 0.0)
            back_two = jnp.where(same_ref[span, 1:2] > 0, shifted_rows(ext, m, 2), 0.0)
            mixed = (
                kernel_ref[2:3, :] * gated[span]
                + kernel_ref[1:2, :] * back_one
                + kernel_ref[0:1, :] * back_two
            )
            bp_ref[span, channels : 2 * channels] = (grad_y[span] * mixed).astype(HALF)
            for k, value in enumerate((back_two, back_one, gated[span])):
                term = jnp.sum(value * gz[span], 0, keepdims=True)
                taps[k] = term if taps[k] is None else taps[k] + term
        gk_ref[...] = jnp.concatenate(taps + [jnp.zeros((5, channels), FLOAT)], 0)
        for m in range(micro):
            span = slice(m * rows, (m + 1) * rows)
            spread[m] = (
                kernel_ref[2:3, :] * gz[span]
                + gz_ext[0, m, 1 : rows + 1, :]
                + gz_ext[1, m, 2 : rows + 2, :]
            )
        edge.wait()
        wrap = (s == sections - 1) & (q == seqs - 1)
        for m in range(micro):
            follow = arrived[m + 1, 0:2, :] if m + 1 < micro else jnp.zeros((2, channels), FLOAT)
            spread[m, rows - 2 : rows, :] += jnp.where(wrap, follow, arrived[m, 0:2, :])
        for m in range(micro):
            span = slice(m * rows, (m + 1) * rows)
            bp_ref[span, 0:channels] = (spread[m] * pc_ref[2, span, :]).astype(HALF)
            bp_ref[span, 2 * channels :] = (spread[m] * pc_ref[0, span, :]).astype(HALF)
        total = back_product(bp_ref[:, 0:channels], win_ref[0])
        total = total + back_product(bp_ref[:, channels : 2 * channels], win_ref[1])
        total = total + back_product(bp_ref[:, 2 * channels :], win_ref[2])
        part[...] = total.astype(HALF)

        def finish(flow, i, total):
            start = x_ref[own_rows(flow, i), :].astype(FLOAT)
            grad_start, grad_gain = norm_back(start, gain_ref[0:1, :], total)
            gg_ref[...] += grad_gain
            return (gh1_ref[kept_rows(i), :] + grad_start).astype(HALF)

        head_total(part, full, inbox, rs, rr, gs, gr, where, heads, finish)
        keep = pl.ds(pl.multiple_of(s * rows, rows), rows)
        edges_ref[0, :, keep, :] = jnp.where(first, full[...], yout_ref[...]).reshape(micro, rows, width)
        part[...] = jnp.where(first, yout_ref[...], full[...])
        swaps = []
        for m in range(micro):
            copy = remote(
                part.at[m * rows : (m + 1) * rows], edges_ref.at[0, m, keep], swap_send.at[m], swap_recv.at[m], partner
            )
            copy.start()
            swaps.append(copy)
        wait_all(swaps)
        carry.wait()

    (bp, grad_taps, grad_gain_conv0, section_edges), (up2_last_in, out2_in, mixers_in) = call(
        conv_backward,
        "conv_backward",
        7,
        [
            ((tokens, 3 * channels), HALF),
            ((8, channels), FLOAT),
            ((1, width), FLOAT),
            ((1, micro, local_rows, width), HALF),
        ],
        [
            pltpu.VMEM((micro, 8 + rows, channels), FLOAT),
            pltpu.VMEM((micro, rows, channels), FLOAT),
            pltpu.VMEM((2, micro, rows + 8, channels), FLOAT),
            pltpu.VMEM((micro, 8, channels), FLOAT),
            pltpu.VMEM((micro, 8, channels), FLOAT),
            pltpu.VMEM((tokens, width), HALF),
            dma(1),
            dma(1),
            dma(micro),
            dma(micro),
        ]
        + part_scratch
        + total_scratch,
        [gh1_low, gh1, projected, edge_gated, same, conv_kernel, conv_out, w_in, x, conv_gains, yout],
        [up2_pieces[3], out2_piece, mixers_piece],
        flops=10**9,
        moved=120 << 20,
    )

    out1 = weight_partial(gh1_low, mixed)
    in1 = weight_partial(n1, bp)
    last_pieces = [(partial1, 1, 0, share), (partial1, 2, 0, share), (out1, 0, 0, share), (in1, 0, 0, share)]
    folded = grad_qk[0:2, :head_width] + grad_qk[0:2, head_width : 2 * head_width]
    gain_rows = jnp.concatenate([grad_gain_conv0, grad_gain_conv1, grad_gain_attn0, grad_gain_attn1], 0)
    small_width = max(share, channels, 2 * head_width)

    def to_width(array):
        return jnp.pad(array, [(0, 0)] * (array.ndim - 1) + [(0, small_width - array.shape[-1])])

    def to_all(array):
        return jnp.broadcast_to(to_width(array), (slots,) + array.shape[:-1] + (small_width,))

    small = jnp.concatenate(
        [
            to_width(gain_rows.reshape(4, slots, share).transpose(1, 0, 2)),
            to_all(folded.reshape(1, 2 * head_width)),
            to_all(grad_taps[0:3]),
        ],
        1,
    )

    def last_sums(small_ref, out_ref, boxes, summed, final, hs, hr, ss, sr, carry):
        where = place()
        s, q, h = where
        others = [(s, q, lax.rem(h + k, heads)) for k in range(1, heads)]
        me = q * sections + s
        peers = [slot_peer(me, j, h) for j in range(1, slots)]
        greet(others + peers)
        copies = []
        for k, peer in enumerate(others):
            copy = remote(small_ref, boxes.at[k], hs.at[k], hr.at[k], peer)
            copy.start()
            copies.append(copy)
        carry.start(where, seqs)
        wait_all(copies)
        over_heads = boxes[0]
        for k in range(1, heads - 1):
            over_heads = over_heads + boxes[k]
        row = lax.broadcasted_iota(jnp.int32, over_heads.shape, 1)
        summed[...] = small_ref[...] + jnp.where(row < 5, over_heads, 0.0)
        copies = []
        for j, peer in enumerate(peers):
            copy = remote(summed.at[peer[0] * seqs + peer[1]], final.at[j], ss.at[j], sr.at[j], peer)
            copy.start()
            copies.append(copy)
        total = summed[s * seqs + q]
        wait_all(copies)
        for j in range(slots - 1):
            total = total + final[j]
        out_ref[...] = total
        carry.wait()

    (sums,), (gate1_in, rise1_in, out1_in, in1_in) = call(
        last_sums,
        "last_sums",
        8,
        [((8, small_width), FLOAT)],
        [
            pltpu.VMEM((heads - 1, slots, 8, small_width), FLOAT),
            pltpu.VMEM((slots, 8, small_width), FLOAT),
            pltpu.VMEM((slots - 1, 8, small_width), FLOAT),
            dma(heads - 1),
            dma(heads - 1),
            dma(slots - 1),
            dma(slots - 1),
        ],
        [small],
        last_pieces,
        moved=150 << 20,
    )

    grad_mixers = weight_total(mixers_piece, mixers_in)
    gate2, rise2 = [
        jnp.concatenate([weight_total(p, a) for p, a in pairs], 0)[:, :hidden_units]
        for pairs in (
            list(zip(up2_pieces[:2], up2_in[:2])),
            list(zip(up2_pieces[2:], [up2_in[2], up2_last_in])),
        )
    ]
    gate1 = weight_total(last_pieces[0], gate1_in)[:, :hidden_units]
    rise1 = weight_total(last_pieces[1], rise1_in)[:, :hidden_units]
    return (
        section_edges,
        sums[0:2, :share],
        weight_total(last_pieces[3], in1_in).reshape(-1, 3, channels),
        sums[5:8, :channels],
        weight_total(last_pieces[2], out1_in).T,
        jnp.stack([gate1, rise1], 1),
        weight_total((partial1, 0, 0, share), down1_in)[:, :hidden_units].T,
        sums[2:4, :share],
        grad_mixers[:, :query_width],
        grad_mixers[:, query_width:].reshape(-1, 2, pair_width // 2),
        sums[4, : 2 * head_width].reshape(2, head_width),
        weight_total(out2_piece, out2_in).T,
        jnp.stack([gate2, rise2], 1),
        weight_total((partial2, 0, 0, share), down2_in)[:, :hidden_units].T,
    )


def solution(mesh):
    return jax.shard_map(
        per_device,
        mesh=mesh,
        in_specs=(
            P("section", None, "seq", None),
            P(),
            P(None, "seq"),
            P(),
            P(None, None, "head"),
            P(None, "head"),
            P("head", None),
            P(None, None, "head"),
            P("head", None),
            P(),
            P(None, "head"),
            P(None, None, "head"),
            P(),
            P("head", None),
            P(None, None, "head"),
            P("head", None),
        ),
        out_specs=(
            P("section", None, "seq", None),
            P(None, ("section", "seq")),
            P(("section", "seq"), None, "head"),
            P(None, "head"),
            P("head", ("section", "seq")),
            P(("section", "seq"), None, "head"),
            P("head", ("section", "seq")),
            P(None, ("section", "seq")),
            P(("section", "seq"), "head"),
            P(("section", "seq"), None, "head"),
            P(),
            P("head", ("section", "seq")),
            P(("section", "seq"), None, "head"),
            P("head", ("section", "seq")),
        ),
        check_vma=False,
    )
```

```python
import functools

import jax
import jax.numpy as jnp
from jax import lax
from jax.experimental import pallas as pl
from jax.experimental.pallas import tpu as pltpu
from jax.sharding import PartitionSpec as P

EPS = 1e-05
THETA = 1000000.0
FLOAT = jnp.float32
HALF = jnp.bfloat16
MESH = pl.DeviceIdType.MESH
VMEM = pl.BlockSpec(memory_space=pltpu.VMEM)
ANY = pl.BlockSpec(memory_space=pl.ANY)


def product(former, latter):
    return jnp.dot(former, latter, preferred_element_type=FLOAT)


def outer_sum(former, latter):
    return lax.dot_general(former, latter, (((0,), (0,)), ((), ())), preferred_element_type=FLOAT)


def back_product(former, latter):
    return lax.dot_general(former, latter, (((1,), (1,)), ((), ())), preferred_element_type=FLOAT)


def norm_apply(values, gain):
    return values * lax.rsqrt(jnp.mean(values * values, -1, keepdims=True) + EPS) * gain


def norm_back(values, gain, grad):
    scale = lax.rsqrt(jnp.mean(values * values, -1, keepdims=True) + EPS)
    weighted = grad * gain
    inner = jnp.mean(weighted * values, -1, keepdims=True)
    grad_values = scale * weighted - values * (scale * scale * scale * inner)
    return grad_values, jnp.sum(grad * values * scale, 0, keepdims=True)


BLOCKS = 8
LAG = 3


def place():
    return lax.axis_index("section"), lax.axis_index("seq"), lax.axis_index("head")


def remote(source, target, send, recv, peer):
    return pltpu.make_async_remote_copy(
        src_ref=source,
        dst_ref=target,
        send_sem=send,
        recv_sem=recv,
        device_id=peer,
        device_id_type=MESH,
    )


def signal(peer):
    pl.semaphore_signal(pltpu.get_barrier_semaphore(), inc=1, device_id=peer, device_id_type=MESH)


def wait_greetings(count):
    pl.semaphore_wait(pltpu.get_barrier_semaphore(), count)


def greet(others, where=None, size=0):
    for peer in others:
        signal(peer)
    if where is None:
        wait_greetings(len(others))
        return
    section, seq, head = where
    end = (head == 0) | (head == size - 1)

    @pl.when(end)
    def _():
        signal((section, seq, jnp.where(head == 0, 1, size - 2)))
        wait_greetings(len(others) + 1)

    @pl.when(jnp.logical_not(end))
    def _():
        signal((section, seq, jnp.minimum(head + 1, size - 1)))
        signal((section, seq, jnp.maximum(head - 1, 0)))
        wait_greetings(len(others) + 2)


def seq_peers(where, seqs):
    section, seq, head = where
    return [(section, lax.rem(seq + k, seqs), head) for k in range(1, seqs)]


def rows_of(index, count):
    return pl.ds(pl.multiple_of(index * count, count), count)


def wait_all(copies):
    for copy in copies:
        copy.wait()


def start_all(copies):
    for copy in copies:
        copy.start()


def loop(count, step):
    def body(i, carried):
        step(i)
        return carried

    lax.fori_loop(0, count, body, 0)


def head_total(part, full, inbox, reduce_send, reduce_recv, gather_send, gather_recv, where, size, finish, filler=None, fillers=0):
    section, seq, head = where
    count = part.shape[0] // (2 * BLOCKS)
    last = size - 1
    end = (head == 0) | (head == last)

    def rows(flow, i):
        return rows_of(flow * BLOCKS + i, count)

    def fill(t):
        if filler is not None:

            @pl.when(t < fillers)
            def _():
                filler(t)

    def fill_rest(start):
        if fillers > start:
            loop(fillers - start, lambda i: filler(start + i))

    def reduced(flow, i, peer):
        return remote(part.at[rows(flow, i)], inbox.at[flow, i], reduce_send.at[flow, i], reduce_recv.at[flow, i], peer)

    def gathered(flow, i, peer):
        span = full.at[rows(flow, i)]
        return remote(span, span, gather_send.at[flow, i], gather_recv.at[flow, i], peer)

    @pl.when(end)
    def _():
        flow = jnp.where(head == 0, 0, 1)
        inner = (section, seq, jnp.where(head == 0, 1, last - 1))
        loop(BLOCKS, lambda i: reduced(1 - flow, i, inner).start())

        def own(i):
            reduced(flow, i, inner).wait_recv()
            total = part[rows(flow, i), :].astype(FLOAT) + inbox[flow, i].astype(FLOAT)
            full[rows(flow, i), :] = finish(flow, i, total)
            gathered(flow, i, inner).start()
            fill(i)

        loop(BLOCKS, own)
        fill_rest(BLOCKS)

        def drain(i):
            gathered(1 - flow, i, inner).wait_recv()
            reduced(1 - flow, i, inner).wait_send()
            gathered(flow, i, inner).wait_send()

        loop(BLOCKS, drain)

    @pl.when(jnp.logical_not(end))
    def _():
        low = head < size // 2
        near = jnp.where(low, 1, 0)
        ahead = (section, seq, jnp.where(low, head + 1, head - 1))
        behind = (section, seq, jnp.where(low, head - 1, head + 1))

        def add(flow, i, peer):
            reduced(flow, i, peer).wait_recv()
            span = rows(flow, i)
            part[span, :] = (part[span, :].astype(FLOAT) + inbox[flow, i].astype(FLOAT)).astype(HALF)
            reduced(flow, i, peer).start()

        def forward(flow, i, peer):
            gathered(flow, i, peer).wait_recv()
            gathered(flow, i, peer).start()

        def lagged(act, first, second, at):
            def step(i):
                fill(at + i)

                @pl.when(i < BLOCKS)
                def _():
                    act(first, i, ahead)

                @pl.when(i >= LAG)
                def _():
                    act(second, i - LAG, behind)

            loop(BLOCKS + LAG, step)

        lagged(add, near, 1 - near, 0)
        lagged(forward, 1 - near, near, BLOCKS + LAG)
        fill_rest(2 * (BLOCKS + LAG))

        def drain(i):
            reduced(near, i, ahead).wait_send()
            reduced(1 - near, i, behind).wait_send()
            gathered(1 - near, i, ahead).wait_send()
            gathered(near, i, behind).wait_send()

        loop(BLOCKS, drain)


class Carried:
    def __init__(self, sources, pieces, targets, sems):
        self.sources, self.pieces, self.targets, self.sems = sources, pieces, targets, sems
        self.copies = []

    def peers(self, where, seqs):
        return seq_peers(where, seqs) if self.pieces else []

    def start(self, where, seqs, chosen=None):
        for at, (array, kind, first, count, left, wide) in enumerate(self.pieces):
            if chosen is not None and at not in chosen:
                continue
            for k, peer in enumerate(seq_peers(where, seqs)):
                source = self.sources[array].at[kind, peer[1], first : first + count, left : left + wide]
                copy = remote(source, self.targets[at].at[k], self.sems[0].at[at, k], self.sems[1].at[at, k], peer)
                copy.start()
                self.copies.append(copy)

    def wait(self):
        wait_all(self.copies)


def turned(values):
    width = values.shape[-1]
    if width == 128:
        lane = lax.broadcasted_iota(jnp.int32, values.shape, 1)
        low = lax.rem(lane, 64) < 32
        return jnp.where(low, -pltpu.roll(values, 96, 1), pltpu.roll(values, 32, 1))
    parts = []
    for start in range(0, width, 64):
        parts += [-values[:, start + 32 : start + 64], values[:, start : start + 32]]
    return jnp.concatenate(parts, -1)


def head_mean(values):
    width = values.shape[-1]
    if width == 64:
        return jnp.mean(values, -1, keepdims=True)
    lane = lax.broadcasted_iota(jnp.int32, values.shape, 1)
    first = jnp.sum(jnp.where(lane < 64, values, 0.0), -1, keepdims=True)
    second = jnp.sum(jnp.where(lane < 64, 0.0, values), -1, keepdims=True)
    return jnp.where(lane < 64, first, second) * (1.0 / 64.0)


def chunks_of(width):
    return [(start, min(128, width - start)) for start in range(0, width, 128)]


def rotary(raw, gain, cosine, sine):
    width = raw.shape[-1]
    normed = raw * lax.rsqrt(head_mean(raw * raw) + EPS) * gain[:, :width]
    return normed * cosine[:, :width] + turned(normed) * sine[:, :width]


def rotary_back(raw, gain, cosine, sine, grad):
    width = raw.shape[-1]
    back = grad * cosine[:, :width] - turned(grad) * sine[:, :width]
    scale = lax.rsqrt(head_mean(raw * raw) + EPS)
    weighted = back * gain[:, :width]
    grad_raw = scale * weighted - raw * (scale * scale * scale * head_mean(weighted * raw))
    return grad_raw, jnp.sum(back * raw * scale, 0, keepdims=True)


def call(body, name, collective, outs, scratch, args, carried=(), flops=0, moved=0):
    params = dict(vmem_limit_bytes=60 << 20)
    if collective is not None:
        params.update(collective_id=collective, has_side_effects=True)
    arrays = []
    pieces = []
    for array, kind, first, count, left, wide in carried:
        known = [i for i, other in enumerate(arrays) if other is array]
        if not known:
            arrays.append(array)
        pieces.append((known[0] if known else len(arrays) - 1, kind, first, count, left, wide))
    n_in, n_out, n_arrays, n_pieces = len(args), len(outs), len(arrays), len(pieces)
    seqs = arrays[0].shape[1] if arrays else 0

    def whole(*refs):
        ins, refs = refs[:n_in], refs[n_in:]
        sources, refs = refs[:n_arrays], refs[n_arrays:]
        results, refs = refs[:n_out], refs[n_out:]
        targets, refs = refs[:n_pieces], refs[n_pieces:]
        own, sems = refs[: len(scratch)], refs[len(scratch) :]
        extra = [Carried(sources, pieces, targets, sems)] if collective is not None else []
        body(*ins, *results, *own, *extra)

    sems = [pltpu.SemaphoreType.DMA((n_pieces, seqs - 1))] * 2 if pieces else []
    shapes = [jax.ShapeDtypeStruct(out[0], out[1]) for out in outs]
    for at, _, _, count, _, wide in pieces:
        shapes.append(jax.ShapeDtypeStruct((seqs - 1, count, wide), arrays[at].dtype))
    results = pl.pallas_call(
        whole,
        name=name,
        out_shape=shapes,
        in_specs=[arg[1] if isinstance(arg, tuple) else VMEM for arg in args] + [ANY] * n_arrays,
        out_specs=[out[2] if len(out) > 2 else VMEM for out in outs] + [ANY] * n_pieces,
        scratch_shapes=list(scratch) + sems,
        compiler_params=pltpu.CompilerParams(**params),
        cost_estimate=pl.CostEstimate(flops=flops, bytes_accessed=moved, transcendentals=0),
    )(*[arg[0] if isinstance(arg, tuple) else arg for arg in args], *arrays)
    return list(results[:n_out]), list(results[n_out:])


def dma(count):
    return pltpu.SemaphoreType.DMA((count,))


def per_device(
    incoming,
    segment_ids,
    positions,
    conv_gains,
    conv_in,
    conv_kernel,
    conv_out,
    conv_gate_up,
    conv_down,
    attn_gains,
    w_query,
    w_keyval,
    qk_gains,
    attn_out,
    attn_gate_up,
    attn_down,
):
    sections = lax.axis_size("section")
    seqs = lax.axis_size("seq")
    heads = lax.axis_size("head")
    section, seq, head = place()
    micro, local_rows, width = incoming.shape[1:]
    rows = local_rows // sections
    tokens = micro * rows
    half_tokens = tokens // 2
    step_rows = half_tokens // BLOCKS
    block_tok = segment_ids.shape[1]
    length = micro * block_tok
    slots = sections * seqs
    channels = conv_in.shape[2]
    hidden_units = conv_down.shape[0]
    head_width = qk_gains.shape[1]
    query_width = w_query.shape[1]
    pair_width = 2 * w_keyval.shape[2]
    kv_local = w_keyval.shape[2] // head_width
    group = query_width // (kv_local * head_width)
    score_scale = head_width ** (-0.5)
    half_model = width // sections
    share = width // (sections * seqs)

    segments = segment_ids.reshape(length)

    def own_tokens(per_token):
        start = seq * local_rows + section * rows
        return lax.dynamic_slice_in_dim(per_token.reshape(micro, block_tok), start, rows, 1).reshape(tokens)

    def moved_back(by):
        return jnp.concatenate([jnp.full((by,), -1, jnp.int32), segments[:-by]])

    local_segments = own_tokens(segments)
    same = jnp.stack([(local_segments == own_tokens(moved_back(by))).astype(FLOAT) for by in (1, 2)], 1)
    local_segments = local_segments[:, None]
    pair_index = lax.broadcasted_iota(jnp.int32, (1, 2 * head_width), 1) % (head_width // 2)
    angle_rates = THETA ** (-2.0 * pair_index.astype(FLOAT) / head_width)
    local_positions = lax.dynamic_slice_in_dim(positions, section * rows, rows, 1).reshape(tokens)
    angles = local_positions.astype(FLOAT)[:, None] * angle_rates
    cosine, sine = jnp.cos(angles), jnp.sin(angles)
    query_gain = jnp.tile(qk_gains[0:1], (1, 2))
    key_gain = jnp.tile(qk_gains[1:2], (1, 2))
    w_in = conv_in.transpose(1, 0, 2)
    w_pair = w_keyval.reshape(width, pair_width)
    first_up = conv_gate_up.transpose(1, 2, 0)
    second_up = attn_gate_up.transpose(1, 2, 0)
    slabs = [(start, min(512, hidden_units - start)) for start in range(0, hidden_units, 512)]
    tile_width = 256
    tiles = -(-hidden_units // tile_width)
    padded_units = tiles * tile_width

    def shifted_rows(ext, micro_at, back):
        return ext[micro_at, 8 - back : 8 - back + rows, :]

    def own_rows(flow, i):
        return rows_of(flow * BLOCKS + i, step_rows)

    def kept_rows(i):
        return rows_of(i, step_rows)

    total_scratch = [pltpu.VMEM((2, BLOCKS, step_rows, width), HALF)] + [
        pltpu.SemaphoreType.DMA((2, BLOCKS)) for _ in range(4)
    ]
    part_scratch = [pltpu.VMEM((tokens, width), HALF)]

    weight_scratch = [
        pltpu.VMEM((2, hidden_units, width), HALF),
        pltpu.VMEM((hidden_units, width), HALF),
        dma(3 * len(slabs)),
    ]

    def weight_loads(up_hbm, down_hbm, up_ref, down_ref, sems):
        copies = []
        for j, (start, count) in enumerate(slabs):
            span = slice(start, start + count)
            pairs = [(up_hbm.at[0, span], up_ref.at[0, span]), (up_hbm.at[1, span], up_ref.at[1, span])]
            pairs.append((down_hbm.at[span], down_ref.at[span]))
            for k, (source, target) in enumerate(pairs):
                copies.append(pltpu.make_async_copy(source, target, sems.at[3 * j + k]))
        return copies

    def conv_forward(
        in_ref, same_ref, gain_ref, win_ref, kernel_ref, wout_ref, attn_gain_ref, up_hbm, down_hbm,
        x_ref, g_ref, n1_ref, pc_ref, edge_ref, y_ref, h1_ref, n2_ref, f1_ref, a1_ref, m_ref, n3_ref,
        other, edges, normed_edges, ext, swap_send, swap_recv, edge_send, edge_recv, up_ref, down_ref, weight_sems, acc,
        part, inbox, rs, rr, gs, gr, inbox2, rs2, rr2, gs2, gr2, carry,
    ):
        where = place()
        s, q, h = where
        partner = (1 - s, q, h)
        following = (s, lax.rem(q + 1, seqs), h)
        preceding = (s, lax.rem(q + seqs - 1, seqs), h)
        weights = weight_loads(up_hbm, down_hbm, up_ref, down_ref, weight_sems)
        start_all(weights)
        greet([partner, following, preceding], where, heads)
        give = pl.multiple_of((1 - s) * rows, rows)
        swap = remote(in_ref.at[0, :, pl.ds(give, rows)], other, swap_send.at[0], swap_recv.at[0], partner)
        swap.start()
        near = remote(in_ref.at[0, :, rows - 16 : rows], edges.at[0], edge_send.at[0], edge_recv.at[0], partner)
        near.start()
        far = remote(
            in_ref.at[0, :, local_rows - 16 : local_rows], edges.at[1], edge_send.at[1], edge_recv.at[1], following
        )
        far.start()
        keep = pl.multiple_of(s * rows, rows)
        swap.wait()
        mine = in_ref[0, :, pl.ds(keep, rows), :].reshape(tokens, width)
        theirs = other[...].reshape(tokens, width)
        first = s == 0
        x = jnp.where(first, mine, theirs)
        x_ref[...] = x
        g_ref[...] = jnp.where(first, theirs, mine)
        n1_ref[...] = norm_apply(x.astype(FLOAT), gain_ref[0:1, :]).astype(HALF)
        near.wait()
        far.wait()
        for m in range(micro):
            before = edges[1, max(m - 1, 0)]
            far_edge = jnp.where(q == 0, before, edges[1, m])
            edge = jnp.where(first, far_edge, edges[0, m]).astype(FLOAT)
            normed_edges[m * 16 : (m + 1) * 16, :] = norm_apply(edge, gain_ref[0:1, :]).astype(HALF)
        for k in range(3):
            pc_ref[k] = product(n1_ref[...], win_ref[k])
        edge_b = product(normed_edges[...], win_ref[0])
        edge_u = product(normed_edges[...], win_ref[2])
        edge_gated = edge_b * edge_u
        gated = pc_ref[0] * pc_ref[2]
        for m in range(micro):
            ext[m, 0:8, :] = edge_gated[m * 16 + 8 : m * 16 + 16, :]
            edge_ref[m] = edge_gated[m * 16 + 8 : m * 16 + 16, :]
            ext[m, 8 : 8 + rows, :] = gated[m * rows : (m + 1) * rows, :]
        for m in range(micro):
            span = slice(m * rows, (m + 1) * rows)
            mixed = (
                kernel_ref[2:3, :] * gated[span]
                + kernel_ref[1:2, :] * jnp.where(same_ref[span, 0:1] > 0, shifted_rows(ext, m, 1), 0.0)
                + kernel_ref[0:1, :] * jnp.where(same_ref[span, 1:2] > 0, shifted_rows(ext, m, 2), 0.0)
            )
            y_ref[span, :] = (pc_ref[1, span, :] * mixed).astype(HALF)
        part[...] = product(y_ref[...], wout_ref[...]).astype(HALF)

        def finish(flow, i, total):
            hidden = x_ref[own_rows(flow, i), :].astype(FLOAT) + total
            h1_ref[kept_rows(i), :] = hidden
            return norm_apply(hidden, gain_ref[1:2, :]).astype(HALF)

        head_total(part, n2_ref, inbox, rs, rr, gs, gr, where, heads, finish)
        for j, (start, count) in enumerate(slabs):
            wait_all(weights[3 * j : 3 * j + 3])
            span = slice(start, start + count)
            gate = back_product(n2_ref[...], up_ref[0, span, :])
            rise = back_product(n2_ref[...], up_ref[1, span, :])
            f1_ref[0, :, span] = gate
            f1_ref[1, :, span] = rise
            active = (gate / (1.0 + jnp.exp(-gate)) * rise).astype(HALF)
            a1_ref[:, span] = active
            term = product(active, down_ref[span, :])
            if j == 0:
                acc[...] = term
            else:
                acc[...] += term
        part[...] = acc[...].astype(HALF)

        def finish_middle(flow, i, total):
            middle = (h1_ref[kept_rows(i), :] + total).astype(HALF).astype(FLOAT)
            m_ref[kept_rows(i), :] = middle
            return norm_apply(middle, attn_gain_ref[0:1, :]).astype(HALF)

        head_total(part, n3_ref, inbox2, rs2, rr2, gs2, gr2, where, heads, finish_middle)

    (x, g, n1, projected, edge_gated, mixed, h1, n2, f1, a1, middle, n3), _ = call(
        conv_forward,
        "conv_forward",
        0,
        [
            ((tokens, width), HALF),
            ((tokens, width), HALF),
            ((tokens, width), HALF),
            ((3, tokens, channels), FLOAT),
            ((micro, 8, channels), FLOAT),
            ((tokens, channels), HALF),
            ((half_tokens, width), FLOAT),
            ((tokens, width), HALF),
            ((2, tokens, hidden_units), FLOAT),
            ((tokens, hidden_units), HALF),
            ((half_tokens, width), FLOAT),
            ((tokens, width), HALF),
        ],
        [
            pltpu.VMEM((micro, rows, width), HALF),
            pltpu.VMEM((2, micro, 16, width), HALF),
            pltpu.VMEM((micro * 16, width), HALF),
            pltpu.VMEM((micro, 8 + rows, channels), FLOAT),
            dma(1),
            dma(1),
            dma(2),
            dma(2),
        ]
        + weight_scratch
        + [pltpu.VMEM((tokens, width), FLOAT)]
        + part_scratch
        + total_scratch
        + total_scratch,
        [incoming, same, conv_gains, w_in, conv_kernel, conv_out, attn_gains, (first_up, ANY), (conv_down, ANY)],
        flops=5 * 10**9,
        moved=200 << 20,
    )


    def transposed(array_ref, given_ref):
        start = pl.multiple_of(lax.axis_index("section") * half_model, 128)
        own = array_ref[:, pl.ds(start, half_model)]
        both = jnp.concatenate([own, given_ref[...]], 0)
        return both.astype(FLOAT).T.astype(HALF)

    def half_swaps(arrays, targets, send, recv, where):
        s, q, h = where
        copies = []
        for k, (array_ref, target) in enumerate(zip(arrays, targets)):
            start = pl.multiple_of((1 - s) * half_model, 128)
            copies.append(remote(array_ref.at[:, pl.ds(start, half_model)], target, send.at[k], recv.at[k], (1 - s, q, h)))
        return copies

    def latter_swap(latter, kind, start, count, send, recv, where):
        s, q, h = where
        return remote(
            latter.at[kind, 0:tokens, start : start + count],
            latter.at[kind, tokens : 2 * tokens, start : start + count],
            send,
            recv,
            (1 - s, q, h),
        )

    def gradient_tiles(former, latter, stage, partial_hbm, first_in, local_sems, send, recv, where, at_once):
        peers = seq_peers(where, seqs)

        def split(t):
            kind = lax.div(t, tiles)
            at = lax.rem(t, tiles)
            return kind, pl.ds(pl.multiple_of(at * tile_width, tile_width), tile_width)

        def stored(t, dest):
            kind, columns = split(t)
            return pltpu.make_async_copy(
                stage.at[kind, dest, :, columns], partial_hbm.at[kind, dest, :, columns], local_sems.at[t, dest]
            )

        def sent(t, k):
            kind, columns = split(t)
            return remote(
                stage.at[kind, peers[k][1], :, columns], first_in.at[k, :, columns], send.at[t, k], recv.at[t, k], peers[k]
            )

        def tile(t):
            kind, columns = split(t)
            use = jnp.where(kind == 0, 0, 1)
            result = product(former[use], latter[kind, :, columns]).astype(HALF)
            stage[kind, :, :, columns] = result.reshape(seqs, share, tile_width)
            for dest in range(seqs):
                stored(t, dest).start()

            @pl.when(t < at_once)
            def _():
                for k in range(seqs - 1):
                    sent(t, k).start()

        def finish():
            def stored_all(t):
                for dest in range(seqs):
                    stored(t, dest).wait()

            def sent_all(t):
                for k in range(seqs - 1):
                    sent(t, k).wait()

            loop(3 * tiles, stored_all)
            loop(at_once, sent_all)

        return tile, finish

    ffn_scratch = weight_scratch + [
        pltpu.VMEM((tokens, width), FLOAT),
        pltpu.VMEM((2, tokens, half_model), HALF),
        pltpu.VMEM((2, half_model, 2 * tokens), HALF),
        pltpu.VMEM((3, 2 * tokens, padded_units), HALF),
        pltpu.VMEM((3, seqs, share, padded_units), HALF),
        dma(2),
        dma(2),
        pltpu.SemaphoreType.DMA((3, len(slabs))),
        pltpu.SemaphoreType.DMA((3, len(slabs))),
        pltpu.SemaphoreType.DMA((3 * tiles, seqs)),
        pltpu.SemaphoreType.DMA((tiles, seqs - 1)),
        pltpu.SemaphoreType.DMA((tiles, seqs - 1)),
    ]
    few_tiles = (tiles + 1) // 2

    def partial_outs(at_once):
        return [
            ((3, seqs, share, padded_units), HALF, ANY),
            ((seqs - 1, share, at_once * tile_width), HALF, ANY),
        ]

    def slot_peer(me, j, h):
        other = lax.rem(me + j, slots)
        return (lax.rem(other, sections), lax.div(other, sections), h)

    def query_rows(ref, m, c):
        block = ref[m * rows : (m + 1) * rows, :]
        base = c * group * head_width
        return jnp.concatenate(
            [block[:, base + r * head_width : base + (r + 1) * head_width] for r in range(group)], 0
        )

    def keys_of(all_ref, at, c, kind):
        block = all_ref[:, at * rows : (at + 1) * rows, :].reshape(block_tok, pair_width)
        base = kind * kv_local * head_width + c * head_width
        return block[:, base : base + head_width]

    def allowed_pairs(segq_ref, seg_ref, m, at, s, q):
        own_segments = segq_ref[m * rows : (m + 1) * rows, :]
        allowed = own_segments == seg_ref[at : at + 1, :]
        if at == m:
            base = q * local_rows + s * rows
            order = base + lax.broadcasted_iota(jnp.int32, (rows, block_tok), 0)
            allowed = allowed & (lax.broadcasted_iota(jnp.int32, (rows, block_tok), 1) <= order)
        bias = jnp.where(allowed, 0.0, -1e30)
        return jnp.concatenate([bias] * group, 0)

    def probabilities(rows_in, keys, biases):
        scores = [
            jnp.where(bias < 0, -1e30, back_product(rows_in, key) * score_scale)
            for key, bias in zip(keys, biases)
        ]
        summit = functools.reduce(jnp.maximum, [jnp.max(part, -1, keepdims=True) for part in scores])
        raised = [jnp.exp(part - summit) for part in scores]
        total = functools.reduce(jnp.add, [jnp.sum(part, -1, keepdims=True) for part in raised])
        inverse = 1.0 / total
        return [part * inverse for part in raised]

    def gather_pairs(all_ref, me, where, send, recv, near_send, near_recv):
        s, q, h = where
        partner = (1 - s, q, h)
        far = []
        for k, peer in enumerate(seq_peers(where, seqs)):
            copy = remote(all_ref.at[me], all_ref.at[me], send.at[k], recv.at[k], peer)
            copy.start()
            far.append(copy)
        near = [remote(all_ref.at[me], all_ref.at[me], near_send.at[0], near_recv.at[0], partner)]
        near[0].start()

        def pass_on():
            for k in range(1, seqs):
                far[k - 1].wait()
                slot = lax.rem(q + seqs - k, seqs) * sections + s
                copy = remote(all_ref.at[slot], all_ref.at[slot], near_send.at[k], near_recv.at[k], partner)
                copy.start()
                near.append(copy)
            wait_all(near)

        return pass_on

    def attention_forward(
        n3_ref, wq_ref, wp_ref, cos_ref, sin_ref, qg_ref, kg_ref, segq_ref, seg_ref, wo_ref, m_ref, gain_ref,
        qr_ref, r_ref, q_ref, all_ref, o_ref, h2_ref, n4_ref,
        send, recv, near_send, near_recv, part, inbox, rs, rr, gs, gr, carry,
    ):
        where = place()
        s, q, h = where
        me = q * sections + s
        greet([(1 - s, q, h)] + seq_peers(where, seqs), where, heads)
        cos, sin = cos_ref[...], sin_ref[...]
        r_ref[...] = product(n3_ref[...], wp_ref[...])
        half_pair = pair_width // 2
        for start, size in chunks_of(half_pair):
            span = slice(start, start + size)
            all_ref[me, :, span] = rotary(r_ref[:, span], kg_ref[...], cos, sin).astype(HALF)
        all_ref[me, :, half_pair:] = r_ref[:, half_pair:].astype(HALF)
        pass_on = gather_pairs(all_ref, me, where, send, recv, near_send, near_recv)
        qr_ref[...] = product(n3_ref[...], wq_ref[...])
        for start, size in chunks_of(query_width):
            span = slice(start, start + size)
            q_ref[:, span] = rotary(qr_ref[:, span], qg_ref[...], cos, sin).astype(HALF)
        pass_on()
        for m in range(micro):
            biases = [allowed_pairs(segq_ref, seg_ref, m, at, s, q) for at in range(m + 1)]
            results = []
            for c in range(kv_local):
                keys = [keys_of(all_ref, at, c, 0) for at in range(m + 1)]
                weights = probabilities(query_rows(q_ref, m, c), keys, biases)
                total = functools.reduce(
                    jnp.add,
                    [product(weights[at].astype(HALF), keys_of(all_ref, at, c, 1)) for at in range(m + 1)],
                )
                results += [total[r * rows : (r + 1) * rows] for r in range(group)]
            o_ref[m * rows : (m + 1) * rows, :] = jnp.concatenate(results, -1).astype(HALF)
        part[...] = product(o_ref[...], wo_ref[...]).astype(HALF)

        def finish(flow, i, total):
            hidden = m_ref[kept_rows(i), :] + total
            h2_ref[kept_rows(i), :] = hidden
            return norm_apply(hidden, gain_ref[1:2, :]).astype(HALF)

        head_total(part, n4_ref, inbox, rs, rr, gs, gr, where, heads, finish)

    (query_raw, pair_raw, queries, all_pairs, attended, h2, n4), _ = call(
        attention_forward,
        "attention_forward",
        2,
        [
            ((tokens, query_width), FLOAT),
            ((tokens, pair_width), FLOAT),
            ((tokens, query_width), HALF),
            ((slots, tokens, pair_width), HALF),
            ((tokens, query_width), HALF),
            ((half_tokens, width), FLOAT),
            ((tokens, width), HALF),
        ],
        [dma(seqs - 1), dma(seqs - 1), dma(seqs), dma(seqs)] + part_scratch + total_scratch,
        [
            n3, w_query, w_pair, cosine, sine, query_gain, key_gain, local_segments, segment_ids,
            attn_out, middle, attn_gains,
        ],
        flops=4 * 10**9,
        moved=150 << 20,
    )

    def slab_width(start, count):
        return min(-(-count // tile_width) * tile_width, padded_units - start)

    def clear_padding(latter):
        if padded_units > hidden_units:
            latter[:, :, hidden_units:] = jnp.zeros((3, 2 * tokens, padded_units - hidden_units), HALF)

    def second_ffn(
        n4_ref, g_ref, h2_ref, gain_ref, up_hbm, down_hbm,
        py_ref, gh2_ref, low_ref, gg_ref, partial_hbm, first_in,
        acc_y, up_ref, down_ref, weight_sems, acc, given, former, latter, stage, hs, hr, ls, lr, local_sems, ts, tr,
        part, inbox, rs, rr, gs, gr, carry,
    ):
        where = place()
        s, q, h = where
        weights = weight_loads(up_hbm, down_hbm, up_ref, down_ref, weight_sems)
        start_all(weights)
        clear_padding(latter)
        greet([(1 - s, q, h)] + seq_peers(where, seqs), where, heads)
        halves = half_swaps([g_ref, n4_ref], [given.at[0], given.at[1]], hs, hr, where)
        start_all(halves)
        gg_ref[...] = jnp.zeros_like(gg_ref)
        swaps = []
        for j, (start, count) in enumerate(slabs):
            wait_all(weights[3 * j : 3 * j + 3])
            span = slice(start, start + count)
            gate = back_product(n4_ref[...], up_ref[0, span, :])
            rise = back_product(n4_ref[...], up_ref[1, span, :])
            grad_active = back_product(g_ref[...], down_ref[span, :])
            chance = 1.0 / (1.0 + jnp.exp(-gate))
            silu = gate * chance
            active = (silu * rise).astype(HALF)
            grad_gate = (grad_active * rise * (chance * (1.0 + gate * (1.0 - chance)))).astype(HALF)
            grad_rise = (grad_active * silu).astype(HALF)
            latter[0, 0:tokens, span] = active
            latter[1, 0:tokens, span] = grad_gate
            latter[2, 0:tokens, span] = grad_rise
            for kind in range(3):
                swap = latter_swap(
                    latter, kind, start, slab_width(start, count), ls.at[kind, j], lr.at[kind, j], where
                )
                swap.start()
                swaps.append(swap)
            term = product(grad_gate, up_ref[0, span, :]) + product(grad_rise, up_ref[1, span, :])
            term_y = product(active, down_ref[span, :])
            if j == 0:
                acc[...] = term
                acc_y[...] = term_y
            else:
                acc[...] += term
                acc_y[...] += term_y
        part[...] = acc[...].astype(HALF)

        for flow, holder in ((0, 0), (1, heads - 1)):

            @pl.when(h == holder)
            def _(flow=flow):
                acc_y[flow * half_tokens : (flow + 1) * half_tokens, :] += h2_ref[...]

        py_ref[...] = acc_y[...].astype(HALF)
        wait_all(halves)
        former[0] = transposed(g_ref, given.at[0])
        former[1] = transposed(n4_ref, given.at[1])
        wait_all(swaps)
        tile, tiles_done = gradient_tiles(
            former, latter, stage, partial_hbm, first_in, local_sems, ts, tr, where, few_tiles
        )

        def finish(flow, i, total):
            grad_hidden, grad_gain = norm_back(h2_ref[kept_rows(i), :], gain_ref[1:2, :], total)
            grad = g_ref[own_rows(flow, i), :].astype(FLOAT) + grad_hidden
            gh2_ref[kept_rows(i), :] = grad
            gg_ref[...] += grad_gain
            return grad.astype(HALF)

        head_total(part, low_ref, inbox, rs, rr, gs, gr, where, heads, finish, tile, 3 * tiles)
        tiles_done()

    (part_y, gh2, gh2_low, grad_gain_attn1, partial2, down2_in), _ = call(
        second_ffn,
        "second_ffn",
        4,
        [
            ((tokens, width), HALF),
            ((half_tokens, width), FLOAT),
            ((tokens, width), HALF),
            ((1, width), FLOAT),
        ]
        + partial_outs(few_tiles),
        [pltpu.VMEM((tokens, width), FLOAT)] + ffn_scratch + part_scratch + total_scratch,
        [n4, g, h2, attn_gains, (second_up, ANY), (attn_down, ANY)],
        flops=12 * 10**9,
        moved=150 << 20,
    )
    yout = lax.psum(part_y, "head")
    half_share = share // 2
    few_wide = few_tiles * tile_width
    up2_pieces = [
        (partial2, kind, first, half_share, 0, padded_units) for kind in (1, 2) for first in (0, half_share)
    ]
    down2_piece = (partial2, 0, 0, share, few_wide, padded_units - few_wide)

    def attention_backward(
        glow_ref, wo_ref, q_ref, all_ref, segq_ref, seg_ref,
        qr_ref, r_ref, cos_ref, sin_ref, qg_ref, kg_ref, wq_ref, wp_ref, m_ref, gh2_ref, gain_ref,
        bq_ref, br_ref, low_ref, gg_ref, gqk_ref,
        grads, totals, gq_ref, gp_ref, near_slots, pair_slots, ns, nr, ps, pr,
        part, inbox, rs, rr, gs, gr, carry,
    ):
        where = place()
        s, q, h = where
        partner = (1 - s, q, h)
        peers = seq_peers(where, seqs)
        greet([partner] + peers, where, heads)
        carry.start(where, seqs, [0])
        gg_ref[...] = jnp.zeros_like(gg_ref)
        gqk_ref[...] = jnp.zeros_like(gqk_ref)
        grads[...] = back_product(glow_ref[...], wo_ref[...]).astype(HALF)
        for m in range(micro):
            biases = [allowed_pairs(segq_ref, seg_ref, m, at, s, q) for at in range(m + 1)]
            results = []
            for c in range(kv_local):
                keys = [keys_of(all_ref, at, c, 0) for at in range(m + 1)]
                values = [keys_of(all_ref, at, c, 1) for at in range(m + 1)]
                rows_in = query_rows(q_ref, m, c)
                grad_rows = query_rows(grads, m, c)
                chances = probabilities(rows_in, keys, biases)
                grad_chances = [back_product(grad_rows, value) for value in values]
                inner = functools.reduce(
                    jnp.add,
                    [jnp.sum(a * b, -1, keepdims=True) for a, b in zip(grad_chances, chances)],
                )
                total = None
                for at in range(m + 1):
                    grad_scores = (chances[at] * (grad_chances[at] - inner)).astype(HALF)
                    term = product(grad_scores, keys[at])
                    total = term if total is None else total + term
                    grad_key = outer_sum(grad_scores, rows_in) * score_scale
                    grad_value = outer_sum(chances[at].astype(HALF), grad_rows)
                    if at == m:
                        totals[at, c] = grad_key
                        totals[at, kv_local + c] = grad_value
                    else:
                        totals[at, c] += grad_key
                        totals[at, kv_local + c] += grad_value
                total = total * score_scale
                results += [total[r * rows : (r + 1) * rows] for r in range(group)]
            gq_ref[m * rows : (m + 1) * rows, :] = jnp.concatenate(results, -1)
        for at in range(micro):
            joined = jnp.concatenate([totals[at, k] for k in range(2 * kv_local)], -1).astype(HALF)
            gp_ref[:, at * rows : (at + 1) * rows, :] = joined.reshape(slots, rows, pair_width)
        near = []
        for other in range(seqs):
            copy = remote(gp_ref.at[other * sections + 1 - s], near_slots.at[other], ns.at[other], nr.at[other], partner)
            copy.start()
            near.append(copy)
        cos, sin = cos_ref[...], sin_ref[...]
        copies = []
        wait_all(near)
        for other in range(seqs):
            mine = gp_ref[other * sections + s].astype(FLOAT)
            near_slots[other] = (mine + near_slots[other].astype(FLOAT)).astype(HALF)
        for k, peer in enumerate(peers):
            copy = remote(near_slots.at[peer[1]], pair_slots.at[k], ps.at[k], pr.at[k], peer)
            copy.start()
            copies.append(copy)
        carry.start(where, seqs, [1, 2, 3])
        for start, size in chunks_of(query_width):
            span = slice(start, start + size)
            grad_raw, grad_gain = rotary_back(qr_ref[:, span], qg_ref[...], cos, sin, gq_ref[:, span])
            bq_ref[:, span] = grad_raw.astype(HALF)
            gqk_ref[0:1, :size] += grad_gain
        partial = back_product(bq_ref[...], wq_ref[...])
        wait_all(copies)
        grad_pair = near_slots[q].astype(FLOAT)
        for j in range(seqs - 1):
            grad_pair = grad_pair + pair_slots[j].astype(FLOAT)
        half_pair = pair_width // 2
        for start, size in chunks_of(half_pair):
            span = slice(start, start + size)
            grad_raw, grad_gain = rotary_back(r_ref[:, span], kg_ref[...], cos, sin, grad_pair[:, span])
            br_ref[:, span] = grad_raw.astype(HALF)
            gqk_ref[1:2, :size] += grad_gain
        br_ref[:, half_pair:] = grad_pair[:, half_pair:].astype(HALF)
        part[...] = (partial + back_product(br_ref[...], wp_ref[...])).astype(HALF)

        def finish(flow, i, total):
            grad_entry, grad_gain = norm_back(m_ref[kept_rows(i), :], gain_ref[0:1, :], total)
            gg_ref[...] += grad_gain
            return (gh2_ref[kept_rows(i), :] + grad_entry).astype(HALF)

        head_total(part, low_ref, inbox, rs, rr, gs, gr, where, heads, finish)
        carry.wait()

    (bq, br, gm_low, grad_gain_attn0, grad_qk), up2_in = call(
        attention_backward,
        "attention_backward",
        5,
        [
            ((tokens, query_width), HALF),
            ((tokens, pair_width), HALF),
            ((tokens, width), HALF),
            ((1, width), FLOAT),
            ((8, 128), FLOAT),
        ],
        [
            pltpu.VMEM((tokens, query_width), HALF),
            pltpu.VMEM((micro, 2 * kv_local, block_tok, head_width), FLOAT),
            pltpu.VMEM((tokens, query_width), FLOAT),
            pltpu.VMEM((slots, tokens, pair_width), HALF),
            pltpu.VMEM((seqs, tokens, pair_width), HALF),
            pltpu.VMEM((seqs - 1, tokens, pair_width), HALF),
            dma(seqs),
            dma(seqs),
            dma(seqs - 1),
            dma(seqs - 1),
        ]
        + part_scratch
        + total_scratch,
        [
            gh2_low, attn_out, queries, all_pairs, local_segments, segment_ids,
            query_raw, pair_raw, cosine, sine, query_gain, key_gain, w_query, w_pair, middle, gh2, attn_gains,
        ],
        up2_pieces[:3] + [down2_piece],
        flops=6 * 10**9,
        moved=130 << 20,
    )

    def first_ffn_back(
        gm_ref, n2_ref, f1_ref, a1_ref, h1_ref, gain_ref, up_hbm, down_hbm,
        gh1_ref, low_ref, gg_ref, partial_hbm, first_in,
        up_ref, down_ref, weight_sems, acc, given, former, latter, stage, hs, hr, ls, lr, local_sems, ts, tr,
        part, inbox, rs, rr, gs, gr, carry,
    ):
        where = place()
        s, q, h = where
        weights = weight_loads(up_hbm, down_hbm, up_ref, down_ref, weight_sems)
        start_all(weights)
        clear_padding(latter)
        latter[0, 0:tokens, 0:hidden_units] = a1_ref[...]
        greet([(1 - s, q, h)] + seq_peers(where, seqs), where, heads)
        carry.start(where, seqs)
        halves = half_swaps([gm_ref, n2_ref], [given.at[0], given.at[1]], hs, hr, where)
        start_all(halves)
        gg_ref[...] = jnp.zeros_like(gg_ref)
        swaps = []
        for j, (start, count) in enumerate(slabs):
            wait_all(weights[3 * j : 3 * j + 3])
            span = slice(start, start + count)
            gate = f1_ref[0, :, span]
            rise = f1_ref[1, :, span]
            grad_active = back_product(gm_ref[...], down_ref[span, :])
            chance = 1.0 / (1.0 + jnp.exp(-gate))
            grad_gate = (grad_active * rise * (chance * (1.0 + gate * (1.0 - chance)))).astype(HALF)
            grad_rise = (grad_active * (gate * chance)).astype(HALF)
            latter[1, 0:tokens, span] = grad_gate
            latter[2, 0:tokens, span] = grad_rise
            for kind in range(3):
                swap = latter_swap(
                    latter, kind, start, slab_width(start, count), ls.at[kind, j], lr.at[kind, j], where
                )
                swap.start()
                swaps.append(swap)
            term = product(grad_gate, up_ref[0, span, :]) + product(grad_rise, up_ref[1, span, :])
            if j == 0:
                acc[...] = term
            else:
                acc[...] += term
        part[...] = acc[...].astype(HALF)
        wait_all(halves)
        former[0] = transposed(gm_ref, given.at[0])
        former[1] = transposed(n2_ref, given.at[1])
        wait_all(swaps)
        tile, tiles_done = gradient_tiles(
            former, latter, stage, partial_hbm, first_in, local_sems, ts, tr, where, tiles
        )

        def finish(flow, i, total):
            grad_hidden, grad_gain = norm_back(h1_ref[kept_rows(i), :], gain_ref[1:2, :], total)
            gg_ref[...] += grad_gain
            grad = gm_ref[own_rows(flow, i), :].astype(FLOAT) + grad_hidden
            gh1_ref[kept_rows(i), :] = grad
            return grad.astype(HALF)

        head_total(part, low_ref, inbox, rs, rr, gs, gr, where, heads, finish, tile, 3 * tiles)
        tiles_done()
        carry.wait()

    (gh1, gh1_low, grad_gain_conv1, partial1, down1_in), up2_last_in = call(
        first_ffn_back,
        "first_ffn_back",
        6,
        [((half_tokens, width), FLOAT), ((tokens, width), HALF), ((1, width), FLOAT)] + partial_outs(tiles),
        ffn_scratch + part_scratch + total_scratch,
        [gm_low, n2, f1, a1, h1, conv_gains, (first_up, ANY), (conv_down, ANY)],
        up2_pieces[3:],
        flops=9 * 10**9,
        moved=150 << 20,
    )
    small_width = max(share, channels, 2 * head_width)
    widths = [query_width, query_width + pair_width, channels, 3 * channels]

    def conv_backward(
        low_ref, gh1_ref, pc_ref, edge_ref, same_ref, kernel_ref, wout_ref, win_ref, x_ref, gain_ref, yout_ref,
        ghlow_ref, n3_ref, n1_ref, o_ref, bq_ref, br_ref, mixed_ref, small_in,
        partial1, partial2, down1_in, down2_a, gate2_a, gate2_b, rise2_a, down2_b, rise2_b,
        edges_ref, sums_ref, gout2_ref, gmix_ref, gout1_ref, gin_ref, gdown2, gup2, gdown1, gup1,
        bp_ref, ext, spread, gz_ext, outgoing, arrived, full, gg_ref, edge_send, edge_recv, swap_send, swap_recv,
        given, former, latter0, latter1, latter2, latter3, stage0, stage1, stage2, stage3, in0, in1, in2, in3,
        hs, hr, ls, lr, ms, mr, bulk_in, bulk_own, bs, br_sem, own_sem,
        bufs, buf_sems, down_stage, up_stage, out_sems,
        packed, boxes, summed, final, zs, zr, ss, sr,
        part, inbox, rs, rr, gs, gr, carry,
    ):
        where = place()
        s, q, h = where
        first = s == 0
        partner = (1 - s, q, h)
        preceding = (1 - s, jnp.where(first, lax.rem(q + seqs - 1, seqs), q), h)
        following = (1 - s, jnp.where(first, q, lax.rem(q + 1, seqs)), h)
        others = [(s, q, lax.rem(h + k, heads)) for k in range(1, heads)]
        me = q * sections + s
        slot_peers = [slot_peer(me, j, h) for j in range(1, slots)]
        peers = seq_peers(where, seqs)
        latters, stages, incomes = [latter0, latter1, latter2, latter3], [stage0, stage1, stage2, stage3], [in0, in1, in2, in3]
        own_bulk = [pltpu.make_async_copy(partial1.at[kind + 1, q], bulk_own.at[kind], own_sem.at[kind]) for kind in range(2)]
        start_all(own_bulk)

        def load(slot, own, pieces):
            copies = [pltpu.make_async_copy(own, bufs.at[slot, 0], buf_sems.at[slot, 0])]
            for k, (piece, start, count, left, wide) in enumerate(pieces):
                target = bufs.at[slot, 1:seqs, start : start + count, left : left + wide]
                copies.append(pltpu.make_async_copy(piece, target, buf_sems.at[slot, 1 + k]))
            start_all(copies)
            return copies

        halves_of = ((0, half_share, 0, padded_units), (half_share, half_share, 0, padded_units))
        loads = [
            load(
                0,
                partial2.at[0, q],
                [(down2_a, 0, share, 0, few_wide), (down2_b, 0, share, few_wide, padded_units - few_wide)],
            ),
            load(1, partial2.at[1, q], [(gate2_a, *halves_of[0]), (gate2_b, *halves_of[1])]),
            load(2, partial2.at[2, q], [(rise2_a, *halves_of[0]), (rise2_b, *halves_of[1])]),
            load(3, partial1.at[0, q], [(down1_in, 0, share, 0, padded_units)]),
        ]
        greet([partner, preceding, following] + others + slot_peers, where, heads)
        latters[0][0:tokens, :] = o_ref[...]
        latters[1][0:tokens, 0:query_width] = bq_ref[...]
        latters[1][0:tokens, query_width:] = br_ref[...]
        latters[2][0:tokens, :] = mixed_ref[...]
        former_refs = [ghlow_ref, n3_ref, low_ref, n1_ref]
        halves = half_swaps(former_refs, [given.at[k] for k in range(4)], hs, hr, where)
        start_all(halves)
        swaps = [
            remote(latters[k].at[0:tokens], latters[k].at[tokens : 2 * tokens], ls.at[k], lr.at[k], partner) for k in range(4)
        ]
        start_all(swaps[:3])
        gg_ref[...] = jnp.zeros_like(gg_ref)
        gated = pc_ref[0] * pc_ref[2]
        grad_y = back_product(low_ref[...], wout_ref[...])
        gz = grad_y * pc_ref[1]
        zero = jnp.zeros((8, channels), FLOAT)
        for m in range(micro):
            span = slice(m * rows, (m + 1) * rows)
            one = jnp.where(same_ref[span, 0:1] > 0, gz[span], 0.0) * kernel_ref[1:2, :]
            two = jnp.where(same_ref[span, 1:2] > 0, gz[span], 0.0) * kernel_ref[0:1, :]
            gz_ext[0, m, 0:rows, :] = one
            gz_ext[0, m, rows : rows + 8, :] = zero
            gz_ext[1, m, 0:rows, :] = two
            gz_ext[1, m, rows : rows + 8, :] = zero
            outgoing[m] = zero
            outgoing[m, 0:1, :] = two[0:1]
            outgoing[m, 1:2, :] = one[0:1] + two[1:2]
        edge = remote(outgoing, arrived, edge_send.at[0], edge_recv.at[0], preceding)
        edge.start()
        bulk = []
        for kind in range(2):
            for k, peer in enumerate(peers):
                bulk.append(
                    remote(partial1.at[kind + 1, peer[1]], bulk_in.at[kind, k], bs.at[kind, k], br_sem.at[kind, k], peer)
                )
        start_all(bulk)
        taps = [None, None, None]
        for m in range(micro):
            span = slice(m * rows, (m + 1) * rows)
            ext[m, 0:8, :] = edge_ref[m]
            ext[m, 8 : 8 + rows, :] = gated[span]
            back_one = jnp.where(same_ref[span, 0:1] > 0, shifted_rows(ext, m, 1), 0.0)
            back_two = jnp.where(same_ref[span, 1:2] > 0, shifted_rows(ext, m, 2), 0.0)
            mixed = (
                kernel_ref[2:3, :] * gated[span]
                + kernel_ref[1:2, :] * back_one
                + kernel_ref[0:1, :] * back_two
            )
            bp_ref[span, channels : 2 * channels] = (grad_y[span] * mixed).astype(HALF)
            for k, value in enumerate((back_two, back_one, gated[span])):
                term = jnp.sum(value * gz[span], 0, keepdims=True)
                taps[k] = term if taps[k] is None else taps[k] + term
        for m in range(micro):
            span = slice(m * rows, (m + 1) * rows)
            spread[m] = (
                kernel_ref[2:3, :] * gz[span]
                + gz_ext[0, m, 1 : rows + 1, :]
                + gz_ext[1, m, 2 : rows + 2, :]
            )
        edge.wait()
        wrap = (s == sections - 1) & (q == seqs - 1)
        for m in range(micro):
            follow = arrived[m + 1, 0:2, :] if m + 1 < micro else jnp.zeros((2, channels), FLOAT)
            spread[m, rows - 2 : rows, :] += jnp.where(wrap, follow, arrived[m, 0:2, :])
        for m in range(micro):
            span = slice(m * rows, (m + 1) * rows)
            bp_ref[span, 0:channels] = (spread[m] * pc_ref[2, span, :]).astype(HALF)
            bp_ref[span, 2 * channels :] = (spread[m] * pc_ref[0, span, :]).astype(HALF)
        latters[3][0:tokens, :] = bp_ref[...]
        swaps[3].start()
        total = back_product(bp_ref[:, 0:channels], win_ref[0])
        total = total + back_product(bp_ref[:, channels : 2 * channels], win_ref[1])
        total = total + back_product(bp_ref[:, 2 * channels :], win_ref[2])
        part[...] = total.astype(HALF)

        def finish(flow, i, total):
            start = x_ref[own_rows(flow, i), :].astype(FLOAT)
            grad_start, grad_gain = norm_back(start, gain_ref[0:1, :], total)
            gg_ref[...] += grad_gain
            return (gh1_ref[kept_rows(i), :] + grad_start).astype(HALF)

        head_total(part, full, inbox, rs, rr, gs, gr, where, heads, finish)
        keep = pl.ds(pl.multiple_of(s * rows, rows), rows)
        edges_ref[0, :, keep, :] = jnp.where(first, full[...], yout_ref[...]).reshape(micro, rows, width)
        part[...] = jnp.where(first, yout_ref[...], full[...])
        edge_swaps = []
        for m in range(micro):
            copy = remote(
                part.at[m * rows : (m + 1) * rows], edges_ref.at[0, m, keep], swap_send.at[m], swap_recv.at[m], partner
            )
            copy.start()
            edge_swaps.append(copy)
        packed[...] = small_in[...]
        packed[:, 5:8, 0:channels] = jnp.broadcast_to(jnp.concatenate(taps, 0)[None], (slots, 3, channels))
        for d in range(slots):
            packed[d, 0:1, 0:share] = gg_ref[:, d * share : (d + 1) * share]
        over = []
        for k, peer in enumerate(others):
            copy = remote(packed, boxes.at[k], zs.at[k], zr.at[k], peer)
            copy.start()
            over.append(copy)
        wait_all(halves)
        sends = []
        for k in range(4):
            former[...] = transposed(former_refs[k], given.at[k])
            swaps[k].wait()
            result = product(former[...], latters[k][...]).astype(HALF)
            stages[k][...] = result.reshape(seqs, share, widths[k])
            for j, peer in enumerate(peers):
                copy = remote(stages[k].at[peer[1]], incomes[k].at[j], ms.at[k, j], mr.at[k, j], peer)
                copy.start()
                sends.append(copy)
            if k == 0:
                wait_all(over)
                over_heads = boxes[0]
                for j in range(1, heads - 1):
                    over_heads = over_heads + boxes[j]
                row = lax.broadcasted_iota(jnp.int32, over_heads.shape, 1)
                summed[...] = packed[...] + jnp.where(row < 5, over_heads, 0.0)
                across = []
                for j, peer in enumerate(slot_peers):
                    copy = remote(summed.at[peer[0] * seqs + peer[1]], final.at[j], ss.at[j], sr.at[j], peer)
                    copy.start()
                    across.append(copy)

        def summed_up(own, arrivals):
            total = own.astype(FLOAT)
            for piece in arrivals:
                total = total + piece.astype(FLOAT)
            return total[:, :hidden_units]

        outs = []

        def leave(source, target, at):
            copy = pltpu.make_async_copy(source, target, out_sems.at[at])
            copy.start()
            outs.append(copy)

        def from_buffer(slot):
            wait_all(loads[slot])
            return summed_up(bufs[slot, 0], [bufs[slot, k] for k in range(1, seqs)])

        down_stage[0] = from_buffer(0).astype(HALF)
        leave(down_stage.at[0], gdown2, 0)
        up_stage[0, 0] = from_buffer(1).astype(HALF)
        up_stage[0, 1] = from_buffer(2).astype(HALF)
        leave(up_stage.at[0], gup2, 1)
        down_stage[1] = from_buffer(3).astype(HALF)
        leave(down_stage.at[1], gdown1, 2)
        wait_all(own_bulk)
        for kind in range(2):
            wait_all(bulk[kind * (seqs - 1) : (kind + 1) * (seqs - 1)])
            up_stage[1, kind] = summed_up(bulk_own[kind], [bulk_in[kind, k] for k in range(seqs - 1)]).astype(HALF)
        leave(up_stage.at[1], gup1, 3)
        wait_all(edge_swaps)
        wait_all(across)
        total = summed[s * seqs + q]
        for j in range(slots - 1):
            total = total + final[j]
        sums_ref[...] = total
        wait_all(sends)
        for k, target in enumerate((gout2_ref, gmix_ref, gout1_ref, None)):
            total = stages[k][q].astype(FLOAT)
            for j in range(seqs - 1):
                total = total + incomes[k][j].astype(FLOAT)
            if target is None:
                for c in range(3):
                    gin_ref[c] = total[:, c * channels : (c + 1) * channels].astype(HALF)
            else:
                target[...] = total.astype(HALF)
        wait_all(outs)

    folded = grad_qk[0:2, :head_width] + grad_qk[0:2, head_width : 2 * head_width]
    gain_rows = jnp.concatenate(
        [jnp.zeros_like(grad_gain_conv1), grad_gain_conv1, grad_gain_attn0, grad_gain_attn1], 0
    )

    def to_width(array):
        return jnp.pad(array, [(0, 0)] * (array.ndim - 1) + [(0, small_width - array.shape[-1])])

    small = jnp.concatenate(
        [
            to_width(gain_rows.reshape(4, slots, share).transpose(1, 0, 2)),
            jnp.broadcast_to(to_width(folded.reshape(1, 1, 2 * head_width)), (slots, 1, small_width)),
            jnp.zeros((slots, 3, small_width), FLOAT),
        ],
        1,
    )

    def dma_grid(*shape):
        return pltpu.SemaphoreType.DMA(shape)

    (section_edges, sums, gout2, gmix, gout1, gin, gdown2, gup2, gdown1, gup1), _ = call(
        conv_backward,
        "conv_backward",
        7,
        [
            ((1, micro, local_rows, width), HALF),
            ((8, small_width), FLOAT),
            ((share, widths[0]), HALF),
            ((share, widths[1]), HALF),
            ((share, widths[2]), HALF),
            ((3, share, channels), HALF),
            ((share, hidden_units), HALF, ANY),
            ((2, share, hidden_units), HALF, ANY),
            ((share, hidden_units), HALF, ANY),
            ((2, share, hidden_units), HALF, ANY),
        ],
        [
            pltpu.VMEM((tokens, 3 * channels), HALF),
            pltpu.VMEM((micro, 8 + rows, channels), FLOAT),
            pltpu.VMEM((micro, rows, channels), FLOAT),
            pltpu.VMEM((2, micro, rows + 8, channels), FLOAT),
            pltpu.VMEM((micro, 8, channels), FLOAT),
            pltpu.VMEM((micro, 8, channels), FLOAT),
            pltpu.VMEM((tokens, width), HALF),
            pltpu.VMEM((1, width), FLOAT),
            dma(1),
            dma(1),
            dma(micro),
            dma(micro),
            pltpu.VMEM((4, tokens, half_model), HALF),
            pltpu.VMEM((half_model, 2 * tokens), HALF),
        ]
        + [pltpu.VMEM((2 * tokens, size), HALF) for size in widths]
        + [pltpu.VMEM((seqs, share, size), HALF) for size in widths]
        + [pltpu.VMEM((seqs - 1, share, size), HALF) for size in widths]
        + [
            dma(4),
            dma(4),
            dma(4),
            dma(4),
            dma_grid(4, seqs - 1),
            dma_grid(4, seqs - 1),
            pltpu.VMEM((2, seqs - 1, share, padded_units), HALF),
            pltpu.VMEM((2, share, padded_units), HALF),
            dma_grid(2, seqs - 1),
            dma_grid(2, seqs - 1),
            dma(2),
            pltpu.VMEM((4, seqs, share, padded_units), HALF),
            dma_grid(4, 3),
            pltpu.VMEM((2, share, hidden_units), HALF),
            pltpu.VMEM((2, 2, share, hidden_units), HALF),
            dma(4),
            pltpu.VMEM((slots, 8, small_width), FLOAT),
            pltpu.VMEM((heads - 1, slots, 8, small_width), FLOAT),
            pltpu.VMEM((slots, 8, small_width), FLOAT),
            pltpu.VMEM((slots - 1, 8, small_width), FLOAT),
            dma(heads - 1),
            dma(heads - 1),
            dma(slots - 1),
            dma(slots - 1),
        ]
        + part_scratch
        + total_scratch,
        [
            gh1_low, gh1, projected, edge_gated, same, conv_kernel, conv_out, w_in, x, conv_gains, yout,
            gh2_low, n3, n1, attended, bq, br, mixed, small,
        ]
        + [(array, ANY) for array in [partial1, partial2, down1_in, down2_in] + up2_in + up2_last_in],
        flops=5 * 10**9,
        moved=300 << 20,
    )
    def results(
        edges_in, sums_in, gout2_in, gmix_in, gout1_in, gin_in, gdown2_in, gup2_in, gdown1_in, gup1_in,
        edges_out, cgain_out, gin_out, taps_out, gout1_out, gup1_out, gdown1_out,
        again_out, gq_out, gkv_out, gqk_out, gout2_out, gup2_out, gdown2_out,
        down_in, up_in, down_stage, up_stage, edges_held, in_sems, out_sems, edge_sem,
    ):
        edges_load = pltpu.make_async_copy(edges_in, edges_held, edge_sem.at[0])
        edges_load.start()
        loads = [
            pltpu.make_async_copy(source, target, in_sems.at[k])
            for k, (source, target) in enumerate(
                [(gdown1_in, down_in.at[0]), (gup1_in, up_in.at[0]), (gdown2_in, down_in.at[1]), (gup2_in, up_in.at[1])]
            )
        ]
        start_all(loads)
        stores = []
        for k, (down_out, up_out) in enumerate(((gdown1_out, gup1_out), (gdown2_out, gup2_out))):
            loads[2 * k].wait()
            down_stage[k] = down_in[k].astype(FLOAT)
            stores.append(pltpu.make_async_copy(down_stage.at[k], down_out, out_sems.at[2 * k]))
            stores[-1].start()
            loads[2 * k + 1].wait()
            for kind in range(2):
                up_stage[k, :, kind, :] = up_in[k, kind].astype(FLOAT)
            stores.append(pltpu.make_async_copy(up_stage.at[k], up_out, out_sems.at[2 * k + 1]))
            stores[-1].start()
        cgain_out[...] = sums_in[0:2, 0:share]
        again_out[...] = sums_in[2:4, 0:share]
        taps_out[...] = sums_in[5:8, 0:channels]
        for kind in range(2):
            gqk_out[kind : kind + 1, :] = sums_in[4:5, kind * head_width : (kind + 1) * head_width]
            start = query_width + kind * (pair_width // 2)
            gkv_out[:, kind, :] = gmix_in[:, start : start + pair_width // 2].astype(FLOAT)
        gq_out[...] = gmix_in[:, 0:query_width].astype(FLOAT)
        gout1_out[...] = gout1_in[...].astype(FLOAT)
        gout2_out[...] = gout2_in[...].astype(FLOAT)
        gin_out[...] = gin_in[...].astype(FLOAT)
        edges_load.wait()
        stores.append(pltpu.make_async_copy(edges_held, edges_out, edge_sem.at[1]))
        stores[-1].start()
        wait_all(stores)

    (
        section_edges, cgain, gin, taps, gout1, gup1, gdown1, again, gq, gkv, gqk, gout2, gup2, gdown2,
    ), _ = call(
        results,
        "results",
        None,
        [
            ((1, micro, local_rows, width), HALF, ANY),
            ((2, share), FLOAT),
            ((3, share, channels), FLOAT),
            ((3, channels), FLOAT),
            ((share, channels), FLOAT),
            ((share, 2, hidden_units), FLOAT, ANY),
            ((share, hidden_units), FLOAT, ANY),
            ((2, share), FLOAT),
            ((share, query_width), FLOAT),
            ((share, 2, pair_width // 2), FLOAT),
            ((2, head_width), FLOAT),
            ((share, query_width), FLOAT),
            ((share, 2, hidden_units), FLOAT, ANY),
            ((share, hidden_units), FLOAT, ANY),
        ],
        [
            pltpu.VMEM((2, share, hidden_units), HALF),
            pltpu.VMEM((2, 2, share, hidden_units), HALF),
            pltpu.VMEM((2, share, hidden_units), FLOAT),
            pltpu.VMEM((2, share, 2, hidden_units), FLOAT),
            pltpu.VMEM((1, micro, local_rows, width), HALF),
            dma(4),
            dma(4),
            dma(2),
        ],
        [(section_edges, ANY), sums, gout2, gmix, gout1, gin]
        + [(array, ANY) for array in (gdown2, gup2, gdown1, gup1)],
        moved=25 << 20,
    )
    return (
        section_edges,
        cgain,
        gin.transpose(1, 0, 2),
        taps,
        gout1.T,
        gup1,
        gdown1.T,
        again,
        gq,
        gkv,
        gqk,
        gout2.T,
        gup2,
        gdown2.T,
    )


def solution(mesh):
    return jax.shard_map(
        per_device,
        mesh=mesh,
        in_specs=(
            P("section", None, "seq", None),
            P(),
            P(None, "seq"),
            P(),
            P(None, None, "head"),
            P(None, "head"),
            P("head", None),
            P(None, None, "head"),
            P("head", None),
            P(),
            P(None, "head"),
            P(None, None, "head"),
            P(),
            P("head", None),
            P(None, None, "head"),
            P("head", None),
        ),
        out_specs=(
            P("section", None, "seq", None),
            P(None, ("section", "seq")),
            P(("section", "seq"), None, "head"),
            P(None, "head"),
            P("head", ("section", "seq")),
            P(("section", "seq"), None, "head"),
            P("head", ("section", "seq")),
            P(None, ("section", "seq")),
            P(("section", "seq"), "head"),
            P(("section", "seq"), None, "head"),
            P(),
            P("head", ("section", "seq")),
            P(("section", "seq"), None, "head"),
            P("head", ("section", "seq")),
        ),
        check_vma=False,
    )
```

```python
import functools

import jax
import jax.numpy as jnp
from jax import lax
from jax.experimental import pallas as pl
from jax.experimental.pallas import tpu as pltpu
from jax.sharding import PartitionSpec as P

EPS = 1e-05
THETA = 1000000.0
FLOAT = jnp.float32
HALF = jnp.bfloat16
MESH = pl.DeviceIdType.MESH
VMEM = pl.BlockSpec(memory_space=pltpu.VMEM)
ANY = pl.BlockSpec(memory_space=pl.ANY)


def product(former, latter):
    return jnp.dot(former, latter, preferred_element_type=FLOAT)


def outer_sum(former, latter):
    return lax.dot_general(former, latter, (((0,), (0,)), ((), ())), preferred_element_type=FLOAT)


def back_product(former, latter):
    return lax.dot_general(former, latter, (((1,), (1,)), ((), ())), preferred_element_type=FLOAT)


def norm_apply(values, gain):
    return values * lax.rsqrt(jnp.mean(values * values, -1, keepdims=True) + EPS) * gain


def norm_back(values, gain, grad):
    scale = lax.rsqrt(jnp.mean(values * values, -1, keepdims=True) + EPS)
    weighted = grad * gain
    inner = jnp.mean(weighted * values, -1, keepdims=True)
    grad_values = scale * weighted - values * (scale * scale * scale * inner)
    return grad_values, jnp.sum(grad * values * scale, 0, keepdims=True)


BLOCKS = 8
LAG = 3
END_FIRST = 10
MIDDLE_FIRST = 3


def place():
    return lax.axis_index("section"), lax.axis_index("seq"), lax.axis_index("head")


def remote(source, target, send, recv, peer):
    return pltpu.make_async_remote_copy(
        src_ref=source,
        dst_ref=target,
        send_sem=send,
        recv_sem=recv,
        device_id=peer,
        device_id_type=MESH,
    )


def signal(peer):
    pl.semaphore_signal(pltpu.get_barrier_semaphore(), inc=1, device_id=peer, device_id_type=MESH)


def wait_greetings(count):
    pl.semaphore_wait(pltpu.get_barrier_semaphore(), count)


def greet(others, where=None, size=0):
    for peer in others:
        signal(peer)
    if where is None:
        wait_greetings(len(others))
        return
    section, seq, head = where
    end = (head == 0) | (head == size - 1)

    @pl.when(end)
    def _():
        signal((section, seq, jnp.where(head == 0, 1, size - 2)))
        wait_greetings(len(others) + 1)

    @pl.when(jnp.logical_not(end))
    def _():
        signal((section, seq, jnp.minimum(head + 1, size - 1)))
        signal((section, seq, jnp.maximum(head - 1, 0)))
        wait_greetings(len(others) + 2)


def seq_peers(where, seqs):
    section, seq, head = where
    return [(section, lax.rem(seq + k, seqs), head) for k in range(1, seqs)]


def rows_of(index, count):
    return pl.ds(pl.multiple_of(index * count, count), count)


def wait_all(copies):
    for copy in copies:
        copy.wait()


def start_all(copies):
    for copy in copies:
        copy.start()


def loop(count, step):
    def body(i, carried):
        step(i)
        return carried

    lax.fori_loop(0, count, body, 0)


def head_total(part, full, inbox, reduce_send, reduce_recv, gather_send, gather_recv, where, size, finish, filler=None, fillers=0):
    section, seq, head = where
    count = part.shape[0] // (2 * BLOCKS)
    last = size - 1
    end = (head == 0) | (head == last)

    def rows(flow, i):
        return rows_of(flow * BLOCKS + i, count)

    def fill(t):
        if filler is not None:

            @pl.when(t < fillers)
            def _():
                filler(t)

    def fill_rest(start, stop=fillers):
        stop = min(stop, fillers)
        if stop > start:
            loop(stop - start, lambda i: filler(start + i))

    def reduced(flow, i, peer):
        return remote(part.at[rows(flow, i)], inbox.at[flow, i], reduce_send.at[flow, i], reduce_recv.at[flow, i], peer)

    def gathered(flow, i, peer):
        span = full.at[rows(flow, i)]
        return remote(span, span, gather_send.at[flow, i], gather_recv.at[flow, i], peer)

    @pl.when(end)
    def _():
        flow = jnp.where(head == 0, 0, 1)
        inner = (section, seq, jnp.where(head == 0, 1, last - 1))
        loop(BLOCKS, lambda i: reduced(1 - flow, i, inner).start())
        fill_rest(0, END_FIRST)

        def own(i):
            reduced(flow, i, inner).wait_recv()
            total = part[rows(flow, i), :].astype(FLOAT) + inbox[flow, i].astype(FLOAT)
            full[rows(flow, i), :] = finish(flow, i, total)
            gathered(flow, i, inner).start()
            fill(END_FIRST + i)

        loop(BLOCKS, own)
        fill_rest(END_FIRST + BLOCKS)

        def drain(i):
            gathered(1 - flow, i, inner).wait_recv()
            reduced(1 - flow, i, inner).wait_send()
            gathered(flow, i, inner).wait_send()

        loop(BLOCKS, drain)

    @pl.when(jnp.logical_not(end))
    def _():
        low = head < size // 2
        near = jnp.where(low, 1, 0)
        ahead = (section, seq, jnp.where(low, head + 1, head - 1))
        behind = (section, seq, jnp.where(low, head - 1, head + 1))

        def add(flow, i, peer):
            reduced(flow, i, peer).wait_recv()
            span = rows(flow, i)
            part[span, :] = (part[span, :].astype(FLOAT) + inbox[flow, i].astype(FLOAT)).astype(HALF)
            reduced(flow, i, peer).start()

        def forward(flow, i, peer):
            gathered(flow, i, peer).wait_recv()
            gathered(flow, i, peer).start()

        def lagged(act, first, second, at):
            def step(i):
                fill(at + i)

                @pl.when(i < BLOCKS)
                def _():
                    act(first, i, ahead)

                @pl.when(i >= LAG)
                def _():
                    act(second, i - LAG, behind)

            loop(BLOCKS + LAG, step)

        fill_rest(0, MIDDLE_FIRST)
        lagged(add, near, 1 - near, MIDDLE_FIRST)
        lagged(forward, 1 - near, near, MIDDLE_FIRST + BLOCKS + LAG)
        fill_rest(MIDDLE_FIRST + 2 * (BLOCKS + LAG))

        def drain(i):
            reduced(near, i, ahead).wait_send()
            reduced(1 - near, i, behind).wait_send()
            gathered(1 - near, i, ahead).wait_send()
            gathered(near, i, behind).wait_send()

        loop(BLOCKS, drain)


def turned(values):
    width = values.shape[-1]
    if width == 128:
        lane = lax.broadcasted_iota(jnp.int32, values.shape, 1)
        low = lax.rem(lane, 64) < 32
        return jnp.where(low, -pltpu.roll(values, 96, 1), pltpu.roll(values, 32, 1))
    parts = []
    for start in range(0, width, 64):
        parts += [-values[:, start + 32 : start + 64], values[:, start : start + 32]]
    return jnp.concatenate(parts, -1)


def head_mean(values):
    width = values.shape[-1]
    if width == 64:
        return jnp.mean(values, -1, keepdims=True)
    lane = lax.broadcasted_iota(jnp.int32, values.shape, 1)
    first = jnp.sum(jnp.where(lane < 64, values, 0.0), -1, keepdims=True)
    second = jnp.sum(jnp.where(lane < 64, 0.0, values), -1, keepdims=True)
    return jnp.where(lane < 64, first, second) * (1.0 / 64.0)


def chunks_of(width):
    return [(start, min(128, width - start)) for start in range(0, width, 128)]


def rotary(raw, gain, cosine, sine):
    width = raw.shape[-1]
    normed = raw * lax.rsqrt(head_mean(raw * raw) + EPS) * gain[:, :width]
    return normed * cosine[:, :width] + turned(normed) * sine[:, :width]


def rotary_back(raw, gain, cosine, sine, grad):
    width = raw.shape[-1]
    back = grad * cosine[:, :width] - turned(grad) * sine[:, :width]
    scale = lax.rsqrt(head_mean(raw * raw) + EPS)
    weighted = back * gain[:, :width]
    grad_raw = scale * weighted - raw * (scale * scale * scale * head_mean(weighted * raw))
    return grad_raw, jnp.sum(back * raw * scale, 0, keepdims=True)


def call(body, name, collective, outs, scratch, args, flops=0, moved=0):
    params = dict(vmem_limit_bytes=60 << 20)
    if collective is not None:
        params.update(collective_id=collective, has_side_effects=True)
    results = pl.pallas_call(
        body,
        name=name,
        out_shape=[jax.ShapeDtypeStruct(out[0], out[1]) for out in outs],
        in_specs=[arg[1] if isinstance(arg, tuple) else VMEM for arg in args],
        out_specs=[out[2] if len(out) > 2 else VMEM for out in outs],
        scratch_shapes=list(scratch),
        compiler_params=pltpu.CompilerParams(**params),
        cost_estimate=pl.CostEstimate(flops=flops, bytes_accessed=moved, transcendentals=0),
    )(*[arg[0] if isinstance(arg, tuple) else arg for arg in args])
    return list(results)


def dma(count):
    return pltpu.SemaphoreType.DMA((count,))


def per_device(
    incoming,
    segment_ids,
    positions,
    conv_gains,
    conv_in,
    conv_kernel,
    conv_out,
    conv_gate_up,
    conv_down,
    attn_gains,
    w_query,
    w_keyval,
    qk_gains,
    attn_out,
    attn_gate_up,
    attn_down,
):
    sections = lax.axis_size("section")
    seqs = lax.axis_size("seq")
    heads = lax.axis_size("head")
    section, seq, head = place()
    micro, local_rows, width = incoming.shape[1:]
    rows = local_rows // sections
    tokens = micro * rows
    half_tokens = tokens // 2
    step_rows = half_tokens // BLOCKS
    block_tok = segment_ids.shape[1]
    length = micro * block_tok
    slots = sections * seqs
    channels = conv_in.shape[2]
    hidden_units = conv_down.shape[0]
    head_width = qk_gains.shape[1]
    query_width = w_query.shape[1]
    pair_width = 2 * w_keyval.shape[2]
    kv_local = w_keyval.shape[2] // head_width
    group = query_width // (kv_local * head_width)
    score_scale = head_width ** (-0.5)
    half_model = width // sections
    share = width // (sections * seqs)

    segments = segment_ids.reshape(length)

    def own_tokens(per_token):
        start = seq * local_rows + section * rows
        return lax.dynamic_slice_in_dim(per_token.reshape(micro, block_tok), start, rows, 1).reshape(tokens)

    def moved_back(by):
        return jnp.concatenate([jnp.full((by,), -1, jnp.int32), segments[:-by]])

    local_segments = own_tokens(segments)
    same = jnp.stack([(local_segments == own_tokens(moved_back(by))).astype(FLOAT) for by in (1, 2)], 1)
    local_segments = local_segments[:, None]
    pair_index = lax.broadcasted_iota(jnp.int32, (1, 2 * head_width), 1) % (head_width // 2)
    angle_rates = THETA ** (-2.0 * pair_index.astype(FLOAT) / head_width)
    local_positions = lax.dynamic_slice_in_dim(positions, section * rows, rows, 1).reshape(tokens)
    angles = local_positions.astype(FLOAT)[:, None] * angle_rates
    cosine, sine = jnp.cos(angles), jnp.sin(angles)
    query_gain = jnp.tile(qk_gains[0:1], (1, 2))
    key_gain = jnp.tile(qk_gains[1:2], (1, 2))
    w_in = conv_in.transpose(1, 0, 2)
    w_pair = w_keyval.reshape(width, pair_width)
    first_up = conv_gate_up.transpose(1, 2, 0)
    second_up = attn_gate_up.transpose(1, 2, 0)
    slabs = [(start, min(512, hidden_units - start)) for start in range(0, hidden_units, 512)]
    tile_width = 256
    tiles = -(-hidden_units // tile_width)
    padded_units = tiles * tile_width

    def shifted_rows(ext, micro_at, back):
        return ext[micro_at, 8 - back : 8 - back + rows, :]

    def own_rows(flow, i):
        return rows_of(flow * BLOCKS + i, step_rows)

    def kept_rows(i):
        return rows_of(i, step_rows)

    total_scratch = [pltpu.VMEM((2, BLOCKS, step_rows, width), HALF)] + [
        pltpu.SemaphoreType.DMA((2, BLOCKS)) for _ in range(4)
    ]
    part_scratch = [pltpu.VMEM((tokens, width), HALF)]

    weight_scratch = [
        pltpu.VMEM((2, hidden_units, width), HALF),
        pltpu.VMEM((hidden_units, width), HALF),
        dma(3 * len(slabs)),
    ]

    def weight_loads(up_hbm, down_hbm, up_ref, down_ref, sems):
        copies = []
        for j, (start, count) in enumerate(slabs):
            span = slice(start, start + count)
            pairs = [(up_hbm.at[0, span], up_ref.at[0, span]), (up_hbm.at[1, span], up_ref.at[1, span])]
            pairs.append((down_hbm.at[span], down_ref.at[span]))
            for k, (source, target) in enumerate(pairs):
                copies.append(pltpu.make_async_copy(source, target, sems.at[3 * j + k]))
        return copies

    def conv_forward(
        in_ref, same_ref, gain_ref, win_ref, kernel_ref, wout_ref, attn_gain_ref, up_hbm, down_hbm,
        x_ref, g_ref, n1_ref, pc_ref, edge_ref, y_ref, h1_ref, n2_ref, f1_ref, a1_ref, m_ref, n3_ref,
        other, edges, normed_edges, ext, swap_send, swap_recv, edge_send, edge_recv, up_ref, down_ref, weight_sems, acc,
        part, inbox, rs, rr, gs, gr, inbox2, rs2, rr2, gs2, gr2,
    ):
        where = place()
        s, q, h = where
        partner = (1 - s, q, h)
        following = (s, lax.rem(q + 1, seqs), h)
        preceding = (s, lax.rem(q + seqs - 1, seqs), h)
        weights = weight_loads(up_hbm, down_hbm, up_ref, down_ref, weight_sems)
        start_all(weights)
        greet([partner, following, preceding], where, heads)
        give = pl.multiple_of((1 - s) * rows, rows)
        swap = remote(in_ref.at[0, :, pl.ds(give, rows)], other, swap_send.at[0], swap_recv.at[0], partner)
        swap.start()
        near = remote(in_ref.at[0, :, rows - 16 : rows], edges.at[0], edge_send.at[0], edge_recv.at[0], partner)
        near.start()
        far = remote(
            in_ref.at[0, :, local_rows - 16 : local_rows], edges.at[1], edge_send.at[1], edge_recv.at[1], following
        )
        far.start()
        keep = pl.multiple_of(s * rows, rows)
        swap.wait()
        mine = in_ref[0, :, pl.ds(keep, rows), :].reshape(tokens, width)
        theirs = other[...].reshape(tokens, width)
        first = s == 0
        x = jnp.where(first, mine, theirs)
        x_ref[...] = x
        g_ref[...] = jnp.where(first, theirs, mine)
        n1_ref[...] = norm_apply(x.astype(FLOAT), gain_ref[0:1, :]).astype(HALF)
        near.wait()
        far.wait()
        for m in range(micro):
            before = edges[1, max(m - 1, 0)]
            far_edge = jnp.where(q == 0, before, edges[1, m])
            edge = jnp.where(first, far_edge, edges[0, m]).astype(FLOAT)
            normed_edges[m * 16 : (m + 1) * 16, :] = norm_apply(edge, gain_ref[0:1, :]).astype(HALF)
        for k in range(3):
            pc_ref[k] = product(n1_ref[...], win_ref[k])
        edge_b = product(normed_edges[...], win_ref[0])
        edge_u = product(normed_edges[...], win_ref[2])
        edge_gated = edge_b * edge_u
        gated = pc_ref[0] * pc_ref[2]
        for m in range(micro):
            ext[m, 0:8, :] = edge_gated[m * 16 + 8 : m * 16 + 16, :]
            edge_ref[m] = edge_gated[m * 16 + 8 : m * 16 + 16, :]
            ext[m, 8 : 8 + rows, :] = gated[m * rows : (m + 1) * rows, :]
        for m in range(micro):
            span = slice(m * rows, (m + 1) * rows)
            mixed = (
                kernel_ref[2:3, :] * gated[span]
                + kernel_ref[1:2, :] * jnp.where(same_ref[span, 0:1] > 0, shifted_rows(ext, m, 1), 0.0)
                + kernel_ref[0:1, :] * jnp.where(same_ref[span, 1:2] > 0, shifted_rows(ext, m, 2), 0.0)
            )
            y_ref[span, :] = (pc_ref[1, span, :] * mixed).astype(HALF)
        part[...] = product(y_ref[...], wout_ref[...]).astype(HALF)

        def finish(flow, i, total):
            hidden = x_ref[own_rows(flow, i), :].astype(FLOAT) + total
            h1_ref[kept_rows(i), :] = hidden
            return norm_apply(hidden, gain_ref[1:2, :]).astype(HALF)

        head_total(part, n2_ref, inbox, rs, rr, gs, gr, where, heads, finish)
        for j, (start, count) in enumerate(slabs):
            wait_all(weights[3 * j : 3 * j + 3])
            span = slice(start, start + count)
            gate = back_product(n2_ref[...], up_ref[0, span, :])
            rise = back_product(n2_ref[...], up_ref[1, span, :])
            f1_ref[0, :, span] = gate
            f1_ref[1, :, span] = rise
            active = (gate / (1.0 + jnp.exp(-gate)) * rise).astype(HALF)
            a1_ref[:, span] = active
            term = product(active, down_ref[span, :])
            if j == 0:
                acc[...] = term
            else:
                acc[...] += term
        part[...] = acc[...].astype(HALF)

        def finish_middle(flow, i, total):
            middle = (h1_ref[kept_rows(i), :] + total).astype(HALF).astype(FLOAT)
            m_ref[kept_rows(i), :] = middle
            return norm_apply(middle, attn_gain_ref[0:1, :]).astype(HALF)

        head_total(part, n3_ref, inbox2, rs2, rr2, gs2, gr2, where, heads, finish_middle)

    (x, g, n1, projected, edge_gated, mixed, h1, n2, f1, a1, middle, n3) = call(
        conv_forward,
        "conv_forward",
        0,
        [
            ((tokens, width), HALF),
            ((tokens, width), HALF),
            ((tokens, width), HALF),
            ((3, tokens, channels), FLOAT),
            ((micro, 8, channels), FLOAT),
            ((tokens, channels), HALF),
            ((half_tokens, width), FLOAT),
            ((tokens, width), HALF),
            ((2, tokens, hidden_units), FLOAT),
            ((tokens, hidden_units), HALF),
            ((half_tokens, width), FLOAT),
            ((tokens, width), HALF),
        ],
        [
            pltpu.VMEM((micro, rows, width), HALF),
            pltpu.VMEM((2, micro, 16, width), HALF),
            pltpu.VMEM((micro * 16, width), HALF),
            pltpu.VMEM((micro, 8 + rows, channels), FLOAT),
            dma(1),
            dma(1),
            dma(2),
            dma(2),
        ]
        + weight_scratch
        + [pltpu.VMEM((tokens, width), FLOAT)]
        + part_scratch
        + total_scratch
        + total_scratch,
        [incoming, same, conv_gains, w_in, conv_kernel, conv_out, attn_gains, (first_up, ANY), (conv_down, ANY)],
        flops=5 * 10**9,
        moved=200 << 20,
    )


    grid_rows = seqs // 2
    first_blocks = 3 * grid_rows - 2
    half_share = share // 2

    def grid_place(q):
        return lax.div(q, 2), lax.rem(q, 2)

    def first_stage(source, target, send, recv, where):
        s, q, h = where
        a, b = grid_place(q)
        copies = []
        for row in range(grid_rows):
            copies.append((source(row * 2 + 1 - b, 0), row, (s, a * 2 + 1 - b, h)))
        for k in range(1, grid_rows):
            row = lax.rem(a + k, grid_rows)
            for column in range(2):
                copies.append((source(row * 2 + column, 1), grid_rows + 2 * (k - 1) + column, (s, row * 2 + b, h)))
        return [remote(block, target(i), send.at[i], recv.at[i], peer) for block, i, peer in copies]

    def passed_blocks(where):
        s, q, h = where
        a, b = grid_place(q)
        blocks = []
        for k in range(1, grid_rows):
            row = lax.rem(a + k, grid_rows)
            blocks.append((row * 2 + b, 0, [row], (s, row * 2 + b, h)))
        arrived = [grid_rows + 2 * j + 1 - b for j in range(grid_rows - 1)]
        blocks.append((a * 2 + 1 - b, 1, arrived, (s, a * 2 + 1 - b, h)))
        return blocks

    def half_rows(side):
        return slice(side * half_share, (side + 1) * half_share)

    def combine(passing, arrived, where):
        for i, (_, _, sources, _) in enumerate(passed_blocks(where)):
            total = passing(i)[...].astype(FLOAT)
            for source in sources:
                total = total + arrived[source].astype(FLOAT)
            passing(i)[...] = total.astype(HALF)

    def second_stage(passing, target, send, recv, where):
        return [
            remote(passing(i), target.at[i], send.at[i], recv.at[i], peer)
            for i, (_, _, _, peer) in enumerate(passed_blocks(where))
        ]

    def load_passing(partial, passing, sems, where):
        return [
            pltpu.make_async_copy(partial.at[dest, half_rows(side)], passing.at[i], sems.at[i])
            for i, (dest, side, _, _) in enumerate(passed_blocks(where))
        ]

    def two_halves(own, arrived, passed, where):
        a, b = grid_place(where[1])
        upper = own[half_rows(0), :].astype(FLOAT) + arrived[a].astype(FLOAT)
        for k in range(grid_rows - 1):
            upper = upper + passed[k].astype(FLOAT)
        lower = own[half_rows(1), :].astype(FLOAT) + passed[grid_rows - 1].astype(FLOAT)
        for j in range(grid_rows - 1):
            lower = lower + arrived[grid_rows + 2 * j + b].astype(FLOAT)
        return upper, lower

    def dma_grid(*shape):
        return pltpu.SemaphoreType.DMA(shape)

    def first_shape(count):
        return ((count, first_blocks, half_share, padded_units), HALF, ANY)

    def second_shape(count):
        return ((count, grid_rows, half_share, padded_units), HALF, ANY)

    def passing_scratch(count):
        return [
            pltpu.VMEM((count, grid_rows, half_share, padded_units), HALF),
            pltpu.VMEM((count, first_blocks, half_share, padded_units), HALF),
            dma_grid(count, grid_rows + 1),
            dma_grid(count, grid_rows),
            dma_grid(count, grid_rows),
        ]

    def pass_loads(partial, kinds, arrived, passing, held, sems, where):
        copies = []
        for k, kind in enumerate(kinds):
            copies += load_passing(partial.at[kind], passing.at[k], sems.at[k], where)
            copies.append(pltpu.make_async_copy(arrived.at[k], held.at[k], sems.at[k, grid_rows]))
        return copies

    def pass_sends(count, passing, held, target, send, recv, where):
        copies = []
        for k in range(count):
            combine(lambda i, k=k: passing.at[k, i], held.at[k], where)
            sends = second_stage(lambda i, k=k: passing.at[k, i], target.at[k], send.at[k], recv.at[k], where)
            start_all(sends)
            copies += sends
        return copies

    def transposed(array_ref, given_ref):
        start = pl.multiple_of(lax.axis_index("section") * half_model, 128)
        own = array_ref[:, pl.ds(start, half_model)]
        both = jnp.concatenate([own, given_ref[...]], 0)
        return both.astype(FLOAT).T.astype(HALF)

    def half_swaps(arrays, targets, send, recv, where):
        s, q, h = where
        copies = []
        for k, (array_ref, target) in enumerate(zip(arrays, targets)):
            start = pl.multiple_of((1 - s) * half_model, 128)
            copies.append(remote(array_ref.at[:, pl.ds(start, half_model)], target, send.at[k], recv.at[k], (1 - s, q, h)))
        return copies

    def latter_swap(latter, kind, start, count, send, recv, where):
        s, q, h = where
        return remote(
            latter.at[kind, 0:tokens, start : start + count],
            latter.at[kind, tokens : 2 * tokens, start : start + count],
            send,
            recv,
            (1 - s, q, h),
        )

    def gradient_tiles(former, latter, stage, partial_hbm, first_in, local_sems, send, recv, where):
        def split(t):
            kind = lax.div(t, tiles)
            at = lax.rem(t, tiles)
            return kind, pl.ds(pl.multiple_of(at * tile_width, tile_width), tile_width)

        def stored(t, dest):
            kind, columns = split(t)
            return pltpu.make_async_copy(
                stage.at[kind, dest, :, columns], partial_hbm.at[kind, dest, :, columns], local_sems.at[t, dest]
            )

        def sent(t):
            kind, columns = split(t)
            return first_stage(
                lambda dest, side: stage.at[kind, dest, half_rows(side), columns],
                lambda i: first_in.at[kind, i, :, columns],
                send.at[t],
                recv.at[t],
                where,
            )

        def tile(t):
            kind, columns = split(t)
            use = jnp.where(kind == 0, 0, 1)
            result = product(former[use], latter[kind, :, columns]).astype(HALF)
            stage[kind, :, :, columns] = result.reshape(seqs, share, tile_width)

            @pl.when(t < 2 * tiles)
            def _():
                start_all(sent(t))

            for dest in range(seqs):
                stored(t, dest).start()

        def finish():
            def stored_all(t):
                for dest in range(seqs):
                    stored(t, dest).wait()

            loop(3 * tiles, stored_all)
            loop(2 * tiles, lambda t: wait_all(sent(t)))

        return tile, finish

    ffn_scratch = weight_scratch + [
        pltpu.VMEM((tokens, width), FLOAT),
        pltpu.VMEM((2, tokens, half_model), HALF),
        pltpu.VMEM((2, half_model, 2 * tokens), HALF),
        pltpu.VMEM((3, 2 * tokens, padded_units), HALF),
        pltpu.VMEM((3, seqs, share, padded_units), HALF),
        dma(2),
        dma(2),
        pltpu.SemaphoreType.DMA((3, len(slabs))),
        pltpu.SemaphoreType.DMA((3, len(slabs))),
        pltpu.SemaphoreType.DMA((3 * tiles, seqs)),
        pltpu.SemaphoreType.DMA((2 * tiles, first_blocks)),
        pltpu.SemaphoreType.DMA((2 * tiles, first_blocks)),
    ]
    partial_outs = [((3, seqs, share, padded_units), HALF, ANY), first_shape(2)]


    def slot_peer(me, j, h):
        other = lax.rem(me + j, slots)
        return (lax.rem(other, sections), lax.div(other, sections), h)

    def query_rows(ref, m, c):
        block = ref[m * rows : (m + 1) * rows, :]
        base = c * group * head_width
        return jnp.concatenate(
            [block[:, base + r * head_width : base + (r + 1) * head_width] for r in range(group)], 0
        )

    def keys_of(all_ref, at, c, kind):
        block = all_ref[:, at * rows : (at + 1) * rows, :].reshape(block_tok, pair_width)
        base = kind * kv_local * head_width + c * head_width
        return block[:, base : base + head_width]

    def allowed_pairs(segq_ref, seg_ref, m, at, s, q):
        own_segments = segq_ref[m * rows : (m + 1) * rows, :]
        allowed = own_segments == seg_ref[at : at + 1, :]
        if at == m:
            base = q * local_rows + s * rows
            order = base + lax.broadcasted_iota(jnp.int32, (rows, block_tok), 0)
            allowed = allowed & (lax.broadcasted_iota(jnp.int32, (rows, block_tok), 1) <= order)
        bias = jnp.where(allowed, 0.0, -1e30)
        return jnp.concatenate([bias] * group, 0)

    def probabilities(rows_in, keys, biases):
        scores = [
            jnp.where(bias < 0, -1e30, back_product(rows_in, key) * score_scale)
            for key, bias in zip(keys, biases)
        ]
        summit = functools.reduce(jnp.maximum, [jnp.max(part, -1, keepdims=True) for part in scores])
        raised = [jnp.exp(part - summit) for part in scores]
        total = functools.reduce(jnp.add, [jnp.sum(part, -1, keepdims=True) for part in raised])
        inverse = 1.0 / total
        return [part * inverse for part in raised]

    def gather_pairs(all_ref, me, where, send, recv, near_send, near_recv):
        s, q, h = where
        partner = (1 - s, q, h)
        far = []
        for k, peer in enumerate(seq_peers(where, seqs)):
            copy = remote(all_ref.at[me], all_ref.at[me], send.at[k], recv.at[k], peer)
            copy.start()
            far.append(copy)
        near = [remote(all_ref.at[me], all_ref.at[me], near_send.at[0], near_recv.at[0], partner)]
        near[0].start()

        def pass_on():
            for k in range(1, seqs):
                far[k - 1].wait()
                slot = lax.rem(q + seqs - k, seqs) * sections + s
                copy = remote(all_ref.at[slot], all_ref.at[slot], near_send.at[k], near_recv.at[k], partner)
                copy.start()
                near.append(copy)
            wait_all(near)

        return pass_on

    def attention_forward(
        n3_ref, wq_ref, wp_ref, cos_ref, sin_ref, qg_ref, kg_ref, segq_ref, seg_ref, wo_ref, m_ref, gain_ref,
        qr_ref, r_ref, q_ref, all_ref, o_ref, h2_ref, n4_ref,
        send, recv, near_send, near_recv, part, inbox, rs, rr, gs, gr,
    ):
        where = place()
        s, q, h = where
        me = q * sections + s
        greet([(1 - s, q, h)] + seq_peers(where, seqs), where, heads)
        cos, sin = cos_ref[...], sin_ref[...]
        r_ref[...] = product(n3_ref[...], wp_ref[...])
        half_pair = pair_width // 2
        for start, size in chunks_of(half_pair):
            span = slice(start, start + size)
            all_ref[me, :, span] = rotary(r_ref[:, span], kg_ref[...], cos, sin).astype(HALF)
        all_ref[me, :, half_pair:] = r_ref[:, half_pair:].astype(HALF)
        pass_on = gather_pairs(all_ref, me, where, send, recv, near_send, near_recv)
        qr_ref[...] = product(n3_ref[...], wq_ref[...])
        for start, size in chunks_of(query_width):
            span = slice(start, start + size)
            q_ref[:, span] = rotary(qr_ref[:, span], qg_ref[...], cos, sin).astype(HALF)
        pass_on()
        for m in range(micro):
            biases = [allowed_pairs(segq_ref, seg_ref, m, at, s, q) for at in range(m + 1)]
            results = []
            for c in range(kv_local):
                keys = [keys_of(all_ref, at, c, 0) for at in range(m + 1)]
                weights = probabilities(query_rows(q_ref, m, c), keys, biases)
                total = functools.reduce(
                    jnp.add,
                    [product(weights[at].astype(HALF), keys_of(all_ref, at, c, 1)) for at in range(m + 1)],
                )
                results += [total[r * rows : (r + 1) * rows] for r in range(group)]
            o_ref[m * rows : (m + 1) * rows, :] = jnp.concatenate(results, -1).astype(HALF)
        part[...] = product(o_ref[...], wo_ref[...]).astype(HALF)

        def finish(flow, i, total):
            hidden = m_ref[kept_rows(i), :] + total
            h2_ref[kept_rows(i), :] = hidden
            return norm_apply(hidden, gain_ref[1:2, :]).astype(HALF)

        head_total(part, n4_ref, inbox, rs, rr, gs, gr, where, heads, finish)

    (query_raw, pair_raw, queries, all_pairs, attended, h2, n4) = call(
        attention_forward,
        "attention_forward",
        2,
        [
            ((tokens, query_width), FLOAT),
            ((tokens, pair_width), FLOAT),
            ((tokens, query_width), HALF),
            ((slots, tokens, pair_width), HALF),
            ((tokens, query_width), HALF),
            ((half_tokens, width), FLOAT),
            ((tokens, width), HALF),
        ],
        [dma(seqs - 1), dma(seqs - 1), dma(seqs), dma(seqs)] + part_scratch + total_scratch,
        [
            n3, w_query, w_pair, cosine, sine, query_gain, key_gain, local_segments, segment_ids,
            attn_out, middle, attn_gains,
        ],
        flops=4 * 10**9,
        moved=150 << 20,
    )

    def slab_width(start, count):
        return min(-(-count // tile_width) * tile_width, padded_units - start)

    def clear_padding(latter):
        if padded_units > hidden_units:
            latter[:, :, hidden_units:] = jnp.zeros((3, 2 * tokens, padded_units - hidden_units), HALF)

    def second_ffn(
        n4_ref, g_ref, h2_ref, gain_ref, up_hbm, down_hbm,
        py_ref, gh2_ref, low_ref, gg_ref, partial_hbm, first_in,
        acc_y, up_ref, down_ref, weight_sems, acc, given, former, latter, stage, hs, hr, ls, lr, local_sems, ts, tr,
        part, inbox, rs, rr, gs, gr,
    ):
        where = place()
        s, q, h = where
        weights = weight_loads(up_hbm, down_hbm, up_ref, down_ref, weight_sems)
        start_all(weights)
        clear_padding(latter)
        greet([(1 - s, q, h)] + seq_peers(where, seqs), where, heads)
        halves = half_swaps([g_ref, n4_ref], [given.at[0], given.at[1]], hs, hr, where)
        start_all(halves)
        gg_ref[...] = jnp.zeros_like(gg_ref)
        swaps = []
        for j, (start, count) in enumerate(slabs):
            wait_all(weights[3 * j : 3 * j + 3])
            span = slice(start, start + count)
            gate = back_product(n4_ref[...], up_ref[0, span, :])
            rise = back_product(n4_ref[...], up_ref[1, span, :])
            grad_active = back_product(g_ref[...], down_ref[span, :])
            chance = 1.0 / (1.0 + jnp.exp(-gate))
            silu = gate * chance
            active = (silu * rise).astype(HALF)
            grad_gate = (grad_active * rise * (chance * (1.0 + gate * (1.0 - chance)))).astype(HALF)
            grad_rise = (grad_active * silu).astype(HALF)
            latter[0, 0:tokens, span] = active
            latter[1, 0:tokens, span] = grad_gate
            latter[2, 0:tokens, span] = grad_rise
            for kind in range(3):
                swap = latter_swap(
                    latter, kind, start, slab_width(start, count), ls.at[kind, j], lr.at[kind, j], where
                )
                swap.start()
                swaps.append(swap)
            term = product(grad_gate, up_ref[0, span, :]) + product(grad_rise, up_ref[1, span, :])
            term_y = product(active, down_ref[span, :])
            if j == 0:
                acc[...] = term
                acc_y[...] = term_y
            else:
                acc[...] += term
                acc_y[...] += term_y
        part[...] = acc[...].astype(HALF)

        for flow, holder in ((0, 0), (1, heads - 1)):

            @pl.when(h == holder)
            def _(flow=flow):
                acc_y[flow * half_tokens : (flow + 1) * half_tokens, :] += h2_ref[...]

        py_ref[...] = acc_y[...].astype(HALF)
        tile, tiles_done = gradient_tiles(
            former, latter, stage, partial_hbm, first_in, local_sems, ts, tr, where
        )

        def filler(t):
            for k, array_ref in enumerate((g_ref, n4_ref)):

                @pl.when(t == k)
                def _(k=k, array_ref=array_ref):
                    halves[k].wait()
                    if k:
                        wait_all(swaps)
                    former[k] = transposed(array_ref, given.at[k])

            @pl.when(t >= 2)
            def _():
                tile(t - 2)

        def finish(flow, i, total):
            grad_hidden, grad_gain = norm_back(h2_ref[kept_rows(i), :], gain_ref[1:2, :], total)
            grad = g_ref[own_rows(flow, i), :].astype(FLOAT) + grad_hidden
            gh2_ref[kept_rows(i), :] = grad
            gg_ref[...] += grad_gain
            return grad.astype(HALF)

        head_total(part, low_ref, inbox, rs, rr, gs, gr, where, heads, finish, filler, 3 * tiles + 2)
        tiles_done()

    (part_y, gh2, gh2_low, grad_gain_attn1, partial2, first2) = call(
        second_ffn,
        "second_ffn",
        4,
        [
            ((tokens, width), HALF),
            ((half_tokens, width), FLOAT),
            ((tokens, width), HALF),
            ((1, width), FLOAT),
        ]
        + partial_outs,
        [pltpu.VMEM((tokens, width), FLOAT)] + ffn_scratch + part_scratch + total_scratch,
        [n4, g, h2, attn_gains, (second_up, ANY), (attn_down, ANY)],
        flops=12 * 10**9,
        moved=150 << 20,
    )
    yout = lax.psum(part_y, "head")
    def attention_backward(
        glow_ref, wo_ref, q_ref, all_ref, segq_ref, seg_ref,
        qr_ref, r_ref, cos_ref, sin_ref, qg_ref, kg_ref, wq_ref, wp_ref, m_ref, gh2_ref, gain_ref, partial2_hbm, first2_hbm,
        bq_ref, br_ref, low_ref, gg_ref, gqk_ref, second_in, first_in,
        grads, totals, gq_ref, gp_ref, near_slots, pair_slots, ns, nr, ps, pr,
        passing, held, load_sems, vs, vr, fs, fr,
        part, inbox, rs, rr, gs, gr,
    ):
        where = place()
        s, q, h = where
        partner = (1 - s, q, h)
        peers = seq_peers(where, seqs)
        loads = pass_loads(partial2_hbm, (0, 1), first2_hbm, passing, held, load_sems, where)
        start_all(loads)
        greet([partner] + peers, where, heads)
        wait_all(loads)
        travelling = pass_sends(2, passing, held, second_in, vs, vr, where)
        gg_ref[...] = jnp.zeros_like(gg_ref)
        gqk_ref[...] = jnp.zeros_like(gqk_ref)
        grads[...] = back_product(glow_ref[...], wo_ref[...]).astype(HALF)
        for m in range(micro):
            biases = [allowed_pairs(segq_ref, seg_ref, m, at, s, q) for at in range(m + 1)]
            results = []
            for c in range(kv_local):
                keys = [keys_of(all_ref, at, c, 0) for at in range(m + 1)]
                values = [keys_of(all_ref, at, c, 1) for at in range(m + 1)]
                rows_in = query_rows(q_ref, m, c)
                grad_rows = query_rows(grads, m, c)
                chances = probabilities(rows_in, keys, biases)
                grad_chances = [back_product(grad_rows, value) for value in values]
                inner = functools.reduce(
                    jnp.add,
                    [jnp.sum(a * b, -1, keepdims=True) for a, b in zip(grad_chances, chances)],
                )
                total = None
                for at in range(m + 1):
                    grad_scores = (chances[at] * (grad_chances[at] - inner)).astype(HALF)
                    term = product(grad_scores, keys[at])
                    total = term if total is None else total + term
                    grad_key = outer_sum(grad_scores, rows_in) * score_scale
                    grad_value = outer_sum(chances[at].astype(HALF), grad_rows)
                    if at == m:
                        totals[at, c] = grad_key
                        totals[at, kv_local + c] = grad_value
                    else:
                        totals[at, c] += grad_key
                        totals[at, kv_local + c] += grad_value
                total = total * score_scale
                results += [total[r * rows : (r + 1) * rows] for r in range(group)]
            gq_ref[m * rows : (m + 1) * rows, :] = jnp.concatenate(results, -1)
        for at in range(micro):
            joined = jnp.concatenate([totals[at, k] for k in range(2 * kv_local)], -1).astype(HALF)
            gp_ref[:, at * rows : (at + 1) * rows, :] = joined.reshape(slots, rows, pair_width)
        near = []
        for other in range(seqs):
            copy = remote(gp_ref.at[other * sections + 1 - s], near_slots.at[other], ns.at[other], nr.at[other], partner)
            copy.start()
            near.append(copy)
        cos, sin = cos_ref[...], sin_ref[...]
        copies = []
        wait_all(near)
        for other in range(seqs):
            mine = gp_ref[other * sections + s].astype(FLOAT)
            near_slots[other] = (mine + near_slots[other].astype(FLOAT)).astype(HALF)
        for k, peer in enumerate(peers):
            copy = remote(near_slots.at[peer[1]], pair_slots.at[k], ps.at[k], pr.at[k], peer)
            copy.start()
            copies.append(copy)
        later = first_stage(
            lambda dest, side: partial2_hbm.at[2, dest, half_rows(side)], lambda i: first_in.at[0, i], fs, fr, where
        )
        start_all(later)
        travelling += later
        for start, size in chunks_of(query_width):
            span = slice(start, start + size)
            grad_raw, grad_gain = rotary_back(qr_ref[:, span], qg_ref[...], cos, sin, gq_ref[:, span])
            bq_ref[:, span] = grad_raw.astype(HALF)
            gqk_ref[0:1, :size] += grad_gain
        partial = back_product(bq_ref[...], wq_ref[...])
        wait_all(copies)
        grad_pair = near_slots[q].astype(FLOAT)
        for j in range(seqs - 1):
            grad_pair = grad_pair + pair_slots[j].astype(FLOAT)
        half_pair = pair_width // 2
        for start, size in chunks_of(half_pair):
            span = slice(start, start + size)
            grad_raw, grad_gain = rotary_back(r_ref[:, span], kg_ref[...], cos, sin, grad_pair[:, span])
            br_ref[:, span] = grad_raw.astype(HALF)
            gqk_ref[1:2, :size] += grad_gain
        br_ref[:, half_pair:] = grad_pair[:, half_pair:].astype(HALF)
        part[...] = (partial + back_product(br_ref[...], wp_ref[...])).astype(HALF)

        def finish(flow, i, total):
            grad_entry, grad_gain = norm_back(m_ref[kept_rows(i), :], gain_ref[0:1, :], total)
            gg_ref[...] += grad_gain
            return (gh2_ref[kept_rows(i), :] + grad_entry).astype(HALF)

        head_total(part, low_ref, inbox, rs, rr, gs, gr, where, heads, finish)
        wait_all(travelling)

    (bq, br, gm_low, grad_gain_attn0, grad_qk, second2, first2_last) = call(
        attention_backward,
        "attention_backward",
        5,
        [
            ((tokens, query_width), HALF),
            ((tokens, pair_width), HALF),
            ((tokens, width), HALF),
            ((1, width), FLOAT),
            ((8, 128), FLOAT),
            second_shape(2),
            first_shape(1),
        ],
        [
            pltpu.VMEM((tokens, query_width), HALF),
            pltpu.VMEM((micro, 2 * kv_local, block_tok, head_width), FLOAT),
            pltpu.VMEM((tokens, query_width), FLOAT),
            pltpu.VMEM((slots, tokens, pair_width), HALF),
            pltpu.VMEM((seqs, tokens, pair_width), HALF),
            pltpu.VMEM((seqs - 1, tokens, pair_width), HALF),
            dma(seqs),
            dma(seqs),
            dma(seqs - 1),
            dma(seqs - 1),
        ]
        + passing_scratch(2)
        + [dma(first_blocks), dma(first_blocks)]
        + part_scratch
        + total_scratch,
        [
            gh2_low, attn_out, queries, all_pairs, local_segments, segment_ids,
            query_raw, pair_raw, cosine, sine, query_gain, key_gain, w_query, w_pair, middle, gh2, attn_gains,
            (partial2, ANY), (first2, ANY),
        ],
        flops=6 * 10**9,
        moved=130 << 20,
    )

    def first_ffn_back(
        gm_ref, n2_ref, f1_ref, a1_ref, h1_ref, gain_ref, up_hbm, down_hbm, partial2_hbm, first2_hbm,
        gh1_ref, low_ref, gg_ref, partial_hbm, first_in, second_in,
        up_ref, down_ref, weight_sems, acc, given, former, latter, stage, hs, hr, ls, lr, local_sems, ts, tr,
        passing, held, load_sems, vs, vr,
        part, inbox, rs, rr, gs, gr,
    ):
        where = place()
        s, q, h = where
        weights = weight_loads(up_hbm, down_hbm, up_ref, down_ref, weight_sems)
        loads = pass_loads(partial2_hbm, (2,), first2_hbm, passing, held, load_sems, where)
        start_all(loads)
        start_all(weights)
        clear_padding(latter)
        latter[0, 0:tokens, 0:hidden_units] = a1_ref[...]
        greet([(1 - s, q, h)] + seq_peers(where, seqs), where, heads)
        wait_all(loads)
        travelling = pass_sends(1, passing, held, second_in, vs, vr, where)
        halves = half_swaps([gm_ref, n2_ref], [given.at[0], given.at[1]], hs, hr, where)
        start_all(halves)
        gg_ref[...] = jnp.zeros_like(gg_ref)
        swaps = []
        for j, (start, count) in enumerate(slabs):
            wait_all(weights[3 * j : 3 * j + 3])
            span = slice(start, start + count)
            gate = f1_ref[0, :, span]
            rise = f1_ref[1, :, span]
            grad_active = back_product(gm_ref[...], down_ref[span, :])
            chance = 1.0 / (1.0 + jnp.exp(-gate))
            grad_gate = (grad_active * rise * (chance * (1.0 + gate * (1.0 - chance)))).astype(HALF)
            grad_rise = (grad_active * (gate * chance)).astype(HALF)
            latter[1, 0:tokens, span] = grad_gate
            latter[2, 0:tokens, span] = grad_rise
            for kind in range(3):
                swap = latter_swap(
                    latter, kind, start, slab_width(start, count), ls.at[kind, j], lr.at[kind, j], where
                )
                swap.start()
                swaps.append(swap)
            term = product(grad_gate, up_ref[0, span, :]) + product(grad_rise, up_ref[1, span, :])
            if j == 0:
                acc[...] = term
            else:
                acc[...] += term
        part[...] = acc[...].astype(HALF)
        tile, tiles_done = gradient_tiles(
            former, latter, stage, partial_hbm, first_in, local_sems, ts, tr, where
        )

        def filler(t):
            for k, array_ref in enumerate((gm_ref, n2_ref)):

                @pl.when(t == k)
                def _(k=k, array_ref=array_ref):
                    halves[k].wait()
                    if k:
                        wait_all(swaps)
                    former[k] = transposed(array_ref, given.at[k])

            @pl.when(t >= 2)
            def _():
                tile(t - 2)

        def finish(flow, i, total):
            grad_hidden, grad_gain = norm_back(h1_ref[kept_rows(i), :], gain_ref[1:2, :], total)
            gg_ref[...] += grad_gain
            grad = gm_ref[own_rows(flow, i), :].astype(FLOAT) + grad_hidden
            gh1_ref[kept_rows(i), :] = grad
            return grad.astype(HALF)

        head_total(part, low_ref, inbox, rs, rr, gs, gr, where, heads, finish, filler, 3 * tiles + 2)
        tiles_done()
        wait_all(travelling)

    (gh1, gh1_low, grad_gain_conv1, partial1, first1, second2_last) = call(
        first_ffn_back,
        "first_ffn_back",
        6,
        [((half_tokens, width), FLOAT), ((tokens, width), HALF), ((1, width), FLOAT)] + partial_outs + [second_shape(1)],
        ffn_scratch + passing_scratch(1) + part_scratch + total_scratch,
        [gm_low, n2, f1, a1, h1, conv_gains, (first_up, ANY), (conv_down, ANY), (partial2, ANY), (first2_last, ANY)],
        flops=9 * 10**9,
        moved=150 << 20,
    )
    small_width = max(share, channels, 2 * head_width)
    widths = [query_width, query_width + pair_width, channels, 3 * channels]

    def conv_backward(
        low_ref, gh1_ref, pc_ref, edge_ref, same_ref, kernel_ref, wout_ref, win_ref, x_ref, gain_ref, yout_ref,
        ghlow_ref, n3_ref, n1_ref, o_ref, bq_ref, br_ref, mixed_ref, small_in,
        partial1, partial2, first1, first2, first2_last, second2, second2_last,
        edges_ref, sums_ref, gout2_ref, gmix_ref, gout1_ref, gin_ref, gdown2, gup2, gdown1, gup1,
        bp_ref, ext, spread, gz_ext, outgoing, arrived, full, gg_ref, edge_send, edge_recv, swap_send, swap_recv,
        given, former, latter0, latter1, latter2, latter3, stage0, stage1, stage2, stage3,
        in0, in1, in2, in3, turn0, turn1, turn2, turn3, hs, hr, ls, lr, ms, mr, us, ur,
        own_buf, first_buf, second_buf, passing, item_sems, vs, vr, fs, fr, down_stage, up_stage, out_sems,
        packed, boxes, summed, final, zs, zr, ss, sr,
        part, inbox, rs, rr, gs, gr,
    ):
        where = place()
        s, q, h = where
        first = s == 0
        partner = (1 - s, q, h)
        preceding = (1 - s, jnp.where(first, lax.rem(q + seqs - 1, seqs), q), h)
        following = (1 - s, jnp.where(first, q, lax.rem(q + 1, seqs)), h)
        others = [(s, q, lax.rem(h + k, heads)) for k in range(1, heads)]
        me = q * sections + s
        slot_peers = [slot_peer(me, j, h) for j in range(1, slots)]
        peers = seq_peers(where, seqs)
        latters, stages = [latter0, latter1, latter2, latter3], [stage0, stage1, stage2, stage3]
        incomes, turns = [in0, in1, in2, in3], [turn0, turn1, turn2, turn3]
        loads = []
        sources = [
            (partial2.at[0], first2.at[0], second2.at[0]),
            (partial2.at[1], first2.at[1], second2.at[1]),
            (partial2.at[2], first2_last.at[0], second2_last.at[0]),
            (partial1.at[0], first1.at[0], None),
            (partial1.at[1], first1.at[1], None),
            (partial1.at[2], None, None),
        ]
        for n, (partial, arrived_hbm, passed_hbm) in enumerate(sources):
            copies = [pltpu.make_async_copy(partial.at[q], own_buf.at[n], item_sems.at[n, 0])]
            if arrived_hbm is not None:
                copies.append(pltpu.make_async_copy(arrived_hbm, first_buf.at[n], item_sems.at[n, 1]))
            if passed_hbm is not None:
                copies.append(pltpu.make_async_copy(passed_hbm, second_buf.at[n], item_sems.at[n, 2]))
            else:
                copies += load_passing(partial, passing.at[n - 3], item_sems.at[n, pl.ds(3, grid_rows)], where)
            loads.append(copies)
        for copies in loads[3:] + loads[:3]:
            start_all(copies)
        greet([partner, preceding, following] + others + slot_peers, where, heads)
        latters[0][0:tokens, :] = o_ref[...]
        latters[1][0:tokens, 0:query_width] = bq_ref[...]
        latters[1][0:tokens, query_width:] = br_ref[...]
        latters[2][0:tokens, :] = mixed_ref[...]
        former_refs = [ghlow_ref, n3_ref, low_ref, n1_ref]
        halves = half_swaps(former_refs, [given.at[k] for k in range(4)], hs, hr, where)
        start_all(halves)
        swaps = [
            remote(latters[k].at[0:tokens], latters[k].at[tokens : 2 * tokens], ls.at[k], lr.at[k], partner) for k in range(4)
        ]
        start_all(swaps[:3])
        gg_ref[...] = jnp.zeros_like(gg_ref)
        gated = pc_ref[0] * pc_ref[2]
        grad_y = back_product(low_ref[...], wout_ref[...])
        gz = grad_y * pc_ref[1]
        zero = jnp.zeros((8, channels), FLOAT)
        for m in range(micro):
            span = slice(m * rows, (m + 1) * rows)
            one = jnp.where(same_ref[span, 0:1] > 0, gz[span], 0.0) * kernel_ref[1:2, :]
            two = jnp.where(same_ref[span, 1:2] > 0, gz[span], 0.0) * kernel_ref[0:1, :]
            gz_ext[0, m, 0:rows, :] = one
            gz_ext[0, m, rows : rows + 8, :] = zero
            gz_ext[1, m, 0:rows, :] = two
            gz_ext[1, m, rows : rows + 8, :] = zero
            outgoing[m] = zero
            outgoing[m, 0:1, :] = two[0:1]
            outgoing[m, 1:2, :] = one[0:1] + two[1:2]
        edge = remote(outgoing, arrived, edge_send.at[0], edge_recv.at[0], preceding)
        edge.start()
        bulk = []
        for n in (3, 4):
            wait_all(loads[n])
            combine(lambda i, n=n: passing.at[n - 3, i], first_buf.at[n], where)
            sends = second_stage(
                lambda i, n=n: passing.at[n - 3, i], second_buf.at[n], vs.at[n - 3], vr.at[n - 3], where
            )
            start_all(sends)
            bulk.append(sends)
        last_first = first_stage(
            lambda dest, side: partial1.at[2, dest, half_rows(side)], lambda i: first_buf.at[5, i], fs, fr, where
        )
        start_all(last_first)
        taps = [None, None, None]
        for m in range(micro):
            span = slice(m * rows, (m + 1) * rows)
            ext[m, 0:8, :] = edge_ref[m]
            ext[m, 8 : 8 + rows, :] = gated[span]
            back_one = jnp.where(same_ref[span, 0:1] > 0, shifted_rows(ext, m, 1), 0.0)
            back_two = jnp.where(same_ref[span, 1:2] > 0, shifted_rows(ext, m, 2), 0.0)
            mixed = (
                kernel_ref[2:3, :] * gated[span]
                + kernel_ref[1:2, :] * back_one
                + kernel_ref[0:1, :] * back_two
            )
            bp_ref[span, channels : 2 * channels] = (grad_y[span] * mixed).astype(HALF)
            for k, value in enumerate((back_two, back_one, gated[span])):
                term = jnp.sum(value * gz[span], 0, keepdims=True)
                taps[k] = term if taps[k] is None else taps[k] + term
        for m in range(micro):
            span = slice(m * rows, (m + 1) * rows)
            spread[m] = (
                kernel_ref[2:3, :] * gz[span]
                + gz_ext[0, m, 1 : rows + 1, :]
                + gz_ext[1, m, 2 : rows + 2, :]
            )
        edge.wait()
        wrap = (s == sections - 1) & (q == seqs - 1)
        for m in range(micro):
            follow = arrived[m + 1, 0:2, :] if m + 1 < micro else jnp.zeros((2, channels), FLOAT)
            spread[m, rows - 2 : rows, :] += jnp.where(wrap, follow, arrived[m, 0:2, :])
        for m in range(micro):
            span = slice(m * rows, (m + 1) * rows)
            bp_ref[span, 0:channels] = (spread[m] * pc_ref[2, span, :]).astype(HALF)
            bp_ref[span, 2 * channels :] = (spread[m] * pc_ref[0, span, :]).astype(HALF)
        latters[3][0:tokens, :] = bp_ref[...]
        swaps[3].start()
        total = back_product(bp_ref[:, 0:channels], win_ref[0])
        total = total + back_product(bp_ref[:, channels : 2 * channels], win_ref[1])
        total = total + back_product(bp_ref[:, 2 * channels :], win_ref[2])
        part[...] = total.astype(HALF)

        def finish(flow, i, total):
            start = x_ref[own_rows(flow, i), :].astype(FLOAT)
            grad_start, grad_gain = norm_back(start, gain_ref[0:1, :], total)
            gg_ref[...] += grad_gain
            return (gh1_ref[kept_rows(i), :] + grad_start).astype(HALF)

        mixer_sends = [
            first_stage(
                lambda dest, side, k=k: stages[k].at[dest, half_rows(side)],
                lambda i, k=k: incomes[k].at[i],
                ms.at[k],
                mr.at[k],
                where,
            )
            for k in range(4)
        ]

        def mixer_step(t):
            for k in range(4):

                @pl.when(t == 2 * k)
                def _(k=k):
                    halves[k].wait()
                    former[...] = transposed(former_refs[k], given.at[k])

                @pl.when(t == 2 * k + 1)
                def _(k=k):
                    swaps[k].wait()
                    result = product(former[...], latters[k][...]).astype(HALF)
                    stages[k][...] = result.reshape(seqs, share, widths[k])
                    start_all(mixer_sends[k])

        head_total(part, full, inbox, rs, rr, gs, gr, where, heads, finish, mixer_step, 8)
        keep = pl.ds(pl.multiple_of(s * rows, rows), rows)
        edges_ref[0, :, keep, :] = jnp.where(first, full[...], yout_ref[...]).reshape(micro, rows, width)
        part[...] = jnp.where(first, yout_ref[...], full[...])
        edge_swaps = []
        for m in range(micro):
            copy = remote(
                part.at[m * rows : (m + 1) * rows], edges_ref.at[0, m, keep], swap_send.at[m], swap_recv.at[m], partner
            )
            copy.start()
            edge_swaps.append(copy)
        packed[...] = small_in[...]
        packed[:, 5:8, 0:channels] = jnp.broadcast_to(jnp.concatenate(taps, 0)[None], (slots, 3, channels))
        for d in range(slots):
            packed[d, 0:1, 0:share] = gg_ref[:, d * share : (d + 1) * share]
        over = []
        for k, peer in enumerate(others):
            copy = remote(packed, boxes.at[k], zs.at[k], zr.at[k], peer)
            copy.start()
            over.append(copy)
        def passed_on(n):
            sends = second_stage(
                lambda i: passing.at[n - 3, i], second_buf.at[n], vs.at[n - 3], vr.at[n - 3], where
            )
            start_all(sends)
            bulk.append(sends)

        wait_all(last_first)
        wait_all(loads[5])
        combine(lambda i: passing.at[2, i], first_buf.at[5], where)
        passed_on(5)
        wait_all(over)
        over_heads = boxes[0]
        for j in range(1, heads - 1):
            over_heads = over_heads + boxes[j]
        row = lax.broadcasted_iota(jnp.int32, over_heads.shape, 1)
        summed[...] = packed[...] + jnp.where(row < 5, over_heads, 0.0)
        across = []
        for j, peer in enumerate(slot_peers):
            copy = remote(summed.at[peer[0] * seqs + peer[1]], final.at[j], ss.at[j], sr.at[j], peer)
            copy.start()
            across.append(copy)
        outs = []

        def leave(source, target, at):
            copy = pltpu.make_async_copy(source, target, out_sems.at[at])
            copy.start()
            outs.append(copy)

        def fill_stage(n, target):
            upper, lower = two_halves(own_buf.at[n], first_buf.at[n], second_buf.at[n], where)
            target[half_rows(0), :] = upper[:, :hidden_units].astype(HALF)
            target[half_rows(1), :] = lower[:, :hidden_units].astype(HALF)

        def second_half_items():
            for n in range(3):
                wait_all(loads[n])
            fill_stage(0, down_stage.at[0])
            leave(down_stage.at[0], gdown2, 0)
            for kind in range(2):
                fill_stage(1 + kind, up_stage.at[0, kind])
            leave(up_stage.at[0], gup2, 1)

        mixer_turns = []
        for k in range(4):
            wait_all(mixer_sends[k])
            blocks = passed_blocks(where)

            def passing_block(i, k=k):
                return stages[k].at[blocks[i][0], half_rows(blocks[i][1])]

            combine(passing_block, incomes[k], where)
            sends = second_stage(passing_block, turns[k], us.at[k], ur.at[k], where)
            start_all(sends)
            mixer_turns.append(sends)
            if k == 1:
                second_half_items()
        for n in (3, 4, 5):
            wait_all(bulk[n - 3])
            if n == 3:
                fill_stage(3, down_stage.at[1])
                leave(down_stage.at[1], gdown1, 2)
            else:
                fill_stage(n, up_stage.at[1, n - 4])
        leave(up_stage.at[1], gup1, 3)
        wait_all(edge_swaps)
        wait_all(across)
        total = summed[s * seqs + q]
        for j in range(slots - 1):
            total = total + final[j]
        sums_ref[...] = total
        for k, target in enumerate((gout2_ref, gmix_ref, gout1_ref, None)):
            wait_all(mixer_turns[k])
            for side, value in enumerate(two_halves(stages[k].at[q], incomes[k], turns[k], where)):
                value = value.astype(HALF)
                if target is None:
                    for c in range(3):
                        gin_ref[c, half_rows(side), :] = value[:, c * channels : (c + 1) * channels]
                else:
                    target[half_rows(side), :] = value
        wait_all(outs)

    folded = grad_qk[0:2, :head_width] + grad_qk[0:2, head_width : 2 * head_width]
    gain_rows = jnp.concatenate(
        [jnp.zeros_like(grad_gain_conv1), grad_gain_conv1, grad_gain_attn0, grad_gain_attn1], 0
    )

    def to_width(array):
        return jnp.pad(array, [(0, 0)] * (array.ndim - 1) + [(0, small_width - array.shape[-1])])

    small = jnp.concatenate(
        [
            to_width(gain_rows.reshape(4, slots, share).transpose(1, 0, 2)),
            jnp.broadcast_to(to_width(folded.reshape(1, 1, 2 * head_width)), (slots, 1, small_width)),
            jnp.zeros((slots, 3, small_width), FLOAT),
        ],
        1,
    )

    (section_edges, sums, gout2, gmix, gout1, gin, gdown2, gup2, gdown1, gup1) = call(
        conv_backward,
        "conv_backward",
        7,
        [
            ((1, micro, local_rows, width), HALF),
            ((8, small_width), FLOAT),
            ((share, widths[0]), HALF),
            ((share, widths[1]), HALF),
            ((share, widths[2]), HALF),
            ((3, share, channels), HALF),
            ((share, hidden_units), HALF, ANY),
            ((2, share, hidden_units), HALF, ANY),
            ((share, hidden_units), HALF, ANY),
            ((2, share, hidden_units), HALF, ANY),
        ],
        [
            pltpu.VMEM((tokens, 3 * channels), HALF),
            pltpu.VMEM((micro, 8 + rows, channels), FLOAT),
            pltpu.VMEM((micro, rows, channels), FLOAT),
            pltpu.VMEM((2, micro, rows + 8, channels), FLOAT),
            pltpu.VMEM((micro, 8, channels), FLOAT),
            pltpu.VMEM((micro, 8, channels), FLOAT),
            pltpu.VMEM((tokens, width), HALF),
            pltpu.VMEM((1, width), FLOAT),
            dma(1),
            dma(1),
            dma(micro),
            dma(micro),
            pltpu.VMEM((4, tokens, half_model), HALF),
            pltpu.VMEM((half_model, 2 * tokens), HALF),
        ]
        + [pltpu.VMEM((2 * tokens, size), HALF) for size in widths]
        + [pltpu.VMEM((seqs, share, size), HALF) for size in widths]
        + [pltpu.VMEM((first_blocks, half_share, size), HALF) for size in widths]
        + [pltpu.VMEM((grid_rows, half_share, size), HALF) for size in widths]
        + [
            dma(4),
            dma(4),
            dma(4),
            dma(4),
            dma_grid(4, first_blocks),
            dma_grid(4, first_blocks),
            dma_grid(4, grid_rows),
            dma_grid(4, grid_rows),
            pltpu.VMEM((6, share, padded_units), HALF),
            pltpu.VMEM((6, first_blocks, half_share, padded_units), HALF),
            pltpu.VMEM((6, grid_rows, half_share, padded_units), HALF),
            pltpu.VMEM((3, grid_rows, half_share, padded_units), HALF),
            dma_grid(6, 3 + grid_rows),
            dma_grid(3, grid_rows),
            dma_grid(3, grid_rows),
            dma(first_blocks),
            dma(first_blocks),
            pltpu.VMEM((2, share, hidden_units), HALF),
            pltpu.VMEM((2, 2, share, hidden_units), HALF),
            dma(4),
            pltpu.VMEM((slots, 8, small_width), FLOAT),
            pltpu.VMEM((heads - 1, slots, 8, small_width), FLOAT),
            pltpu.VMEM((slots, 8, small_width), FLOAT),
            pltpu.VMEM((slots - 1, 8, small_width), FLOAT),
            dma(heads - 1),
            dma(heads - 1),
            dma(slots - 1),
            dma(slots - 1),
        ]
        + part_scratch
        + total_scratch,
        [
            gh1_low, gh1, projected, edge_gated, same, conv_kernel, conv_out, w_in, x, conv_gains, yout,
            gh2_low, n3, n1, attended, bq, br, mixed, small,
        ]
        + [(array, ANY) for array in (partial1, partial2, first1, first2, first2_last, second2, second2_last)],
        flops=5 * 10**9,
        moved=300 << 20,
    )
    def results(
        edges_in, sums_in, gout2_in, gmix_in, gout1_in, gin_in, gdown2_in, gup2_in, gdown1_in, gup1_in,
        edges_out, cgain_out, gin_out, taps_out, gout1_out, gup1_out, gdown1_out,
        again_out, gq_out, gkv_out, gqk_out, gout2_out, gup2_out, gdown2_out,
        down_in, up_in, down_stage, up_stage, edges_held, in_sems, out_sems, edge_sem,
    ):
        edges_load = pltpu.make_async_copy(edges_in, edges_held, edge_sem.at[0])
        edges_load.start()
        loads = [
            pltpu.make_async_copy(source, target, in_sems.at[k])
            for k, (source, target) in enumerate(
                [(gdown1_in, down_in.at[0]), (gup1_in, up_in.at[0]), (gdown2_in, down_in.at[1]), (gup2_in, up_in.at[1])]
            )
        ]
        start_all(loads)
        stores = []
        for k, (down_out, up_out) in enumerate(((gdown1_out, gup1_out), (gdown2_out, gup2_out))):
            loads[2 * k].wait()
            down_stage[k] = down_in[k].astype(FLOAT)
            stores.append(pltpu.make_async_copy(down_stage.at[k], down_out, out_sems.at[2 * k]))
            stores[-1].start()
            loads[2 * k + 1].wait()
            for kind in range(2):
                up_stage[k, :, kind, :] = up_in[k, kind].astype(FLOAT)
            stores.append(pltpu.make_async_copy(up_stage.at[k], up_out, out_sems.at[2 * k + 1]))
            stores[-1].start()
        cgain_out[...] = sums_in[0:2, 0:share]
        again_out[...] = sums_in[2:4, 0:share]
        taps_out[...] = sums_in[5:8, 0:channels]
        for kind in range(2):
            gqk_out[kind : kind + 1, :] = sums_in[4:5, kind * head_width : (kind + 1) * head_width]
            start = query_width + kind * (pair_width // 2)
            gkv_out[:, kind, :] = gmix_in[:, start : start + pair_width // 2].astype(FLOAT)
        gq_out[...] = gmix_in[:, 0:query_width].astype(FLOAT)
        gout1_out[...] = gout1_in[...].astype(FLOAT)
        gout2_out[...] = gout2_in[...].astype(FLOAT)
        gin_out[...] = gin_in[...].astype(FLOAT)
        edges_load.wait()
        stores.append(pltpu.make_async_copy(edges_held, edges_out, edge_sem.at[1]))
        stores[-1].start()
        wait_all(stores)

    (
        section_edges, cgain, gin, taps, gout1, gup1, gdown1, again, gq, gkv, gqk, gout2, gup2, gdown2,
    ) = call(
        results,
        "results",
        None,
        [
            ((1, micro, local_rows, width), HALF, ANY),
            ((2, share), FLOAT),
            ((3, share, channels), FLOAT),
            ((3, channels), FLOAT),
            ((share, channels), FLOAT),
            ((share, 2, hidden_units), FLOAT, ANY),
            ((share, hidden_units), FLOAT, ANY),
            ((2, share), FLOAT),
            ((share, query_width), FLOAT),
            ((share, 2, pair_width // 2), FLOAT),
            ((2, head_width), FLOAT),
            ((share, query_width), FLOAT),
            ((share, 2, hidden_units), FLOAT, ANY),
            ((share, hidden_units), FLOAT, ANY),
        ],
        [
            pltpu.VMEM((2, share, hidden_units), HALF),
            pltpu.VMEM((2, 2, share, hidden_units), HALF),
            pltpu.VMEM((2, share, hidden_units), FLOAT),
            pltpu.VMEM((2, share, 2, hidden_units), FLOAT),
            pltpu.VMEM((1, micro, local_rows, width), HALF),
            dma(4),
            dma(4),
            dma(2),
        ],
        [(section_edges, ANY), sums, gout2, gmix, gout1, gin]
        + [(array, ANY) for array in (gdown2, gup2, gdown1, gup1)],
        moved=25 << 20,
    )
    return (
        section_edges,
        cgain,
        gin.transpose(1, 0, 2),
        taps,
        gout1.T,
        gup1,
        gdown1.T,
        again,
        gq,
        gkv,
        gqk,
        gout2.T,
        gup2,
        gdown2.T,
    )


def solution(mesh):
    return jax.shard_map(
        per_device,
        mesh=mesh,
        in_specs=(
            P("section", None, "seq", None),
            P(),
            P(None, "seq"),
            P(),
            P(None, None, "head"),
            P(None, "head"),
            P("head", None),
            P(None, None, "head"),
            P("head", None),
            P(),
            P(None, "head"),
            P(None, None, "head"),
            P(),
            P("head", None),
            P(None, None, "head"),
            P("head", None),
        ),
        out_specs=(
            P("section", None, "seq", None),
            P(None, ("section", "seq")),
            P(("section", "seq"), None, "head"),
            P(None, "head"),
            P("head", ("section", "seq")),
            P(("section", "seq"), None, "head"),
            P("head", ("section", "seq")),
            P(None, ("section", "seq")),
            P(("section", "seq"), "head"),
            P(("section", "seq"), None, "head"),
            P(),
            P("head", ("section", "seq")),
            P(("section", "seq"), None, "head"),
            P("head", ("section", "seq")),
        ),
        check_vma=False,
    )
```

```python
import functools

import jax
import jax.numpy as jnp
from jax import lax
from jax.experimental import pallas as pl
from jax.experimental.pallas import tpu as pltpu
from jax.sharding import PartitionSpec as P

EPS = 1e-05
THETA = 1000000.0
FLOAT = jnp.float32
HALF = jnp.bfloat16
MESH = pl.DeviceIdType.MESH
VMEM = pl.BlockSpec(memory_space=pltpu.VMEM)
ANY = pl.BlockSpec(memory_space=pl.ANY)


def product(former, latter):
    return jnp.dot(former, latter, preferred_element_type=FLOAT)


def outer_sum(former, latter):
    return lax.dot_general(former, latter, (((0,), (0,)), ((), ())), preferred_element_type=FLOAT)


def back_product(former, latter):
    return lax.dot_general(former, latter, (((1,), (1,)), ((), ())), preferred_element_type=FLOAT)


def norm_apply(values, gain):
    return values * lax.rsqrt(jnp.mean(values * values, -1, keepdims=True) + EPS) * gain


def norm_back(values, gain, grad):
    scale = lax.rsqrt(jnp.mean(values * values, -1, keepdims=True) + EPS)
    weighted = grad * gain
    inner = jnp.mean(weighted * values, -1, keepdims=True)
    grad_values = scale * weighted - values * (scale * scale * scale * inner)
    return grad_values, jnp.sum(grad * values * scale, 0, keepdims=True)


BLOCKS = 8
LAG = 3
END_FIRST = 10
MIDDLE_FIRST = 3


def place():
    return lax.axis_index("section"), lax.axis_index("seq"), lax.axis_index("head")


def remote(source, target, send, recv, peer):
    return pltpu.make_async_remote_copy(
        src_ref=source,
        dst_ref=target,
        send_sem=send,
        recv_sem=recv,
        device_id=peer,
        device_id_type=MESH,
    )


def signal(peer):
    pl.semaphore_signal(pltpu.get_barrier_semaphore(), inc=1, device_id=peer, device_id_type=MESH)


def wait_greetings(count):
    pl.semaphore_wait(pltpu.get_barrier_semaphore(), count)


def greet(others, where=None, size=0):
    for peer in others:
        signal(peer)
    if where is None:
        wait_greetings(len(others))
        return
    section, seq, head = where
    end = (head == 0) | (head == size - 1)

    @pl.when(end)
    def _():
        signal((section, seq, jnp.where(head == 0, 1, size - 2)))
        wait_greetings(len(others) + 1)

    @pl.when(jnp.logical_not(end))
    def _():
        signal((section, seq, jnp.minimum(head + 1, size - 1)))
        signal((section, seq, jnp.maximum(head - 1, 0)))
        wait_greetings(len(others) + 2)


def seq_peers(where, seqs):
    section, seq, head = where
    return [(section, lax.rem(seq + k, seqs), head) for k in range(1, seqs)]


def rows_of(index, count):
    return pl.ds(pl.multiple_of(index * count, count), count)


def wait_all(copies):
    for copy in copies:
        copy.wait()


def start_all(copies):
    for copy in copies:
        copy.start()


def loop(count, step):
    def body(i, carried):
        step(i)
        return carried

    lax.fori_loop(0, count, body, 0)


def head_total(part, full, inbox, reduce_send, reduce_recv, gather_send, gather_recv, where, size, finish, filler=None, fillers=0):
    section, seq, head = where
    count = part.shape[0] // (2 * BLOCKS)
    last = size - 1
    end = (head == 0) | (head == last)

    def rows(flow, i):
        return rows_of(flow * BLOCKS + i, count)

    def fill(t):
        if filler is not None:

            @pl.when(t < fillers)
            def _():
                filler(t)

    def fill_rest(start, stop=fillers):
        stop = min(stop, fillers)
        if stop > start:
            loop(stop - start, lambda i: filler(start + i))

    def reduced(flow, i, peer):
        return remote(part.at[rows(flow, i)], inbox.at[flow, i], reduce_send.at[flow, i], reduce_recv.at[flow, i], peer)

    def gathered(flow, i, peer):
        span = full.at[rows(flow, i)]
        return remote(span, span, gather_send.at[flow, i], gather_recv.at[flow, i], peer)

    @pl.when(end)
    def _():
        flow = jnp.where(head == 0, 0, 1)
        inner = (section, seq, jnp.where(head == 0, 1, last - 1))
        loop(BLOCKS, lambda i: reduced(1 - flow, i, inner).start())
        fill_rest(0, END_FIRST)

        def own(i):
            reduced(flow, i, inner).wait_recv()
            total = part[rows(flow, i), :].astype(FLOAT) + inbox[flow, i].astype(FLOAT)
            full[rows(flow, i), :] = finish(flow, i, total)
            gathered(flow, i, inner).start()
            fill(END_FIRST + i)

        loop(BLOCKS, own)
        fill_rest(END_FIRST + BLOCKS)

        def drain(i):
            gathered(1 - flow, i, inner).wait_recv()
            reduced(1 - flow, i, inner).wait_send()
            gathered(flow, i, inner).wait_send()

        loop(BLOCKS, drain)

    @pl.when(jnp.logical_not(end))
    def _():
        low = head < size // 2
        near = jnp.where(low, 1, 0)
        ahead = (section, seq, jnp.where(low, head + 1, head - 1))
        behind = (section, seq, jnp.where(low, head - 1, head + 1))

        def add(flow, i, peer):
            reduced(flow, i, peer).wait_recv()
            span = rows(flow, i)
            part[span, :] = (part[span, :].astype(FLOAT) + inbox[flow, i].astype(FLOAT)).astype(HALF)
            reduced(flow, i, peer).start()

        def forward(flow, i, peer):
            gathered(flow, i, peer).wait_recv()
            gathered(flow, i, peer).start()

        def lagged(act, first, second, at):
            def step(i):
                fill(at + i)

                @pl.when(i < BLOCKS)
                def _():
                    act(first, i, ahead)

                @pl.when(i >= LAG)
                def _():
                    act(second, i - LAG, behind)

            loop(BLOCKS + LAG, step)

        fill_rest(0, MIDDLE_FIRST)
        lagged(add, near, 1 - near, MIDDLE_FIRST)
        lagged(forward, 1 - near, near, MIDDLE_FIRST + BLOCKS + LAG)
        fill_rest(MIDDLE_FIRST + 2 * (BLOCKS + LAG))

        def drain(i):
            reduced(near, i, ahead).wait_send()
            reduced(1 - near, i, behind).wait_send()
            gathered(1 - near, i, ahead).wait_send()
            gathered(near, i, behind).wait_send()

        loop(BLOCKS, drain)


def turned(values):
    width = values.shape[-1]
    if width == 128:
        lane = lax.broadcasted_iota(jnp.int32, values.shape, 1)
        low = lax.rem(lane, 64) < 32
        return jnp.where(low, -pltpu.roll(values, 96, 1), pltpu.roll(values, 32, 1))
    parts = []
    for start in range(0, width, 64):
        parts += [-values[:, start + 32 : start + 64], values[:, start : start + 32]]
    return jnp.concatenate(parts, -1)


def head_mean(values):
    width = values.shape[-1]
    if width == 64:
        return jnp.mean(values, -1, keepdims=True)
    lane = lax.broadcasted_iota(jnp.int32, values.shape, 1)
    first = jnp.sum(jnp.where(lane < 64, values, 0.0), -1, keepdims=True)
    second = jnp.sum(jnp.where(lane < 64, 0.0, values), -1, keepdims=True)
    return jnp.where(lane < 64, first, second) * (1.0 / 64.0)


def chunks_of(width):
    return [(start, min(128, width - start)) for start in range(0, width, 128)]


def rotary(raw, gain, cosine, sine):
    width = raw.shape[-1]
    normed = raw * lax.rsqrt(head_mean(raw * raw) + EPS) * gain[:, :width]
    return normed * cosine[:, :width] + turned(normed) * sine[:, :width]


def rotary_back(raw, gain, cosine, sine, grad):
    width = raw.shape[-1]
    back = grad * cosine[:, :width] - turned(grad) * sine[:, :width]
    scale = lax.rsqrt(head_mean(raw * raw) + EPS)
    weighted = back * gain[:, :width]
    grad_raw = scale * weighted - raw * (scale * scale * scale * head_mean(weighted * raw))
    return grad_raw, jnp.sum(back * raw * scale, 0, keepdims=True)


LAZY = "lazy"
LATE = "late"


class Moves:
    def __init__(self, incoming, leaving):
        self.incoming, self.leaving, self.left = incoming, leaving, []
        for _, copy in incoming:
            copy.start()

    def ready(self, *refs):
        for ref in refs:
            for known, copy in self.incoming:
                if known is ref:
                    copy.wait()

    def leave(self, *refs):
        for ref in refs:
            for known, copy in self.leaving:
                if known is ref:
                    copy.start()
                    self.left.append(copy)

    def finish(self):
        wait_all(self.left)


def call(body, name, collective, outs, scratch, args, flops=0, moved=0):
    params = dict(vmem_limit_bytes=60 << 20)
    if collective is not None:
        params.update(collective_id=collective, has_side_effects=True)
    lazy = [n for n, arg in enumerate(args) if isinstance(arg, tuple) and arg[1] is LAZY]
    late = [n for n, out in enumerate(outs) if len(out) > 2 and out[2] is LATE]
    arrays = [arg[0] if isinstance(arg, tuple) else arg for arg in args]
    extra = [pltpu.VMEM(arrays[n].shape, arrays[n].dtype) for n in lazy]
    extra += [pltpu.VMEM(outs[n][0], outs[n][1]) for n in late]
    moves = len(lazy) + len(late)
    if moves:
        extra.append(pltpu.SemaphoreType.DMA((moves,)))

    def whole(*refs):
        refs = list(refs)
        held = refs[len(refs) - len(extra) :]
        refs = refs[: len(refs) - len(extra)]
        incoming, leaving = [], []
        for at, n in enumerate(lazy):
            incoming.append((held[at], pltpu.make_async_copy(refs[n], held[at], held[-1].at[at])))
            refs[n] = held[at]
        for at, n in enumerate(late):
            place_at = len(args) + n
            kept = held[len(lazy) + at]
            leaving.append((kept, pltpu.make_async_copy(kept, refs[place_at], held[-1].at[len(lazy) + at])))
            refs[place_at] = kept
        travel = Moves(incoming, leaving)
        body(*refs, travel)
        travel.finish()

    def spec(mark):
        return ANY if mark is LAZY or mark is LATE else mark

    results = pl.pallas_call(
        whole,
        name=name,
        out_shape=[jax.ShapeDtypeStruct(out[0], out[1]) for out in outs],
        in_specs=[spec(arg[1]) if isinstance(arg, tuple) else VMEM for arg in args],
        out_specs=[spec(out[2]) if len(out) > 2 else VMEM for out in outs],
        scratch_shapes=list(scratch) + extra,
        compiler_params=pltpu.CompilerParams(**params),
        cost_estimate=pl.CostEstimate(flops=flops, bytes_accessed=moved, transcendentals=0),
    )(*arrays)
    return list(results)


def dma(count):
    return pltpu.SemaphoreType.DMA((count,))


def per_device(
    incoming,
    segment_ids,
    positions,
    conv_gains,
    conv_in,
    conv_kernel,
    conv_out,
    conv_gate_up,
    conv_down,
    attn_gains,
    w_query,
    w_keyval,
    qk_gains,
    attn_out,
    attn_gate_up,
    attn_down,
):
    sections = lax.axis_size("section")
    seqs = lax.axis_size("seq")
    heads = lax.axis_size("head")
    section, seq, head = place()
    micro, local_rows, width = incoming.shape[1:]
    rows = local_rows // sections
    tokens = micro * rows
    half_tokens = tokens // 2
    step_rows = half_tokens // BLOCKS
    block_tok = segment_ids.shape[1]
    length = micro * block_tok
    slots = sections * seqs
    channels = conv_in.shape[2]
    hidden_units = conv_down.shape[0]
    head_width = qk_gains.shape[1]
    query_width = w_query.shape[1]
    pair_width = 2 * w_keyval.shape[2]
    kv_local = w_keyval.shape[2] // head_width
    group = query_width // (kv_local * head_width)
    score_scale = head_width ** (-0.5)
    half_model = width // sections
    share = width // (sections * seqs)

    segments = segment_ids.reshape(length)

    def own_tokens(per_token):
        start = seq * local_rows + section * rows
        return lax.dynamic_slice_in_dim(per_token.reshape(micro, block_tok), start, rows, 1).reshape(tokens)

    def moved_back(by):
        return jnp.concatenate([jnp.full((by,), -1, jnp.int32), segments[:-by]])

    local_segments = own_tokens(segments)
    same = jnp.stack([(local_segments == own_tokens(moved_back(by))).astype(FLOAT) for by in (1, 2)], 1)
    local_segments = local_segments[:, None]
    pair_index = lax.broadcasted_iota(jnp.int32, (1, 2 * head_width), 1) % (head_width // 2)
    angle_rates = THETA ** (-2.0 * pair_index.astype(FLOAT) / head_width)
    local_positions = lax.dynamic_slice_in_dim(positions, section * rows, rows, 1).reshape(tokens)
    angles = local_positions.astype(FLOAT)[:, None] * angle_rates
    cosine, sine = jnp.cos(angles), jnp.sin(angles)
    query_gain = jnp.tile(qk_gains[0:1], (1, 2))
    key_gain = jnp.tile(qk_gains[1:2], (1, 2))
    w_in = conv_in.transpose(1, 0, 2)
    w_pair = w_keyval.reshape(width, pair_width)
    first_up = conv_gate_up.transpose(1, 2, 0)
    second_up = attn_gate_up.transpose(1, 2, 0)
    slabs = [(start, min(512, hidden_units - start)) for start in range(0, hidden_units, 512)]
    tile_width = 256
    tiles = -(-hidden_units // tile_width)
    padded_units = tiles * tile_width

    def shifted_rows(ext, micro_at, back):
        return ext[micro_at, 8 - back : 8 - back + rows, :]

    def own_rows(flow, i):
        return rows_of(flow * BLOCKS + i, step_rows)

    def kept_rows(i):
        return rows_of(i, step_rows)

    total_scratch = [pltpu.VMEM((2, BLOCKS, step_rows, width), HALF)] + [
        pltpu.SemaphoreType.DMA((2, BLOCKS)) for _ in range(4)
    ]
    part_scratch = [pltpu.VMEM((tokens, width), HALF)]

    weight_scratch = [
        pltpu.VMEM((2, hidden_units, width), HALF),
        pltpu.VMEM((hidden_units, width), HALF),
        dma(3 * len(slabs)),
    ]

    def weight_loads(up_hbm, down_hbm, up_ref, down_ref, sems):
        copies = []
        for j, (start, count) in enumerate(slabs):
            span = slice(start, start + count)
            pairs = [(up_hbm.at[0, span], up_ref.at[0, span]), (up_hbm.at[1, span], up_ref.at[1, span])]
            pairs.append((down_hbm.at[span], down_ref.at[span]))
            for k, (source, target) in enumerate(pairs):
                copies.append(pltpu.make_async_copy(source, target, sems.at[3 * j + k]))
        return copies

    def conv_forward(
        in_ref, same_ref, gain_ref, win_ref, kernel_ref, wout_ref, attn_gain_ref, up_hbm, down_hbm,
        x_ref, g_ref, n1_ref, pc_ref, edge_ref, y_ref, h1_ref, n2_ref, f1_ref, a1_ref, m_ref, n3_ref,
        other, edges, normed_edges, ext, swap_send, swap_recv, edge_send, edge_recv, up_ref, down_ref, weight_sems, acc,
        part, inbox, rs, rr, gs, gr, inbox2, rs2, rr2, gs2, gr2, travel,
    ):
        where = place()
        s, q, h = where
        partner = (1 - s, q, h)
        following = (s, lax.rem(q + 1, seqs), h)
        preceding = (s, lax.rem(q + seqs - 1, seqs), h)
        weights = weight_loads(up_hbm, down_hbm, up_ref, down_ref, weight_sems)
        start_all(weights)
        greet([partner, following, preceding], where, heads)
        give = pl.multiple_of((1 - s) * rows, rows)
        swap = remote(in_ref.at[0, :, pl.ds(give, rows)], other, swap_send.at[0], swap_recv.at[0], partner)
        swap.start()
        near = remote(in_ref.at[0, :, rows - 16 : rows], edges.at[0], edge_send.at[0], edge_recv.at[0], partner)
        near.start()
        far = remote(
            in_ref.at[0, :, local_rows - 16 : local_rows], edges.at[1], edge_send.at[1], edge_recv.at[1], following
        )
        far.start()
        keep = pl.multiple_of(s * rows, rows)
        swap.wait()
        mine = in_ref[0, :, pl.ds(keep, rows), :].reshape(tokens, width)
        theirs = other[...].reshape(tokens, width)
        first = s == 0
        x = jnp.where(first, mine, theirs)
        x_ref[...] = x
        g_ref[...] = jnp.where(first, theirs, mine)
        n1_ref[...] = norm_apply(x.astype(FLOAT), gain_ref[0:1, :]).astype(HALF)
        near.wait()
        far.wait()
        for m in range(micro):
            before = edges[1, max(m - 1, 0)]
            far_edge = jnp.where(q == 0, before, edges[1, m])
            edge = jnp.where(first, far_edge, edges[0, m]).astype(FLOAT)
            normed_edges[m * 16 : (m + 1) * 16, :] = norm_apply(edge, gain_ref[0:1, :]).astype(HALF)
        travel.ready(win_ref)
        for k in range(3):
            pc_ref[k] = product(n1_ref[...], win_ref[k])
        edge_b = product(normed_edges[...], win_ref[0])
        edge_u = product(normed_edges[...], win_ref[2])
        edge_gated = edge_b * edge_u
        gated = pc_ref[0] * pc_ref[2]
        for m in range(micro):
            ext[m, 0:8, :] = edge_gated[m * 16 + 8 : m * 16 + 16, :]
            edge_ref[m] = edge_gated[m * 16 + 8 : m * 16 + 16, :]
            ext[m, 8 : 8 + rows, :] = gated[m * rows : (m + 1) * rows, :]
        for m in range(micro):
            span = slice(m * rows, (m + 1) * rows)
            mixed = (
                kernel_ref[2:3, :] * gated[span]
                + kernel_ref[1:2, :] * jnp.where(same_ref[span, 0:1] > 0, shifted_rows(ext, m, 1), 0.0)
                + kernel_ref[0:1, :] * jnp.where(same_ref[span, 1:2] > 0, shifted_rows(ext, m, 2), 0.0)
            )
            y_ref[span, :] = (pc_ref[1, span, :] * mixed).astype(HALF)
        travel.ready(wout_ref)
        part[...] = product(y_ref[...], wout_ref[...]).astype(HALF)
        travel.leave(x_ref, g_ref, n1_ref, pc_ref, edge_ref, y_ref)

        def finish(flow, i, total):
            hidden = x_ref[own_rows(flow, i), :].astype(FLOAT) + total
            h1_ref[kept_rows(i), :] = hidden
            return norm_apply(hidden, gain_ref[1:2, :]).astype(HALF)

        head_total(part, n2_ref, inbox, rs, rr, gs, gr, where, heads, finish)
        travel.leave(h1_ref, n2_ref)
        for j, (start, count) in enumerate(slabs):
            wait_all(weights[3 * j : 3 * j + 3])
            span = slice(start, start + count)
            gate = back_product(n2_ref[...], up_ref[0, span, :])
            rise = back_product(n2_ref[...], up_ref[1, span, :])
            f1_ref[0, :, span] = gate
            f1_ref[1, :, span] = rise
            active = (gate / (1.0 + jnp.exp(-gate)) * rise).astype(HALF)
            a1_ref[:, span] = active
            term = product(active, down_ref[span, :])
            if j == 0:
                acc[...] = term
            else:
                acc[...] += term
        part[...] = acc[...].astype(HALF)
        travel.leave(f1_ref, a1_ref)

        def finish_middle(flow, i, total):
            middle = (h1_ref[kept_rows(i), :] + total).astype(HALF).astype(FLOAT)
            m_ref[kept_rows(i), :] = middle
            return norm_apply(middle, attn_gain_ref[0:1, :]).astype(HALF)

        head_total(part, n3_ref, inbox2, rs2, rr2, gs2, gr2, where, heads, finish_middle)

    (x, g, n1, projected, edge_gated, mixed, h1, n2, f1, a1, middle, n3) = call(
        conv_forward,
        "conv_forward",
        0,
        [
            ((tokens, width), HALF, LATE),
            ((tokens, width), HALF, LATE),
            ((tokens, width), HALF, LATE),
            ((3, tokens, channels), FLOAT, LATE),
            ((micro, 8, channels), FLOAT, LATE),
            ((tokens, channels), HALF, LATE),
            ((half_tokens, width), FLOAT, LATE),
            ((tokens, width), HALF, LATE),
            ((2, tokens, hidden_units), FLOAT, LATE),
            ((tokens, hidden_units), HALF, LATE),
            ((half_tokens, width), FLOAT),
            ((tokens, width), HALF),
        ],
        [
            pltpu.VMEM((micro, rows, width), HALF),
            pltpu.VMEM((2, micro, 16, width), HALF),
            pltpu.VMEM((micro * 16, width), HALF),
            pltpu.VMEM((micro, 8 + rows, channels), FLOAT),
            dma(1),
            dma(1),
            dma(2),
            dma(2),
        ]
        + weight_scratch
        + [pltpu.VMEM((tokens, width), FLOAT)]
        + part_scratch
        + total_scratch
        + total_scratch,
        [incoming, same, conv_gains, (w_in, LAZY), conv_kernel, (conv_out, LAZY), attn_gains, (first_up, ANY), (conv_down, ANY)],
        flops=5 * 10**9,
        moved=200 << 20,
    )


    grid_rows = seqs // 2
    first_blocks = 3 * grid_rows - 2
    half_share = share // 2

    def grid_place(q):
        return lax.div(q, 2), lax.rem(q, 2)

    def first_stage(source, target, send, recv, where):
        s, q, h = where
        a, b = grid_place(q)
        copies = []
        for row in range(grid_rows):
            copies.append((source(row * 2 + 1 - b, 0), row, (s, a * 2 + 1 - b, h)))
        for k in range(1, grid_rows):
            row = lax.rem(a + k, grid_rows)
            for column in range(2):
                copies.append((source(row * 2 + column, 1), grid_rows + 2 * (k - 1) + column, (s, row * 2 + b, h)))
        return [remote(block, target(i), send.at[i], recv.at[i], peer) for block, i, peer in copies]

    def passed_blocks(where):
        s, q, h = where
        a, b = grid_place(q)
        blocks = []
        for k in range(1, grid_rows):
            row = lax.rem(a + k, grid_rows)
            blocks.append((row * 2 + b, 0, [row], (s, row * 2 + b, h)))
        arrived = [grid_rows + 2 * j + 1 - b for j in range(grid_rows - 1)]
        blocks.append((a * 2 + 1 - b, 1, arrived, (s, a * 2 + 1 - b, h)))
        return blocks

    def half_rows(side):
        return slice(side * half_share, (side + 1) * half_share)

    def combine(passing, arrived, where, own=None):
        for i, (_, _, sources, _) in enumerate(passed_blocks(where)):
            total = (passing if own is None else own)(i)[...].astype(FLOAT)
            for source in sources:
                total = total + arrived[source].astype(FLOAT)
            passing(i)[...] = total.astype(HALF)

    def second_stage(passing, target, send, recv, where):
        return [
            remote(passing(i), target.at[i], send.at[i], recv.at[i], peer)
            for i, (_, _, _, peer) in enumerate(passed_blocks(where))
        ]

    def load_passing(partial, passing, sems, where):
        return [
            pltpu.make_async_copy(partial.at[dest, half_rows(side)], passing.at[i], sems.at[i])
            for i, (dest, side, _, _) in enumerate(passed_blocks(where))
        ]

    def two_halves(own, arrived, passed, where):
        a, b = grid_place(where[1])
        upper = own[half_rows(0), :].astype(FLOAT) + arrived[a].astype(FLOAT)
        for k in range(grid_rows - 1):
            upper = upper + passed[k].astype(FLOAT)
        lower = own[half_rows(1), :].astype(FLOAT) + passed[grid_rows - 1].astype(FLOAT)
        for j in range(grid_rows - 1):
            lower = lower + arrived[grid_rows + 2 * j + b].astype(FLOAT)
        return upper, lower

    def dma_grid(*shape):
        return pltpu.SemaphoreType.DMA(shape)

    def first_shape(count):
        return ((count, first_blocks, half_share, padded_units), HALF, ANY)

    def second_shape(count):
        return ((count, grid_rows, half_share, padded_units), HALF, ANY)

    def passing_scratch(count):
        return [
            pltpu.VMEM((count, grid_rows, half_share, padded_units), HALF),
            pltpu.VMEM((count, first_blocks, half_share, padded_units), HALF),
            dma_grid(count, grid_rows + 1),
            dma_grid(count, grid_rows),
            dma_grid(count, grid_rows),
        ]

    def pass_loads(partial, kinds, arrived, passing, held, sems, where):
        copies = []
        for k, kind in enumerate(kinds):
            copies += load_passing(partial.at[kind], passing.at[k], sems.at[k], where)
            copies.append(pltpu.make_async_copy(arrived.at[k], held.at[k], sems.at[k, grid_rows]))
        return copies

    def pass_sends(count, passing, held, target, send, recv, where):
        copies = []
        for k in range(count):
            combine(lambda i, k=k: passing.at[k, i], held.at[k], where)
            sends = second_stage(lambda i, k=k: passing.at[k, i], target.at[k], send.at[k], recv.at[k], where)
            start_all(sends)
            copies += sends
        return copies

    small_rows = tokens // heads
    widths = [query_width, query_width + pair_width, channels, 3 * channels]

    def head_others(where):
        s, q, h = where
        return [(s, q, lax.rem(h + k, heads)) for k in range(1, heads)]

    def mixer_sends(stages, incomes, send, recv, where):
        return [
            first_stage(
                lambda dest, side, stage=stage: stage.at[dest, half_rows(side)],
                lambda i, income=income: income.at[i],
                send.at[k],
                recv.at[k],
                where,
            )
            for k, (stage, income) in enumerate(zip(stages, incomes))
        ]

    def mixer_steps(formers, latters, stages, given, former, halves, swaps, sends):
        def step(t):
            for k in range(len(formers)):

                @pl.when(t == 2 * k)
                def _(k=k):
                    halves[k].wait()
                    former[...] = transposed(formers[k], given.at[k])

                @pl.when(t == 2 * k + 1)
                def _(k=k):
                    swaps[k].wait()
                    result = product(former[...], latters[k][...]).astype(HALF)
                    stages[k][...] = result.reshape(seqs, share, result.shape[1])
                    start_all(sends[k])

        return step

    def mixer_second(stages, incomes, passes, turns, send, recv, where):
        blocks = passed_blocks(where)
        turning = []
        for k, (stage, income, passed, turn) in enumerate(zip(stages, incomes, passes, turns)):

            def own_block(i, stage=stage):
                return stage.at[blocks[i][0], half_rows(blocks[i][1])]

            def moved(i, stage=stage, passed=passed):
                return own_block(i, stage) if passed is None else passed.at[i]

            combine(moved, income, where, own_block)
            sends = second_stage(moved, turn, send.at[k], recv.at[k], where)
            start_all(sends)
            turning.append(sends)
        return turning

    def latter_swaps(latters, send, recv, partner):
        return [
            remote(latter.at[0:tokens], latter.at[tokens : 2 * tokens], send.at[k], recv.at[k], partner)
            for k, latter in enumerate(latters)
        ]

    def first_sums(count):
        return [((first_blocks, half_share, size), HALF) for size in count]

    def transposed(array_ref, given_ref):
        start = pl.multiple_of(lax.axis_index("section") * half_model, 128)
        own = array_ref[:, pl.ds(start, half_model)]
        both = jnp.concatenate([own, given_ref[...]], 0)
        return both.astype(FLOAT).T.astype(HALF)

    def half_swaps(arrays, targets, send, recv, where):
        s, q, h = where
        copies = []
        for k, (array_ref, target) in enumerate(zip(arrays, targets)):
            start = pl.multiple_of((1 - s) * half_model, 128)
            copies.append(remote(array_ref.at[:, pl.ds(start, half_model)], target, send.at[k], recv.at[k], (1 - s, q, h)))
        return copies

    def latter_swap(latter, kind, start, count, send, recv, where):
        s, q, h = where
        return remote(
            latter.at[kind, 0:tokens, start : start + count],
            latter.at[kind, tokens : 2 * tokens, start : start + count],
            send,
            recv,
            (1 - s, q, h),
        )

    def gradient_tiles(former, latter, stage, partial_hbm, first_in, local_sems, send, recv, where, kinds):
        def split(t):
            kind = lax.div(t, tiles)
            at = lax.rem(t, tiles)
            return kind, pl.ds(pl.multiple_of(at * tile_width, tile_width), tile_width)

        def stored(t, dest):
            kind, columns = split(t)
            return pltpu.make_async_copy(
                stage.at[kind, dest, :, columns], partial_hbm.at[kind, dest, :, columns], local_sems.at[t, dest]
            )

        def sent(t):
            kind, columns = split(t)
            return first_stage(
                lambda dest, side: stage.at[kind, dest, half_rows(side), columns],
                lambda i: first_in.at[kind, i, :, columns],
                send.at[t],
                recv.at[t],
                where,
            )

        def tile(t):
            kind, columns = split(t)
            use = jnp.where(kind == 0, 0, 1)
            result = product(former[use], latter[kind, :, columns]).astype(HALF)
            stage[kind, :, :, columns] = result.reshape(seqs, share, tile_width)

            @pl.when(t < kinds * tiles)
            def _():
                start_all(sent(t))

            for dest in range(seqs):
                stored(t, dest).start()

        def finish():
            def stored_all(t):
                for dest in range(seqs):
                    stored(t, dest).wait()

            loop(3 * tiles, stored_all)
            loop(kinds * tiles, lambda t: wait_all(sent(t)))

        return tile, finish

    ffn_scratch = weight_scratch + [
        pltpu.VMEM((tokens, width), FLOAT),
        pltpu.VMEM((2, tokens, half_model), HALF),
        pltpu.VMEM((2, half_model, 2 * tokens), HALF),
        pltpu.VMEM((3, 2 * tokens, padded_units), HALF),
        pltpu.VMEM((3, seqs, share, padded_units), HALF),
        dma(2),
        dma(2),
        pltpu.SemaphoreType.DMA((3, len(slabs))),
        pltpu.SemaphoreType.DMA((3, len(slabs))),
        pltpu.SemaphoreType.DMA((3 * tiles, seqs)),
        pltpu.SemaphoreType.DMA((3 * tiles, first_blocks)),
        pltpu.SemaphoreType.DMA((3 * tiles, first_blocks)),
    ]
    def partial_outs(kinds):
        return [((3, seqs, share, padded_units), HALF, ANY), first_shape(kinds)]


    def slot_peer(me, j, h):
        other = lax.rem(me + j, slots)
        return (lax.rem(other, sections), lax.div(other, sections), h)

    def query_rows(ref, m, c):
        block = ref[m * rows : (m + 1) * rows, :]
        base = c * group * head_width
        return jnp.concatenate(
            [block[:, base + r * head_width : base + (r + 1) * head_width] for r in range(group)], 0
        )

    def keys_of(all_ref, at, c, kind):
        block = all_ref[:, at * rows : (at + 1) * rows, :].reshape(block_tok, pair_width)
        base = kind * kv_local * head_width + c * head_width
        return block[:, base : base + head_width]

    def allowed_pairs(segq_ref, seg_ref, m, at, s, q):
        own_segments = segq_ref[m * rows : (m + 1) * rows, :]
        allowed = own_segments == seg_ref[at : at + 1, :]
        if at == m:
            base = q * local_rows + s * rows
            order = base + lax.broadcasted_iota(jnp.int32, (rows, block_tok), 0)
            allowed = allowed & (lax.broadcasted_iota(jnp.int32, (rows, block_tok), 1) <= order)
        bias = jnp.where(allowed, 0.0, -1e30)
        return jnp.concatenate([bias] * group, 0)

    def probabilities(rows_in, keys, biases):
        scores = [
            jnp.where(bias < 0, -1e30, back_product(rows_in, key) * score_scale)
            for key, bias in zip(keys, biases)
        ]
        summit = functools.reduce(jnp.maximum, [jnp.max(part, -1, keepdims=True) for part in scores])
        raised = [jnp.exp(part - summit) for part in scores]
        total = functools.reduce(jnp.add, [jnp.sum(part, -1, keepdims=True) for part in raised])
        inverse = 1.0 / total
        return [part * inverse for part in raised]

    def gather_pairs(all_ref, me, where, send, recv, near_send, near_recv):
        s, q, h = where
        partner = (1 - s, q, h)
        far = []
        for k, peer in enumerate(seq_peers(where, seqs)):
            copy = remote(all_ref.at[me], all_ref.at[me], send.at[k], recv.at[k], peer)
            copy.start()
            far.append(copy)
        near = [remote(all_ref.at[me], all_ref.at[me], near_send.at[0], near_recv.at[0], partner)]
        near[0].start()

        def pass_on():
            for k in range(1, seqs):
                far[k - 1].wait()
                slot = lax.rem(q + seqs - k, seqs) * sections + s
                copy = remote(all_ref.at[slot], all_ref.at[slot], near_send.at[k], near_recv.at[k], partner)
                copy.start()
                near.append(copy)
            wait_all(near)

        return pass_on

    def attention_forward(
        n3_ref, wq_ref, wp_ref, cos_ref, sin_ref, qg_ref, kg_ref, segq_ref, seg_ref, wo_ref, m_ref, gain_ref,
        qr_ref, r_ref, q_ref, all_ref, o_ref, h2_ref, n4_ref,
        send, recv, near_send, near_recv, part, inbox, rs, rr, gs, gr, travel,
    ):
        where = place()
        s, q, h = where
        me = q * sections + s
        greet([(1 - s, q, h)] + seq_peers(where, seqs), where, heads)
        cos, sin = cos_ref[...], sin_ref[...]
        r_ref[...] = product(n3_ref[...], wp_ref[...])
        half_pair = pair_width // 2
        for start, size in chunks_of(half_pair):
            span = slice(start, start + size)
            all_ref[me, :, span] = rotary(r_ref[:, span], kg_ref[...], cos, sin).astype(HALF)
        all_ref[me, :, half_pair:] = r_ref[:, half_pair:].astype(HALF)
        pass_on = gather_pairs(all_ref, me, where, send, recv, near_send, near_recv)
        travel.ready(wq_ref)
        qr_ref[...] = product(n3_ref[...], wq_ref[...])
        for start, size in chunks_of(query_width):
            span = slice(start, start + size)
            q_ref[:, span] = rotary(qr_ref[:, span], qg_ref[...], cos, sin).astype(HALF)
        travel.leave(r_ref, qr_ref, q_ref)
        pass_on()
        travel.leave(all_ref)
        for m in range(micro):
            biases = [allowed_pairs(segq_ref, seg_ref, m, at, s, q) for at in range(m + 1)]
            results = []
            for c in range(kv_local):
                keys = [keys_of(all_ref, at, c, 0) for at in range(m + 1)]
                weights = probabilities(query_rows(q_ref, m, c), keys, biases)
                total = functools.reduce(
                    jnp.add,
                    [product(weights[at].astype(HALF), keys_of(all_ref, at, c, 1)) for at in range(m + 1)],
                )
                results += [total[r * rows : (r + 1) * rows] for r in range(group)]
            o_ref[m * rows : (m + 1) * rows, :] = jnp.concatenate(results, -1).astype(HALF)
        travel.leave(o_ref)
        travel.ready(wo_ref, m_ref)
        part[...] = product(o_ref[...], wo_ref[...]).astype(HALF)

        def finish(flow, i, total):
            hidden = m_ref[kept_rows(i), :] + total
            h2_ref[kept_rows(i), :] = hidden
            return norm_apply(hidden, gain_ref[1:2, :]).astype(HALF)

        head_total(part, n4_ref, inbox, rs, rr, gs, gr, where, heads, finish)

    (query_raw, pair_raw, queries, all_pairs, attended, h2, n4) = call(
        attention_forward,
        "attention_forward",
        2,
        [
            ((tokens, query_width), FLOAT, LATE),
            ((tokens, pair_width), FLOAT, LATE),
            ((tokens, query_width), HALF, LATE),
            ((slots, tokens, pair_width), HALF, LATE),
            ((tokens, query_width), HALF, LATE),
            ((half_tokens, width), FLOAT),
            ((tokens, width), HALF),
        ],
        [dma(seqs - 1), dma(seqs - 1), dma(seqs), dma(seqs)] + part_scratch + total_scratch,
        [
            n3, (w_query, LAZY), w_pair, cosine, sine, query_gain, key_gain, local_segments, segment_ids,
            (attn_out, LAZY), (middle, LAZY), attn_gains,
        ],
        flops=4 * 10**9,
        moved=150 << 20,
    )

    def slab_width(start, count):
        return min(-(-count // tile_width) * tile_width, padded_units - start)

    def clear_padding(latter):
        if padded_units > hidden_units:
            latter[:, :, hidden_units:] = jnp.zeros((3, 2 * tokens, padded_units - hidden_units), HALF)

    def second_ffn(
        n4_ref, g_ref, h2_ref, gain_ref, up_hbm, down_hbm,
        py_ref, gh2_ref, low_ref, gg_ref, partial_hbm, first_in,
        acc_y, up_ref, down_ref, weight_sems, acc, given, former, latter, stage, hs, hr, ls, lr, local_sems, ts, tr,
        part, inbox, rs, rr, gs, gr, travel,
    ):
        where = place()
        s, q, h = where
        weights = weight_loads(up_hbm, down_hbm, up_ref, down_ref, weight_sems)
        start_all(weights)
        clear_padding(latter)
        greet([(1 - s, q, h)] + seq_peers(where, seqs), where, heads)
        halves = half_swaps([g_ref, n4_ref], [given.at[0], given.at[1]], hs, hr, where)
        start_all(halves)
        gg_ref[...] = jnp.zeros_like(gg_ref)
        swaps = []
        for j, (start, count) in enumerate(slabs):
            wait_all(weights[3 * j : 3 * j + 3])
            span = slice(start, start + count)
            gate = back_product(n4_ref[...], up_ref[0, span, :])
            rise = back_product(n4_ref[...], up_ref[1, span, :])
            grad_active = back_product(g_ref[...], down_ref[span, :])
            chance = 1.0 / (1.0 + jnp.exp(-gate))
            silu = gate * chance
            active = (silu * rise).astype(HALF)
            grad_gate = (grad_active * rise * (chance * (1.0 + gate * (1.0 - chance)))).astype(HALF)
            grad_rise = (grad_active * silu).astype(HALF)
            latter[0, 0:tokens, span] = active
            latter[1, 0:tokens, span] = grad_gate
            latter[2, 0:tokens, span] = grad_rise
            for kind in range(3):
                swap = latter_swap(
                    latter, kind, start, slab_width(start, count), ls.at[kind, j], lr.at[kind, j], where
                )
                swap.start()
                swaps.append(swap)
            term = product(grad_gate, up_ref[0, span, :]) + product(grad_rise, up_ref[1, span, :])
            term_y = product(active, down_ref[span, :])
            if j == 0:
                acc[...] = term
                acc_y[...] = term_y
            else:
                acc[...] += term
                acc_y[...] += term_y
        part[...] = acc[...].astype(HALF)

        travel.ready(h2_ref)
        for flow, holder in ((0, 0), (1, heads - 1)):

            @pl.when(h == holder)
            def _(flow=flow):
                acc_y[flow * half_tokens : (flow + 1) * half_tokens, :] += h2_ref[...]

        py_ref[...] = acc_y[...].astype(HALF)
        travel.leave(py_ref)
        tile, tiles_done = gradient_tiles(
            former, latter, stage, partial_hbm, first_in, local_sems, ts, tr, where, 2
        )

        def filler(t):
            for k, array_ref in enumerate((g_ref, n4_ref)):

                @pl.when(t == k)
                def _(k=k, array_ref=array_ref):
                    halves[k].wait()
                    if k:
                        wait_all(swaps)
                    former[k] = transposed(array_ref, given.at[k])

            @pl.when(t >= 2)
            def _():
                tile(t - 2)

        def finish(flow, i, total):
            grad_hidden, grad_gain = norm_back(h2_ref[kept_rows(i), :], gain_ref[1:2, :], total)
            grad = g_ref[own_rows(flow, i), :].astype(FLOAT) + grad_hidden
            gh2_ref[kept_rows(i), :] = grad
            gg_ref[...] += grad_gain
            return grad.astype(HALF)

        head_total(part, low_ref, inbox, rs, rr, gs, gr, where, heads, finish, filler, 3 * tiles + 2)
        tiles_done()

    (part_y, gh2, gh2_low, grad_gain_attn1, partial2, first2) = call(
        second_ffn,
        "second_ffn",
        4,
        [
            ((tokens, width), HALF, LATE),
            ((half_tokens, width), FLOAT),
            ((tokens, width), HALF),
            ((1, width), FLOAT),
        ]
        + partial_outs(2),
        [pltpu.VMEM((tokens, width), FLOAT)] + ffn_scratch + part_scratch + total_scratch,
        [n4, g, (h2, LAZY), attn_gains, (second_up, ANY), (attn_down, ANY)],
        flops=12 * 10**9,
        moved=150 << 20,
    )
    def attention_backward(
        glow_ref, wo_ref, q_ref, all_ref, segq_ref, seg_ref,
        qr_ref, r_ref, cos_ref, sin_ref, qg_ref, kg_ref, wq_ref, wp_ref, m_ref, gh2_ref, gain_ref, py_ref, n3_ref, o_ref, partial2_hbm, first2_hbm,
        low_ref, gg_ref, gqk_ref, yown_ref, stage0, stage1, in0, in1, second_in, first_in,
        bq_ref, br_ref, grads, totals, gq_ref, gp_ref, near_slots, pair_slots, ns, nr, ps, pr,
        passing, held, load_sems, vs, vr, fs, fr,
        ybox, ys, yr, given, former, latter0, latter1, hs, hr, ls, lr, ms, mr,
        part, inbox, rs, rr, gs, gr, travel,
    ):
        where = place()
        s, q, h = where
        partner = (1 - s, q, h)
        peers = seq_peers(where, seqs)
        loads = pass_loads(partial2_hbm, (0, 1), first2_hbm, passing, held, load_sems, where)
        start_all(loads)
        others = head_others(where)
        latters = [latter0, latter1]
        greet([partner] + peers + others, where, heads)
        wait_all(loads)
        travelling = pass_sends(2, passing, held, second_in, vs, vr, where)
        travel.ready(py_ref, n3_ref, o_ref)
        latter0[0:tokens, :] = o_ref[...]
        ysends = [
            remote(py_ref.at[rows_of(peer[2], small_rows)], ybox.at[n], ys.at[n], yr.at[n], peer)
            for n, peer in enumerate(others)
        ]
        start_all(ysends)
        halves = half_swaps([glow_ref, n3_ref], [given.at[0], given.at[1]], hs, hr, where)
        start_all(halves)
        swaps = latter_swaps(latters, ls, lr, partner)
        swaps[0].start()
        gg_ref[...] = jnp.zeros_like(gg_ref)
        gqk_ref[...] = jnp.zeros_like(gqk_ref)
        grads[...] = back_product(glow_ref[...], wo_ref[...]).astype(HALF)
        for m in range(micro):
            biases = [allowed_pairs(segq_ref, seg_ref, m, at, s, q) for at in range(m + 1)]
            results = []
            for c in range(kv_local):
                keys = [keys_of(all_ref, at, c, 0) for at in range(m + 1)]
                values = [keys_of(all_ref, at, c, 1) for at in range(m + 1)]
                rows_in = query_rows(q_ref, m, c)
                grad_rows = query_rows(grads, m, c)
                chances = probabilities(rows_in, keys, biases)
                grad_chances = [back_product(grad_rows, value) for value in values]
                inner = functools.reduce(
                    jnp.add,
                    [jnp.sum(a * b, -1, keepdims=True) for a, b in zip(grad_chances, chances)],
                )
                total = None
                for at in range(m + 1):
                    grad_scores = (chances[at] * (grad_chances[at] - inner)).astype(HALF)
                    term = product(grad_scores, keys[at])
                    total = term if total is None else total + term
                    grad_key = outer_sum(grad_scores, rows_in) * score_scale
                    grad_value = outer_sum(chances[at].astype(HALF), grad_rows)
                    if at == m:
                        totals[at, c] = grad_key
                        totals[at, kv_local + c] = grad_value
                    else:
                        totals[at, c] += grad_key
                        totals[at, kv_local + c] += grad_value
                total = total * score_scale
                results += [total[r * rows : (r + 1) * rows] for r in range(group)]
            gq_ref[m * rows : (m + 1) * rows, :] = jnp.concatenate(results, -1)
        for at in range(micro):
            joined = jnp.concatenate([totals[at, k] for k in range(2 * kv_local)], -1).astype(HALF)
            gp_ref[:, at * rows : (at + 1) * rows, :] = joined.reshape(slots, rows, pair_width)
        near = []
        for other in range(seqs):
            copy = remote(gp_ref.at[other * sections + 1 - s], near_slots.at[other], ns.at[other], nr.at[other], partner)
            copy.start()
            near.append(copy)
        copies = []
        wait_all(near)
        travel.ready(qr_ref, r_ref, cos_ref, sin_ref, wq_ref, wp_ref, m_ref, gh2_ref)
        for other in range(seqs):
            mine = gp_ref[other * sections + s].astype(FLOAT)
            near_slots[other] = (mine + near_slots[other].astype(FLOAT)).astype(HALF)
        for k, peer in enumerate(peers):
            copy = remote(near_slots.at[peer[1]], pair_slots.at[k], ps.at[k], pr.at[k], peer)
            copy.start()
            copies.append(copy)
        later = first_stage(
            lambda dest, side: partial2_hbm.at[2, dest, half_rows(side)], lambda i: first_in.at[0, i], fs, fr, where
        )
        start_all(later)
        travelling += later
        cos, sin = cos_ref[...], sin_ref[...]
        for start, size in chunks_of(query_width):
            span = slice(start, start + size)
            grad_raw, grad_gain = rotary_back(qr_ref[:, span], qg_ref[...], cos, sin, gq_ref[:, span])
            bq_ref[:, span] = grad_raw.astype(HALF)
            gqk_ref[0:1, :size] += grad_gain
        partial = back_product(bq_ref[...], wq_ref[...])
        wait_all(copies)
        grad_pair = near_slots[q].astype(FLOAT)
        for j in range(seqs - 1):
            grad_pair = grad_pair + pair_slots[j].astype(FLOAT)
        half_pair = pair_width // 2
        for start, size in chunks_of(half_pair):
            span = slice(start, start + size)
            grad_raw, grad_gain = rotary_back(r_ref[:, span], kg_ref[...], cos, sin, grad_pair[:, span])
            br_ref[:, span] = grad_raw.astype(HALF)
            gqk_ref[1:2, :size] += grad_gain
        br_ref[:, half_pair:] = grad_pair[:, half_pair:].astype(HALF)
        latter1[0:tokens, 0:query_width] = bq_ref[...]
        latter1[0:tokens, query_width:] = br_ref[...]
        swaps[1].start()
        part[...] = (partial + back_product(br_ref[...], wp_ref[...])).astype(HALF)
        wait_all(ysends)
        produced = py_ref[rows_of(h, small_rows), :].astype(FLOAT)
        for n in range(heads - 1):
            produced = produced + ybox[n].astype(FLOAT)
        yown_ref[...] = produced.astype(HALF)
        sends = mixer_sends([stage0, stage1], [in0, in1], ms, mr, where)
        mixer_step = mixer_steps([glow_ref, n3_ref], latters, [stage0, stage1], given, former, halves, swaps, sends)

        def finish(flow, i, total):
            grad_entry, grad_gain = norm_back(m_ref[kept_rows(i), :], gain_ref[0:1, :], total)
            gg_ref[...] += grad_gain
            return (gh2_ref[kept_rows(i), :] + grad_entry).astype(HALF)

        head_total(part, low_ref, inbox, rs, rr, gs, gr, where, heads, finish, mixer_step, 4)
        for copies in sends:
            wait_all(copies)
        wait_all(travelling)

    (gm_low, grad_gain_attn0, grad_qk, y_own, stage0, stage1, in0, in1, second2, first2_last) = call(
        attention_backward,
        "attention_backward",
        5,
        [
            ((tokens, width), HALF),
            ((1, width), FLOAT),
            ((8, 128), FLOAT),
            ((small_rows, width), HALF),
            ((seqs, share, widths[0]), HALF),
            ((seqs, share, widths[1]), HALF),
            *first_sums(widths[:2]),
            second_shape(2),
            first_shape(1),
        ],
        [
            pltpu.VMEM((tokens, query_width), HALF),
            pltpu.VMEM((tokens, pair_width), HALF),
            pltpu.VMEM((tokens, query_width), HALF),
            pltpu.VMEM((micro, 2 * kv_local, block_tok, head_width), FLOAT),
            pltpu.VMEM((tokens, query_width), FLOAT),
            pltpu.VMEM((slots, tokens, pair_width), HALF),
            pltpu.VMEM((seqs, tokens, pair_width), HALF),
            pltpu.VMEM((seqs - 1, tokens, pair_width), HALF),
            dma(seqs),
            dma(seqs),
            dma(seqs - 1),
            dma(seqs - 1),
        ]
        + passing_scratch(2)
        + [dma(first_blocks), dma(first_blocks)]
        + [
            pltpu.VMEM((heads - 1, small_rows, width), HALF),
            dma(heads - 1),
            dma(heads - 1),
            pltpu.VMEM((2, tokens, half_model), HALF),
            pltpu.VMEM((half_model, 2 * tokens), HALF),
            pltpu.VMEM((2 * tokens, widths[0]), HALF),
            pltpu.VMEM((2 * tokens, widths[1]), HALF),
            dma(2),
            dma(2),
            dma(2),
            dma(2),
            dma_grid(2, first_blocks),
            dma_grid(2, first_blocks),
        ]
        + part_scratch
        + total_scratch,
        [
            gh2_low, attn_out, queries, all_pairs, local_segments, segment_ids,
            (query_raw, LAZY), (pair_raw, LAZY), (cosine, LAZY), (sine, LAZY), query_gain, key_gain,
            (w_query, LAZY), (w_pair, LAZY), (middle, LAZY), (gh2, LAZY), attn_gains,
            (part_y, LAZY), (n3, LAZY), (attended, LAZY), (partial2, ANY), (first2, ANY),
        ],
        flops=6 * 10**9,
        moved=130 << 20,
    )

    def first_ffn_back(
        gm_ref, n2_ref, f1_ref, a1_ref, h1_ref, gain_ref, yown_ref, stage0, stage1, in0, in1, up_hbm, down_hbm, partial2_hbm, first2_hbm,
        gh1_ref, low_ref, gg_ref, yout_ref, turn0, turn1, partial_hbm, first_in, second_in,
        up_ref, down_ref, weight_sems, acc, given, former, latter, stage, hs, hr, ls, lr, local_sems, ts, tr,
        passing, held, load_sems, vs, vr, ys, yr, pass0, pass1, us, ur,
        part, inbox, rs, rr, gs, gr, travel,
    ):
        where = place()
        s, q, h = where
        weights = weight_loads(up_hbm, down_hbm, up_ref, down_ref, weight_sems)
        loads = pass_loads(partial2_hbm, (2,), first2_hbm, passing, held, load_sems, where)
        start_all(loads)
        start_all(weights)
        clear_padding(latter)
        others = head_others(where)
        own_y = rows_of(h, small_rows)
        greet([(1 - s, q, h)] + seq_peers(where, seqs) + others, where, heads)
        travel.ready(yown_ref, n2_ref, a1_ref)
        yout_ref[own_y, :] = yown_ref[...]
        ysends = [
            remote(yout_ref.at[own_y], yout_ref.at[own_y], ys.at[n], yr.at[n], peer) for n, peer in enumerate(others)
        ]
        start_all(ysends)
        wait_all(loads)
        travelling = pass_sends(1, passing, held, second_in, vs, vr, where)
        halves = half_swaps([gm_ref, n2_ref], [given.at[0], given.at[1]], hs, hr, where)
        start_all(halves)
        gg_ref[...] = jnp.zeros_like(gg_ref)
        latter[0, 0:tokens, 0:hidden_units] = a1_ref[...]
        travel.ready(stage0, stage1, in0, in1)
        turning = mixer_second([stage0, stage1], [in0, in1], [pass0, pass1], [turn0, turn1], us, ur, where)
        tile, tiles_done = gradient_tiles(
            former, latter, stage, partial_hbm, first_in, local_sems, ts, tr, where, 3
        )
        active_swaps = [
            latter_swap(latter, 0, start, slab_width(start, count), ls.at[0, j], lr.at[0, j], where)
            for j, (start, count) in enumerate(slabs)
        ]
        start_all(active_swaps)
        swaps = []
        travel.ready(f1_ref, h1_ref)
        for j, (start, count) in enumerate(slabs):
            wait_all(weights[3 * j : 3 * j + 3])
            span = slice(start, start + count)
            gate = f1_ref[0, :, span]
            rise = f1_ref[1, :, span]
            grad_active = back_product(gm_ref[...], down_ref[span, :])
            chance = 1.0 / (1.0 + jnp.exp(-gate))
            grad_gate = (grad_active * rise * (chance * (1.0 + gate * (1.0 - chance)))).astype(HALF)
            grad_rise = (grad_active * (gate * chance)).astype(HALF)
            latter[1, 0:tokens, span] = grad_gate
            latter[2, 0:tokens, span] = grad_rise
            for kind in range(1, 3):
                swap = latter_swap(
                    latter, kind, start, slab_width(start, count), ls.at[kind, j], lr.at[kind, j], where
                )
                swap.start()
                swaps.append(swap)
            term = product(grad_gate, up_ref[0, span, :]) + product(grad_rise, up_ref[1, span, :])
            if j == 0:
                acc[...] = term
                halves[0].wait()
                wait_all(active_swaps)
                former[0] = transposed(gm_ref, given.at[0])
                loop(tiles, tile)
            else:
                acc[...] += term
        part[...] = acc[...].astype(HALF)
        def filler(t):
            @pl.when(t == 0)
            def _():
                halves[1].wait()
                wait_all(swaps)
                former[1] = transposed(n2_ref, given.at[1])

            @pl.when(t >= 1)
            def _():
                tile(tiles + t - 1)

        def finish(flow, i, total):
            grad_hidden, grad_gain = norm_back(h1_ref[kept_rows(i), :], gain_ref[1:2, :], total)
            gg_ref[...] += grad_gain
            grad = gm_ref[own_rows(flow, i), :].astype(FLOAT) + grad_hidden
            gh1_ref[kept_rows(i), :] = grad
            return grad.astype(HALF)

        head_total(part, low_ref, inbox, rs, rr, gs, gr, where, heads, finish, filler, 2 * tiles + 1)
        tiles_done()
        wait_all(travelling)
        wait_all(ysends)
        for copies in turning:
            wait_all(copies)

    (gh1, gh1_low, grad_gain_conv1, yout, turn0, turn1, partial1, first1, second2_last) = call(
        first_ffn_back,
        "first_ffn_back",
        6,
        [((half_tokens, width), FLOAT), ((tokens, width), HALF), ((1, width), FLOAT), ((tokens, width), HALF)]
        + [((grid_rows, half_share, size), HALF) for size in widths[:2]]
        + partial_outs(3)
        + [second_shape(1)],
        ffn_scratch + passing_scratch(1)
        + [dma(heads - 1), dma(heads - 1)]
        + [pltpu.VMEM((grid_rows, half_share, size), HALF) for size in widths[:2]]
        + [dma_grid(2, grid_rows), dma_grid(2, grid_rows)]
        + part_scratch + total_scratch,
        [gm_low, (n2, LAZY), (f1, LAZY), (a1, LAZY), (h1, LAZY), conv_gains, (y_own, LAZY),
         (stage0, LAZY), (stage1, LAZY), (in0, LAZY), (in1, LAZY), (first_up, ANY), (conv_down, ANY), (partial2, ANY), (first2_last, ANY)],
        flops=9 * 10**9,
        moved=150 << 20,
    )
    small_width = max(share, channels, 2 * head_width)

    def conv_backward(
        low_ref, gh1_ref, pc_ref, edge_ref, same_ref, kernel_ref, wout_ref, win_ref, x_ref, gain_ref, yout_ref,
        n1_ref, mixed_ref, stage0, stage1, in0, in1, turn0, turn1, small_in,
        partial1, partial2, first1, first2, first2_last, second2, second2_last,
        edges_ref, sums_ref, gout2_ref, gmix_ref, gout1_ref, gin_ref, gdown2, gup2, gdown1, gup1,
        bp_ref, ext, spread, gz_ext, outgoing, arrived, full, gg_ref, edge_send, edge_recv, swap_send, swap_recv,
        given, former, latter2, latter3, stage2, stage3, in2, in3, turn2, turn3, hs, hr, ls, lr, ms, mr, us, ur,
        own_buf, first_buf, second_buf, passing, item_sems, vs, vr, down_stage, up_stage, out_sems,
        packed, boxes, summed, final, zs, zr, ss, sr,
        part, inbox, rs, rr, gs, gr, travel,
    ):
        where = place()
        s, q, h = where
        first = s == 0
        partner = (1 - s, q, h)
        preceding = (1 - s, jnp.where(first, lax.rem(q + seqs - 1, seqs), q), h)
        following = (1 - s, jnp.where(first, q, lax.rem(q + 1, seqs)), h)
        others = head_others(where)
        me = q * sections + s
        slot_peers = [slot_peer(me, j, h) for j in range(1, slots)]
        peers = seq_peers(where, seqs)
        latters, stages = [latter2, latter3], [stage0, stage1, stage2, stage3]
        incomes, turns = [in0, in1, in2, in3], [turn0, turn1, turn2, turn3]
        loads = []
        sources = [
            (partial2.at[0], first2.at[0], second2.at[0]),
            (partial2.at[1], first2.at[1], second2.at[1]),
            (partial2.at[2], first2_last.at[0], second2_last.at[0]),
            (partial1.at[0], first1.at[0], None),
            (partial1.at[1], first1.at[1], None),
            (partial1.at[2], first1.at[2], None),
        ]
        for n, (partial, arrived_hbm, passed_hbm) in enumerate(sources):
            copies = [pltpu.make_async_copy(partial.at[q], own_buf.at[n], item_sems.at[n, 0])]
            if arrived_hbm is not None:
                copies.append(pltpu.make_async_copy(arrived_hbm, first_buf.at[n], item_sems.at[n, 1]))
            if passed_hbm is not None:
                copies.append(pltpu.make_async_copy(passed_hbm, second_buf.at[n], item_sems.at[n, 2]))
            else:
                copies += load_passing(partial, passing.at[n - 3], item_sems.at[n, pl.ds(3, grid_rows)], where)
            loads.append(copies)
        for copies in loads[3:] + loads[:3]:
            start_all(copies)
        greet([partner, preceding, following] + others + slot_peers, where, heads)
        travel.ready(n1_ref, mixed_ref)
        latter2[0:tokens, :] = mixed_ref[...]
        halves = half_swaps([low_ref, n1_ref], [given.at[0], given.at[1]], hs, hr, where)
        start_all(halves)
        swaps = latter_swaps(latters, ls, lr, partner)
        swaps[0].start()
        gg_ref[...] = jnp.zeros_like(gg_ref)
        gated = pc_ref[0] * pc_ref[2]
        grad_y = back_product(low_ref[...], wout_ref[...])
        gz = grad_y * pc_ref[1]
        zero = jnp.zeros((8, channels), FLOAT)
        for m in range(micro):
            span = slice(m * rows, (m + 1) * rows)
            one = jnp.where(same_ref[span, 0:1] > 0, gz[span], 0.0) * kernel_ref[1:2, :]
            two = jnp.where(same_ref[span, 1:2] > 0, gz[span], 0.0) * kernel_ref[0:1, :]
            gz_ext[0, m, 0:rows, :] = one
            gz_ext[0, m, rows : rows + 8, :] = zero
            gz_ext[1, m, 0:rows, :] = two
            gz_ext[1, m, rows : rows + 8, :] = zero
            outgoing[m] = zero
            outgoing[m, 0:1, :] = two[0:1]
            outgoing[m, 1:2, :] = one[0:1] + two[1:2]
        edge = remote(outgoing, arrived, edge_send.at[0], edge_recv.at[0], preceding)
        edge.start()
        bulk = []
        for n in (3, 4, 5):
            wait_all(loads[n])
            combine(lambda i, n=n: passing.at[n - 3, i], first_buf.at[n], where)
            sends = second_stage(
                lambda i, n=n: passing.at[n - 3, i], second_buf.at[n], vs.at[n - 3], vr.at[n - 3], where
            )
            start_all(sends)
            bulk.append(sends)
        taps = [None, None, None]
        for m in range(micro):
            span = slice(m * rows, (m + 1) * rows)
            ext[m, 0:8, :] = edge_ref[m]
            ext[m, 8 : 8 + rows, :] = gated[span]
            back_one = jnp.where(same_ref[span, 0:1] > 0, shifted_rows(ext, m, 1), 0.0)
            back_two = jnp.where(same_ref[span, 1:2] > 0, shifted_rows(ext, m, 2), 0.0)
            mixed = (
                kernel_ref[2:3, :] * gated[span]
                + kernel_ref[1:2, :] * back_one
                + kernel_ref[0:1, :] * back_two
            )
            bp_ref[span, channels : 2 * channels] = (grad_y[span] * mixed).astype(HALF)
            for k, value in enumerate((back_two, back_one, gated[span])):
                term = jnp.sum(value * gz[span], 0, keepdims=True)
                taps[k] = term if taps[k] is None else taps[k] + term
        for m in range(micro):
            span = slice(m * rows, (m + 1) * rows)
            spread[m] = (
                kernel_ref[2:3, :] * gz[span]
                + gz_ext[0, m, 1 : rows + 1, :]
                + gz_ext[1, m, 2 : rows + 2, :]
            )
        edge.wait()
        wrap = (s == sections - 1) & (q == seqs - 1)
        for m in range(micro):
            follow = arrived[m + 1, 0:2, :] if m + 1 < micro else jnp.zeros((2, channels), FLOAT)
            spread[m, rows - 2 : rows, :] += jnp.where(wrap, follow, arrived[m, 0:2, :])
        for m in range(micro):
            span = slice(m * rows, (m + 1) * rows)
            bp_ref[span, 0:channels] = (spread[m] * pc_ref[2, span, :]).astype(HALF)
            bp_ref[span, 2 * channels :] = (spread[m] * pc_ref[0, span, :]).astype(HALF)
        latter3[0:tokens, :] = bp_ref[...]
        swaps[1].start()
        travel.ready(win_ref, x_ref, gh1_ref, yout_ref, small_in)
        total = back_product(bp_ref[:, 0:channels], win_ref[0])
        total = total + back_product(bp_ref[:, channels : 2 * channels], win_ref[1])
        total = total + back_product(bp_ref[:, 2 * channels :], win_ref[2])
        part[...] = total.astype(HALF)

        def finish(flow, i, total):
            start = x_ref[own_rows(flow, i), :].astype(FLOAT)
            grad_start, grad_gain = norm_back(start, gain_ref[0:1, :], total)
            gg_ref[...] += grad_gain
            return (gh1_ref[kept_rows(i), :] + grad_start).astype(HALF)

        sent = mixer_sends(stages[2:], incomes[2:], ms, mr, where)
        mixer_step = mixer_steps([low_ref, n1_ref], latters, stages[2:], given, former, halves, swaps, sent)
        head_total(part, full, inbox, rs, rr, gs, gr, where, heads, finish, mixer_step, 4)
        keep = pl.ds(pl.multiple_of(s * rows, rows), rows)
        edges_ref[0, :, keep, :] = jnp.where(first, full[...], yout_ref[...]).reshape(micro, rows, width)
        part[...] = jnp.where(first, yout_ref[...], full[...])
        edge_swaps = []
        for m in range(micro):
            copy = remote(
                part.at[m * rows : (m + 1) * rows], edges_ref.at[0, m, keep], swap_send.at[m], swap_recv.at[m], partner
            )
            copy.start()
            edge_swaps.append(copy)
        packed[...] = small_in[...]
        packed[:, 5:8, 0:channels] = jnp.broadcast_to(jnp.concatenate(taps, 0)[None], (slots, 3, channels))
        for d in range(slots):
            packed[d, 0:1, 0:share] = gg_ref[:, d * share : (d + 1) * share]
        over = []
        for k, peer in enumerate(others):
            copy = remote(packed, boxes.at[k], zs.at[k], zr.at[k], peer)
            copy.start()
            over.append(copy)
        wait_all(over)
        over_heads = boxes[0]
        for j in range(1, heads - 1):
            over_heads = over_heads + boxes[j]
        row = lax.broadcasted_iota(jnp.int32, over_heads.shape, 1)
        summed[...] = packed[...] + jnp.where(row < 5, over_heads, 0.0)
        across = []
        for j, peer in enumerate(slot_peers):
            copy = remote(summed.at[peer[0] * seqs + peer[1]], final.at[j], ss.at[j], sr.at[j], peer)
            copy.start()
            across.append(copy)
        outs = []

        def leave(source, target, at):
            copy = pltpu.make_async_copy(source, target, out_sems.at[at])
            copy.start()
            outs.append(copy)

        def fill_stage(n, target):
            upper, lower = two_halves(own_buf.at[n], first_buf.at[n], second_buf.at[n], where)
            target[half_rows(0), :] = upper[:, :hidden_units].astype(HALF)
            target[half_rows(1), :] = lower[:, :hidden_units].astype(HALF)

        def second_half_items():
            for n in range(3):
                wait_all(loads[n])
            fill_stage(0, down_stage.at[0])
            leave(down_stage.at[0], gdown2, 0)
            for kind in range(2):
                fill_stage(1 + kind, up_stage.at[0, kind])
            leave(up_stage.at[0], gup2, 1)

        for copies in sent:
            wait_all(copies)
        mixer_turns = mixer_second(stages[2:], incomes[2:], [None, None], turns[2:], us, ur, where)
        travel.ready(stage0, stage1, in0, in1, turn0, turn1)
        second_half_items()
        for n in (3, 4, 5):
            wait_all(bulk[n - 3])
            if n == 3:
                fill_stage(3, down_stage.at[1])
                leave(down_stage.at[1], gdown1, 2)
            else:
                fill_stage(n, up_stage.at[1, n - 4])
        leave(up_stage.at[1], gup1, 3)
        wait_all(edge_swaps)
        wait_all(across)
        total = summed[s * seqs + q]
        for j in range(slots - 1):
            total = total + final[j]
        sums_ref[...] = total
        for k, target in enumerate((gout2_ref, gmix_ref, gout1_ref, None)):
            if k >= 2:
                wait_all(mixer_turns[k - 2])
            for side, value in enumerate(two_halves(stages[k].at[q], incomes[k], turns[k], where)):
                value = value.astype(HALF)
                if target is None:
                    for c in range(3):
                        gin_ref[c, half_rows(side), :] = value[:, c * channels : (c + 1) * channels]
                else:
                    target[half_rows(side), :] = value
        wait_all(outs)

    folded = grad_qk[0:2, :head_width] + grad_qk[0:2, head_width : 2 * head_width]
    gain_rows = jnp.concatenate(
        [jnp.zeros_like(grad_gain_conv1), grad_gain_conv1, grad_gain_attn0, grad_gain_attn1], 0
    )

    def to_width(array):
        return jnp.pad(array, [(0, 0)] * (array.ndim - 1) + [(0, small_width - array.shape[-1])])

    small = jnp.concatenate(
        [
            to_width(gain_rows.reshape(4, slots, share).transpose(1, 0, 2)),
            jnp.broadcast_to(to_width(folded.reshape(1, 1, 2 * head_width)), (slots, 1, small_width)),
            jnp.zeros((slots, 3, small_width), FLOAT),
        ],
        1,
    )

    (section_edges, sums, gout2, gmix, gout1, gin, gdown2, gup2, gdown1, gup1) = call(
        conv_backward,
        "conv_backward",
        7,
        [
            ((1, micro, local_rows, width), HALF),
            ((8, small_width), FLOAT),
            ((share, widths[0]), HALF),
            ((share, widths[1]), HALF),
            ((share, widths[2]), HALF),
            ((3, share, channels), HALF),
            ((share, hidden_units), HALF, ANY),
            ((2, share, hidden_units), HALF, ANY),
            ((share, hidden_units), HALF, ANY),
            ((2, share, hidden_units), HALF, ANY),
        ],
        [
            pltpu.VMEM((tokens, 3 * channels), HALF),
            pltpu.VMEM((micro, 8 + rows, channels), FLOAT),
            pltpu.VMEM((micro, rows, channels), FLOAT),
            pltpu.VMEM((2, micro, rows + 8, channels), FLOAT),
            pltpu.VMEM((micro, 8, channels), FLOAT),
            pltpu.VMEM((micro, 8, channels), FLOAT),
            pltpu.VMEM((tokens, width), HALF),
            pltpu.VMEM((1, width), FLOAT),
            dma(1),
            dma(1),
            dma(micro),
            dma(micro),
            pltpu.VMEM((2, tokens, half_model), HALF),
            pltpu.VMEM((half_model, 2 * tokens), HALF),
        ]
        + [pltpu.VMEM((2 * tokens, size), HALF) for size in widths[2:]]
        + [pltpu.VMEM((seqs, share, size), HALF) for size in widths[2:]]
        + [pltpu.VMEM((first_blocks, half_share, size), HALF) for size in widths[2:]]
        + [pltpu.VMEM((grid_rows, half_share, size), HALF) for size in widths[2:]]
        + [
            dma(2),
            dma(2),
            dma(2),
            dma(2),
            dma_grid(2, first_blocks),
            dma_grid(2, first_blocks),
            dma_grid(2, grid_rows),
            dma_grid(2, grid_rows),
            pltpu.VMEM((6, share, padded_units), HALF),
            pltpu.VMEM((6, first_blocks, half_share, padded_units), HALF),
            pltpu.VMEM((6, grid_rows, half_share, padded_units), HALF),
            pltpu.VMEM((3, grid_rows, half_share, padded_units), HALF),
            dma_grid(6, 3 + grid_rows),
            dma_grid(3, grid_rows),
            dma_grid(3, grid_rows),
            pltpu.VMEM((2, share, hidden_units), HALF),
            pltpu.VMEM((2, 2, share, hidden_units), HALF),
            dma(4),
            pltpu.VMEM((slots, 8, small_width), FLOAT),
            pltpu.VMEM((heads - 1, slots, 8, small_width), FLOAT),
            pltpu.VMEM((slots, 8, small_width), FLOAT),
            pltpu.VMEM((slots - 1, 8, small_width), FLOAT),
            dma(heads - 1),
            dma(heads - 1),
            dma(slots - 1),
            dma(slots - 1),
        ]
        + part_scratch
        + total_scratch,
        [
            gh1_low, (gh1, LAZY), projected, edge_gated, same, conv_kernel, conv_out, (w_in, LAZY), (x, LAZY), conv_gains,
            (yout, LAZY), (n1, LAZY), (mixed, LAZY), (stage0, LAZY), (stage1, LAZY), (in0, LAZY), (in1, LAZY), (turn0, LAZY), (turn1, LAZY),
            (small, LAZY),
        ]
        + [(array, ANY) for array in (partial1, partial2, first1, first2, first2_last, second2, second2_last)],
        flops=5 * 10**9,
        moved=300 << 20,
    )
    def results(
        edges_in, sums_in, gout2_in, gmix_in, gout1_in, gin_in, gdown2_in, gup2_in, gdown1_in, gup1_in,
        edges_out, cgain_out, gin_out, taps_out, gout1_out, gup1_out, gdown1_out,
        again_out, gq_out, gkv_out, gqk_out, gout2_out, gup2_out, gdown2_out,
        down_in, up_in, down_stage, up_stage, edges_held, in_sems, out_sems, edge_sem, travel,
    ):
        edges_load = pltpu.make_async_copy(edges_in, edges_held, edge_sem.at[0])
        edges_load.start()
        loads = [
            pltpu.make_async_copy(source, target, in_sems.at[k])
            for k, (source, target) in enumerate(
                [(gdown1_in, down_in.at[0]), (gup1_in, up_in.at[0]), (gdown2_in, down_in.at[1]), (gup2_in, up_in.at[1])]
            )
        ]
        start_all(loads)
        stores = []
        for k, (down_out, up_out) in enumerate(((gdown1_out, gup1_out), (gdown2_out, gup2_out))):
            loads[2 * k].wait()
            down_stage[k] = down_in[k].astype(FLOAT)
            stores.append(pltpu.make_async_copy(down_stage.at[k], down_out, out_sems.at[2 * k]))
            stores[-1].start()
            loads[2 * k + 1].wait()
            for kind in range(2):
                up_stage[k, :, kind, :] = up_in[k, kind].astype(FLOAT)
            stores.append(pltpu.make_async_copy(up_stage.at[k], up_out, out_sems.at[2 * k + 1]))
            stores[-1].start()
        cgain_out[...] = sums_in[0:2, 0:share]
        again_out[...] = sums_in[2:4, 0:share]
        taps_out[...] = sums_in[5:8, 0:channels]
        for kind in range(2):
            gqk_out[kind : kind + 1, :] = sums_in[4:5, kind * head_width : (kind + 1) * head_width]
            start = query_width + kind * (pair_width // 2)
            gkv_out[:, kind, :] = gmix_in[:, start : start + pair_width // 2].astype(FLOAT)
        gq_out[...] = gmix_in[:, 0:query_width].astype(FLOAT)
        gout1_out[...] = gout1_in[...].astype(FLOAT)
        gout2_out[...] = gout2_in[...].astype(FLOAT)
        gin_out[...] = gin_in[...].astype(FLOAT)
        edges_load.wait()
        stores.append(pltpu.make_async_copy(edges_held, edges_out, edge_sem.at[1]))
        stores[-1].start()
        wait_all(stores)

    (
        section_edges, cgain, gin, taps, gout1, gup1, gdown1, again, gq, gkv, gqk, gout2, gup2, gdown2,
    ) = call(
        results,
        "results",
        None,
        [
            ((1, micro, local_rows, width), HALF, ANY),
            ((2, share), FLOAT),
            ((3, share, channels), FLOAT),
            ((3, channels), FLOAT),
            ((share, channels), FLOAT),
            ((share, 2, hidden_units), FLOAT, ANY),
            ((share, hidden_units), FLOAT, ANY),
            ((2, share), FLOAT),
            ((share, query_width), FLOAT),
            ((share, 2, pair_width // 2), FLOAT),
            ((2, head_width), FLOAT),
            ((share, query_width), FLOAT),
            ((share, 2, hidden_units), FLOAT, ANY),
            ((share, hidden_units), FLOAT, ANY),
        ],
        [
            pltpu.VMEM((2, share, hidden_units), HALF),
            pltpu.VMEM((2, 2, share, hidden_units), HALF),
            pltpu.VMEM((2, share, hidden_units), FLOAT),
            pltpu.VMEM((2, share, 2, hidden_units), FLOAT),
            pltpu.VMEM((1, micro, local_rows, width), HALF),
            dma(4),
            dma(4),
            dma(2),
        ],
        [(section_edges, ANY), sums, gout2, gmix, gout1, gin]
        + [(array, ANY) for array in (gdown2, gup2, gdown1, gup1)],
        moved=25 << 20,
    )
    return (
        section_edges,
        cgain,
        gin.transpose(1, 0, 2),
        taps,
        gout1.T,
        gup1,
        gdown1.T,
        again,
        gq,
        gkv,
        gqk,
        gout2.T,
        gup2,
        gdown2.T,
    )


def solution(mesh):
    return jax.shard_map(
        per_device,
        mesh=mesh,
        in_specs=(
            P("section", None, "seq", None),
            P(),
            P(None, "seq"),
            P(),
            P(None, None, "head"),
            P(None, "head"),
            P("head", None),
            P(None, None, "head"),
            P("head", None),
            P(),
            P(None, "head"),
            P(None, None, "head"),
            P(),
            P("head", None),
            P(None, None, "head"),
            P("head", None),
        ),
        out_specs=(
            P("section", None, "seq", None),
            P(None, ("section", "seq")),
            P(("section", "seq"), None, "head"),
            P(None, "head"),
            P("head", ("section", "seq")),
            P(("section", "seq"), None, "head"),
            P("head", ("section", "seq")),
            P(None, ("section", "seq")),
            P(("section", "seq"), "head"),
            P(("section", "seq"), None, "head"),
            P(),
            P("head", ("section", "seq")),
            P(("section", "seq"), None, "head"),
            P("head", ("section", "seq")),
        ),
        check_vma=False,
    )
```

```python
import functools

import jax
import jax.numpy as jnp
from jax import lax
from jax.experimental import pallas as pl
from jax.experimental.pallas import tpu as pltpu
from jax.sharding import PartitionSpec as P

EPS = 1e-05
THETA = 1000000.0
FLOAT = jnp.float32
HALF = jnp.bfloat16
MESH = pl.DeviceIdType.MESH
VMEM = pl.BlockSpec(memory_space=pltpu.VMEM)
ANY = pl.BlockSpec(memory_space=pl.ANY)


def product(former, latter):
    return jnp.dot(former, latter, preferred_element_type=FLOAT)


def outer_sum(former, latter):
    return lax.dot_general(former, latter, (((0,), (0,)), ((), ())), preferred_element_type=FLOAT)


def back_product(former, latter):
    return lax.dot_general(former, latter, (((1,), (1,)), ((), ())), preferred_element_type=FLOAT)


def norm_apply(values, gain):
    return values * lax.rsqrt(jnp.mean(values * values, -1, keepdims=True) + EPS) * gain


def norm_back(values, gain, grad):
    scale = lax.rsqrt(jnp.mean(values * values, -1, keepdims=True) + EPS)
    weighted = grad * gain
    inner = jnp.mean(weighted * values, -1, keepdims=True)
    grad_values = scale * weighted - values * (scale * scale * scale * inner)
    return grad_values, jnp.sum(grad * values * scale, 0, keepdims=True)


BLOCKS = 8
LAG = 3
END_FIRST = 10
MIDDLE_FIRST = 3


def place():
    return lax.axis_index("section"), lax.axis_index("seq"), lax.axis_index("head")


def remote(source, target, send, recv, peer):
    return pltpu.make_async_remote_copy(
        src_ref=source,
        dst_ref=target,
        send_sem=send,
        recv_sem=recv,
        device_id=peer,
        device_id_type=MESH,
    )


def signal(peer):
    pl.semaphore_signal(pltpu.get_barrier_semaphore(), inc=1, device_id=peer, device_id_type=MESH)


def wait_greetings(count):
    pl.semaphore_wait(pltpu.get_barrier_semaphore(), count)


def greet(others, where=None, size=0):
    for peer in others:
        signal(peer)
    if where is None:
        wait_greetings(len(others))
        return
    section, seq, head = where
    end = (head == 0) | (head == size - 1)

    @pl.when(end)
    def _():
        signal((section, seq, jnp.where(head == 0, 1, size - 2)))
        wait_greetings(len(others) + 1)

    @pl.when(jnp.logical_not(end))
    def _():
        signal((section, seq, jnp.minimum(head + 1, size - 1)))
        signal((section, seq, jnp.maximum(head - 1, 0)))
        wait_greetings(len(others) + 2)


def seq_peers(where, seqs):
    section, seq, head = where
    return [(section, lax.rem(seq + k, seqs), head) for k in range(1, seqs)]


def rows_of(index, count):
    return pl.ds(pl.multiple_of(index * count, count), count)


def wait_all(copies):
    for copy in copies:
        copy.wait()


def start_all(copies):
    for copy in copies:
        copy.start()


def loop(count, step):
    def body(i, carried):
        step(i)
        return carried

    lax.fori_loop(0, count, body, 0)


def head_total(part, full, inbox, reduce_send, reduce_recv, gather_send, gather_recv, where, size, finish, filler=None, fillers=0):
    section, seq, head = where
    count = part.shape[0] // (2 * BLOCKS)
    last = size - 1
    end = (head == 0) | (head == last)

    def rows(flow, i):
        return rows_of(flow * BLOCKS + i, count)

    def fill(t):
        if filler is not None:

            @pl.when(t < fillers)
            def _():
                filler(t)

    def fill_rest(start, stop=fillers):
        stop = min(stop, fillers)
        if stop > start:
            loop(stop - start, lambda i: filler(start + i))

    def reduced(flow, i, peer):
        return remote(part.at[rows(flow, i)], inbox.at[flow, i], reduce_send.at[flow, i], reduce_recv.at[flow, i], peer)

    def gathered(flow, i, peer):
        span = full.at[rows(flow, i)]
        return remote(span, span, gather_send.at[flow, i], gather_recv.at[flow, i], peer)

    @pl.when(end)
    def _():
        flow = jnp.where(head == 0, 0, 1)
        inner = (section, seq, jnp.where(head == 0, 1, last - 1))
        loop(BLOCKS, lambda i: reduced(1 - flow, i, inner).start())
        fill_rest(0, END_FIRST)

        def own(i):
            reduced(flow, i, inner).wait_recv()
            total = part[rows(flow, i), :].astype(FLOAT) + inbox[flow, i].astype(FLOAT)
            full[rows(flow, i), :] = finish(flow, i, total)
            gathered(flow, i, inner).start()
            fill(END_FIRST + i)

        loop(BLOCKS, own)
        fill_rest(END_FIRST + BLOCKS)

        def drain(i):
            gathered(1 - flow, i, inner).wait_recv()
            reduced(1 - flow, i, inner).wait_send()
            gathered(flow, i, inner).wait_send()

        loop(BLOCKS, drain)

    @pl.when(jnp.logical_not(end))
    def _():
        low = head < size // 2
        near = jnp.where(low, 1, 0)
        ahead = (section, seq, jnp.where(low, head + 1, head - 1))
        behind = (section, seq, jnp.where(low, head - 1, head + 1))

        def add(flow, i, peer):
            reduced(flow, i, peer).wait_recv()
            span = rows(flow, i)
            part[span, :] = (part[span, :].astype(FLOAT) + inbox[flow, i].astype(FLOAT)).astype(HALF)
            reduced(flow, i, peer).start()

        def forward(flow, i, peer):
            gathered(flow, i, peer).wait_recv()
            gathered(flow, i, peer).start()

        def lagged(act, first, second, at):
            def step(i):
                fill(at + i)

                @pl.when(i < BLOCKS)
                def _():
                    act(first, i, ahead)

                @pl.when(i >= LAG)
                def _():
                    act(second, i - LAG, behind)

            loop(BLOCKS + LAG, step)

        fill_rest(0, MIDDLE_FIRST)
        lagged(add, near, 1 - near, MIDDLE_FIRST)
        lagged(forward, 1 - near, near, MIDDLE_FIRST + BLOCKS + LAG)
        fill_rest(MIDDLE_FIRST + 2 * (BLOCKS + LAG))

        def drain(i):
            reduced(near, i, ahead).wait_send()
            reduced(1 - near, i, behind).wait_send()
            gathered(1 - near, i, ahead).wait_send()
            gathered(near, i, behind).wait_send()

        loop(BLOCKS, drain)


def turned(values):
    width = values.shape[-1]
    if width == 128:
        lane = lax.broadcasted_iota(jnp.int32, values.shape, 1)
        low = lax.rem(lane, 64) < 32
        return jnp.where(low, -pltpu.roll(values, 96, 1), pltpu.roll(values, 32, 1))
    parts = []
    for start in range(0, width, 64):
        parts += [-values[:, start + 32 : start + 64], values[:, start : start + 32]]
    return jnp.concatenate(parts, -1)


def head_mean(values):
    width = values.shape[-1]
    if width == 64:
        return jnp.mean(values, -1, keepdims=True)
    lane = lax.broadcasted_iota(jnp.int32, values.shape, 1)
    first = jnp.sum(jnp.where(lane < 64, values, 0.0), -1, keepdims=True)
    second = jnp.sum(jnp.where(lane < 64, 0.0, values), -1, keepdims=True)
    return jnp.where(lane < 64, first, second) * (1.0 / 64.0)


def chunks_of(width):
    return [(start, min(128, width - start)) for start in range(0, width, 128)]


def rotary(raw, gain, cosine, sine):
    width = raw.shape[-1]
    normed = raw * lax.rsqrt(head_mean(raw * raw) + EPS) * gain[:, :width]
    return normed * cosine[:, :width] + turned(normed) * sine[:, :width]


def rotary_back(raw, gain, cosine, sine, grad):
    width = raw.shape[-1]
    back = grad * cosine[:, :width] - turned(grad) * sine[:, :width]
    scale = lax.rsqrt(head_mean(raw * raw) + EPS)
    weighted = back * gain[:, :width]
    grad_raw = scale * weighted - raw * (scale * scale * scale * head_mean(weighted * raw))
    return grad_raw, jnp.sum(back * raw * scale, 0, keepdims=True)


LAZY = "lazy"
LATE = "late"


class Moves:
    def __init__(self, incoming, leaving):
        self.incoming, self.leaving, self.left = incoming, leaving, []
        for _, copy in incoming:
            copy.start()

    def ready(self, *refs):
        for ref in refs:
            for known, copy in self.incoming:
                if known is ref:
                    copy.wait()

    def leave(self, *refs):
        for ref in refs:
            for known, copy in self.leaving:
                if known is ref:
                    copy.start()
                    self.left.append(copy)

    def finish(self):
        wait_all(self.left)


def call(body, name, collective, outs, scratch, args, flops=0, moved=0):
    params = dict(vmem_limit_bytes=60 << 20)
    if collective is not None:
        params.update(collective_id=collective, has_side_effects=True)
    lazy = [n for n, arg in enumerate(args) if isinstance(arg, tuple) and arg[1] is LAZY]
    late = [n for n, out in enumerate(outs) if len(out) > 2 and out[2] is LATE]
    arrays = [arg[0] if isinstance(arg, tuple) else arg for arg in args]
    extra = [pltpu.VMEM(arrays[n].shape, arrays[n].dtype) for n in lazy]
    extra += [pltpu.VMEM(outs[n][0], outs[n][1]) for n in late]
    moves = len(lazy) + len(late)
    if moves:
        extra.append(pltpu.SemaphoreType.DMA((moves,)))

    def whole(*refs):
        refs = list(refs)
        held = refs[len(refs) - len(extra) :]
        refs = refs[: len(refs) - len(extra)]
        incoming, leaving = [], []
        for at, n in enumerate(lazy):
            incoming.append((held[at], pltpu.make_async_copy(refs[n], held[at], held[-1].at[at])))
            refs[n] = held[at]
        for at, n in enumerate(late):
            place_at = len(args) + n
            kept = held[len(lazy) + at]
            leaving.append((kept, pltpu.make_async_copy(kept, refs[place_at], held[-1].at[len(lazy) + at])))
            refs[place_at] = kept
        travel = Moves(incoming, leaving)
        body(*refs, travel)
        travel.finish()

    def spec(mark):
        return ANY if mark is LAZY or mark is LATE else mark

    results = pl.pallas_call(
        whole,
        name=name,
        out_shape=[jax.ShapeDtypeStruct(out[0], out[1]) for out in outs],
        in_specs=[spec(arg[1]) if isinstance(arg, tuple) else VMEM for arg in args],
        out_specs=[spec(out[2]) if len(out) > 2 else VMEM for out in outs],
        scratch_shapes=list(scratch) + extra,
        compiler_params=pltpu.CompilerParams(**params),
        cost_estimate=pl.CostEstimate(flops=flops, bytes_accessed=moved, transcendentals=0),
    )(*arrays)
    return list(results)


def dma(count):
    return pltpu.SemaphoreType.DMA((count,))


def per_device(
    incoming,
    segment_ids,
    positions,
    conv_gains,
    conv_in,
    conv_kernel,
    conv_out,
    conv_gate_up,
    conv_down,
    attn_gains,
    w_query,
    w_keyval,
    qk_gains,
    attn_out,
    attn_gate_up,
    attn_down,
):
    sections = lax.axis_size("section")
    seqs = lax.axis_size("seq")
    heads = lax.axis_size("head")
    section, seq, head = place()
    micro, local_rows, width = incoming.shape[1:]
    rows = local_rows // sections
    tokens = micro * rows
    half_tokens = tokens // 2
    step_rows = half_tokens // BLOCKS
    block_tok = segment_ids.shape[1]
    length = micro * block_tok
    slots = sections * seqs
    channels = conv_in.shape[2]
    hidden_units = conv_down.shape[0]
    head_width = qk_gains.shape[1]
    query_width = w_query.shape[1]
    pair_width = 2 * w_keyval.shape[2]
    kv_local = w_keyval.shape[2] // head_width
    group = query_width // (kv_local * head_width)
    score_scale = head_width ** (-0.5)
    half_model = width // sections
    share = width // (sections * seqs)

    pair_index = lax.broadcasted_iota(jnp.int32, (1, 2 * head_width), 1) % (head_width // 2)
    angle_rates = THETA ** (-2.0 * pair_index.astype(FLOAT) / head_width)
    local_positions = lax.dynamic_slice_in_dim(positions, section * rows, rows, 1).reshape(tokens)
    angles = local_positions.astype(FLOAT)[:, None] * angle_rates
    cosine, sine = jnp.cos(angles), jnp.sin(angles)
    w_in = conv_in.transpose(1, 0, 2)
    w_pair = w_keyval.reshape(width, pair_width)
    first_up = conv_gate_up.transpose(1, 2, 0)
    second_up = attn_gate_up.transpose(1, 2, 0)
    slabs = [(start, min(512, hidden_units - start)) for start in range(0, hidden_units, 512)]
    tile_width = 256
    tiles = -(-hidden_units // tile_width)
    padded_units = tiles * tile_width

    def own_column(seg_ref, m, back):
        start = lax.axis_index("seq") * local_rows + lax.axis_index("section") * rows - back
        wanted = start + lax.broadcasted_iota(jnp.int32, (rows, block_tok), 0)
        lane = lax.broadcasted_iota(jnp.int32, (rows, block_tok), 1)
        found = jnp.where(lane == wanted, seg_ref[m : m + 1, :].astype(FLOAT), 0.0)
        if back and m:
            found = found + jnp.where(lane == wanted + block_tok, seg_ref[m - 1 : m, :].astype(FLOAT), 0.0)
        elif back:
            found = found + jnp.where((wanted < 0) & (lane == 0), -1.0, 0.0)
        return jnp.sum(found, -1, keepdims=True)

    def twice(row):
        return jnp.concatenate([row, row], -1)

    def shifted_rows(ext, micro_at, back):
        return ext[micro_at, 8 - back : 8 - back + rows, :]

    def own_rows(flow, i):
        return rows_of(flow * BLOCKS + i, step_rows)

    def kept_rows(i):
        return rows_of(i, step_rows)

    total_scratch = [pltpu.VMEM((2, BLOCKS, step_rows, width), HALF)] + [
        pltpu.SemaphoreType.DMA((2, BLOCKS)) for _ in range(4)
    ]
    part_scratch = [pltpu.VMEM((tokens, width), HALF)]

    weight_scratch = [
        pltpu.VMEM((2, hidden_units, width), HALF),
        pltpu.VMEM((hidden_units, width), HALF),
        dma(3 * len(slabs)),
    ]

    def weight_loads(up_hbm, down_hbm, up_ref, down_ref, sems):
        copies = []
        for j, (start, count) in enumerate(slabs):
            span = slice(start, start + count)
            pairs = [(up_hbm.at[0, span], up_ref.at[0, span]), (up_hbm.at[1, span], up_ref.at[1, span])]
            pairs.append((down_hbm.at[span], down_ref.at[span]))
            for k, (source, target) in enumerate(pairs):
                copies.append(pltpu.make_async_copy(source, target, sems.at[3 * j + k]))
        return copies

    def conv_forward(
        in_ref, gain_ref, win_ref, kernel_ref, wout_ref, attn_gain_ref, up_hbm, down_hbm, seg_ref,
        x_ref, g_ref, n1_ref, pc_ref, edge_ref, y_ref, h1_ref, n2_ref, f1_ref, a1_ref, m_ref, n3_ref, same_ref, segq_ref,
        other, edges, normed_edges, ext, swap_send, swap_recv, edge_send, edge_recv, up_ref, down_ref, weight_sems, acc,
        part, inbox, rs, rr, gs, gr, inbox2, rs2, rr2, gs2, gr2, travel,
    ):
        where = place()
        s, q, h = where
        partner = (1 - s, q, h)
        following = (s, lax.rem(q + 1, seqs), h)
        preceding = (s, lax.rem(q + seqs - 1, seqs), h)
        weights = weight_loads(up_hbm, down_hbm, up_ref, down_ref, weight_sems)
        start_all(weights)
        greet([partner, following, preceding] + seq_peers(where, seqs), where, heads)
        give = pl.multiple_of((1 - s) * rows, rows)
        swap = remote(in_ref.at[0, :, pl.ds(give, rows)], other, swap_send.at[0], swap_recv.at[0], partner)
        swap.start()
        near = remote(in_ref.at[0, :, rows - 16 : rows], edges.at[0], edge_send.at[0], edge_recv.at[0], partner)
        near.start()
        far = remote(
            in_ref.at[0, :, local_rows - 16 : local_rows], edges.at[1], edge_send.at[1], edge_recv.at[1], following
        )
        far.start()
        keep = pl.multiple_of(s * rows, rows)
        for m in range(micro):
            span = slice(m * rows, (m + 1) * rows)
            column = own_column(seg_ref, m, 0)
            segq_ref[span, :] = column
            for back in (1, 2):
                same_ref[span, back - 1 : back] = jnp.where(column == own_column(seg_ref, m, back), 1.0, 0.0)
        swap.wait()
        mine = in_ref[0, :, pl.ds(keep, rows), :].reshape(tokens, width)
        theirs = other[...].reshape(tokens, width)
        first = s == 0
        x = jnp.where(first, mine, theirs)
        x_ref[...] = x
        g_ref[...] = jnp.where(first, theirs, mine)
        n1_ref[...] = norm_apply(x.astype(FLOAT), gain_ref[0:1, :]).astype(HALF)
        near.wait()
        far.wait()
        for m in range(micro):
            before = edges[1, max(m - 1, 0)]
            far_edge = jnp.where(q == 0, before, edges[1, m])
            edge = jnp.where(first, far_edge, edges[0, m]).astype(FLOAT)
            normed_edges[m * 16 : (m + 1) * 16, :] = norm_apply(edge, gain_ref[0:1, :]).astype(HALF)
        travel.ready(win_ref)
        for k in range(3):
            pc_ref[k] = product(n1_ref[...], win_ref[k])
        edge_b = product(normed_edges[...], win_ref[0])
        edge_u = product(normed_edges[...], win_ref[2])
        edge_gated = edge_b * edge_u
        gated = pc_ref[0] * pc_ref[2]
        for m in range(micro):
            ext[m, 0:8, :] = edge_gated[m * 16 + 8 : m * 16 + 16, :]
            edge_ref[m] = edge_gated[m * 16 + 8 : m * 16 + 16, :]
            ext[m, 8 : 8 + rows, :] = gated[m * rows : (m + 1) * rows, :]
        for m in range(micro):
            span = slice(m * rows, (m + 1) * rows)
            mixed = (
                kernel_ref[2:3, :] * gated[span]
                + kernel_ref[1:2, :] * jnp.where(same_ref[span, 0:1] > 0, shifted_rows(ext, m, 1), 0.0)
                + kernel_ref[0:1, :] * jnp.where(same_ref[span, 1:2] > 0, shifted_rows(ext, m, 2), 0.0)
            )
            y_ref[span, :] = (pc_ref[1, span, :] * mixed).astype(HALF)
        travel.ready(wout_ref)
        part[...] = product(y_ref[...], wout_ref[...]).astype(HALF)
        travel.leave(x_ref, g_ref, n1_ref, pc_ref, edge_ref, y_ref, same_ref, segq_ref)

        def finish(flow, i, total):
            hidden = x_ref[own_rows(flow, i), :].astype(FLOAT) + total
            h1_ref[kept_rows(i), :] = hidden
            return norm_apply(hidden, gain_ref[1:2, :]).astype(HALF)

        head_total(part, n2_ref, inbox, rs, rr, gs, gr, where, heads, finish)
        travel.leave(h1_ref, n2_ref)
        for j, (start, count) in enumerate(slabs):
            wait_all(weights[3 * j : 3 * j + 3])
            span = slice(start, start + count)
            gate = back_product(n2_ref[...], up_ref[0, span, :])
            rise = back_product(n2_ref[...], up_ref[1, span, :])
            f1_ref[0, :, span] = gate
            f1_ref[1, :, span] = rise
            active = (gate / (1.0 + jnp.exp(-gate)) * rise).astype(HALF)
            a1_ref[:, span] = active
            term = product(active, down_ref[span, :])
            if j == 0:
                acc[...] = term
            else:
                acc[...] += term
        part[...] = acc[...].astype(HALF)
        travel.leave(f1_ref, a1_ref)

        def finish_middle(flow, i, total):
            middle = (h1_ref[kept_rows(i), :] + total).astype(HALF).astype(FLOAT)
            m_ref[kept_rows(i), :] = middle
            return norm_apply(middle, attn_gain_ref[0:1, :]).astype(HALF)

        head_total(part, n3_ref, inbox2, rs2, rr2, gs2, gr2, where, heads, finish_middle)
        travel.leave(m_ref, n3_ref)


    grid_rows = seqs // 2
    first_blocks = 3 * grid_rows - 2
    half_share = share // 2

    def grid_place(q):
        return lax.div(q, 2), lax.rem(q, 2)

    def first_stage(source, target, send, recv, where):
        s, q, h = where
        a, b = grid_place(q)
        copies = []
        for row in range(grid_rows):
            copies.append((source(row * 2 + 1 - b, 0), row, (s, a * 2 + 1 - b, h)))
        for k in range(1, grid_rows):
            row = lax.rem(a + k, grid_rows)
            for column in range(2):
                copies.append((source(row * 2 + column, 1), grid_rows + 2 * (k - 1) + column, (s, row * 2 + b, h)))
        return [remote(block, target(i), send.at[i], recv.at[i], peer) for block, i, peer in copies]

    def passed_blocks(where):
        s, q, h = where
        a, b = grid_place(q)
        blocks = []
        for k in range(1, grid_rows):
            row = lax.rem(a + k, grid_rows)
            blocks.append((row * 2 + b, 0, [row], (s, row * 2 + b, h)))
        arrived = [grid_rows + 2 * j + 1 - b for j in range(grid_rows - 1)]
        blocks.append((a * 2 + 1 - b, 1, arrived, (s, a * 2 + 1 - b, h)))
        return blocks

    def half_rows(side):
        return slice(side * half_share, (side + 1) * half_share)

    def combine(passing, arrived, where, own=None):
        for i, (_, _, sources, _) in enumerate(passed_blocks(where)):
            total = (passing if own is None else own)(i)[...].astype(FLOAT)
            for source in sources:
                total = total + arrived[source].astype(FLOAT)
            passing(i)[...] = total.astype(HALF)

    def second_stage(passing, target, send, recv, where):
        return [
            remote(passing(i), target.at[i], send.at[i], recv.at[i], peer)
            for i, (_, _, _, peer) in enumerate(passed_blocks(where))
        ]

    def load_passing(partial, passing, sems, where):
        return [
            pltpu.make_async_copy(partial.at[dest, half_rows(side)], passing.at[i], sems.at[i])
            for i, (dest, side, _, _) in enumerate(passed_blocks(where))
        ]

    def two_halves(own, arrived, passed, where):
        a, b = grid_place(where[1])
        upper = own[half_rows(0), :].astype(FLOAT) + arrived[a].astype(FLOAT)
        for k in range(grid_rows - 1):
            upper = upper + passed[k].astype(FLOAT)
        lower = own[half_rows(1), :].astype(FLOAT) + passed[grid_rows - 1].astype(FLOAT)
        for j in range(grid_rows - 1):
            lower = lower + arrived[grid_rows + 2 * j + b].astype(FLOAT)
        return upper, lower

    def dma_grid(*shape):
        return pltpu.SemaphoreType.DMA(shape)

    def first_shape(count):
        return ((count, first_blocks, half_share, padded_units), HALF, ANY)

    def second_shape(count):
        return ((count, grid_rows, half_share, padded_units), HALF, ANY)

    def passing_scratch(count):
        return [
            pltpu.VMEM((count, grid_rows, half_share, padded_units), HALF),
            pltpu.VMEM((count, first_blocks, half_share, padded_units), HALF),
            dma_grid(count, grid_rows + 1),
            dma_grid(count, grid_rows),
            dma_grid(count, grid_rows),
        ]

    def pass_loads(partial, kinds, arrived, passing, held, sems, where):
        copies = []
        for k, kind in enumerate(kinds):
            copies += load_passing(partial.at[kind], passing.at[k], sems.at[k], where)
            copies.append(pltpu.make_async_copy(arrived.at[k], held.at[k], sems.at[k, grid_rows]))
        return copies

    def pass_sends(count, passing, held, target, send, recv, where):
        copies = []
        for k in range(count):
            combine(lambda i, k=k: passing.at[k, i], held.at[k], where)
            sends = second_stage(lambda i, k=k: passing.at[k, i], target.at[k], send.at[k], recv.at[k], where)
            start_all(sends)
            copies += sends
        return copies

    small_rows = tokens // heads
    widths = [query_width, query_width + pair_width, channels, 3 * channels]

    def head_others(where):
        s, q, h = where
        return [(s, q, lax.rem(h + k, heads)) for k in range(1, heads)]

    def mixer_sends(stages, incomes, send, recv, where):
        return [
            first_stage(
                lambda dest, side, stage=stage: stage.at[dest, half_rows(side)],
                lambda i, income=income: income.at[i],
                send.at[k],
                recv.at[k],
                where,
            )
            for k, (stage, income) in enumerate(zip(stages, incomes))
        ]

    def mixer_steps(formers, latters, stages, given, former, halves, swaps, sends):
        def step(t):
            for k in range(len(formers)):

                @pl.when(t == 2 * k)
                def _(k=k):
                    halves[k].wait()
                    former[...] = transposed(formers[k], given.at[k])

                @pl.when(t == 2 * k + 1)
                def _(k=k):
                    swaps[k].wait()
                    result = product(former[...], latters[k][...]).astype(HALF)
                    stages[k][...] = result.reshape(seqs, share, result.shape[1])
                    start_all(sends[k])

        return step

    def mixer_second(stages, incomes, passes, turns, send, recv, where):
        blocks = passed_blocks(where)
        turning = []
        for k, (stage, income, passed, turn) in enumerate(zip(stages, incomes, passes, turns)):

            def own_block(i, stage=stage):
                return stage.at[blocks[i][0], half_rows(blocks[i][1])]

            def moved(i, stage=stage, passed=passed):
                return own_block(i, stage) if passed is None else passed.at[i]

            combine(moved, income, where, own_block)
            sends = second_stage(moved, turn, send.at[k], recv.at[k], where)
            start_all(sends)
            turning.append(sends)
        return turning

    def latter_swaps(latters, send, recv, partner):
        return [
            remote(latter.at[0:tokens], latter.at[tokens : 2 * tokens], send.at[k], recv.at[k], partner)
            for k, latter in enumerate(latters)
        ]

    def first_sums(count):
        return [((first_blocks, half_share, size), HALF) for size in count]

    def transposed(array_ref, given_ref):
        start = pl.multiple_of(lax.axis_index("section") * half_model, 128)
        own = array_ref[:, pl.ds(start, half_model)]
        both = jnp.concatenate([own, given_ref[...]], 0)
        return both.astype(FLOAT).T.astype(HALF)

    def half_swaps(arrays, targets, send, recv, where):
        s, q, h = where
        copies = []
        for k, (array_ref, target) in enumerate(zip(arrays, targets)):
            start = pl.multiple_of((1 - s) * half_model, 128)
            copies.append(remote(array_ref.at[:, pl.ds(start, half_model)], target, send.at[k], recv.at[k], (1 - s, q, h)))
        return copies

    def latter_swap(latter, kind, start, count, send, recv, where):
        s, q, h = where
        return remote(
            latter.at[kind, 0:tokens, start : start + count],
            latter.at[kind, tokens : 2 * tokens, start : start + count],
            send,
            recv,
            (1 - s, q, h),
        )

    def gradient_tiles(former, latter, stage, partial_hbm, first_in, local_sems, send, recv, where, kinds):
        def split(t):
            kind = lax.div(t, tiles)
            at = lax.rem(t, tiles)
            return kind, pl.ds(pl.multiple_of(at * tile_width, tile_width), tile_width)

        def stored(t, dest):
            kind, columns = split(t)
            return pltpu.make_async_copy(
                stage.at[kind, dest, :, columns], partial_hbm.at[kind, dest, :, columns], local_sems.at[t, dest]
            )

        def sent(t):
            kind, columns = split(t)
            return first_stage(
                lambda dest, side: stage.at[kind, dest, half_rows(side), columns],
                lambda i: first_in.at[kind, i, :, columns],
                send.at[t],
                recv.at[t],
                where,
            )

        def tile(t):
            kind, columns = split(t)
            use = jnp.where(kind == 0, 0, 1)
            result = product(former[use], latter[kind, :, columns]).astype(HALF)
            stage[kind, :, :, columns] = result.reshape(seqs, share, tile_width)

            @pl.when(t < kinds * tiles)
            def _():
                start_all(sent(t))

            for dest in range(seqs):
                stored(t, dest).start()

        def finish():
            def stored_all(t):
                for dest in range(seqs):
                    stored(t, dest).wait()

            loop(3 * tiles, stored_all)
            loop(kinds * tiles, lambda t: wait_all(sent(t)))

        return tile, finish

    ffn_scratch = weight_scratch + [
        pltpu.VMEM((tokens, width), FLOAT),
        pltpu.VMEM((2, tokens, half_model), HALF),
        pltpu.VMEM((2, half_model, 2 * tokens), HALF),
        pltpu.VMEM((3, 2 * tokens, padded_units), HALF),
        pltpu.VMEM((3, seqs, share, padded_units), HALF),
        dma(2),
        dma(2),
        pltpu.SemaphoreType.DMA((3, len(slabs))),
        pltpu.SemaphoreType.DMA((3, len(slabs))),
        pltpu.SemaphoreType.DMA((3 * tiles, seqs)),
        pltpu.SemaphoreType.DMA((3 * tiles, first_blocks)),
        pltpu.SemaphoreType.DMA((3 * tiles, first_blocks)),
    ]
    def partial_outs(kinds):
        return [((3, seqs, share, padded_units), HALF, ANY), first_shape(kinds)]


    def slot_peer(me, j, h):
        other = lax.rem(me + j, slots)
        return (lax.rem(other, sections), lax.div(other, sections), h)

    def query_rows(ref, m, c):
        block = ref[m * rows : (m + 1) * rows, :]
        base = c * group * head_width
        return jnp.concatenate(
            [block[:, base + r * head_width : base + (r + 1) * head_width] for r in range(group)], 0
        )

    def keys_of(all_ref, at, c, kind):
        block = all_ref[:, at * rows : (at + 1) * rows, :].reshape(block_tok, pair_width)
        base = kind * kv_local * head_width + c * head_width
        return block[:, base : base + head_width]

    def allowed_pairs(segq_ref, seg_ref, m, at, s, q):
        own_segments = segq_ref[m * rows : (m + 1) * rows, :]
        allowed = own_segments == seg_ref[at : at + 1, :].astype(FLOAT)
        if at == m:
            base = q * local_rows + s * rows
            order = base + lax.broadcasted_iota(jnp.int32, (rows, block_tok), 0)
            allowed = allowed & (lax.broadcasted_iota(jnp.int32, (rows, block_tok), 1) <= order)
        bias = jnp.where(allowed, 0.0, -1e30)
        return jnp.concatenate([bias] * group, 0)

    def probabilities(rows_in, keys, biases):
        scores = [
            jnp.where(bias < 0, -1e30, back_product(rows_in, key) * score_scale)
            for key, bias in zip(keys, biases)
        ]
        summit = functools.reduce(jnp.maximum, [jnp.max(part, -1, keepdims=True) for part in scores])
        raised = [jnp.exp(part - summit) for part in scores]
        total = functools.reduce(jnp.add, [jnp.sum(part, -1, keepdims=True) for part in raised])
        inverse = 1.0 / total
        return [part * inverse for part in raised]

    def gather_pairs(all_ref, me, where, send, recv, near_send, near_recv):
        s, q, h = where
        partner = (1 - s, q, h)
        far = []
        for k, peer in enumerate(seq_peers(where, seqs)):
            copy = remote(all_ref.at[me], all_ref.at[me], send.at[k], recv.at[k], peer)
            copy.start()
            far.append(copy)
        near = [remote(all_ref.at[me], all_ref.at[me], near_send.at[0], near_recv.at[0], partner)]
        near[0].start()

        def pass_on():
            for k in range(1, seqs):
                far[k - 1].wait()
                slot = lax.rem(q + seqs - k, seqs) * sections + s
                copy = remote(all_ref.at[slot], all_ref.at[slot], near_send.at[k], near_recv.at[k], partner)
                copy.start()
                near.append(copy)
            wait_all(near)

        return pass_on

    def attention_forward(
        n3_ref, wq_ref, wp_ref, cos_ref, sin_ref, qk_ref, segq_ref, seg_ref, wo_ref, m_ref, gain_ref,
        qr_ref, r_ref, q_ref, all_ref, o_ref, h2_ref, n4_ref,
        send, recv, near_send, near_recv, part, inbox, rs, rr, gs, gr, travel,
    ):
        where = place()
        s, q, h = where
        me = q * sections + s
        travel.ready(wp_ref, cos_ref, sin_ref)
        cos, sin = cos_ref[...], sin_ref[...]
        r_ref[...] = product(n3_ref[...], wp_ref[...])
        half_pair = pair_width // 2
        for start, size in chunks_of(half_pair):
            span = slice(start, start + size)
            all_ref[me, :, span] = rotary(r_ref[:, span], twice(qk_ref[1:2, :]), cos, sin).astype(HALF)
        all_ref[me, :, half_pair:] = r_ref[:, half_pair:].astype(HALF)
        pass_on = gather_pairs(all_ref, me, where, send, recv, near_send, near_recv)
        travel.ready(wq_ref)
        qr_ref[...] = product(n3_ref[...], wq_ref[...])
        for start, size in chunks_of(query_width):
            span = slice(start, start + size)
            q_ref[:, span] = rotary(qr_ref[:, span], twice(qk_ref[0:1, :]), cos, sin).astype(HALF)
        travel.leave(r_ref, qr_ref, q_ref)
        pass_on()
        travel.leave(all_ref)
        for m in range(micro):
            biases = [allowed_pairs(segq_ref, seg_ref, m, at, s, q) for at in range(m + 1)]
            results = []
            for c in range(kv_local):
                keys = [keys_of(all_ref, at, c, 0) for at in range(m + 1)]
                weights = probabilities(query_rows(q_ref, m, c), keys, biases)
                total = functools.reduce(
                    jnp.add,
                    [product(weights[at].astype(HALF), keys_of(all_ref, at, c, 1)) for at in range(m + 1)],
                )
                results += [total[r * rows : (r + 1) * rows] for r in range(group)]
            o_ref[m * rows : (m + 1) * rows, :] = jnp.concatenate(results, -1).astype(HALF)
        travel.leave(o_ref)
        travel.ready(wo_ref)
        part[...] = product(o_ref[...], wo_ref[...]).astype(HALF)

        def finish(flow, i, total):
            hidden = m_ref[kept_rows(i), :] + total
            h2_ref[kept_rows(i), :] = hidden
            return norm_apply(hidden, gain_ref[1:2, :]).astype(HALF)

        head_total(part, n4_ref, inbox, rs, rr, gs, gr, where, heads, finish)

    def forward(
        in_ref, gain_ref, win_ref, kernel_ref, wout_ref, attn_gain_ref, up_hbm, down_hbm, seg_ref,
        wq_ref, wp_ref, cos_ref, sin_ref, qk_ref, wo_ref,
        x_ref, g_ref, n1_ref, pc_ref, edge_ref, y_ref, h1_ref, n2_ref, f1_ref, a1_ref, m_ref, n3_ref, same_ref, segq_ref,
        qr_ref, r_ref, q_ref, all_ref, o_ref, h2_ref, n4_ref, *rest,
    ):
        travel, rest = rest[-1], rest[:-1]
        split = len(conv_scratch)
        conv_forward(
            in_ref, gain_ref, win_ref, kernel_ref, wout_ref, attn_gain_ref, up_hbm, down_hbm, seg_ref,
            x_ref, g_ref, n1_ref, pc_ref, edge_ref, y_ref, h1_ref, n2_ref, f1_ref, a1_ref, m_ref, n3_ref,
            same_ref, segq_ref, *rest[:split], travel,
        )
        part = rest[part_at]
        attention_forward(
            n3_ref, wq_ref, wp_ref, cos_ref, sin_ref, qk_ref, segq_ref, seg_ref, wo_ref, m_ref, attn_gain_ref,
            qr_ref, r_ref, q_ref, all_ref, o_ref, h2_ref, n4_ref, *rest[split : split + 4], part, *rest[split + 4 :], travel,
        )

    conv_scratch = (
            [
                pltpu.VMEM((micro, rows, width), HALF),
                pltpu.VMEM((2, micro, 16, width), HALF),
                pltpu.VMEM((micro * 16, width), HALF),
                pltpu.VMEM((micro, 8 + rows, channels), FLOAT),
                dma(1),
                dma(1),
                dma(2),
                dma(2),
            ]
            + weight_scratch
            + [pltpu.VMEM((tokens, width), FLOAT)]
            + part_scratch
            + total_scratch
            + total_scratch
    )
    part_at = len(conv_scratch) - 2 * len(total_scratch) - 1
    (
        x, g, n1, projected, edge_gated, mixed, h1, n2, f1, a1, middle, n3, same, local_segments,
        query_raw, pair_raw, queries, all_pairs, attended, h2, n4,
    ) = call(
        forward,
        "forward",
        0,
        [
            ((tokens, width), HALF, LATE),
            ((tokens, width), HALF, LATE),
            ((tokens, width), HALF, LATE),
            ((3, tokens, channels), FLOAT, LATE),
            ((micro, 8, channels), FLOAT, LATE),
            ((tokens, channels), HALF, LATE),
            ((half_tokens, width), FLOAT, LATE),
            ((tokens, width), HALF, LATE),
            ((2, tokens, hidden_units), FLOAT, LATE),
            ((tokens, hidden_units), HALF, LATE),
            ((half_tokens, width), FLOAT, LATE),
            ((tokens, width), HALF, LATE),
            ((tokens, 2), FLOAT, LATE),
            ((tokens, 1), FLOAT, LATE),
            ((tokens, query_width), FLOAT, LATE),
            ((tokens, pair_width), FLOAT, LATE),
            ((tokens, query_width), HALF, LATE),
            ((slots, tokens, pair_width), HALF, LATE),
            ((tokens, query_width), HALF, LATE),
            ((half_tokens, width), FLOAT),
            ((tokens, width), HALF),
        ],
        conv_scratch + [dma(seqs - 1), dma(seqs - 1), dma(seqs), dma(seqs)] + total_scratch,
        [
            incoming, conv_gains, (w_in, LAZY), conv_kernel, (conv_out, LAZY), attn_gains,
            (first_up, ANY), (conv_down, ANY), segment_ids,
            (w_query, LAZY), (w_pair, LAZY), (cosine, LAZY), (sine, LAZY), qk_gains, (attn_out, LAZY),
        ],
        flops=9 * 10**9,
        moved=350 << 20,
    )

    def slab_width(start, count):
        return min(-(-count // tile_width) * tile_width, padded_units - start)

    def clear_padding(latter):
        if padded_units > hidden_units:
            latter[:, :, hidden_units:] = jnp.zeros((3, 2 * tokens, padded_units - hidden_units), HALF)

    def second_ffn(
        n4_ref, g_ref, h2_ref, gain_ref, up_hbm, down_hbm,
        py_ref, gh2_ref, low_ref, gg_ref, partial_hbm, first_in,
        acc_y, up_ref, down_ref, weight_sems, acc, given, former, latter, stage, hs, hr, ls, lr, local_sems, ts, tr,
        part, inbox, rs, rr, gs, gr, travel,
    ):
        where = place()
        s, q, h = where
        weights = weight_loads(up_hbm, down_hbm, up_ref, down_ref, weight_sems)
        start_all(weights)
        clear_padding(latter)
        greet([(1 - s, q, h)] + seq_peers(where, seqs), where, heads)
        halves = half_swaps([g_ref, n4_ref], [given.at[0], given.at[1]], hs, hr, where)
        start_all(halves)
        gg_ref[...] = jnp.zeros_like(gg_ref)
        swaps = []
        for j, (start, count) in enumerate(slabs):
            wait_all(weights[3 * j : 3 * j + 3])
            span = slice(start, start + count)
            gate = back_product(n4_ref[...], up_ref[0, span, :])
            rise = back_product(n4_ref[...], up_ref[1, span, :])
            grad_active = back_product(g_ref[...], down_ref[span, :])
            chance = 1.0 / (1.0 + jnp.exp(-gate))
            silu = gate * chance
            active = (silu * rise).astype(HALF)
            grad_gate = (grad_active * rise * (chance * (1.0 + gate * (1.0 - chance)))).astype(HALF)
            grad_rise = (grad_active * silu).astype(HALF)
            latter[0, 0:tokens, span] = active
            latter[1, 0:tokens, span] = grad_gate
            latter[2, 0:tokens, span] = grad_rise
            for kind in range(3):
                swap = latter_swap(
                    latter, kind, start, slab_width(start, count), ls.at[kind, j], lr.at[kind, j], where
                )
                swap.start()
                swaps.append(swap)
            term = product(grad_gate, up_ref[0, span, :]) + product(grad_rise, up_ref[1, span, :])
            term_y = product(active, down_ref[span, :])
            if j == 0:
                acc[...] = term
                acc_y[...] = term_y
            else:
                acc[...] += term
                acc_y[...] += term_y
        part[...] = acc[...].astype(HALF)

        travel.ready(h2_ref)
        for flow, holder in ((0, 0), (1, heads - 1)):

            @pl.when(h == holder)
            def _(flow=flow):
                acc_y[flow * half_tokens : (flow + 1) * half_tokens, :] += h2_ref[...]

        py_ref[...] = acc_y[...].astype(HALF)
        travel.leave(py_ref)
        tile, tiles_done = gradient_tiles(
            former, latter, stage, partial_hbm, first_in, local_sems, ts, tr, where, 2
        )

        def filler(t):
            for k, array_ref in enumerate((g_ref, n4_ref)):

                @pl.when(t == k)
                def _(k=k, array_ref=array_ref):
                    halves[k].wait()
                    if k:
                        wait_all(swaps)
                    former[k] = transposed(array_ref, given.at[k])

            @pl.when(t >= 2)
            def _():
                tile(t - 2)

        def finish(flow, i, total):
            grad_hidden, grad_gain = norm_back(h2_ref[kept_rows(i), :], gain_ref[1:2, :], total)
            grad = g_ref[own_rows(flow, i), :].astype(FLOAT) + grad_hidden
            gh2_ref[kept_rows(i), :] = grad
            gg_ref[...] += grad_gain
            return grad.astype(HALF)

        head_total(part, low_ref, inbox, rs, rr, gs, gr, where, heads, finish, filler, 3 * tiles + 2)
        tiles_done()

    (part_y, gh2, gh2_low, grad_gain_attn1, partial2, first2) = call(
        second_ffn,
        "second_ffn",
        4,
        [
            ((tokens, width), HALF, LATE),
            ((half_tokens, width), FLOAT),
            ((tokens, width), HALF),
            ((1, width), FLOAT),
        ]
        + partial_outs(2),
        [pltpu.VMEM((tokens, width), FLOAT)] + ffn_scratch + part_scratch + total_scratch,
        [n4, g, (h2, LAZY), attn_gains, (second_up, ANY), (attn_down, ANY)],
        flops=12 * 10**9,
        moved=150 << 20,
    )
    def attention_backward(
        glow_ref, wo_ref, q_ref, all_ref, segq_ref, seg_ref,
        qr_ref, r_ref, cos_ref, sin_ref, qk_ref, wq_ref, wp_ref, m_ref, gh2_ref, gain_ref, py_ref, n3_ref, o_ref, partial2_hbm, first2_hbm,
        low_ref, gg_ref, gqk_ref, yown_ref, stage0, stage1, in0, in1, second_in, first_in,
        bq_ref, br_ref, grads, totals, gq_ref, gp_ref, near_slots, pair_slots, ns, nr, ps, pr,
        passing, held, load_sems, vs, vr, fs, fr,
        ybox, ys, yr, given, former, latter0, latter1, hs, hr, ls, lr, ms, mr,
        part, inbox, rs, rr, gs, gr, travel,
    ):
        where = place()
        s, q, h = where
        partner = (1 - s, q, h)
        peers = seq_peers(where, seqs)
        loads = pass_loads(partial2_hbm, (0, 1), first2_hbm, passing, held, load_sems, where)
        loads += load_passing(partial2_hbm.at[2], passing.at[2], load_sems.at[2], where)
        start_all(loads)
        others = head_others(where)
        latters = [latter0, latter1]
        greet([partner] + peers + others, where, heads)
        later = first_stage(
            lambda dest, side: partial2_hbm.at[2, dest, half_rows(side)], lambda i: first_in.at[0, i], fs, fr, where
        )
        start_all(later)
        travel.ready(py_ref, n3_ref, o_ref)
        latter0[0:tokens, :] = o_ref[...]
        ysends = [
            remote(py_ref.at[rows_of(peer[2], small_rows)], ybox.at[n], ys.at[n], yr.at[n], peer)
            for n, peer in enumerate(others)
        ]
        start_all(ysends)
        halves = half_swaps([glow_ref, n3_ref], [given.at[0], given.at[1]], hs, hr, where)
        start_all(halves)
        swaps = latter_swaps(latters, ls, lr, partner)
        swaps[0].start()
        gg_ref[...] = jnp.zeros_like(gg_ref)
        gqk_ref[...] = jnp.zeros_like(gqk_ref)
        grads[...] = back_product(glow_ref[...], wo_ref[...]).astype(HALF)
        for m in range(micro):
            biases = [allowed_pairs(segq_ref, seg_ref, m, at, s, q) for at in range(m + 1)]
            results = []
            for c in range(kv_local):
                keys = [keys_of(all_ref, at, c, 0) for at in range(m + 1)]
                values = [keys_of(all_ref, at, c, 1) for at in range(m + 1)]
                rows_in = query_rows(q_ref, m, c)
                grad_rows = query_rows(grads, m, c)
                chances = probabilities(rows_in, keys, biases)
                grad_chances = [back_product(grad_rows, value) for value in values]
                inner = functools.reduce(
                    jnp.add,
                    [jnp.sum(a * b, -1, keepdims=True) for a, b in zip(grad_chances, chances)],
                )
                total = None
                for at in range(m + 1):
                    grad_scores = (chances[at] * (grad_chances[at] - inner)).astype(HALF)
                    term = product(grad_scores, keys[at])
                    total = term if total is None else total + term
                    grad_key = outer_sum(grad_scores, rows_in) * score_scale
                    grad_value = outer_sum(chances[at].astype(HALF), grad_rows)
                    if at == m:
                        totals[at, c] = grad_key
                        totals[at, kv_local + c] = grad_value
                    else:
                        totals[at, c] += grad_key
                        totals[at, kv_local + c] += grad_value
                total = total * score_scale
                results += [total[r * rows : (r + 1) * rows] for r in range(group)]
            gq_ref[m * rows : (m + 1) * rows, :] = jnp.concatenate(results, -1)
        for at in range(micro):
            joined = jnp.concatenate([totals[at, k] for k in range(2 * kv_local)], -1).astype(HALF)
            gp_ref[:, at * rows : (at + 1) * rows, :] = joined.reshape(slots, rows, pair_width)
        near = []
        for other in range(seqs):
            copy = remote(gp_ref.at[other * sections + 1 - s], near_slots.at[other], ns.at[other], nr.at[other], partner)
            copy.start()
            near.append(copy)
        copies = []
        wait_all(near)
        travel.ready(qr_ref, r_ref, cos_ref, sin_ref, wq_ref, wp_ref, m_ref, gh2_ref)
        for other in range(seqs):
            mine = gp_ref[other * sections + s].astype(FLOAT)
            near_slots[other] = (mine + near_slots[other].astype(FLOAT)).astype(HALF)
        for k, peer in enumerate(peers):
            copy = remote(near_slots.at[peer[1]], pair_slots.at[k], ps.at[k], pr.at[k], peer)
            copy.start()
            copies.append(copy)
        cos, sin = cos_ref[...], sin_ref[...]
        for start, size in chunks_of(query_width):
            span = slice(start, start + size)
            grad_raw, grad_gain = rotary_back(qr_ref[:, span], twice(qk_ref[0:1, :]), cos, sin, gq_ref[:, span])
            bq_ref[:, span] = grad_raw.astype(HALF)
            gqk_ref[0:1, :size] += grad_gain
        partial = back_product(bq_ref[...], wq_ref[...])
        wait_all(loads)
        travelling = pass_sends(2, passing, held, second_in, vs, vr, where)
        wait_all(copies)
        grad_pair = near_slots[q].astype(FLOAT)
        for j in range(seqs - 1):
            grad_pair = grad_pair + pair_slots[j].astype(FLOAT)
        half_pair = pair_width // 2
        for start, size in chunks_of(half_pair):
            span = slice(start, start + size)
            grad_raw, grad_gain = rotary_back(r_ref[:, span], twice(qk_ref[1:2, :]), cos, sin, grad_pair[:, span])
            br_ref[:, span] = grad_raw.astype(HALF)
            gqk_ref[1:2, :size] += grad_gain
        br_ref[:, half_pair:] = grad_pair[:, half_pair:].astype(HALF)
        wait_all(later)
        combine(lambda i: passing.at[2, i], first_in.at[0], where)
        turning = second_stage(lambda i: passing.at[2, i], second_in.at[2], vs.at[2], vr.at[2], where)
        start_all(turning)
        travelling += turning
        travel.leave(first_in)
        latter1[0:tokens, 0:query_width] = bq_ref[...]
        latter1[0:tokens, query_width:] = br_ref[...]
        swaps[1].start()
        part[...] = (partial + back_product(br_ref[...], wp_ref[...])).astype(HALF)
        wait_all(ysends)
        produced = py_ref[rows_of(h, small_rows), :].astype(FLOAT)
        for n in range(heads - 1):
            produced = produced + ybox[n].astype(FLOAT)
        yown_ref[...] = produced.astype(HALF)
        sends = mixer_sends([stage0, stage1], [in0, in1], ms, mr, where)
        mixer_step = mixer_steps([glow_ref, n3_ref], latters, [stage0, stage1], given, former, halves, swaps, sends)

        def finish(flow, i, total):
            grad_entry, grad_gain = norm_back(m_ref[kept_rows(i), :], gain_ref[0:1, :], total)
            gg_ref[...] += grad_gain
            return (gh2_ref[kept_rows(i), :] + grad_entry).astype(HALF)

        head_total(part, low_ref, inbox, rs, rr, gs, gr, where, heads, finish, mixer_step, 4)
        for copies in sends:
            wait_all(copies)
        wait_all(travelling)

    (gm_low, grad_gain_attn0, grad_qk, y_own, stage0, stage1, in0, in1, second2, first2_last) = call(
        attention_backward,
        "attention_backward",
        5,
        [
            ((tokens, width), HALF),
            ((1, width), FLOAT),
            ((8, 128), FLOAT),
            ((small_rows, width), HALF),
            ((seqs, share, widths[0]), HALF),
            ((seqs, share, widths[1]), HALF),
            *first_sums(widths[:2]),
            second_shape(3),
            ((1, first_blocks, half_share, padded_units), HALF, LATE),
        ],
        [
            pltpu.VMEM((tokens, query_width), HALF),
            pltpu.VMEM((tokens, pair_width), HALF),
            pltpu.VMEM((tokens, query_width), HALF),
            pltpu.VMEM((micro, 2 * kv_local, block_tok, head_width), FLOAT),
            pltpu.VMEM((tokens, query_width), FLOAT),
            pltpu.VMEM((slots, tokens, pair_width), HALF),
            pltpu.VMEM((seqs, tokens, pair_width), HALF),
            pltpu.VMEM((seqs - 1, tokens, pair_width), HALF),
            dma(seqs),
            dma(seqs),
            dma(seqs - 1),
            dma(seqs - 1),
        ]
        + passing_scratch(3)
        + [dma(first_blocks), dma(first_blocks)]
        + [
            pltpu.VMEM((heads - 1, small_rows, width), HALF),
            dma(heads - 1),
            dma(heads - 1),
            pltpu.VMEM((2, tokens, half_model), HALF),
            pltpu.VMEM((half_model, 2 * tokens), HALF),
            pltpu.VMEM((2 * tokens, widths[0]), HALF),
            pltpu.VMEM((2 * tokens, widths[1]), HALF),
            dma(2),
            dma(2),
            dma(2),
            dma(2),
            dma_grid(2, first_blocks),
            dma_grid(2, first_blocks),
        ]
        + part_scratch
        + total_scratch,
        [
            gh2_low, attn_out, queries, all_pairs, local_segments, segment_ids,
            (query_raw, LAZY), (pair_raw, LAZY), (cosine, LAZY), (sine, LAZY), qk_gains,
            (w_query, LAZY), (w_pair, LAZY), (middle, LAZY), (gh2, LAZY), attn_gains,
            (part_y, LAZY), (n3, LAZY), (attended, LAZY), (partial2, ANY), (first2, ANY),
        ],
        flops=6 * 10**9,
        moved=130 << 20,
    )

    def first_ffn_back(
        gm_ref, n2_ref, f1_ref, a1_ref, h1_ref, gain_ref, yown_ref, stage0, stage1, in0, in1, up_hbm, down_hbm,
        gh1_ref, low_ref, gg_ref, yout_ref, turn0, turn1, partial_hbm, first_in,
        up_ref, down_ref, weight_sems, acc, given, former, latter, stage, hs, hr, ls, lr, local_sems, ts, tr,
        ys, yr, pass0, pass1, us, ur,
        part, inbox, rs, rr, gs, gr, travel,
    ):
        where = place()
        s, q, h = where
        weights = weight_loads(up_hbm, down_hbm, up_ref, down_ref, weight_sems)
        start_all(weights)
        clear_padding(latter)
        others = head_others(where)
        own_y = rows_of(h, small_rows)
        greet([(1 - s, q, h)] + seq_peers(where, seqs) + others, where, heads)
        travel.ready(yown_ref, n2_ref, a1_ref)
        yout_ref[own_y, :] = yown_ref[...]
        ysends = [
            remote(yout_ref.at[own_y], yout_ref.at[own_y], ys.at[n], yr.at[n], peer) for n, peer in enumerate(others)
        ]
        start_all(ysends)
        halves = half_swaps([gm_ref, n2_ref], [given.at[0], given.at[1]], hs, hr, where)
        start_all(halves)
        gg_ref[...] = jnp.zeros_like(gg_ref)
        latter[0, 0:tokens, 0:hidden_units] = a1_ref[...]
        travel.ready(stage0, stage1, in0, in1)
        turning = mixer_second([stage0, stage1], [in0, in1], [pass0, pass1], [turn0, turn1], us, ur, where)
        tile, tiles_done = gradient_tiles(
            former, latter, stage, partial_hbm, first_in, local_sems, ts, tr, where, 3
        )
        active_swaps = [
            latter_swap(latter, 0, start, slab_width(start, count), ls.at[0, j], lr.at[0, j], where)
            for j, (start, count) in enumerate(slabs)
        ]
        start_all(active_swaps)
        swaps = []
        travel.ready(f1_ref, h1_ref)
        for j, (start, count) in enumerate(slabs):
            wait_all(weights[3 * j : 3 * j + 3])
            span = slice(start, start + count)
            gate = f1_ref[0, :, span]
            rise = f1_ref[1, :, span]
            grad_active = back_product(gm_ref[...], down_ref[span, :])
            chance = 1.0 / (1.0 + jnp.exp(-gate))
            grad_gate = (grad_active * rise * (chance * (1.0 + gate * (1.0 - chance)))).astype(HALF)
            grad_rise = (grad_active * (gate * chance)).astype(HALF)
            latter[1, 0:tokens, span] = grad_gate
            latter[2, 0:tokens, span] = grad_rise
            for kind in range(1, 3):
                swap = latter_swap(
                    latter, kind, start, slab_width(start, count), ls.at[kind, j], lr.at[kind, j], where
                )
                swap.start()
                swaps.append(swap)
            term = product(grad_gate, up_ref[0, span, :]) + product(grad_rise, up_ref[1, span, :])
            if j == 0:
                acc[...] = term
                halves[0].wait()
                wait_all(active_swaps)
                former[0] = transposed(gm_ref, given.at[0])
                loop(tiles, tile)
            else:
                acc[...] += term
        part[...] = acc[...].astype(HALF)
        def filler(t):
            @pl.when(t == 0)
            def _():
                halves[1].wait()
                wait_all(swaps)
                former[1] = transposed(n2_ref, given.at[1])

            @pl.when(t >= 1)
            def _():
                tile(tiles + t - 1)

        def finish(flow, i, total):
            grad_hidden, grad_gain = norm_back(h1_ref[kept_rows(i), :], gain_ref[1:2, :], total)
            gg_ref[...] += grad_gain
            grad = gm_ref[own_rows(flow, i), :].astype(FLOAT) + grad_hidden
            gh1_ref[kept_rows(i), :] = grad
            return grad.astype(HALF)

        head_total(part, low_ref, inbox, rs, rr, gs, gr, where, heads, finish, filler, 2 * tiles + 1)
        tiles_done()
        wait_all(ysends)
        for copies in turning:
            wait_all(copies)

    (gh1, gh1_low, grad_gain_conv1, yout, turn0, turn1, partial1, first1) = call(
        first_ffn_back,
        "first_ffn_back",
        6,
        [((half_tokens, width), FLOAT), ((tokens, width), HALF), ((1, width), FLOAT), ((tokens, width), HALF)]
        + [((grid_rows, half_share, size), HALF) for size in widths[:2]]
        + partial_outs(3),
        ffn_scratch + [dma(heads - 1), dma(heads - 1)]
        + [pltpu.VMEM((grid_rows, half_share, size), HALF) for size in widths[:2]]
        + [dma_grid(2, grid_rows), dma_grid(2, grid_rows)]
        + part_scratch + total_scratch,
        [gm_low, (n2, LAZY), (f1, LAZY), (a1, LAZY), (h1, LAZY), conv_gains, (y_own, LAZY),
         (stage0, LAZY), (stage1, LAZY), (in0, LAZY), (in1, LAZY), (first_up, ANY), (conv_down, ANY)],
        flops=9 * 10**9,
        moved=150 << 20,
    )
    small_width = max(share, channels, 2 * head_width)

    def conv_backward(
        low_ref, gh1_ref, pc_ref, edge_ref, same_ref, kernel_ref, wout_ref, win_ref, x_ref, gain_ref, yout_ref,
        n1_ref, mixed_ref, stage0, stage1, in0, in1, turn0, turn1, small_in,
        partial1, partial2, first1, first2, first2_last, second2,
        edges_ref, sums_ref, gout2_ref, gmix_ref, gout1_ref, gin_ref, gdown2, gup2, gdown1, gup1,
        bp_ref, ext, spread, gz_ext, outgoing, arrived, full, gg_ref, edge_send, edge_recv, swap_send, swap_recv,
        given, former, latter2, latter3, stage2, stage3, in2, in3, turn2, turn3, hs, hr, ls, lr, ms, mr, us, ur,
        own_buf, first_buf, second_buf, passing, item_sems, vs, vr, down_stage, up_stage, out_sems,
        packed, boxes, summed, final, zs, zr, ss, sr,
        part, inbox, rs, rr, gs, gr, travel,
    ):
        where = place()
        s, q, h = where
        first = s == 0
        partner = (1 - s, q, h)
        preceding = (1 - s, jnp.where(first, lax.rem(q + seqs - 1, seqs), q), h)
        following = (1 - s, jnp.where(first, q, lax.rem(q + 1, seqs)), h)
        others = head_others(where)
        me = q * sections + s
        slot_peers = [slot_peer(me, j, h) for j in range(1, slots)]
        peers = seq_peers(where, seqs)
        latters, stages = [latter2, latter3], [stage0, stage1, stage2, stage3]
        incomes, turns = [in0, in1, in2, in3], [turn0, turn1, turn2, turn3]
        loads = []
        sources = [
            (partial2.at[0], first2.at[0], second2.at[0]),
            (partial2.at[1], first2.at[1], second2.at[1]),
            (partial2.at[2], first2_last.at[0], second2.at[2]),
            (partial1.at[0], first1.at[0], None),
            (partial1.at[1], first1.at[1], None),
            (partial1.at[2], first1.at[2], None),
        ]
        for n, (partial, arrived_hbm, passed_hbm) in enumerate(sources):
            copies = [pltpu.make_async_copy(partial.at[q], own_buf.at[n], item_sems.at[n, 0])]
            if arrived_hbm is not None:
                copies.append(pltpu.make_async_copy(arrived_hbm, first_buf.at[n], item_sems.at[n, 1]))
            if passed_hbm is not None:
                copies.append(pltpu.make_async_copy(passed_hbm, second_buf.at[n], item_sems.at[n, 2]))
            else:
                copies += load_passing(partial, passing.at[n - 3], item_sems.at[n, pl.ds(3, grid_rows)], where)
            loads.append(copies)
        for copies in loads[3:] + loads[:3]:
            start_all(copies)
        greet([partner, preceding, following] + others + slot_peers, where, heads)
        travel.ready(n1_ref, mixed_ref)
        latter2[0:tokens, :] = mixed_ref[...]
        halves = half_swaps([low_ref, n1_ref], [given.at[0], given.at[1]], hs, hr, where)
        start_all(halves)
        swaps = latter_swaps(latters, ls, lr, partner)
        swaps[0].start()
        gg_ref[...] = jnp.zeros_like(gg_ref)
        gated = pc_ref[0] * pc_ref[2]
        grad_y = back_product(low_ref[...], wout_ref[...])
        gz = grad_y * pc_ref[1]
        zero = jnp.zeros((8, channels), FLOAT)
        for m in range(micro):
            span = slice(m * rows, (m + 1) * rows)
            one = jnp.where(same_ref[span, 0:1] > 0, gz[span], 0.0) * kernel_ref[1:2, :]
            two = jnp.where(same_ref[span, 1:2] > 0, gz[span], 0.0) * kernel_ref[0:1, :]
            gz_ext[0, m, 0:rows, :] = one
            gz_ext[0, m, rows : rows + 8, :] = zero
            gz_ext[1, m, 0:rows, :] = two
            gz_ext[1, m, rows : rows + 8, :] = zero
            outgoing[m] = zero
            outgoing[m, 0:1, :] = two[0:1]
            outgoing[m, 1:2, :] = one[0:1] + two[1:2]
        edge = remote(outgoing, arrived, edge_send.at[0], edge_recv.at[0], preceding)
        edge.start()
        bulk = []
        for n in (3, 4, 5):
            wait_all(loads[n])
            combine(lambda i, n=n: passing.at[n - 3, i], first_buf.at[n], where)
            sends = second_stage(
                lambda i, n=n: passing.at[n - 3, i], second_buf.at[n], vs.at[n - 3], vr.at[n - 3], where
            )
            start_all(sends)
            bulk.append(sends)
        taps = [None, None, None]
        for m in range(micro):
            span = slice(m * rows, (m + 1) * rows)
            ext[m, 0:8, :] = edge_ref[m]
            ext[m, 8 : 8 + rows, :] = gated[span]
            back_one = jnp.where(same_ref[span, 0:1] > 0, shifted_rows(ext, m, 1), 0.0)
            back_two = jnp.where(same_ref[span, 1:2] > 0, shifted_rows(ext, m, 2), 0.0)
            mixed = (
                kernel_ref[2:3, :] * gated[span]
                + kernel_ref[1:2, :] * back_one
                + kernel_ref[0:1, :] * back_two
            )
            bp_ref[span, channels : 2 * channels] = (grad_y[span] * mixed).astype(HALF)
            for k, value in enumerate((back_two, back_one, gated[span])):
                term = jnp.sum(value * gz[span], 0, keepdims=True)
                taps[k] = term if taps[k] is None else taps[k] + term
        for m in range(micro):
            span = slice(m * rows, (m + 1) * rows)
            spread[m] = (
                kernel_ref[2:3, :] * gz[span]
                + gz_ext[0, m, 1 : rows + 1, :]
                + gz_ext[1, m, 2 : rows + 2, :]
            )
        edge.wait()
        wrap = (s == sections - 1) & (q == seqs - 1)
        for m in range(micro):
            follow = arrived[m + 1, 0:2, :] if m + 1 < micro else jnp.zeros((2, channels), FLOAT)
            spread[m, rows - 2 : rows, :] += jnp.where(wrap, follow, arrived[m, 0:2, :])
        for m in range(micro):
            span = slice(m * rows, (m + 1) * rows)
            bp_ref[span, 0:channels] = (spread[m] * pc_ref[2, span, :]).astype(HALF)
            bp_ref[span, 2 * channels :] = (spread[m] * pc_ref[0, span, :]).astype(HALF)
        latter3[0:tokens, :] = bp_ref[...]
        swaps[1].start()
        travel.ready(win_ref, x_ref, gh1_ref, yout_ref, small_in)
        total = back_product(bp_ref[:, 0:channels], win_ref[0])
        total = total + back_product(bp_ref[:, channels : 2 * channels], win_ref[1])
        total = total + back_product(bp_ref[:, 2 * channels :], win_ref[2])
        part[...] = total.astype(HALF)

        def finish(flow, i, total):
            start = x_ref[own_rows(flow, i), :].astype(FLOAT)
            grad_start, grad_gain = norm_back(start, gain_ref[0:1, :], total)
            gg_ref[...] += grad_gain
            return (gh1_ref[kept_rows(i), :] + grad_start).astype(HALF)

        sent = mixer_sends(stages[2:], incomes[2:], ms, mr, where)
        mixer_step = mixer_steps([low_ref, n1_ref], latters, stages[2:], given, former, halves, swaps, sent)
        head_total(part, full, inbox, rs, rr, gs, gr, where, heads, finish, mixer_step, 4)
        keep = pl.ds(pl.multiple_of(s * rows, rows), rows)
        edges_ref[0, :, keep, :] = jnp.where(first, full[...], yout_ref[...]).reshape(micro, rows, width)
        part[...] = jnp.where(first, yout_ref[...], full[...])
        edge_swaps = []
        for m in range(micro):
            copy = remote(
                part.at[m * rows : (m + 1) * rows], edges_ref.at[0, m, keep], swap_send.at[m], swap_recv.at[m], partner
            )
            copy.start()
            edge_swaps.append(copy)
        packed[...] = small_in[...]
        packed[:, 5:8, 0:channels] = jnp.broadcast_to(jnp.concatenate(taps, 0)[None], (slots, 3, channels))
        for d in range(slots):
            packed[d, 0:1, 0:share] = gg_ref[:, d * share : (d + 1) * share]
        over = []
        for k, peer in enumerate(others):
            copy = remote(packed, boxes.at[k], zs.at[k], zr.at[k], peer)
            copy.start()
            over.append(copy)
        wait_all(over)
        over_heads = boxes[0]
        for j in range(1, heads - 1):
            over_heads = over_heads + boxes[j]
        row = lax.broadcasted_iota(jnp.int32, over_heads.shape, 1)
        summed[...] = packed[...] + jnp.where(row < 5, over_heads, 0.0)
        across = []
        for j, peer in enumerate(slot_peers):
            copy = remote(summed.at[peer[0] * seqs + peer[1]], final.at[j], ss.at[j], sr.at[j], peer)
            copy.start()
            across.append(copy)
        outs = []

        def leave(source, target, at):
            copy = pltpu.make_async_copy(source, target, out_sems.at[at])
            copy.start()
            outs.append(copy)

        def fill_stage(n, target):
            upper, lower = two_halves(own_buf.at[n], first_buf.at[n], second_buf.at[n], where)
            target[half_rows(0), :] = upper[:, :hidden_units].astype(HALF)
            target[half_rows(1), :] = lower[:, :hidden_units].astype(HALF)

        def second_half_items():
            for n in range(3):
                wait_all(loads[n])
            fill_stage(0, down_stage.at[0])
            leave(down_stage.at[0], gdown2, 0)
            for kind in range(2):
                fill_stage(1 + kind, up_stage.at[0, kind])
            leave(up_stage.at[0], gup2, 1)

        for copies in sent:
            wait_all(copies)
        mixer_turns = mixer_second(stages[2:], incomes[2:], [None, None], turns[2:], us, ur, where)
        travel.ready(stage0, stage1, in0, in1, turn0, turn1)
        second_half_items()
        for n in (3, 4, 5):
            wait_all(bulk[n - 3])
            if n == 3:
                fill_stage(3, down_stage.at[1])
                leave(down_stage.at[1], gdown1, 2)
            else:
                fill_stage(n, up_stage.at[1, n - 4])
        leave(up_stage.at[1], gup1, 3)
        wait_all(edge_swaps)
        wait_all(across)
        total = summed[s * seqs + q]
        for j in range(slots - 1):
            total = total + final[j]
        sums_ref[...] = total
        for k, target in enumerate((gout2_ref, gmix_ref, gout1_ref, None)):
            if k >= 2:
                wait_all(mixer_turns[k - 2])
            for side, value in enumerate(two_halves(stages[k].at[q], incomes[k], turns[k], where)):
                value = value.astype(HALF)
                if target is None:
                    for c in range(3):
                        gin_ref[c, half_rows(side), :] = value[:, c * channels : (c + 1) * channels]
                else:
                    target[half_rows(side), :] = value
        wait_all(outs)

    folded = grad_qk[0:2, :head_width] + grad_qk[0:2, head_width : 2 * head_width]
    gain_rows = jnp.concatenate(
        [jnp.zeros_like(grad_gain_conv1), grad_gain_conv1, grad_gain_attn0, grad_gain_attn1], 0
    )

    def to_width(array):
        return jnp.pad(array, [(0, 0)] * (array.ndim - 1) + [(0, small_width - array.shape[-1])])

    small = jnp.concatenate(
        [
            to_width(gain_rows.reshape(4, slots, share).transpose(1, 0, 2)),
            jnp.broadcast_to(to_width(folded.reshape(1, 1, 2 * head_width)), (slots, 1, small_width)),
            jnp.zeros((slots, 3, small_width), FLOAT),
        ],
        1,
    )

    (section_edges, sums, gout2, gmix, gout1, gin, gdown2, gup2, gdown1, gup1) = call(
        conv_backward,
        "conv_backward",
        7,
        [
            ((1, micro, local_rows, width), HALF),
            ((8, small_width), FLOAT),
            ((share, widths[0]), HALF),
            ((share, widths[1]), HALF),
            ((share, widths[2]), HALF),
            ((3, share, channels), HALF),
            ((share, hidden_units), HALF, ANY),
            ((2, share, hidden_units), HALF, ANY),
            ((share, hidden_units), HALF, ANY),
            ((2, share, hidden_units), HALF, ANY),
        ],
        [
            pltpu.VMEM((tokens, 3 * channels), HALF),
            pltpu.VMEM((micro, 8 + rows, channels), FLOAT),
            pltpu.VMEM((micro, rows, channels), FLOAT),
            pltpu.VMEM((2, micro, rows + 8, channels), FLOAT),
            pltpu.VMEM((micro, 8, channels), FLOAT),
            pltpu.VMEM((micro, 8, channels), FLOAT),
            pltpu.VMEM((tokens, width), HALF),
            pltpu.VMEM((1, width), FLOAT),
            dma(1),
            dma(1),
            dma(micro),
            dma(micro),
            pltpu.VMEM((2, tokens, half_model), HALF),
            pltpu.VMEM((half_model, 2 * tokens), HALF),
        ]
        + [pltpu.VMEM((2 * tokens, size), HALF) for size in widths[2:]]
        + [pltpu.VMEM((seqs, share, size), HALF) for size in widths[2:]]
        + [pltpu.VMEM((first_blocks, half_share, size), HALF) for size in widths[2:]]
        + [pltpu.VMEM((grid_rows, half_share, size), HALF) for size in widths[2:]]
        + [
            dma(2),
            dma(2),
            dma(2),
            dma(2),
            dma_grid(2, first_blocks),
            dma_grid(2, first_blocks),
            dma_grid(2, grid_rows),
            dma_grid(2, grid_rows),
            pltpu.VMEM((6, share, padded_units), HALF),
            pltpu.VMEM((6, first_blocks, half_share, padded_units), HALF),
            pltpu.VMEM((6, grid_rows, half_share, padded_units), HALF),
            pltpu.VMEM((3, grid_rows, half_share, padded_units), HALF),
            dma_grid(6, 3 + grid_rows),
            dma_grid(3, grid_rows),
            dma_grid(3, grid_rows),
            pltpu.VMEM((2, share, hidden_units), HALF),
            pltpu.VMEM((2, 2, share, hidden_units), HALF),
            dma(4),
            pltpu.VMEM((slots, 8, small_width), FLOAT),
            pltpu.VMEM((heads - 1, slots, 8, small_width), FLOAT),
            pltpu.VMEM((slots, 8, small_width), FLOAT),
            pltpu.VMEM((slots - 1, 8, small_width), FLOAT),
            dma(heads - 1),
            dma(heads - 1),
            dma(slots - 1),
            dma(slots - 1),
        ]
        + part_scratch
        + total_scratch,
        [
            gh1_low, (gh1, LAZY), projected, edge_gated, same, conv_kernel, conv_out, (w_in, LAZY), (x, LAZY), conv_gains,
            (yout, LAZY), (n1, LAZY), (mixed, LAZY), (stage0, LAZY), (stage1, LAZY), (in0, LAZY), (in1, LAZY), (turn0, LAZY), (turn1, LAZY),
            (small, LAZY),
        ]
        + [(array, ANY) for array in (partial1, partial2, first1, first2, first2_last, second2)],
        flops=5 * 10**9,
        moved=300 << 20,
    )
    def results(
        edges_in, sums_in, gout2_in, gmix_in, gout1_in, gin_in, gdown2_in, gup2_in, gdown1_in, gup1_in,
        edges_out, cgain_out, gin_out, taps_out, gout1_out, gup1_out, gdown1_out,
        again_out, gq_out, gkv_out, gqk_out, gout2_out, gup2_out, gdown2_out,
        down_in, up_in, down_stage, up_stage, edges_held, in_sems, out_sems, edge_sem, travel,
    ):
        edges_load = pltpu.make_async_copy(edges_in, edges_held, edge_sem.at[0])
        edges_load.start()
        loads = [
            pltpu.make_async_copy(source, target, in_sems.at[k])
            for k, (source, target) in enumerate(
                [(gdown1_in, down_in.at[0]), (gup1_in, up_in.at[0]), (gdown2_in, down_in.at[1]), (gup2_in, up_in.at[1])]
            )
        ]
        start_all(loads)
        stores = []
        for k, (down_out, up_out) in enumerate(((gdown1_out, gup1_out), (gdown2_out, gup2_out))):
            loads[2 * k].wait()
            down_stage[k] = down_in[k].astype(FLOAT)
            stores.append(pltpu.make_async_copy(down_stage.at[k], down_out, out_sems.at[2 * k]))
            stores[-1].start()
            loads[2 * k + 1].wait()
            for kind in range(2):
                up_stage[k, :, kind, :] = up_in[k, kind].astype(FLOAT)
            stores.append(pltpu.make_async_copy(up_stage.at[k], up_out, out_sems.at[2 * k + 1]))
            stores[-1].start()
        cgain_out[...] = sums_in[0:2, 0:share]
        again_out[...] = sums_in[2:4, 0:share]
        taps_out[...] = sums_in[5:8, 0:channels]
        for kind in range(2):
            gqk_out[kind : kind + 1, :] = sums_in[4:5, kind * head_width : (kind + 1) * head_width]
            start = query_width + kind * (pair_width // 2)
            gkv_out[:, kind, :] = gmix_in[:, start : start + pair_width // 2].astype(FLOAT)
        gq_out[...] = gmix_in[:, 0:query_width].astype(FLOAT)
        gout1_out[...] = gout1_in[...].astype(FLOAT)
        gout2_out[...] = gout2_in[...].astype(FLOAT)
        gin_out[...] = gin_in[...].astype(FLOAT)
        edges_load.wait()
        stores.append(pltpu.make_async_copy(edges_held, edges_out, edge_sem.at[1]))
        stores[-1].start()
        wait_all(stores)

    (
        section_edges, cgain, gin, taps, gout1, gup1, gdown1, again, gq, gkv, gqk, gout2, gup2, gdown2,
    ) = call(
        results,
        "results",
        None,
        [
            ((1, micro, local_rows, width), HALF, ANY),
            ((2, share), FLOAT),
            ((3, share, channels), FLOAT),
            ((3, channels), FLOAT),
            ((share, channels), FLOAT),
            ((share, 2, hidden_units), FLOAT, ANY),
            ((share, hidden_units), FLOAT, ANY),
            ((2, share), FLOAT),
            ((share, query_width), FLOAT),
            ((share, 2, pair_width // 2), FLOAT),
            ((2, head_width), FLOAT),
            ((share, query_width), FLOAT),
            ((share, 2, hidden_units), FLOAT, ANY),
            ((share, hidden_units), FLOAT, ANY),
        ],
        [
            pltpu.VMEM((2, share, hidden_units), HALF),
            pltpu.VMEM((2, 2, share, hidden_units), HALF),
            pltpu.VMEM((2, share, hidden_units), FLOAT),
            pltpu.VMEM((2, share, 2, hidden_units), FLOAT),
            pltpu.VMEM((1, micro, local_rows, width), HALF),
            dma(4),
            dma(4),
            dma(2),
        ],
        [(section_edges, ANY), sums, gout2, gmix, gout1, gin]
        + [(array, ANY) for array in (gdown2, gup2, gdown1, gup1)],
        moved=25 << 20,
    )
    return (
        section_edges,
        cgain,
        gin.transpose(1, 0, 2),
        taps,
        gout1.T,
        gup1,
        gdown1.T,
        again,
        gq,
        gkv,
        gqk,
        gout2.T,
        gup2,
        gdown2.T,
    )


def solution(mesh):
    return jax.shard_map(
        per_device,
        mesh=mesh,
        in_specs=(
            P("section", None, "seq", None),
            P(),
            P(None, "seq"),
            P(),
            P(None, None, "head"),
            P(None, "head"),
            P("head", None),
            P(None, None, "head"),
            P("head", None),
            P(),
            P(None, "head"),
            P(None, None, "head"),
            P(),
            P("head", None),
            P(None, None, "head"),
            P("head", None),
        ),
        out_specs=(
            P("section", None, "seq", None),
            P(None, ("section", "seq")),
            P(("section", "seq"), None, "head"),
            P(None, "head"),
            P("head", ("section", "seq")),
            P(("section", "seq"), None, "head"),
            P("head", ("section", "seq")),
            P(None, ("section", "seq")),
            P(("section", "seq"), "head"),
            P(("section", "seq"), None, "head"),
            P(),
            P("head", ("section", "seq")),
            P(("section", "seq"), None, "head"),
            P("head", ("section", "seq")),
        ),
        check_vma=False,
    )
```

```python
import functools

import jax
import jax.numpy as jnp
from jax import lax
from jax.experimental import pallas as pl
from jax.experimental.pallas import tpu as pltpu
from jax.sharding import PartitionSpec as P

EPS = 1e-05
THETA = 1000000.0
FLOAT = jnp.float32
HALF = jnp.bfloat16
MESH = pl.DeviceIdType.MESH
VMEM = pl.BlockSpec(memory_space=pltpu.VMEM)
ANY = pl.BlockSpec(memory_space=pl.ANY)


def product(former, latter):
    return jnp.dot(former, latter, preferred_element_type=FLOAT)


def outer_sum(former, latter):
    return lax.dot_general(former, latter, (((0,), (0,)), ((), ())), preferred_element_type=FLOAT)


def back_product(former, latter):
    return lax.dot_general(former, latter, (((1,), (1,)), ((), ())), preferred_element_type=FLOAT)


def norm_apply(values, gain):
    return values * lax.rsqrt(jnp.mean(values * values, -1, keepdims=True) + EPS) * gain


def norm_back(values, gain, grad):
    scale = lax.rsqrt(jnp.mean(values * values, -1, keepdims=True) + EPS)
    weighted = grad * gain
    inner = jnp.mean(weighted * values, -1, keepdims=True)
    grad_values = scale * weighted - values * (scale * scale * scale * inner)
    return grad_values, jnp.sum(grad * values * scale, 0, keepdims=True)


BLOCKS = 8
LAG = 3
END_FIRST = 10
MIDDLE_FIRST = 3


def place():
    return lax.axis_index("section"), lax.axis_index("seq"), lax.axis_index("head")


def remote(source, target, send, recv, peer):
    return pltpu.make_async_remote_copy(
        src_ref=source,
        dst_ref=target,
        send_sem=send,
        recv_sem=recv,
        device_id=peer,
        device_id_type=MESH,
    )


def signal(peer):
    pl.semaphore_signal(pltpu.get_barrier_semaphore(), inc=1, device_id=peer, device_id_type=MESH)


def wait_greetings(count):
    pl.semaphore_wait(pltpu.get_barrier_semaphore(), count)


def greet(others, where, size):
    for peer in others:
        signal(peer)
    section, seq, head = where
    end = (head == 0) | (head == size - 1)

    @pl.when(end)
    def _():
        signal((section, seq, jnp.where(head == 0, 1, size - 2)))

    @pl.when(jnp.logical_not(end))
    def _():
        signal((section, seq, jnp.minimum(head + 1, size - 1)))
        signal((section, seq, jnp.maximum(head - 1, 0)))

    def met():
        @pl.when(end)
        def _():
            wait_greetings(len(others) + 1)

        @pl.when(jnp.logical_not(end))
        def _():
            wait_greetings(len(others) + 2)

    return met


def seq_peers(where, seqs):
    section, seq, head = where
    return [(section, lax.rem(seq + k, seqs), head) for k in range(1, seqs)]


def rows_of(index, count):
    return pl.ds(pl.multiple_of(index * count, count), count)


def wait_all(copies):
    for copy in copies:
        copy.wait()


def start_all(copies):
    for copy in copies:
        copy.start()


def loop(count, step):
    def body(i, carried):
        step(i)
        return carried

    lax.fori_loop(0, count, body, 0)


def head_total(part, full, inbox, reduce_send, reduce_recv, gather_send, gather_recv, where, size, finish, filler=None, fillers=0):
    section, seq, head = where
    count = part.shape[0] // (2 * BLOCKS)
    last = size - 1
    end = (head == 0) | (head == last)

    def rows(flow, i):
        return rows_of(flow * BLOCKS + i, count)

    def fill(t):
        if filler is not None:

            @pl.when(t < fillers)
            def _():
                filler(t)

    def fill_rest(start, stop=fillers):
        stop = min(stop, fillers)
        if stop > start:
            loop(stop - start, lambda i: filler(start + i))

    def reduced(flow, i, peer):
        return remote(part.at[rows(flow, i)], inbox.at[flow, i], reduce_send.at[flow, i], reduce_recv.at[flow, i], peer)

    def gathered(flow, i, peer):
        span = full.at[rows(flow, i)]
        return remote(span, span, gather_send.at[flow, i], gather_recv.at[flow, i], peer)

    @pl.when(end)
    def _():
        flow = jnp.where(head == 0, 0, 1)
        inner = (section, seq, jnp.where(head == 0, 1, last - 1))
        loop(BLOCKS, lambda i: reduced(1 - flow, i, inner).start())
        fill_rest(0, END_FIRST)

        def own(i):
            reduced(flow, i, inner).wait_recv()
            total = part[rows(flow, i), :].astype(FLOAT) + inbox[flow, i].astype(FLOAT)
            full[rows(flow, i), :] = finish(flow, i, total)
            gathered(flow, i, inner).start()
            fill(END_FIRST + i)

        loop(BLOCKS, own)
        fill_rest(END_FIRST + BLOCKS)

        def drain(i):
            gathered(1 - flow, i, inner).wait_recv()
            reduced(1 - flow, i, inner).wait_send()
            gathered(flow, i, inner).wait_send()

        loop(BLOCKS, drain)

    @pl.when(jnp.logical_not(end))
    def _():
        low = head < size // 2
        near = jnp.where(low, 1, 0)
        ahead = (section, seq, jnp.where(low, head + 1, head - 1))
        behind = (section, seq, jnp.where(low, head - 1, head + 1))

        def add(flow, i, peer):
            reduced(flow, i, peer).wait_recv()
            span = rows(flow, i)
            part[span, :] = (part[span, :].astype(FLOAT) + inbox[flow, i].astype(FLOAT)).astype(HALF)
            reduced(flow, i, peer).start()

        def forward(flow, i, peer):
            gathered(flow, i, peer).wait_recv()
            gathered(flow, i, peer).start()

        def lagged(act, first, second, at):
            def step(i):
                fill(at + i)

                @pl.when(i < BLOCKS)
                def _():
                    act(first, i, ahead)

                @pl.when(i >= LAG)
                def _():
                    act(second, i - LAG, behind)

            loop(BLOCKS + LAG, step)

        fill_rest(0, MIDDLE_FIRST)
        lagged(add, near, 1 - near, MIDDLE_FIRST)
        lagged(forward, 1 - near, near, MIDDLE_FIRST + BLOCKS + LAG)
        fill_rest(MIDDLE_FIRST + 2 * (BLOCKS + LAG))

        def drain(i):
            reduced(near, i, ahead).wait_send()
            reduced(1 - near, i, behind).wait_send()
            gathered(1 - near, i, ahead).wait_send()
            gathered(near, i, behind).wait_send()

        loop(BLOCKS, drain)


def turned(values):
    width = values.shape[-1]
    if width == 128:
        lane = lax.broadcasted_iota(jnp.int32, values.shape, 1)
        low = lax.rem(lane, 64) < 32
        return jnp.where(low, -pltpu.roll(values, 96, 1), pltpu.roll(values, 32, 1))
    parts = []
    for start in range(0, width, 64):
        parts += [-values[:, start + 32 : start + 64], values[:, start : start + 32]]
    return jnp.concatenate(parts, -1)


def head_mean(values):
    width = values.shape[-1]
    if width == 64:
        return jnp.mean(values, -1, keepdims=True)
    lane = lax.broadcasted_iota(jnp.int32, values.shape, 1)
    first = jnp.sum(jnp.where(lane < 64, values, 0.0), -1, keepdims=True)
    second = jnp.sum(jnp.where(lane < 64, 0.0, values), -1, keepdims=True)
    return jnp.where(lane < 64, first, second) * (1.0 / 64.0)


def chunks_of(width):
    return [(start, min(128, width - start)) for start in range(0, width, 128)]


def rotary(raw, gain, cosine, sine):
    width = raw.shape[-1]
    normed = raw * lax.rsqrt(head_mean(raw * raw) + EPS) * gain[:, :width]
    return normed * cosine[:, :width] + turned(normed) * sine[:, :width]


def rotary_back(raw, gain, cosine, sine, grad):
    width = raw.shape[-1]
    back = grad * cosine[:, :width] - turned(grad) * sine[:, :width]
    scale = lax.rsqrt(head_mean(raw * raw) + EPS)
    weighted = back * gain[:, :width]
    grad_raw = scale * weighted - raw * (scale * scale * scale * head_mean(weighted * raw))
    return grad_raw, jnp.sum(back * raw * scale, 0, keepdims=True)


LAZY = "lazy"
LATE = "late"


class Moves:
    def __init__(self, incoming, leaving):
        self.incoming, self.leaving, self.left = incoming, leaving, []

    def begin(self):
        for _, copy in self.incoming:
            copy.start()

    def ready(self, *refs):
        for ref in refs:
            for known, copy in self.incoming:
                if known is ref:
                    copy.wait()

    def leave(self, *refs):
        for ref in refs:
            for known, copy in self.leaving:
                if known is ref:
                    copy.start()
                    self.left.append(copy)

    def finish(self):
        wait_all(self.left)


def call(body, name, collective, outs, scratch, args, flops=0, moved=0, begin=True):
    params = dict(vmem_limit_bytes=60 << 20)
    if collective is not None:
        params.update(collective_id=collective, has_side_effects=True)
    lazy = [n for n, arg in enumerate(args) if isinstance(arg, tuple) and arg[1] is LAZY]
    late = [n for n, out in enumerate(outs) if len(out) > 2 and out[2] is LATE]
    arrays = [arg[0] if isinstance(arg, tuple) else arg for arg in args]
    extra = [pltpu.VMEM(arrays[n].shape, arrays[n].dtype) for n in lazy]
    extra += [pltpu.VMEM(outs[n][0], outs[n][1]) for n in late]
    moves = len(lazy) + len(late)
    if moves:
        extra.append(pltpu.SemaphoreType.DMA((moves,)))

    def whole(*refs):
        refs = list(refs)
        held = refs[len(refs) - len(extra) :]
        refs = refs[: len(refs) - len(extra)]
        incoming, leaving = [], []
        for at, n in enumerate(lazy):
            incoming.append((held[at], pltpu.make_async_copy(refs[n], held[at], held[-1].at[at])))
            refs[n] = held[at]
        for at, n in enumerate(late):
            place_at = len(args) + n
            kept = held[len(lazy) + at]
            leaving.append((kept, pltpu.make_async_copy(kept, refs[place_at], held[-1].at[len(lazy) + at])))
            refs[place_at] = kept
        travel = Moves(incoming, leaving)
        if begin:
            travel.begin()
        body(*refs, travel)
        travel.finish()

    def spec(mark):
        return ANY if mark is LAZY or mark is LATE else mark

    results = pl.pallas_call(
        whole,
        name=name,
        out_shape=[jax.ShapeDtypeStruct(out[0], out[1]) for out in outs],
        in_specs=[spec(arg[1]) if isinstance(arg, tuple) else VMEM for arg in args],
        out_specs=[spec(out[2]) if len(out) > 2 else VMEM for out in outs],
        scratch_shapes=list(scratch) + extra,
        compiler_params=pltpu.CompilerParams(**params),
        cost_estimate=pl.CostEstimate(flops=flops, bytes_accessed=moved, transcendentals=0),
    )(*arrays)
    return list(results)


def dma(count):
    return pltpu.SemaphoreType.DMA((count,))


def per_device(
    incoming,
    segment_ids,
    positions,
    conv_gains,
    conv_in,
    conv_kernel,
    conv_out,
    conv_gate_up,
    conv_down,
    attn_gains,
    w_query,
    w_keyval,
    qk_gains,
    attn_out,
    attn_gate_up,
    attn_down,
):
    sections = lax.axis_size("section")
    seqs = lax.axis_size("seq")
    heads = lax.axis_size("head")
    section, seq, head = place()
    micro, local_rows, width = incoming.shape[1:]
    rows = local_rows // sections
    tokens = micro * rows
    half_tokens = tokens // 2
    step_rows = half_tokens // BLOCKS
    block_tok = segment_ids.shape[1]
    length = micro * block_tok
    slots = sections * seqs
    channels = conv_in.shape[2]
    hidden_units = conv_down.shape[0]
    head_width = qk_gains.shape[1]
    query_width = w_query.shape[1]
    pair_width = 2 * w_keyval.shape[2]
    kv_local = w_keyval.shape[2] // head_width
    group = query_width // (kv_local * head_width)
    score_scale = head_width ** (-0.5)
    half_model = width // sections
    share = width // (sections * seqs)

    pair_index = lax.broadcasted_iota(jnp.int32, (1, 2 * head_width), 1) % (head_width // 2)
    angle_rates = THETA ** (-2.0 * pair_index.astype(FLOAT) / head_width)
    local_positions = lax.dynamic_slice_in_dim(positions, section * rows, rows, 1).reshape(tokens)
    angles = local_positions.astype(FLOAT)[:, None] * angle_rates
    cosine, sine = jnp.cos(angles), jnp.sin(angles)
    w_in = conv_in.transpose(1, 0, 2)
    w_pair = w_keyval.reshape(width, pair_width)
    first_up = conv_gate_up.transpose(1, 2, 0)
    second_up = attn_gate_up.transpose(1, 2, 0)
    slabs = [(start, min(512, hidden_units - start)) for start in range(0, hidden_units, 512)]
    tile_width = 256
    tiles = -(-hidden_units // tile_width)
    padded_units = tiles * tile_width

    def own_column(seg_ref, m, back):
        start = lax.axis_index("seq") * local_rows + lax.axis_index("section") * rows - back
        wanted = start + lax.broadcasted_iota(jnp.int32, (rows, block_tok), 0)
        lane = lax.broadcasted_iota(jnp.int32, (rows, block_tok), 1)
        found = jnp.where(lane == wanted, seg_ref[m : m + 1, :].astype(FLOAT), 0.0)
        if back and m:
            found = found + jnp.where(lane == wanted + block_tok, seg_ref[m - 1 : m, :].astype(FLOAT), 0.0)
        elif back:
            found = found + jnp.where((wanted < 0) & (lane == 0), -1.0, 0.0)
        return jnp.sum(found, -1, keepdims=True)

    def twice(row):
        return jnp.concatenate([row, row], -1)

    def shifted_rows(ext, micro_at, back):
        return ext[micro_at, 8 - back : 8 - back + rows, :]

    def own_rows(flow, i):
        return rows_of(flow * BLOCKS + i, step_rows)

    def kept_rows(i):
        return rows_of(i, step_rows)

    total_scratch = [pltpu.VMEM((2, BLOCKS, step_rows, width), HALF)] + [
        pltpu.SemaphoreType.DMA((2, BLOCKS)) for _ in range(4)
    ]
    part_scratch = [pltpu.VMEM((tokens, width), HALF)]

    weight_scratch = [
        pltpu.VMEM((2, hidden_units, width), HALF),
        pltpu.VMEM((hidden_units, width), HALF),
        dma(3 * len(slabs)),
    ]

    def weight_loads(up_hbm, down_hbm, up_ref, down_ref, sems):
        copies = []
        for j, (start, count) in enumerate(slabs):
            span = slice(start, start + count)
            pairs = [(up_hbm.at[0, span], up_ref.at[0, span]), (up_hbm.at[1, span], up_ref.at[1, span])]
            pairs.append((down_hbm.at[span], down_ref.at[span]))
            for k, (source, target) in enumerate(pairs):
                copies.append(pltpu.make_async_copy(source, target, sems.at[3 * j + k]))
        return copies

    def conv_forward(
        in_ref, gain_ref, win_ref, kernel_ref, wout_ref, attn_gain_ref, up_hbm, down_hbm, seg_ref,
        x_ref, g_ref, n1_ref, pc_ref, edge_ref, y_ref, h1_ref, n2_ref, f1_ref, a1_ref, m_ref, n3_ref, same_ref, segq_ref,
        other, edges, normed_edges, ext, swap_send, swap_recv, edge_send, edge_recv, up_ref, down_ref, weight_sems, acc,
        part, inbox, rs, rr, gs, gr, inbox2, rs2, rr2, gs2, gr2, travel,
    ):
        where = place()
        s, q, h = where
        partner = (1 - s, q, h)
        following = (s, lax.rem(q + 1, seqs), h)
        preceding = (s, lax.rem(q + seqs - 1, seqs), h)
        weights = weight_loads(up_hbm, down_hbm, up_ref, down_ref, weight_sems)
        start_all(weights)
        met = greet([partner, following, preceding] + seq_peers(where, seqs), where, heads)
        for m in range(micro):
            span = slice(m * rows, (m + 1) * rows)
            column = own_column(seg_ref, m, 0)
            segq_ref[span, :] = column
            for back in (1, 2):
                same_ref[span, back - 1 : back] = jnp.where(column == own_column(seg_ref, m, back), 1.0, 0.0)
        met()
        give = pl.multiple_of((1 - s) * rows, rows)
        swap = remote(in_ref.at[0, :, pl.ds(give, rows)], other, swap_send.at[0], swap_recv.at[0], partner)
        swap.start()
        near = remote(in_ref.at[0, :, rows - 16 : rows], edges.at[0], edge_send.at[0], edge_recv.at[0], partner)
        near.start()
        far = remote(
            in_ref.at[0, :, local_rows - 16 : local_rows], edges.at[1], edge_send.at[1], edge_recv.at[1], following
        )
        far.start()
        keep = pl.multiple_of(s * rows, rows)
        swap.wait()
        mine = in_ref[0, :, pl.ds(keep, rows), :].reshape(tokens, width)
        theirs = other[...].reshape(tokens, width)
        first = s == 0
        x = jnp.where(first, mine, theirs)
        x_ref[...] = x
        g_ref[...] = jnp.where(first, theirs, mine)
        n1_ref[...] = norm_apply(x.astype(FLOAT), gain_ref[0:1, :]).astype(HALF)
        near.wait()
        far.wait()
        for m in range(micro):
            before = edges[1, max(m - 1, 0)]
            far_edge = jnp.where(q == 0, before, edges[1, m])
            edge = jnp.where(first, far_edge, edges[0, m]).astype(FLOAT)
            normed_edges[m * 16 : (m + 1) * 16, :] = norm_apply(edge, gain_ref[0:1, :]).astype(HALF)
        travel.ready(win_ref)
        for k in range(3):
            pc_ref[k] = product(n1_ref[...], win_ref[k])
        edge_b = product(normed_edges[...], win_ref[0])
        edge_u = product(normed_edges[...], win_ref[2])
        edge_gated = edge_b * edge_u
        gated = pc_ref[0] * pc_ref[2]
        for m in range(micro):
            ext[m, 0:8, :] = edge_gated[m * 16 + 8 : m * 16 + 16, :]
            edge_ref[m] = edge_gated[m * 16 + 8 : m * 16 + 16, :]
            ext[m, 8 : 8 + rows, :] = gated[m * rows : (m + 1) * rows, :]
        for m in range(micro):
            span = slice(m * rows, (m + 1) * rows)
            mixed = (
                kernel_ref[2:3, :] * gated[span]
                + kernel_ref[1:2, :] * jnp.where(same_ref[span, 0:1] > 0, shifted_rows(ext, m, 1), 0.0)
                + kernel_ref[0:1, :] * jnp.where(same_ref[span, 1:2] > 0, shifted_rows(ext, m, 2), 0.0)
            )
            y_ref[span, :] = (pc_ref[1, span, :] * mixed).astype(HALF)
        travel.ready(wout_ref)
        part[...] = product(y_ref[...], wout_ref[...]).astype(HALF)
        travel.leave(x_ref, g_ref, n1_ref, pc_ref, edge_ref, y_ref, same_ref, segq_ref)

        def finish(flow, i, total):
            hidden = x_ref[own_rows(flow, i), :].astype(FLOAT) + total
            h1_ref[kept_rows(i), :] = hidden
            return norm_apply(hidden, gain_ref[1:2, :]).astype(HALF)

        head_total(part, n2_ref, inbox, rs, rr, gs, gr, where, heads, finish)
        travel.leave(h1_ref, n2_ref)
        for j, (start, count) in enumerate(slabs):
            wait_all(weights[3 * j : 3 * j + 3])
            span = slice(start, start + count)
            gate = back_product(n2_ref[...], up_ref[0, span, :])
            rise = back_product(n2_ref[...], up_ref[1, span, :])
            f1_ref[0, :, span] = gate
            f1_ref[1, :, span] = rise
            active = (gate / (1.0 + jnp.exp(-gate)) * rise).astype(HALF)
            a1_ref[:, span] = active
            term = product(active, down_ref[span, :])
            if j == 0:
                acc[...] = term
            else:
                acc[...] += term
        part[...] = acc[...].astype(HALF)
        travel.leave(f1_ref, a1_ref)

        def finish_middle(flow, i, total):
            middle = (h1_ref[kept_rows(i), :] + total).astype(HALF).astype(FLOAT)
            m_ref[kept_rows(i), :] = middle
            return norm_apply(middle, attn_gain_ref[0:1, :]).astype(HALF)

        head_total(part, n3_ref, inbox2, rs2, rr2, gs2, gr2, where, heads, finish_middle)
        travel.leave(m_ref, n3_ref)


    grid_rows = seqs // 2
    first_blocks = 3 * grid_rows - 2
    half_share = share // 2

    def grid_place(q):
        return lax.div(q, 2), lax.rem(q, 2)

    def first_stage(source, target, send, recv, where):
        s, q, h = where
        a, b = grid_place(q)
        copies = []
        for row in range(grid_rows):
            copies.append((source(row * 2 + 1 - b, 0), row, (s, a * 2 + 1 - b, h)))
        for k in range(1, grid_rows):
            row = lax.rem(a + k, grid_rows)
            for column in range(2):
                copies.append((source(row * 2 + column, 1), grid_rows + 2 * (k - 1) + column, (s, row * 2 + b, h)))
        return [remote(block, target(i), send.at[i], recv.at[i], peer) for block, i, peer in copies]

    def passed_blocks(where):
        s, q, h = where
        a, b = grid_place(q)
        blocks = []
        for k in range(1, grid_rows):
            row = lax.rem(a + k, grid_rows)
            blocks.append((row * 2 + b, 0, [row], (s, row * 2 + b, h)))
        arrived = [grid_rows + 2 * j + 1 - b for j in range(grid_rows - 1)]
        blocks.append((a * 2 + 1 - b, 1, arrived, (s, a * 2 + 1 - b, h)))
        return blocks

    def half_rows(side):
        return slice(side * half_share, (side + 1) * half_share)

    def combine(passing, arrived, where, own=None):
        for i, (_, _, sources, _) in enumerate(passed_blocks(where)):
            total = (passing if own is None else own)(i)[...].astype(FLOAT)
            for source in sources:
                total = total + arrived[source].astype(FLOAT)
            passing(i)[...] = total.astype(HALF)

    def second_stage(passing, target, send, recv, where):
        return [
            remote(passing(i), target.at[i], send.at[i], recv.at[i], peer)
            for i, (_, _, _, peer) in enumerate(passed_blocks(where))
        ]

    def load_passing(partial, passing, sems, where):
        return [
            pltpu.make_async_copy(partial.at[dest, half_rows(side)], passing.at[i], sems.at[i])
            for i, (dest, side, _, _) in enumerate(passed_blocks(where))
        ]

    def two_halves(own, arrived, passed, where):
        a, b = grid_place(where[1])
        upper = own[half_rows(0), :].astype(FLOAT) + arrived[a].astype(FLOAT)
        for k in range(grid_rows - 1):
            upper = upper + passed[k].astype(FLOAT)
        lower = own[half_rows(1), :].astype(FLOAT) + passed[grid_rows - 1].astype(FLOAT)
        for j in range(grid_rows - 1):
            lower = lower + arrived[grid_rows + 2 * j + b].astype(FLOAT)
        return upper, lower

    def dma_grid(*shape):
        return pltpu.SemaphoreType.DMA(shape)

    def first_shape(count):
        return ((count, first_blocks, half_share, padded_units), HALF, ANY)

    def second_shape(count):
        return ((count, grid_rows, half_share, padded_units), HALF, ANY)

    def passing_scratch(count):
        return [
            pltpu.VMEM((count, grid_rows, half_share, padded_units), HALF),
            pltpu.VMEM((count, first_blocks, half_share, padded_units), HALF),
            dma_grid(count, grid_rows + 1),
            dma_grid(count, grid_rows),
            dma_grid(count, grid_rows),
        ]

    def pass_loads(partial, kinds, arrived, passing, held, sems, where):
        copies = []
        for k, kind in enumerate(kinds):
            copies += load_passing(partial.at[kind], passing.at[k], sems.at[k], where)
            copies.append(pltpu.make_async_copy(arrived.at[k], held.at[k], sems.at[k, grid_rows]))
        return copies

    def pass_sends(count, passing, held, target, send, recv, where):
        copies = []
        for k in range(count):
            combine(lambda i, k=k: passing.at[k, i], held.at[k], where)
            sends = second_stage(lambda i, k=k: passing.at[k, i], target.at[k], send.at[k], recv.at[k], where)
            start_all(sends)
            copies += sends
        return copies

    small_rows = tokens // heads
    widths = [query_width, query_width + pair_width, channels, 3 * channels]

    def head_others(where):
        s, q, h = where
        return [(s, q, lax.rem(h + k, heads)) for k in range(1, heads)]

    def mixer_sends(stages, incomes, send, recv, where):
        return [
            first_stage(
                lambda dest, side, stage=stage: stage.at[dest, half_rows(side)],
                lambda i, income=income: income.at[i],
                send.at[k],
                recv.at[k],
                where,
            )
            for k, (stage, income) in enumerate(zip(stages, incomes))
        ]

    def mixer_steps(formers, latters, stages, given, former, halves, swaps, sends):
        def step(t):
            for k in range(len(formers)):

                @pl.when(t == 2 * k)
                def _(k=k):
                    halves[k].wait()
                    former[...] = transposed(formers[k], given.at[k])

                @pl.when(t == 2 * k + 1)
                def _(k=k):
                    swaps[k].wait()
                    result = product(former[...], latters[k][...]).astype(HALF)
                    stages[k][...] = result.reshape(seqs, share, result.shape[1])
                    start_all(sends[k])

        return step

    def mixer_second(stages, incomes, passes, turns, send, recv, where):
        blocks = passed_blocks(where)
        turning = []
        for k, (stage, income, passed, turn) in enumerate(zip(stages, incomes, passes, turns)):

            def own_block(i, stage=stage):
                return stage.at[blocks[i][0], half_rows(blocks[i][1])]

            def moved(i, stage=stage, passed=passed):
                return own_block(i, stage) if passed is None else passed.at[i]

            combine(moved, income, where, own_block)
            turning.append(second_stage(moved, turn, send.at[k], recv.at[k], where))
        return turning

    def latter_swaps(latters, send, recv, partner):
        return [
            remote(latter.at[0:tokens], latter.at[tokens : 2 * tokens], send.at[k], recv.at[k], partner)
            for k, latter in enumerate(latters)
        ]

    def first_sums(count):
        return [((first_blocks, half_share, size), HALF) for size in count]

    def transposed(array_ref, given_ref):
        start = pl.multiple_of(lax.axis_index("section") * half_model, 128)
        own = array_ref[:, pl.ds(start, half_model)]
        both = jnp.concatenate([own, given_ref[...]], 0)
        return both.astype(FLOAT).T.astype(HALF)

    def half_swaps(arrays, targets, send, recv, where):
        s, q, h = where
        copies = []
        for k, (array_ref, target) in enumerate(zip(arrays, targets)):
            start = pl.multiple_of((1 - s) * half_model, 128)
            copies.append(remote(array_ref.at[:, pl.ds(start, half_model)], target, send.at[k], recv.at[k], (1 - s, q, h)))
        return copies

    def latter_swap(latter, kind, start, count, send, recv, where):
        s, q, h = where
        return remote(
            latter.at[kind, 0:tokens, start : start + count],
            latter.at[kind, tokens : 2 * tokens, start : start + count],
            send,
            recv,
            (1 - s, q, h),
        )

    def gradient_tiles(former, latter, stage, partial_hbm, first_in, local_sems, send, recv, where, kinds):
        def split(t):
            kind = lax.div(t, tiles)
            at = lax.rem(t, tiles)
            return kind, pl.ds(pl.multiple_of(at * tile_width, tile_width), tile_width)

        def stored(t):
            kind, columns = split(t)
            return pltpu.make_async_copy(
                stage.at[kind, :, :, columns], partial_hbm.at[kind, :, :, columns], local_sems.at[t]
            )

        def sent(t):
            kind, columns = split(t)
            return first_stage(
                lambda dest, side: stage.at[kind, dest, half_rows(side), columns],
                lambda i: first_in.at[kind, i, :, columns],
                send.at[t],
                recv.at[t],
                where,
            )

        def tile(t):
            kind, columns = split(t)
            use = jnp.where(kind == 0, 0, 1)
            result = product(former[use], latter[kind, :, columns]).astype(HALF)
            stage[kind, :, :, columns] = result.reshape(seqs, share, tile_width)

            @pl.when(t < kinds * tiles)
            def _():
                start_all(sent(t))

            stored(t).start()

        def finish():
            loop(3 * tiles, lambda t: stored(t).wait())
            loop(kinds * tiles, lambda t: wait_all(sent(t)))

        return tile, finish

    ffn_scratch = weight_scratch + [
        pltpu.VMEM((tokens, width), FLOAT),
        pltpu.VMEM((2, tokens, half_model), HALF),
        pltpu.VMEM((2, half_model, 2 * tokens), HALF),
        pltpu.VMEM((3, 2 * tokens, padded_units), HALF),
        pltpu.VMEM((3, seqs, share, padded_units), HALF),
        dma(2),
        dma(2),
        pltpu.SemaphoreType.DMA((3, len(slabs))),
        pltpu.SemaphoreType.DMA((3, len(slabs))),
        pltpu.SemaphoreType.DMA((3 * tiles,)),
        pltpu.SemaphoreType.DMA((3 * tiles, first_blocks)),
        pltpu.SemaphoreType.DMA((3 * tiles, first_blocks)),
    ]
    def partial_outs(kinds):
        return [((3, seqs, share, padded_units), HALF, ANY), first_shape(kinds)]


    def slot_peer(me, j, h):
        other = lax.rem(me + j, slots)
        return (lax.rem(other, sections), lax.div(other, sections), h)

    def query_rows(ref, m, c):
        block = ref[m * rows : (m + 1) * rows, :]
        base = c * group * head_width
        return jnp.concatenate(
            [block[:, base + r * head_width : base + (r + 1) * head_width] for r in range(group)], 0
        )

    def keys_of(all_ref, at, c, kind):
        block = all_ref[:, at * rows : (at + 1) * rows, :].reshape(block_tok, pair_width)
        base = kind * kv_local * head_width + c * head_width
        return block[:, base : base + head_width]

    def allowed_pairs(segq_ref, seg_ref, m, at, s, q):
        own_segments = segq_ref[m * rows : (m + 1) * rows, :]
        allowed = own_segments == seg_ref[at : at + 1, :].astype(FLOAT)
        if at == m:
            base = q * local_rows + s * rows
            order = base + lax.broadcasted_iota(jnp.int32, (rows, block_tok), 0)
            allowed = allowed & (lax.broadcasted_iota(jnp.int32, (rows, block_tok), 1) <= order)
        bias = jnp.where(allowed, 0.0, -1e30)
        return jnp.concatenate([bias] * group, 0)

    def probabilities(rows_in, keys, biases):
        scores = [back_product(rows_in, key) + bias for key, bias in zip(keys, biases)]
        summit = functools.reduce(jnp.maximum, [jnp.max(part, -1, keepdims=True) for part in scores])
        raised = [jnp.exp(part - summit) for part in scores]
        total = functools.reduce(jnp.add, [jnp.sum(part, -1, keepdims=True) for part in raised])
        return raised, 1.0 / total

    def gather_pairs(all_ref, me, where, send, recv, near_send, near_recv):
        s, q, h = where
        partner = (1 - s, q, h)
        far = []
        for k, peer in enumerate(seq_peers(where, seqs)):
            copy = remote(all_ref.at[me], all_ref.at[me], send.at[k], recv.at[k], peer)
            copy.start()
            far.append(copy)
        near = [remote(all_ref.at[me], all_ref.at[me], near_send.at[0], near_recv.at[0], partner)]
        near[0].start()

        def pass_on():
            for k in range(1, seqs):
                far[k - 1].wait()
                slot = lax.rem(q + seqs - k, seqs) * sections + s
                copy = remote(all_ref.at[slot], all_ref.at[slot], near_send.at[k], near_recv.at[k], partner)
                copy.start()
                near.append(copy)
            wait_all(near)

        return pass_on

    def attention_forward(
        n3_ref, wq_ref, wp_ref, cos_ref, sin_ref, qk_ref, segq_ref, seg_ref, wo_ref, m_ref, gain_ref,
        qr_ref, r_ref, q_ref, all_ref, o_ref, h2_ref, n4_ref,
        send, recv, near_send, near_recv, part, inbox, rs, rr, gs, gr, travel,
    ):
        where = place()
        s, q, h = where
        me = q * sections + s
        travel.ready(wp_ref, cos_ref, sin_ref)
        cos, sin = cos_ref[...], sin_ref[...]
        r_ref[...] = product(n3_ref[...], wp_ref[...])
        half_pair = pair_width // 2
        for start, size in chunks_of(half_pair):
            span = slice(start, start + size)
            all_ref[me, :, span] = rotary(r_ref[:, span], twice(qk_ref[1:2, :]), cos, sin).astype(HALF)
        all_ref[me, :, half_pair:] = r_ref[:, half_pair:].astype(HALF)
        pass_on = gather_pairs(all_ref, me, where, send, recv, near_send, near_recv)
        travel.ready(wq_ref)
        qr_ref[...] = product(n3_ref[...], wq_ref[...])
        for start, size in chunks_of(query_width):
            span = slice(start, start + size)
            q_ref[:, span] = rotary(qr_ref[:, span], twice(qk_ref[0:1, :]), cos, sin).astype(HALF)
        travel.leave(r_ref, qr_ref, q_ref)
        pass_on()
        travel.leave(all_ref)
        for m in range(micro):
            biases = [allowed_pairs(segq_ref, seg_ref, m, at, s, q) for at in range(m + 1)]
            results = []
            for c in range(kv_local):
                keys = [keys_of(all_ref, at, c, 0) for at in range(m + 1)]
                raised, inverse = probabilities(query_rows(q_ref, m, c) * HALF(score_scale), keys, biases)
                total = functools.reduce(
                    jnp.add,
                    [
                        product((raised[at] * inverse).astype(HALF), keys_of(all_ref, at, c, 1))
                        for at in range(m + 1)
                    ],
                )
                results += [total[r * rows : (r + 1) * rows] for r in range(group)]
            o_ref[m * rows : (m + 1) * rows, :] = jnp.concatenate(results, -1).astype(HALF)
        travel.leave(o_ref)
        travel.ready(wo_ref)
        part[...] = product(o_ref[...], wo_ref[...]).astype(HALF)

        def finish(flow, i, total):
            hidden = m_ref[kept_rows(i), :] + total
            h2_ref[kept_rows(i), :] = hidden
            return norm_apply(hidden, gain_ref[1:2, :]).astype(HALF)

        head_total(part, n4_ref, inbox, rs, rr, gs, gr, where, heads, finish)

    def forward(
        in_ref, gain_ref, win_ref, kernel_ref, wout_ref, attn_gain_ref, up_hbm, down_hbm, seg_ref,
        wq_ref, wp_ref, cos_ref, sin_ref, qk_ref, wo_ref,
        x_ref, g_ref, n1_ref, pc_ref, edge_ref, y_ref, h1_ref, n2_ref, f1_ref, a1_ref, m_ref, n3_ref, same_ref, segq_ref,
        qr_ref, r_ref, q_ref, all_ref, o_ref, h2_ref, n4_ref, *rest,
    ):
        travel, rest = rest[-1], rest[:-1]
        split = len(conv_scratch)
        conv_forward(
            in_ref, gain_ref, win_ref, kernel_ref, wout_ref, attn_gain_ref, up_hbm, down_hbm, seg_ref,
            x_ref, g_ref, n1_ref, pc_ref, edge_ref, y_ref, h1_ref, n2_ref, f1_ref, a1_ref, m_ref, n3_ref,
            same_ref, segq_ref, *rest[:split], travel,
        )
        part = rest[part_at]
        attention_forward(
            n3_ref, wq_ref, wp_ref, cos_ref, sin_ref, qk_ref, segq_ref, seg_ref, wo_ref, m_ref, attn_gain_ref,
            qr_ref, r_ref, q_ref, all_ref, o_ref, h2_ref, n4_ref, *rest[split : split + 4], part, *rest[split + 4 :], travel,
        )

    conv_scratch = (
            [
                pltpu.VMEM((micro, rows, width), HALF),
                pltpu.VMEM((2, micro, 16, width), HALF),
                pltpu.VMEM((micro * 16, width), HALF),
                pltpu.VMEM((micro, 8 + rows, channels), FLOAT),
                dma(1),
                dma(1),
                dma(2),
                dma(2),
            ]
            + weight_scratch
            + [pltpu.VMEM((tokens, width), FLOAT)]
            + part_scratch
            + total_scratch
            + total_scratch
    )
    part_at = len(conv_scratch) - 2 * len(total_scratch) - 1
    (
        x, g, n1, projected, edge_gated, mixed, h1, n2, f1, a1, middle, n3, same, local_segments,
        query_raw, pair_raw, queries, all_pairs, attended, h2, n4,
    ) = call(
        forward,
        "forward",
        0,
        [
            ((tokens, width), HALF, LATE),
            ((tokens, width), HALF, LATE),
            ((tokens, width), HALF, LATE),
            ((3, tokens, channels), FLOAT, LATE),
            ((micro, 8, channels), FLOAT, LATE),
            ((tokens, channels), HALF, LATE),
            ((half_tokens, width), FLOAT, LATE),
            ((tokens, width), HALF, LATE),
            ((2, tokens, hidden_units), FLOAT, LATE),
            ((tokens, hidden_units), HALF, LATE),
            ((half_tokens, width), FLOAT, LATE),
            ((tokens, width), HALF, LATE),
            ((tokens, 2), FLOAT, LATE),
            ((tokens, 1), FLOAT, LATE),
            ((tokens, query_width), FLOAT, LATE),
            ((tokens, pair_width), FLOAT, LATE),
            ((tokens, query_width), HALF, LATE),
            ((slots, tokens, pair_width), HALF, LATE),
            ((tokens, query_width), HALF, LATE),
            ((half_tokens, width), FLOAT),
            ((tokens, width), HALF),
        ],
        conv_scratch + [dma(seqs - 1), dma(seqs - 1), dma(seqs), dma(seqs)] + total_scratch,
        [
            incoming, conv_gains, (w_in, LAZY), conv_kernel, (conv_out, LAZY), attn_gains,
            (first_up, ANY), (conv_down, ANY), segment_ids,
            (w_query, LAZY), (w_pair, LAZY), (cosine, LAZY), (sine, LAZY), qk_gains, (attn_out, LAZY),
        ],
        flops=9 * 10**9,
        moved=350 << 20,
    )

    def slab_width(start, count):
        return min(-(-count // tile_width) * tile_width, padded_units - start)

    def clear_padding(latter):
        if padded_units > hidden_units:
            latter[:, :, hidden_units:] = jnp.zeros((3, 2 * tokens, padded_units - hidden_units), HALF)

    def second_ffn(
        n4_ref, g_ref, h2_ref, gain_ref, up_hbm, down_hbm,
        py_ref, gh2_ref, low_ref, gg_ref, partial_hbm, first_in,
        acc_y, up_ref, down_ref, weight_sems, acc, given, former, latter, stage, hs, hr, ls, lr, local_sems, ts, tr,
        part, inbox, rs, rr, gs, gr, travel,
    ):
        where = place()
        s, q, h = where
        weights = weight_loads(up_hbm, down_hbm, up_ref, down_ref, weight_sems)
        start_all(weights)
        clear_padding(latter)
        met = greet([(1 - s, q, h)] + seq_peers(where, seqs), where, heads)
        halves = half_swaps([g_ref, n4_ref], [given.at[0], given.at[1]], hs, hr, where)
        gg_ref[...] = jnp.zeros_like(gg_ref)
        swaps = []
        for j, (start, count) in enumerate(slabs):
            wait_all(weights[3 * j : 3 * j + 3])
            span = slice(start, start + count)
            gate = back_product(n4_ref[...], up_ref[0, span, :])
            rise = back_product(n4_ref[...], up_ref[1, span, :])
            grad_active = back_product(g_ref[...], down_ref[span, :])
            chance = 1.0 / (1.0 + jnp.exp(-gate))
            silu = gate * chance
            active = (silu * rise).astype(HALF)
            grad_gate = (grad_active * rise * (chance * (1.0 + gate * (1.0 - chance)))).astype(HALF)
            grad_rise = (grad_active * silu).astype(HALF)
            latter[0, 0:tokens, span] = active
            latter[1, 0:tokens, span] = grad_gate
            latter[2, 0:tokens, span] = grad_rise
            if j == 0:
                met()
                start_all(halves)
            for kind in range(3):
                swap = latter_swap(
                    latter, kind, start, slab_width(start, count), ls.at[kind, j], lr.at[kind, j], where
                )
                swap.start()
                swaps.append(swap)
            term = product(grad_gate, up_ref[0, span, :]) + product(grad_rise, up_ref[1, span, :])
            term_y = product(active, down_ref[span, :])
            if j == 0:
                acc[...] = term
                acc_y[...] = term_y
            else:
                acc[...] += term
                acc_y[...] += term_y
        part[...] = acc[...].astype(HALF)

        travel.ready(h2_ref)
        for flow, holder in ((0, 0), (1, heads - 1)):

            @pl.when(h == holder)
            def _(flow=flow):
                acc_y[flow * half_tokens : (flow + 1) * half_tokens, :] += h2_ref[...]

        py_ref[...] = acc_y[...].astype(HALF)
        travel.leave(py_ref)
        tile, tiles_done = gradient_tiles(
            former, latter, stage, partial_hbm, first_in, local_sems, ts, tr, where, 2
        )

        def filler(t):
            for k, array_ref in enumerate((g_ref, n4_ref)):

                @pl.when(t == k)
                def _(k=k, array_ref=array_ref):
                    halves[k].wait()
                    if k:
                        wait_all(swaps)
                    former[k] = transposed(array_ref, given.at[k])

            @pl.when(t >= 2)
            def _():
                tile(t - 2)

        def finish(flow, i, total):
            grad_hidden, grad_gain = norm_back(h2_ref[kept_rows(i), :], gain_ref[1:2, :], total)
            grad = g_ref[own_rows(flow, i), :].astype(FLOAT) + grad_hidden
            gh2_ref[kept_rows(i), :] = grad
            gg_ref[...] += grad_gain
            return grad.astype(HALF)

        head_total(part, low_ref, inbox, rs, rr, gs, gr, where, heads, finish, filler, 3 * tiles + 2)
        tiles_done()

    (part_y, gh2, gh2_low, grad_gain_attn1, partial2, first2) = call(
        second_ffn,
        "second_ffn",
        4,
        [
            ((tokens, width), HALF, LATE),
            ((half_tokens, width), FLOAT),
            ((tokens, width), HALF),
            ((1, width), FLOAT),
        ]
        + partial_outs(2),
        [pltpu.VMEM((tokens, width), FLOAT)] + ffn_scratch + part_scratch + total_scratch,
        [n4, g, (h2, LAZY), attn_gains, (second_up, ANY), (attn_down, ANY)],
        flops=12 * 10**9,
        moved=150 << 20,
    )
    def attention_backward(
        glow_ref, wo_ref, q_ref, all_ref, segq_ref, seg_ref,
        qr_ref, r_ref, cos_ref, sin_ref, qk_ref, wq_ref, wp_ref, m_ref, gh2_ref, gain_ref, py_ref, n3_ref, o_ref, partial2_hbm, first2_hbm,
        low_ref, gg_ref, gqk_ref, yown_ref, stage0, stage1, in0, in1, second_in, first_in,
        bq_ref, br_ref, grads, totals, gq_ref, gp_ref, near_slots, pair_slots, ns, nr, ps, pr,
        passing, held, load_sems, vs, vr, fs, fr,
        ybox, ys, yr, given, former, latter0, latter1, hs, hr, ls, lr, ms, mr,
        part, inbox, rs, rr, gs, gr, travel,
    ):
        where = place()
        s, q, h = where
        partner = (1 - s, q, h)
        peers = seq_peers(where, seqs)
        loads = pass_loads(partial2_hbm, (0, 1), first2_hbm, passing, held, load_sems, where)
        loads += load_passing(partial2_hbm.at[2], passing.at[2], load_sems.at[2], where)
        start_all(loads)
        others = head_others(where)
        latters = [latter0, latter1]
        met = greet([partner] + peers + others, where, heads)
        grads[...] = back_product(glow_ref[...], wo_ref[...]).astype(HALF)
        met()
        later = first_stage(
            lambda dest, side: partial2_hbm.at[2, dest, half_rows(side)], lambda i: first_in.at[0, i], fs, fr, where
        )
        start_all(later)
        travel.ready(py_ref, n3_ref, o_ref)
        latter0[0:tokens, :] = o_ref[...]
        ysends = [
            remote(py_ref.at[rows_of(peer[2], small_rows)], ybox.at[n], ys.at[n], yr.at[n], peer)
            for n, peer in enumerate(others)
        ]
        start_all(ysends)
        halves = half_swaps([glow_ref, n3_ref], [given.at[0], given.at[1]], hs, hr, where)
        start_all(halves)
        swaps = latter_swaps(latters, ls, lr, partner)
        swaps[0].start()
        gg_ref[...] = jnp.zeros_like(gg_ref)
        gqk_ref[...] = jnp.zeros_like(gqk_ref)
        for m in range(micro):
            biases = [allowed_pairs(segq_ref, seg_ref, m, at, s, q) for at in range(m + 1)]
            results = []
            for c in range(kv_local):
                keys = [keys_of(all_ref, at, c, 0) for at in range(m + 1)]
                values = [keys_of(all_ref, at, c, 1) for at in range(m + 1)]
                rows_in = query_rows(q_ref, m, c) * HALF(score_scale)
                grad_rows = query_rows(grads, m, c)
                raised, inverse = probabilities(rows_in, keys, biases)
                chances = [part * inverse for part in raised]
                grad_chances = [back_product(grad_rows, value) for value in values]
                inner = functools.reduce(
                    jnp.add,
                    [jnp.sum(a * b, -1, keepdims=True) for a, b in zip(grad_chances, chances)],
                )
                total = None
                for at in range(m + 1):
                    grad_scores = (chances[at] * (grad_chances[at] - inner)).astype(HALF)
                    term = product(grad_scores, keys[at])
                    total = term if total is None else total + term
                    grad_key = outer_sum(grad_scores, rows_in)
                    grad_value = outer_sum(chances[at].astype(HALF), grad_rows)
                    if at == m:
                        totals[at, c] = grad_key
                        totals[at, kv_local + c] = grad_value
                    else:
                        totals[at, c] += grad_key
                        totals[at, kv_local + c] += grad_value
                total = total * score_scale
                results += [total[r * rows : (r + 1) * rows] for r in range(group)]
            gq_ref[m * rows : (m + 1) * rows, :] = jnp.concatenate(results, -1)
        for at in range(micro):
            joined = jnp.concatenate([totals[at, k] for k in range(2 * kv_local)], -1).astype(HALF)
            gp_ref[:, at * rows : (at + 1) * rows, :] = joined.reshape(slots, rows, pair_width)
        near = []
        for other in range(seqs):
            copy = remote(gp_ref.at[other * sections + 1 - s], near_slots.at[other], ns.at[other], nr.at[other], partner)
            copy.start()
            near.append(copy)
        copies = []
        wait_all(near)
        travel.ready(qr_ref, r_ref, cos_ref, sin_ref, wq_ref, wp_ref, m_ref, gh2_ref)
        for other in range(seqs):
            mine = gp_ref[other * sections + s].astype(FLOAT)
            near_slots[other] = (mine + near_slots[other].astype(FLOAT)).astype(HALF)
        for k, peer in enumerate(peers):
            copy = remote(near_slots.at[peer[1]], pair_slots.at[k], ps.at[k], pr.at[k], peer)
            copy.start()
            copies.append(copy)
        cos, sin = cos_ref[...], sin_ref[...]
        for start, size in chunks_of(query_width):
            span = slice(start, start + size)
            grad_raw, grad_gain = rotary_back(qr_ref[:, span], twice(qk_ref[0:1, :]), cos, sin, gq_ref[:, span])
            bq_ref[:, span] = grad_raw.astype(HALF)
            gqk_ref[0:1, :size] += grad_gain
        partial = back_product(bq_ref[...], wq_ref[...])
        wait_all(loads)
        travelling = pass_sends(2, passing, held, second_in, vs, vr, where)
        wait_all(copies)
        grad_pair = near_slots[q].astype(FLOAT)
        for j in range(seqs - 1):
            grad_pair = grad_pair + pair_slots[j].astype(FLOAT)
        half_pair = pair_width // 2
        for start, size in chunks_of(half_pair):
            span = slice(start, start + size)
            grad_raw, grad_gain = rotary_back(r_ref[:, span], twice(qk_ref[1:2, :]), cos, sin, grad_pair[:, span])
            br_ref[:, span] = grad_raw.astype(HALF)
            gqk_ref[1:2, :size] += grad_gain
        br_ref[:, half_pair:] = grad_pair[:, half_pair:].astype(HALF)
        wait_all(later)
        combine(lambda i: passing.at[2, i], first_in.at[0], where)
        turning = second_stage(lambda i: passing.at[2, i], second_in.at[2], vs.at[2], vr.at[2], where)
        start_all(turning)
        travelling += turning
        travel.leave(first_in)
        latter1[0:tokens, 0:query_width] = bq_ref[...]
        latter1[0:tokens, query_width:] = br_ref[...]
        swaps[1].start()
        part[...] = (partial + back_product(br_ref[...], wp_ref[...])).astype(HALF)
        wait_all(ysends)
        produced = py_ref[rows_of(h, small_rows), :].astype(FLOAT)
        for n in range(heads - 1):
            produced = produced + ybox[n].astype(FLOAT)
        yown_ref[...] = produced.astype(HALF)
        sends = mixer_sends([stage0, stage1], [in0, in1], ms, mr, where)
        mixer_step = mixer_steps([glow_ref, n3_ref], latters, [stage0, stage1], given, former, halves, swaps, sends)

        def finish(flow, i, total):
            grad_entry, grad_gain = norm_back(m_ref[kept_rows(i), :], gain_ref[0:1, :], total)
            gg_ref[...] += grad_gain
            return (gh2_ref[kept_rows(i), :] + grad_entry).astype(HALF)

        head_total(part, low_ref, inbox, rs, rr, gs, gr, where, heads, finish, mixer_step, 4)
        for copies in sends:
            wait_all(copies)
        wait_all(travelling)

    (gm_low, grad_gain_attn0, grad_qk, y_own, stage0, stage1, in0, in1, second2, first2_last) = call(
        attention_backward,
        "attention_backward",
        5,
        [
            ((tokens, width), HALF),
            ((1, width), FLOAT),
            ((8, 128), FLOAT),
            ((small_rows, width), HALF),
            ((seqs, share, widths[0]), HALF),
            ((seqs, share, widths[1]), HALF),
            *first_sums(widths[:2]),
            second_shape(3),
            ((1, first_blocks, half_share, padded_units), HALF, LATE),
        ],
        [
            pltpu.VMEM((tokens, query_width), HALF),
            pltpu.VMEM((tokens, pair_width), HALF),
            pltpu.VMEM((tokens, query_width), HALF),
            pltpu.VMEM((micro, 2 * kv_local, block_tok, head_width), FLOAT),
            pltpu.VMEM((tokens, query_width), FLOAT),
            pltpu.VMEM((slots, tokens, pair_width), HALF),
            pltpu.VMEM((seqs, tokens, pair_width), HALF),
            pltpu.VMEM((seqs - 1, tokens, pair_width), HALF),
            dma(seqs),
            dma(seqs),
            dma(seqs - 1),
            dma(seqs - 1),
        ]
        + passing_scratch(3)
        + [dma(first_blocks), dma(first_blocks)]
        + [
            pltpu.VMEM((heads - 1, small_rows, width), HALF),
            dma(heads - 1),
            dma(heads - 1),
            pltpu.VMEM((2, tokens, half_model), HALF),
            pltpu.VMEM((half_model, 2 * tokens), HALF),
            pltpu.VMEM((2 * tokens, widths[0]), HALF),
            pltpu.VMEM((2 * tokens, widths[1]), HALF),
            dma(2),
            dma(2),
            dma(2),
            dma(2),
            dma_grid(2, first_blocks),
            dma_grid(2, first_blocks),
        ]
        + part_scratch
        + total_scratch,
        [
            gh2_low, attn_out, queries, all_pairs, local_segments, segment_ids,
            (query_raw, LAZY), (pair_raw, LAZY), (cosine, LAZY), (sine, LAZY), qk_gains,
            (w_query, LAZY), (w_pair, LAZY), (middle, LAZY), (gh2, LAZY), attn_gains,
            (part_y, LAZY), (n3, LAZY), (attended, LAZY), (partial2, ANY), (first2, ANY),
        ],
        flops=6 * 10**9,
        moved=130 << 20,
    )

    def first_ffn_back(
        gm_ref, n2_ref, f1_ref, a1_ref, h1_ref, gain_ref, yown_ref, stage0, stage1, in0, in1, up_hbm, down_hbm,
        gh1_ref, low_ref, gg_ref, yout_ref, turn0, turn1, partial_hbm, first_in,
        up_ref, down_ref, weight_sems, acc, given, former, latter, stage, hs, hr, ls, lr, local_sems, ts, tr,
        ys, yr, pass0, pass1, us, ur,
        part, inbox, rs, rr, gs, gr, travel,
    ):
        where = place()
        s, q, h = where
        weights = weight_loads(up_hbm, down_hbm, up_ref, down_ref, weight_sems)
        start_all(weights)
        clear_padding(latter)
        others = head_others(where)
        own_y = rows_of(h, small_rows)
        met = greet([(1 - s, q, h)] + seq_peers(where, seqs) + others, where, heads)
        travel.ready(yown_ref, n2_ref, a1_ref)
        yout_ref[own_y, :] = yown_ref[...]
        latter[0, 0:tokens, 0:hidden_units] = a1_ref[...]
        travel.ready(stage0, stage1, in0, in1)
        turning = mixer_second([stage0, stage1], [in0, in1], [pass0, pass1], [turn0, turn1], us, ur, where)
        met()
        for copies in turning:
            start_all(copies)
        ysends = [
            remote(yout_ref.at[own_y], yout_ref.at[own_y], ys.at[n], yr.at[n], peer) for n, peer in enumerate(others)
        ]
        start_all(ysends)
        halves = half_swaps([gm_ref, n2_ref], [given.at[0], given.at[1]], hs, hr, where)
        start_all(halves)
        gg_ref[...] = jnp.zeros_like(gg_ref)
        tile, tiles_done = gradient_tiles(
            former, latter, stage, partial_hbm, first_in, local_sems, ts, tr, where, 3
        )
        active_swaps = [
            latter_swap(latter, 0, start, slab_width(start, count), ls.at[0, j], lr.at[0, j], where)
            for j, (start, count) in enumerate(slabs)
        ]
        start_all(active_swaps)
        halves[0].wait()
        former[0] = transposed(gm_ref, given.at[0])
        wait_all(active_swaps)
        loop(tiles, tile)
        swaps = []
        travel.ready(f1_ref, h1_ref)
        for j, (start, count) in enumerate(slabs):
            wait_all(weights[3 * j : 3 * j + 3])
            span = slice(start, start + count)
            gate = f1_ref[0, :, span]
            rise = f1_ref[1, :, span]
            grad_active = back_product(gm_ref[...], down_ref[span, :])
            chance = 1.0 / (1.0 + jnp.exp(-gate))
            grad_gate = (grad_active * rise * (chance * (1.0 + gate * (1.0 - chance)))).astype(HALF)
            grad_rise = (grad_active * (gate * chance)).astype(HALF)
            latter[1, 0:tokens, span] = grad_gate
            latter[2, 0:tokens, span] = grad_rise
            for kind in range(1, 3):
                swap = latter_swap(
                    latter, kind, start, slab_width(start, count), ls.at[kind, j], lr.at[kind, j], where
                )
                swap.start()
                swaps.append(swap)
            term = product(grad_gate, up_ref[0, span, :]) + product(grad_rise, up_ref[1, span, :])
            if j == 0:
                acc[...] = term
            else:
                acc[...] += term
        part[...] = acc[...].astype(HALF)
        def filler(t):
            @pl.when(t == 0)
            def _():
                halves[1].wait()
                wait_all(swaps)
                former[1] = transposed(n2_ref, given.at[1])

            @pl.when(t >= 1)
            def _():
                tile(tiles + t - 1)

        def finish(flow, i, total):
            grad_hidden, grad_gain = norm_back(h1_ref[kept_rows(i), :], gain_ref[1:2, :], total)
            gg_ref[...] += grad_gain
            grad = gm_ref[own_rows(flow, i), :].astype(FLOAT) + grad_hidden
            gh1_ref[kept_rows(i), :] = grad
            return grad.astype(HALF)

        head_total(part, low_ref, inbox, rs, rr, gs, gr, where, heads, finish, filler, 2 * tiles + 1)
        tiles_done()
        wait_all(ysends)
        for copies in turning:
            wait_all(copies)

    (gh1, gh1_low, grad_gain_conv1, yout, turn0, turn1, partial1, first1) = call(
        first_ffn_back,
        "first_ffn_back",
        6,
        [((half_tokens, width), FLOAT), ((tokens, width), HALF), ((1, width), FLOAT), ((tokens, width), HALF)]
        + [((grid_rows, half_share, size), HALF) for size in widths[:2]]
        + partial_outs(3),
        ffn_scratch + [dma(heads - 1), dma(heads - 1)]
        + [pltpu.VMEM((grid_rows, half_share, size), HALF) for size in widths[:2]]
        + [dma_grid(2, grid_rows), dma_grid(2, grid_rows)]
        + part_scratch + total_scratch,
        [gm_low, (n2, LAZY), (f1, LAZY), (a1, LAZY), (h1, LAZY), conv_gains, (y_own, LAZY),
         (stage0, LAZY), (stage1, LAZY), (in0, LAZY), (in1, LAZY), (first_up, ANY), (conv_down, ANY)],
        flops=9 * 10**9,
        moved=150 << 20,
    )
    small_width = max(share, channels, 2 * head_width)

    def conv_backward(
        low_ref, gh1_ref, pc_ref, edge_ref, same_ref, kernel_ref, wout_ref, win_ref, x_ref, gain_ref, yout_ref,
        n1_ref, mixed_ref, stage0, stage1, in0, in1, turn0, turn1, gain1_ref, gain2_ref, gain3_ref, gqk_ref,
        partial1, partial2, first1, first2, first2_last, second2,
        edges_ref, sums_ref, gout2_ref, gmix_ref, gout1_ref, gin_ref, gdown2, gup2, gdown1, gup1,
        bp_ref, ext, spread, gz_ext, outgoing, arrived, full, gg_ref, edge_send, edge_recv, swap_send, swap_recv,
        given, former, latter2, latter3, stage2, stage3, in2, in3, turn2, turn3, hs, hr, ls, lr, ms, mr, us, ur,
        own_buf, first_buf, second_buf, passing, item_sems, vs, vr, down_stage, up_stage, out_sems,
        packed, boxes, summed, final, zs, zr, ss, sr,
        part, inbox, rs, rr, gs, gr, travel,
    ):
        where = place()
        s, q, h = where
        first = s == 0
        partner = (1 - s, q, h)
        preceding = (1 - s, jnp.where(first, lax.rem(q + seqs - 1, seqs), q), h)
        following = (1 - s, jnp.where(first, q, lax.rem(q + 1, seqs)), h)
        others = head_others(where)
        me = q * sections + s
        slot_peers = [slot_peer(me, j, h) for j in range(1, slots)]
        peers = seq_peers(where, seqs)
        latters, stages = [latter2, latter3], [stage0, stage1, stage2, stage3]
        incomes, turns = [in0, in1, in2, in3], [turn0, turn1, turn2, turn3]
        loads = []
        sources = [
            (partial2.at[0], first2.at[0], second2.at[0]),
            (partial2.at[1], first2.at[1], second2.at[1]),
            (partial2.at[2], first2_last.at[0], second2.at[2]),
            (partial1.at[0], first1.at[0], None),
            (partial1.at[1], first1.at[1], None),
            (partial1.at[2], first1.at[2], None),
        ]
        for n, (partial, arrived_hbm, passed_hbm) in enumerate(sources):
            copies = [pltpu.make_async_copy(partial.at[q], own_buf.at[n], item_sems.at[n, 0])]
            if arrived_hbm is not None:
                copies.append(pltpu.make_async_copy(arrived_hbm, first_buf.at[n], item_sems.at[n, 1]))
            if passed_hbm is not None:
                copies.append(pltpu.make_async_copy(passed_hbm, second_buf.at[n], item_sems.at[n, 2]))
            else:
                copies += load_passing(partial, passing.at[n - 3], item_sems.at[n, pl.ds(3, grid_rows)], where)
            loads.append(copies)
        for copies in loads[3:]:
            start_all(copies)
        travel.begin()
        for copies in loads[:3]:
            start_all(copies)
        met = greet([partner, preceding, following] + others + slot_peers, where, heads)
        bulk = []

        def pass_item(n):
            wait_all(loads[n])
            combine(lambda i: passing.at[n - 3, i], first_buf.at[n], where)
            sends = second_stage(
                lambda i: passing.at[n - 3, i], second_buf.at[n], vs.at[n - 3], vr.at[n - 3], where
            )
            start_all(sends)
            bulk.append(sends)

        gg_ref[...] = jnp.zeros_like(gg_ref)
        gated = pc_ref[0] * pc_ref[2]
        grad_y = back_product(low_ref[...], wout_ref[...])
        gz = grad_y * pc_ref[1]
        zero = jnp.zeros((8, channels), FLOAT)
        for m in range(micro):
            span = slice(m * rows, (m + 1) * rows)
            one = jnp.where(same_ref[span, 0:1] > 0, gz[span], 0.0) * kernel_ref[1:2, :]
            two = jnp.where(same_ref[span, 1:2] > 0, gz[span], 0.0) * kernel_ref[0:1, :]
            gz_ext[0, m, 0:rows, :] = one
            gz_ext[0, m, rows : rows + 8, :] = zero
            gz_ext[1, m, 0:rows, :] = two
            gz_ext[1, m, rows : rows + 8, :] = zero
            outgoing[m] = zero
            outgoing[m, 0:1, :] = two[0:1]
            outgoing[m, 1:2, :] = one[0:1] + two[1:2]
        met()
        edge = remote(outgoing, arrived, edge_send.at[0], edge_recv.at[0], preceding)
        edge.start()
        for n in (3, 4, 5):
            pass_item(n)
        travel.ready(n1_ref, mixed_ref)
        latter2[0:tokens, :] = mixed_ref[...]
        halves = half_swaps([low_ref, n1_ref], [given.at[0], given.at[1]], hs, hr, where)
        start_all(halves)
        swaps = latter_swaps(latters, ls, lr, partner)
        swaps[0].start()
        taps = [None, None, None]
        for m in range(micro):
            span = slice(m * rows, (m + 1) * rows)
            ext[m, 0:8, :] = edge_ref[m]
            ext[m, 8 : 8 + rows, :] = gated[span]
            back_one = jnp.where(same_ref[span, 0:1] > 0, shifted_rows(ext, m, 1), 0.0)
            back_two = jnp.where(same_ref[span, 1:2] > 0, shifted_rows(ext, m, 2), 0.0)
            mixed = (
                kernel_ref[2:3, :] * gated[span]
                + kernel_ref[1:2, :] * back_one
                + kernel_ref[0:1, :] * back_two
            )
            bp_ref[span, channels : 2 * channels] = (grad_y[span] * mixed).astype(HALF)
            for k, value in enumerate((back_two, back_one, gated[span])):
                term = jnp.sum(value * gz[span], 0, keepdims=True)
                taps[k] = term if taps[k] is None else taps[k] + term
        for m in range(micro):
            span = slice(m * rows, (m + 1) * rows)
            spread[m] = (
                kernel_ref[2:3, :] * gz[span]
                + gz_ext[0, m, 1 : rows + 1, :]
                + gz_ext[1, m, 2 : rows + 2, :]
            )
        edge.wait()
        wrap = (s == sections - 1) & (q == seqs - 1)
        for m in range(micro):
            follow = arrived[m + 1, 0:2, :] if m + 1 < micro else jnp.zeros((2, channels), FLOAT)
            spread[m, rows - 2 : rows, :] += jnp.where(wrap, follow, arrived[m, 0:2, :])
        for m in range(micro):
            span = slice(m * rows, (m + 1) * rows)
            bp_ref[span, 0:channels] = (spread[m] * pc_ref[2, span, :]).astype(HALF)
            bp_ref[span, 2 * channels :] = (spread[m] * pc_ref[0, span, :]).astype(HALF)
        latter3[0:tokens, :] = bp_ref[...]
        swaps[1].start()
        travel.ready(win_ref, x_ref, gh1_ref, yout_ref)
        total = back_product(bp_ref[:, 0:channels], win_ref[0])
        total = total + back_product(bp_ref[:, channels : 2 * channels], win_ref[1])
        total = total + back_product(bp_ref[:, 2 * channels :], win_ref[2])
        part[...] = total.astype(HALF)

        def finish(flow, i, total):
            start = x_ref[own_rows(flow, i), :].astype(FLOAT)
            grad_start, grad_gain = norm_back(start, gain_ref[0:1, :], total)
            gg_ref[...] += grad_gain
            return (gh1_ref[kept_rows(i), :] + grad_start).astype(HALF)

        sent = mixer_sends(stages[2:], incomes[2:], ms, mr, where)
        mixer_step = mixer_steps([low_ref, n1_ref], latters, stages[2:], given, former, halves, swaps, sent)
        head_total(part, full, inbox, rs, rr, gs, gr, where, heads, finish, mixer_step, 4)
        keep = pl.ds(pl.multiple_of(s * rows, rows), rows)
        edges_ref[0, :, keep, :] = jnp.where(first, full[...], yout_ref[...]).reshape(micro, rows, width)
        part[...] = jnp.where(first, yout_ref[...], full[...])
        edge_swaps = []
        for m in range(micro):
            copy = remote(
                part.at[m * rows : (m + 1) * rows], edges_ref.at[0, m, keep], swap_send.at[m], swap_recv.at[m], partner
            )
            copy.start()
            edge_swaps.append(copy)
        packed[...] = jnp.zeros_like(packed)
        folded = [gqk_ref[n : n + 1, 0:head_width] + gqk_ref[n : n + 1, head_width : 2 * head_width] for n in range(2)]
        folded = jnp.concatenate(folded, -1)
        packed[:, 5:8, 0:channels] = jnp.broadcast_to(jnp.concatenate(taps, 0)[None], (slots, 3, channels))
        for d in range(slots):
            for n, rows_in in enumerate((gg_ref, gain1_ref, gain2_ref, gain3_ref)):
                packed[d, n : n + 1, 0:share] = rows_in[:, d * share : (d + 1) * share]
            packed[d, 4:5, 0 : 2 * head_width] = folded
        over = []
        for k, peer in enumerate(others):
            copy = remote(packed, boxes.at[k], zs.at[k], zr.at[k], peer)
            copy.start()
            over.append(copy)
        wait_all(over)
        over_heads = boxes[0]
        for j in range(1, heads - 1):
            over_heads = over_heads + boxes[j]
        row = lax.broadcasted_iota(jnp.int32, over_heads.shape, 1)
        summed[...] = packed[...] + jnp.where(row < 5, over_heads, 0.0)
        across = []
        for j, peer in enumerate(slot_peers):
            copy = remote(summed.at[peer[0] * seqs + peer[1]], final.at[j], ss.at[j], sr.at[j], peer)
            copy.start()
            across.append(copy)
        outs = []

        def leave(source, target, at):
            copy = pltpu.make_async_copy(source, target, out_sems.at[at])
            copy.start()
            outs.append(copy)

        def fill_stage(n, target):
            upper, lower = two_halves(own_buf.at[n], first_buf.at[n], second_buf.at[n], where)
            target[half_rows(0), :] = upper[:, :hidden_units].astype(HALF)
            target[half_rows(1), :] = lower[:, :hidden_units].astype(HALF)

        def second_half_items():
            for n in range(3):
                wait_all(loads[n])
            fill_stage(0, down_stage.at[0])
            leave(down_stage.at[0], gdown2, 0)
            for kind in range(2):
                fill_stage(1 + kind, up_stage.at[0, kind])
            leave(up_stage.at[0], gup2, 1)

        for copies in sent:
            wait_all(copies)
        mixer_turns = mixer_second(stages[2:], incomes[2:], [None, None], turns[2:], us, ur, where)
        for copies in mixer_turns:
            start_all(copies)
        travel.ready(stage0, stage1, in0, in1, turn0, turn1)
        second_half_items()
        for n in (3, 4, 5):
            wait_all(bulk[n - 3])
            if n == 3:
                fill_stage(3, down_stage.at[1])
                leave(down_stage.at[1], gdown1, 2)
            else:
                fill_stage(n, up_stage.at[1, n - 4])
        leave(up_stage.at[1], gup1, 3)
        wait_all(edge_swaps)
        wait_all(across)
        total = summed[s * seqs + q]
        for j in range(slots - 1):
            total = total + final[j]
        sums_ref[...] = total
        for k, target in enumerate((gout2_ref, gmix_ref, gout1_ref, None)):
            if k >= 2:
                wait_all(mixer_turns[k - 2])
            for side, value in enumerate(two_halves(stages[k].at[q], incomes[k], turns[k], where)):
                value = value.astype(HALF)
                if target is None:
                    for c in range(3):
                        gin_ref[c, half_rows(side), :] = value[:, c * channels : (c + 1) * channels]
                else:
                    target[half_rows(side), :] = value
        wait_all(outs)

    (section_edges, sums, gout2, gmix, gout1, gin, gdown2, gup2, gdown1, gup1) = call(
        conv_backward,
        "conv_backward",
        7,
        [
            ((1, micro, local_rows, width), HALF),
            ((8, small_width), FLOAT),
            ((share, widths[0]), HALF),
            ((share, widths[1]), HALF),
            ((share, widths[2]), HALF),
            ((3, share, channels), HALF),
            ((share, hidden_units), HALF, ANY),
            ((2, share, hidden_units), HALF, ANY),
            ((share, hidden_units), HALF, ANY),
            ((2, share, hidden_units), HALF, ANY),
        ],
        [
            pltpu.VMEM((tokens, 3 * channels), HALF),
            pltpu.VMEM((micro, 8 + rows, channels), FLOAT),
            pltpu.VMEM((micro, rows, channels), FLOAT),
            pltpu.VMEM((2, micro, rows + 8, channels), FLOAT),
            pltpu.VMEM((micro, 8, channels), FLOAT),
            pltpu.VMEM((micro, 8, channels), FLOAT),
            pltpu.VMEM((tokens, width), HALF),
            pltpu.VMEM((1, width), FLOAT),
            dma(1),
            dma(1),
            dma(micro),
            dma(micro),
            pltpu.VMEM((2, tokens, half_model), HALF),
            pltpu.VMEM((half_model, 2 * tokens), HALF),
        ]
        + [pltpu.VMEM((2 * tokens, size), HALF) for size in widths[2:]]
        + [pltpu.VMEM((seqs, share, size), HALF) for size in widths[2:]]
        + [pltpu.VMEM((first_blocks, half_share, size), HALF) for size in widths[2:]]
        + [pltpu.VMEM((grid_rows, half_share, size), HALF) for size in widths[2:]]
        + [
            dma(2),
            dma(2),
            dma(2),
            dma(2),
            dma_grid(2, first_blocks),
            dma_grid(2, first_blocks),
            dma_grid(2, grid_rows),
            dma_grid(2, grid_rows),
            pltpu.VMEM((6, share, padded_units), HALF),
            pltpu.VMEM((6, first_blocks, half_share, padded_units), HALF),
            pltpu.VMEM((6, grid_rows, half_share, padded_units), HALF),
            pltpu.VMEM((3, grid_rows, half_share, padded_units), HALF),
            dma_grid(6, 3 + grid_rows),
            dma_grid(3, grid_rows),
            dma_grid(3, grid_rows),
            pltpu.VMEM((2, share, hidden_units), HALF),
            pltpu.VMEM((2, 2, share, hidden_units), HALF),
            dma(4),
            pltpu.VMEM((slots, 8, small_width), FLOAT),
            pltpu.VMEM((heads - 1, slots, 8, small_width), FLOAT),
            pltpu.VMEM((slots, 8, small_width), FLOAT),
            pltpu.VMEM((slots - 1, 8, small_width), FLOAT),
            dma(heads - 1),
            dma(heads - 1),
            dma(slots - 1),
            dma(slots - 1),
        ]
        + part_scratch
        + total_scratch,
        [
            gh1_low, (gh1, LAZY), projected, edge_gated, same, conv_kernel, conv_out, (w_in, LAZY), (x, LAZY), conv_gains,
            (yout, LAZY), (n1, LAZY), (mixed, LAZY), (stage0, LAZY), (stage1, LAZY), (in0, LAZY), (in1, LAZY), (turn0, LAZY), (turn1, LAZY),
            grad_gain_conv1, grad_gain_attn0, grad_gain_attn1, grad_qk,
        ]
        + [(array, ANY) for array in (partial1, partial2, first1, first2, first2_last, second2)],
        flops=5 * 10**9,
        moved=300 << 20,
        begin=False,
    )
    def results(
        edges_in, sums_in, gout2_in, gmix_in, gout1_in, gin_in, gdown2_in, gup2_in, gdown1_in, gup1_in,
        edges_out, cgain_out, gin_out, taps_out, gout1_out, gup1_out, gdown1_out,
        again_out, gq_out, gkv_out, gqk_out, gout2_out, gup2_out, gdown2_out,
        down_in, up_in, down_stage, up_stage, edges_held, in_sems, out_sems, edge_sem, travel,
    ):
        edges_load = pltpu.make_async_copy(edges_in, edges_held, edge_sem.at[0])
        edges_load.start()
        loads = [
            pltpu.make_async_copy(source, target, in_sems.at[k])
            for k, (source, target) in enumerate(
                [(gdown1_in, down_in.at[0]), (gup1_in, up_in.at[0]), (gdown2_in, down_in.at[1]), (gup2_in, up_in.at[1])]
            )
        ]
        start_all(loads)
        stores = []
        for k, (down_out, up_out) in enumerate(((gdown1_out, gup1_out), (gdown2_out, gup2_out))):
            loads[2 * k].wait()
            down_stage[k] = down_in[k].astype(FLOAT)
            stores.append(pltpu.make_async_copy(down_stage.at[k], down_out, out_sems.at[2 * k]))
            stores[-1].start()
            loads[2 * k + 1].wait()
            for kind in range(2):
                up_stage[k, :, kind, :] = up_in[k, kind].astype(FLOAT)
            stores.append(pltpu.make_async_copy(up_stage.at[k], up_out, out_sems.at[2 * k + 1]))
            stores[-1].start()
        cgain_out[...] = sums_in[0:2, 0:share]
        again_out[...] = sums_in[2:4, 0:share]
        taps_out[...] = sums_in[5:8, 0:channels]
        for kind in range(2):
            gqk_out[kind : kind + 1, :] = sums_in[4:5, kind * head_width : (kind + 1) * head_width]
            start = query_width + kind * (pair_width // 2)
            gkv_out[:, kind, :] = gmix_in[:, start : start + pair_width // 2].astype(FLOAT)
        gq_out[...] = gmix_in[:, 0:query_width].astype(FLOAT)
        gout1_out[...] = gout1_in[...].astype(FLOAT)
        gout2_out[...] = gout2_in[...].astype(FLOAT)
        gin_out[...] = gin_in[...].astype(FLOAT)
        edges_load.wait()
        stores.append(pltpu.make_async_copy(edges_held, edges_out, edge_sem.at[1]))
        stores[-1].start()
        wait_all(stores)

    (
        section_edges, cgain, gin, taps, gout1, gup1, gdown1, again, gq, gkv, gqk, gout2, gup2, gdown2,
    ) = call(
        results,
        "results",
        None,
        [
            ((1, micro, local_rows, width), HALF, ANY),
            ((2, share), FLOAT),
            ((3, share, channels), FLOAT),
            ((3, channels), FLOAT),
            ((share, channels), FLOAT),
            ((share, 2, hidden_units), FLOAT, ANY),
            ((share, hidden_units), FLOAT, ANY),
            ((2, share), FLOAT),
            ((share, query_width), FLOAT),
            ((share, 2, pair_width // 2), FLOAT),
            ((2, head_width), FLOAT),
            ((share, query_width), FLOAT),
            ((share, 2, hidden_units), FLOAT, ANY),
            ((share, hidden_units), FLOAT, ANY),
        ],
        [
            pltpu.VMEM((2, share, hidden_units), HALF),
            pltpu.VMEM((2, 2, share, hidden_units), HALF),
            pltpu.VMEM((2, share, hidden_units), FLOAT),
            pltpu.VMEM((2, share, 2, hidden_units), FLOAT),
            pltpu.VMEM((1, micro, local_rows, width), HALF),
            dma(4),
            dma(4),
            dma(2),
        ],
        [(section_edges, ANY), sums, gout2, gmix, gout1, gin]
        + [(array, ANY) for array in (gdown2, gup2, gdown1, gup1)],
        moved=25 << 20,
    )
    return (
        section_edges,
        cgain,
        gin.transpose(1, 0, 2),
        taps,
        gout1.T,
        gup1,
        gdown1.T,
        again,
        gq,
        gkv,
        gqk,
        gout2.T,
        gup2,
        gdown2.T,
    )


def solution(mesh):
    return jax.shard_map(
        per_device,
        mesh=mesh,
        in_specs=(
            P("section", None, "seq", None),
            P(),
            P(None, "seq"),
            P(),
            P(None, None, "head"),
            P(None, "head"),
            P("head", None),
            P(None, None, "head"),
            P("head", None),
            P(),
            P(None, "head"),
            P(None, None, "head"),
            P(),
            P("head", None),
            P(None, None, "head"),
            P("head", None),
        ),
        out_specs=(
            P("section", None, "seq", None),
            P(None, ("section", "seq")),
            P(("section", "seq"), None, "head"),
            P(None, "head"),
            P("head", ("section", "seq")),
            P(("section", "seq"), None, "head"),
            P("head", ("section", "seq")),
            P(None, ("section", "seq")),
            P(("section", "seq"), "head"),
            P(("section", "seq"), None, "head"),
            P(),
            P("head", ("section", "seq")),
            P(("section", "seq"), None, "head"),
            P("head", ("section", "seq")),
        ),
        check_vma=False,
    )
```

```python
import functools

import jax
import jax.numpy as jnp
from jax import lax
from jax.experimental import pallas as pl
from jax.experimental.pallas import tpu as pltpu
from jax.sharding import PartitionSpec as P

EPS = 1e-05
THETA = 1000000.0
FLOAT = jnp.float32
HALF = jnp.bfloat16
MESH = pl.DeviceIdType.MESH
VMEM = pl.BlockSpec(memory_space=pltpu.VMEM)
ANY = pl.BlockSpec(memory_space=pl.ANY)


def product(former, latter):
    return jnp.dot(former, latter, preferred_element_type=FLOAT)


def outer_sum(former, latter):
    return lax.dot_general(former, latter, (((0,), (0,)), ((), ())), preferred_element_type=FLOAT)


def back_product(former, latter):
    return lax.dot_general(former, latter, (((1,), (1,)), ((), ())), preferred_element_type=FLOAT)


def norm_apply(values, gain):
    return values * lax.rsqrt(jnp.mean(values * values, -1, keepdims=True) + EPS) * gain


def norm_back(values, gain, grad):
    scale = lax.rsqrt(jnp.mean(values * values, -1, keepdims=True) + EPS)
    weighted = grad * gain
    inner = jnp.mean(weighted * values, -1, keepdims=True)
    grad_values = scale * weighted - values * (scale * scale * scale * inner)
    return grad_values, jnp.sum(grad * values * scale, 0, keepdims=True)


BLOCKS = 8
LAG = 3
END_FIRST = 10
MIDDLE_FIRST = 3


def place():
    return lax.axis_index("section"), lax.axis_index("seq"), lax.axis_index("head")


def remote(source, target, send, recv, peer):
    return pltpu.make_async_remote_copy(
        src_ref=source,
        dst_ref=target,
        send_sem=send,
        recv_sem=recv,
        device_id=peer,
        device_id_type=MESH,
    )


def signal(peer):
    pl.semaphore_signal(pltpu.get_barrier_semaphore(), inc=1, device_id=peer, device_id_type=MESH)


def wait_greetings(count):
    pl.semaphore_wait(pltpu.get_barrier_semaphore(), count)


def greet(others, where, size):
    for peer in others:
        signal(peer)
    section, seq, head = where
    end = (head == 0) | (head == size - 1)

    @pl.when(end)
    def _():
        signal((section, seq, jnp.where(head == 0, 1, size - 2)))

    @pl.when(jnp.logical_not(end))
    def _():
        signal((section, seq, jnp.minimum(head + 1, size - 1)))
        signal((section, seq, jnp.maximum(head - 1, 0)))

    def met():
        @pl.when(end)
        def _():
            wait_greetings(len(others) + 1)

        @pl.when(jnp.logical_not(end))
        def _():
            wait_greetings(len(others) + 2)

    return met


def seq_peers(where, seqs):
    section, seq, head = where
    return [(section, lax.rem(seq + k, seqs), head) for k in range(1, seqs)]


def rows_of(index, count):
    return pl.ds(pl.multiple_of(index * count, count), count)


def wait_all(copies):
    for copy in copies:
        copy.wait()


def start_all(copies):
    for copy in copies:
        copy.start()


def loop(count, step):
    def body(i, carried):
        step(i)
        return carried

    lax.fori_loop(0, count, body, 0)


def head_total(part, full, inbox, reduce_send, reduce_recv, gather_send, gather_recv, where, size, finish, filler=None, fillers=0):
    section, seq, head = where
    count = part.shape[0] // (2 * BLOCKS)
    last = size - 1
    end = (head == 0) | (head == last)

    def rows(flow, i):
        return rows_of(flow * BLOCKS + i, count)

    def fill(t):
        if filler is not None:

            @pl.when(t < fillers)
            def _():
                filler(t)

    def fill_rest(start, stop=fillers):
        stop = min(stop, fillers)
        if stop > start:
            loop(stop - start, lambda i: filler(start + i))

    def reduced(flow, i, peer):
        return remote(part.at[rows(flow, i)], inbox.at[flow, i], reduce_send.at[flow, i], reduce_recv.at[flow, i], peer)

    def gathered(flow, i, peer):
        span = full.at[rows(flow, i)]
        return remote(span, span, gather_send.at[flow, i], gather_recv.at[flow, i], peer)

    @pl.when(end)
    def _():
        flow = jnp.where(head == 0, 0, 1)
        inner = (section, seq, jnp.where(head == 0, 1, last - 1))
        loop(BLOCKS, lambda i: reduced(1 - flow, i, inner).start())
        fill_rest(0, END_FIRST)

        def own(i):
            reduced(flow, i, inner).wait_recv()
            total = part[rows(flow, i), :].astype(FLOAT) + inbox[flow, i].astype(FLOAT)
            full[rows(flow, i), :] = finish(flow, i, total)
            gathered(flow, i, inner).start()
            fill(END_FIRST + i)

        loop(BLOCKS, own)
        fill_rest(END_FIRST + BLOCKS)

        def drain(i):
            gathered(1 - flow, i, inner).wait_recv()
            reduced(1 - flow, i, inner).wait_send()
            gathered(flow, i, inner).wait_send()

        loop(BLOCKS, drain)

    @pl.when(jnp.logical_not(end))
    def _():
        low = head < size // 2
        near = jnp.where(low, 1, 0)
        ahead = (section, seq, jnp.where(low, head + 1, head - 1))
        behind = (section, seq, jnp.where(low, head - 1, head + 1))

        def add(flow, i, peer):
            reduced(flow, i, peer).wait_recv()
            span = rows(flow, i)
            part[span, :] = (part[span, :].astype(FLOAT) + inbox[flow, i].astype(FLOAT)).astype(HALF)
            reduced(flow, i, peer).start()

        def forward(flow, i, peer):
            gathered(flow, i, peer).wait_recv()
            gathered(flow, i, peer).start()

        def lagged(act, first, second, at):
            def step(i):
                fill(at + i)

                @pl.when(i < BLOCKS)
                def _():
                    act(first, i, ahead)

                @pl.when(i >= LAG)
                def _():
                    act(second, i - LAG, behind)

            loop(BLOCKS + LAG, step)

        fill_rest(0, MIDDLE_FIRST)
        lagged(add, near, 1 - near, MIDDLE_FIRST)
        lagged(forward, 1 - near, near, MIDDLE_FIRST + BLOCKS + LAG)
        fill_rest(MIDDLE_FIRST + 2 * (BLOCKS + LAG))

        def drain(i):
            reduced(near, i, ahead).wait_send()
            reduced(1 - near, i, behind).wait_send()
            gathered(1 - near, i, ahead).wait_send()
            gathered(near, i, behind).wait_send()

        loop(BLOCKS, drain)


def turned(values):
    width = values.shape[-1]
    if width == 128:
        lane = lax.broadcasted_iota(jnp.int32, values.shape, 1)
        low = lax.rem(lane, 64) < 32
        return jnp.where(low, -pltpu.roll(values, 96, 1), pltpu.roll(values, 32, 1))
    parts = []
    for start in range(0, width, 64):
        parts += [-values[:, start + 32 : start + 64], values[:, start : start + 32]]
    return jnp.concatenate(parts, -1)


def head_mean(values):
    width = values.shape[-1]
    if width == 64:
        return jnp.mean(values, -1, keepdims=True)
    lane = lax.broadcasted_iota(jnp.int32, values.shape, 1)
    first = jnp.sum(jnp.where(lane < 64, values, 0.0), -1, keepdims=True)
    second = jnp.sum(jnp.where(lane < 64, 0.0, values), -1, keepdims=True)
    return jnp.where(lane < 64, first, second) * (1.0 / 64.0)


def chunks_of(width):
    return [(start, min(128, width - start)) for start in range(0, width, 128)]


def rotary(raw, gain, cosine, sine):
    width = raw.shape[-1]
    normed = raw * lax.rsqrt(head_mean(raw * raw) + EPS) * gain[:, :width]
    return normed * cosine[:, :width] + turned(normed) * sine[:, :width]


def rotary_back(raw, gain, cosine, sine, grad):
    width = raw.shape[-1]
    back = grad * cosine[:, :width] - turned(grad) * sine[:, :width]
    scale = lax.rsqrt(head_mean(raw * raw) + EPS)
    weighted = back * gain[:, :width]
    grad_raw = scale * weighted - raw * (scale * scale * scale * head_mean(weighted * raw))
    return grad_raw, jnp.sum(back * raw * scale, 0, keepdims=True)


LAZY = "lazy"
LATE = "late"


class Moves:
    def __init__(self, incoming, leaving):
        self.incoming, self.leaving, self.left, self.begun = incoming, leaving, [], []

    def begin(self, *refs):
        for known, copy in self.incoming:
            if not any(known is ref for ref in self.begun) and (not refs or any(known is ref for ref in refs)):
                copy.start()
                self.begun.append(known)

    def ready(self, *refs):
        for ref in refs:
            for known, copy in self.incoming:
                if known is ref:
                    copy.wait()

    def leave(self, *refs):
        for ref in refs:
            for known, copy in self.leaving:
                if known is ref:
                    copy.start()
                    self.left.append(copy)

    def finish(self):
        wait_all(self.left)


def call(body, name, collective, outs, scratch, args, flops=0, moved=0, begin=True):
    params = dict(vmem_limit_bytes=60 << 20)
    if collective is not None:
        params.update(collective_id=collective, has_side_effects=True)
    lazy = [n for n, arg in enumerate(args) if isinstance(arg, tuple) and arg[1] is LAZY]
    late = [n for n, out in enumerate(outs) if len(out) > 2 and out[2] is LATE]
    arrays = [arg[0] if isinstance(arg, tuple) else arg for arg in args]
    extra = [pltpu.VMEM(arrays[n].shape, arrays[n].dtype) for n in lazy]
    extra += [pltpu.VMEM(outs[n][0], outs[n][1]) for n in late]
    moves = len(lazy) + len(late)
    if moves:
        extra.append(pltpu.SemaphoreType.DMA((moves,)))

    def whole(*refs):
        refs = list(refs)
        held = refs[len(refs) - len(extra) :]
        refs = refs[: len(refs) - len(extra)]
        incoming, leaving = [], []
        for at, n in enumerate(lazy):
            incoming.append((held[at], pltpu.make_async_copy(refs[n], held[at], held[-1].at[at])))
            refs[n] = held[at]
        for at, n in enumerate(late):
            place_at = len(args) + n
            kept = held[len(lazy) + at]
            leaving.append((kept, pltpu.make_async_copy(kept, refs[place_at], held[-1].at[len(lazy) + at])))
            refs[place_at] = kept
        travel = Moves(incoming, leaving)
        if begin:
            travel.begin()
        body(*refs, travel)
        travel.finish()

    def spec(mark):
        return ANY if mark is LAZY or mark is LATE else mark

    results = pl.pallas_call(
        whole,
        name=name,
        out_shape=[jax.ShapeDtypeStruct(out[0], out[1]) for out in outs],
        in_specs=[spec(arg[1]) if isinstance(arg, tuple) else VMEM for arg in args],
        out_specs=[spec(out[2]) if len(out) > 2 else VMEM for out in outs],
        scratch_shapes=list(scratch) + extra,
        compiler_params=pltpu.CompilerParams(**params),
        cost_estimate=pl.CostEstimate(flops=flops, bytes_accessed=moved, transcendentals=0),
    )(*arrays)
    return list(results)


def dma(count):
    return pltpu.SemaphoreType.DMA((count,))


def per_device(
    incoming,
    segment_ids,
    positions,
    conv_gains,
    conv_in,
    conv_kernel,
    conv_out,
    conv_gate_up,
    conv_down,
    attn_gains,
    w_query,
    w_keyval,
    qk_gains,
    attn_out,
    attn_gate_up,
    attn_down,
):
    sections = lax.axis_size("section")
    seqs = lax.axis_size("seq")
    heads = lax.axis_size("head")
    section, seq, head = place()
    micro, local_rows, width = incoming.shape[1:]
    rows = local_rows // sections
    tokens = micro * rows
    half_tokens = tokens // 2
    step_rows = half_tokens // BLOCKS
    block_tok = segment_ids.shape[1]
    length = micro * block_tok
    slots = sections * seqs
    channels = conv_in.shape[2]
    hidden_units = conv_down.shape[0]
    head_width = qk_gains.shape[1]
    query_width = w_query.shape[1]
    pair_width = 2 * w_keyval.shape[2]
    kv_local = w_keyval.shape[2] // head_width
    group = query_width // (kv_local * head_width)
    score_scale = head_width ** (-0.5)
    half_model = width // sections
    share = width // (sections * seqs)

    pair_index = lax.broadcasted_iota(jnp.int32, (1, 2 * head_width), 1) % (head_width // 2)
    angle_rates = THETA ** (-2.0 * pair_index.astype(FLOAT) / head_width)
    local_positions = lax.dynamic_slice_in_dim(positions, section * rows, rows, 1).reshape(tokens)
    angles = local_positions.astype(FLOAT)[:, None] * angle_rates
    cosine, sine = jnp.cos(angles), jnp.sin(angles)
    w_in = conv_in.transpose(1, 0, 2)
    w_pair = w_keyval.reshape(width, pair_width)
    first_up = conv_gate_up.transpose(1, 2, 0)
    second_up = attn_gate_up.transpose(1, 2, 0)
    slabs = [(start, min(512, hidden_units - start)) for start in range(0, hidden_units, 512)]
    tile_width = 256
    tiles = -(-hidden_units // tile_width)
    padded_units = tiles * tile_width

    def own_column(seg_ref, m, back):
        start = lax.axis_index("seq") * local_rows + lax.axis_index("section") * rows - back
        wanted = start + lax.broadcasted_iota(jnp.int32, (rows, block_tok), 0)
        lane = lax.broadcasted_iota(jnp.int32, (rows, block_tok), 1)
        found = jnp.where(lane == wanted, seg_ref[m : m + 1, :].astype(FLOAT), 0.0)
        if back and m:
            found = found + jnp.where(lane == wanted + block_tok, seg_ref[m - 1 : m, :].astype(FLOAT), 0.0)
        elif back:
            found = found + jnp.where((wanted < 0) & (lane == 0), -1.0, 0.0)
        return jnp.sum(found, -1, keepdims=True)

    def twice(row):
        return jnp.concatenate([row, row], -1)

    def shifted_rows(ext, micro_at, back):
        return ext[micro_at, 8 - back : 8 - back + rows, :]

    def own_rows(flow, i):
        return rows_of(flow * BLOCKS + i, step_rows)

    def kept_rows(i):
        return rows_of(i, step_rows)

    total_scratch = [pltpu.VMEM((2, BLOCKS, step_rows, width), HALF)] + [
        pltpu.SemaphoreType.DMA((2, BLOCKS)) for _ in range(4)
    ]
    part_scratch = [pltpu.VMEM((tokens, width), HALF)]

    weight_scratch = [
        pltpu.VMEM((2, hidden_units, width), HALF),
        pltpu.VMEM((hidden_units, width), HALF),
        dma(3 * len(slabs)),
    ]

    def weight_loads(up_hbm, down_hbm, up_ref, down_ref, sems):
        copies = []
        for j, (start, count) in enumerate(slabs):
            span = slice(start, start + count)
            pairs = [(up_hbm.at[0, span], up_ref.at[0, span]), (up_hbm.at[1, span], up_ref.at[1, span])]
            pairs.append((down_hbm.at[span], down_ref.at[span]))
            for k, (source, target) in enumerate(pairs):
                copies.append(pltpu.make_async_copy(source, target, sems.at[3 * j + k]))
        return copies

    def conv_forward(
        in_ref, gain_ref, win_ref, kernel_ref, wout_ref, attn_gain_ref, up_hbm, down_hbm, seg_ref,
        x_ref, g_ref, n1_ref, pc_ref, edge_ref, y_ref, h1_ref, n2_ref, f1_ref, a1_ref, m_ref, n3_ref, same_ref, segq_ref,
        other, edges, normed_edges, ext, swap_send, swap_recv, edge_send, edge_recv, up_ref, down_ref, weight_sems, acc,
        part, inbox, rs, rr, gs, gr, inbox2, rs2, rr2, gs2, gr2, travel,
    ):
        where = place()
        s, q, h = where
        partner = (1 - s, q, h)
        following = (s, lax.rem(q + 1, seqs), h)
        preceding = (s, lax.rem(q + seqs - 1, seqs), h)
        weights = weight_loads(up_hbm, down_hbm, up_ref, down_ref, weight_sems)
        start_all(weights)
        met = greet([partner, following, preceding] + seq_peers(where, seqs), where, heads)
        for m in range(micro):
            span = slice(m * rows, (m + 1) * rows)
            column = own_column(seg_ref, m, 0)
            segq_ref[span, :] = column
            for back in (1, 2):
                same_ref[span, back - 1 : back] = jnp.where(column == own_column(seg_ref, m, back), 1.0, 0.0)
        travel.ready(in_ref)
        met()
        give = pl.multiple_of((1 - s) * rows, rows)
        swap = remote(in_ref.at[0, :, pl.ds(give, rows)], other, swap_send.at[0], swap_recv.at[0], partner)
        swap.start()
        near = remote(in_ref.at[0, :, rows - 16 : rows], edges.at[0], edge_send.at[0], edge_recv.at[0], partner)
        near.start()
        far = remote(
            in_ref.at[0, :, local_rows - 16 : local_rows], edges.at[1], edge_send.at[1], edge_recv.at[1], following
        )
        far.start()
        keep = pl.multiple_of(s * rows, rows)
        swap.wait()
        mine = in_ref[0, :, pl.ds(keep, rows), :].reshape(tokens, width)
        theirs = other[...].reshape(tokens, width)
        first = s == 0
        x = jnp.where(first, mine, theirs)
        x_ref[...] = x
        g_ref[...] = jnp.where(first, theirs, mine)
        n1_ref[...] = norm_apply(x.astype(FLOAT), gain_ref[0:1, :]).astype(HALF)
        near.wait()
        far.wait()
        for m in range(micro):
            before = edges[1, max(m - 1, 0)]
            far_edge = jnp.where(q == 0, before, edges[1, m])
            edge = jnp.where(first, far_edge, edges[0, m]).astype(FLOAT)
            normed_edges[m * 16 : (m + 1) * 16, :] = norm_apply(edge, gain_ref[0:1, :]).astype(HALF)
        travel.ready(win_ref)
        for k in range(3):
            pc_ref[k] = product(n1_ref[...], win_ref[k])
        edge_b = product(normed_edges[...], win_ref[0])
        edge_u = product(normed_edges[...], win_ref[2])
        edge_gated = edge_b * edge_u
        gated = pc_ref[0] * pc_ref[2]
        for m in range(micro):
            ext[m, 0:8, :] = edge_gated[m * 16 + 8 : m * 16 + 16, :]
            edge_ref[m] = edge_gated[m * 16 + 8 : m * 16 + 16, :]
            ext[m, 8 : 8 + rows, :] = gated[m * rows : (m + 1) * rows, :]
        for m in range(micro):
            span = slice(m * rows, (m + 1) * rows)
            mixed = (
                kernel_ref[2:3, :] * gated[span]
                + kernel_ref[1:2, :] * jnp.where(same_ref[span, 0:1] > 0, shifted_rows(ext, m, 1), 0.0)
                + kernel_ref[0:1, :] * jnp.where(same_ref[span, 1:2] > 0, shifted_rows(ext, m, 2), 0.0)
            )
            y_ref[span, :] = (pc_ref[1, span, :] * mixed).astype(HALF)
        travel.ready(wout_ref)
        part[...] = product(y_ref[...], wout_ref[...]).astype(HALF)
        travel.leave(x_ref, g_ref, n1_ref, pc_ref, edge_ref, y_ref, same_ref, segq_ref)

        def finish(flow, i, total):
            hidden = x_ref[own_rows(flow, i), :].astype(FLOAT) + total
            h1_ref[kept_rows(i), :] = hidden
            return norm_apply(hidden, gain_ref[1:2, :]).astype(HALF)

        head_total(part, n2_ref, inbox, rs, rr, gs, gr, where, heads, finish)
        travel.leave(h1_ref, n2_ref)
        for j, (start, count) in enumerate(slabs):
            wait_all(weights[3 * j : 3 * j + 3])
            span = slice(start, start + count)
            gate = back_product(n2_ref[...], up_ref[0, span, :])
            rise = back_product(n2_ref[...], up_ref[1, span, :])
            f1_ref[0, :, span] = gate
            f1_ref[1, :, span] = rise
            active = (gate / (1.0 + jnp.exp(-gate)) * rise).astype(HALF)
            a1_ref[:, span] = active
            term = product(active, down_ref[span, :])
            if j == 0:
                acc[...] = term
            else:
                acc[...] += term
        part[...] = acc[...].astype(HALF)
        travel.leave(f1_ref, a1_ref)

        def finish_middle(flow, i, total):
            middle = (h1_ref[kept_rows(i), :] + total).astype(HALF).astype(FLOAT)
            m_ref[kept_rows(i), :] = middle
            return norm_apply(middle, attn_gain_ref[0:1, :]).astype(HALF)

        head_total(part, n3_ref, inbox2, rs2, rr2, gs2, gr2, where, heads, finish_middle)
        travel.leave(m_ref, n3_ref)


    grid_rows = seqs // 2
    first_blocks = 3 * grid_rows - 2
    half_share = share // 2

    def grid_place(q):
        return lax.div(q, 2), lax.rem(q, 2)

    def first_stage(source, target, send, recv, where):
        s, q, h = where
        a, b = grid_place(q)
        copies = []
        for row in range(grid_rows):
            copies.append((source(row * 2 + 1 - b, 0), row, (s, a * 2 + 1 - b, h)))
        for k in range(1, grid_rows):
            row = lax.rem(a + k, grid_rows)
            for column in range(2):
                copies.append((source(row * 2 + column, 1), grid_rows + 2 * (k - 1) + column, (s, row * 2 + b, h)))
        return [remote(block, target(i), send.at[i], recv.at[i], peer) for block, i, peer in copies]

    def passed_blocks(where):
        s, q, h = where
        a, b = grid_place(q)
        blocks = []
        for k in range(1, grid_rows):
            row = lax.rem(a + k, grid_rows)
            blocks.append((row * 2 + b, 0, [row], (s, row * 2 + b, h)))
        arrived = [grid_rows + 2 * j + 1 - b for j in range(grid_rows - 1)]
        blocks.append((a * 2 + 1 - b, 1, arrived, (s, a * 2 + 1 - b, h)))
        return blocks

    def half_rows(side):
        return slice(side * half_share, (side + 1) * half_share)

    def combine(passing, arrived, where, own=None):
        for i, (_, _, sources, _) in enumerate(passed_blocks(where)):
            total = (passing if own is None else own)(i)[...].astype(FLOAT)
            for source in sources:
                total = total + arrived[source].astype(FLOAT)
            passing(i)[...] = total.astype(HALF)

    def second_stage(passing, target, send, recv, where):
        return [
            remote(passing(i), target.at[i], send.at[i], recv.at[i], peer)
            for i, (_, _, _, peer) in enumerate(passed_blocks(where))
        ]

    def load_passing(partial, passing, sems, where):
        return [
            pltpu.make_async_copy(partial.at[dest, half_rows(side)], passing.at[i], sems.at[i])
            for i, (dest, side, _, _) in enumerate(passed_blocks(where))
        ]

    def two_halves(own, arrived, passed, where):
        a, b = grid_place(where[1])
        upper = own[half_rows(0), :].astype(FLOAT) + arrived[a].astype(FLOAT)
        for k in range(grid_rows - 1):
            upper = upper + passed[k].astype(FLOAT)
        lower = own[half_rows(1), :].astype(FLOAT) + passed[grid_rows - 1].astype(FLOAT)
        for j in range(grid_rows - 1):
            lower = lower + arrived[grid_rows + 2 * j + b].astype(FLOAT)
        return upper, lower

    def dma_grid(*shape):
        return pltpu.SemaphoreType.DMA(shape)

    def first_shape(count):
        return ((count, first_blocks, half_share, padded_units), HALF, ANY)

    def second_shape(count):
        return ((count, grid_rows, half_share, padded_units), HALF, ANY)

    def passing_scratch(count):
        return [
            pltpu.VMEM((count, grid_rows, half_share, padded_units), HALF),
            pltpu.VMEM((count, first_blocks, half_share, padded_units), HALF),
            dma_grid(count, grid_rows + 1),
            dma_grid(count, grid_rows),
            dma_grid(count, grid_rows),
        ]

    def pass_loads(partial, kinds, arrived, passing, held, sems, where):
        copies = []
        for k, kind in enumerate(kinds):
            copies += load_passing(partial.at[kind], passing.at[k], sems.at[k], where)
            copies.append(pltpu.make_async_copy(arrived.at[k], held.at[k], sems.at[k, grid_rows]))
        return copies

    def pass_sends(count, passing, held, target, send, recv, where):
        copies = []
        for k in range(count):
            combine(lambda i, k=k: passing.at[k, i], held.at[k], where)
            sends = second_stage(lambda i, k=k: passing.at[k, i], target.at[k], send.at[k], recv.at[k], where)
            start_all(sends)
            copies += sends
        return copies

    small_rows = tokens // heads
    widths = [query_width, query_width + pair_width, channels, 3 * channels]

    def head_others(where):
        s, q, h = where
        return [(s, q, lax.rem(h + k, heads)) for k in range(1, heads)]

    def mixer_sends(stages, incomes, send, recv, where):
        return [
            first_stage(
                lambda dest, side, stage=stage: stage.at[dest, half_rows(side)],
                lambda i, income=income: income.at[i],
                send.at[k],
                recv.at[k],
                where,
            )
            for k, (stage, income) in enumerate(zip(stages, incomes))
        ]

    def mixer_steps(formers, latters, stages, given, former, halves, swaps, sends):
        def step(t):
            for k in range(len(formers)):

                @pl.when(t == 2 * k)
                def _(k=k):
                    halves[k].wait()
                    former[...] = transposed(formers[k], given.at[k])

                @pl.when(t == 2 * k + 1)
                def _(k=k):
                    swaps[k].wait()
                    result = product(former[...], latters[k][...]).astype(HALF)
                    stages[k][...] = result.reshape(seqs, share, result.shape[1])
                    start_all(sends[k])

        return step

    def mixer_second(stages, incomes, passes, turns, send, recv, where):
        blocks = passed_blocks(where)
        turning = []
        for k, (stage, income, passed, turn) in enumerate(zip(stages, incomes, passes, turns)):

            def own_block(i, stage=stage):
                return stage.at[blocks[i][0], half_rows(blocks[i][1])]

            def moved(i, stage=stage, passed=passed):
                return own_block(i, stage) if passed is None else passed.at[i]

            combine(moved, income, where, own_block)
            turning.append(second_stage(moved, turn, send.at[k], recv.at[k], where))
        return turning

    def latter_swaps(latters, send, recv, partner):
        return [
            remote(latter.at[0:tokens], latter.at[tokens : 2 * tokens], send.at[k], recv.at[k], partner)
            for k, latter in enumerate(latters)
        ]

    def first_sums(count):
        return [((first_blocks, half_share, size), HALF) for size in count]

    def transposed(array_ref, given_ref):
        start = pl.multiple_of(lax.axis_index("section") * half_model, 128)
        own = array_ref[:, pl.ds(start, half_model)]
        both = jnp.concatenate([own, given_ref[...]], 0)
        return both.astype(FLOAT).T.astype(HALF)

    def half_swaps(arrays, targets, send, recv, where):
        s, q, h = where
        copies = []
        for k, (array_ref, target) in enumerate(zip(arrays, targets)):
            start = pl.multiple_of((1 - s) * half_model, 128)
            copies.append(remote(array_ref.at[:, pl.ds(start, half_model)], target, send.at[k], recv.at[k], (1 - s, q, h)))
        return copies

    def latter_swap(latter, kind, start, count, send, recv, where):
        s, q, h = where
        return remote(
            latter.at[kind, 0:tokens, start : start + count],
            latter.at[kind, tokens : 2 * tokens, start : start + count],
            send,
            recv,
            (1 - s, q, h),
        )

    def gradient_tiles(former, latter, stage, partial_hbm, first_in, local_sems, send, recv, where, kinds):
        def split(t):
            kind = lax.div(t, tiles)
            at = lax.rem(t, tiles)
            return kind, pl.ds(pl.multiple_of(at * tile_width, tile_width), tile_width)

        def stored(t):
            kind, columns = split(t)
            return pltpu.make_async_copy(
                stage.at[kind, :, :, columns], partial_hbm.at[kind, :, :, columns], local_sems.at[t]
            )

        def sent(t):
            kind, columns = split(t)
            return first_stage(
                lambda dest, side: stage.at[kind, dest, half_rows(side), columns],
                lambda i: first_in.at[kind, i, :, columns],
                send.at[t],
                recv.at[t],
                where,
            )

        def tile(t):
            kind, columns = split(t)
            use = jnp.where(kind == 0, 0, 1)
            result = product(former[use], latter[kind, :, columns]).astype(HALF)
            stage[kind, :, :, columns] = result.reshape(seqs, share, tile_width)

            @pl.when(t < kinds * tiles)
            def _():
                start_all(sent(t))

            stored(t).start()

        def finish():
            loop(3 * tiles, lambda t: stored(t).wait())
            loop(kinds * tiles, lambda t: wait_all(sent(t)))

        return tile, finish

    ffn_scratch = weight_scratch + [
        pltpu.VMEM((tokens, width), FLOAT),
        pltpu.VMEM((2, tokens, half_model), HALF),
        pltpu.VMEM((2, half_model, 2 * tokens), HALF),
        pltpu.VMEM((3, 2 * tokens, padded_units), HALF),
        pltpu.VMEM((3, seqs, share, padded_units), HALF),
        dma(2),
        dma(2),
        pltpu.SemaphoreType.DMA((3, len(slabs))),
        pltpu.SemaphoreType.DMA((3, len(slabs))),
        pltpu.SemaphoreType.DMA((3 * tiles,)),
        pltpu.SemaphoreType.DMA((3 * tiles, first_blocks)),
        pltpu.SemaphoreType.DMA((3 * tiles, first_blocks)),
    ]
    def partial_outs(kinds):
        return [((3, seqs, share, padded_units), HALF, ANY), first_shape(kinds)]


    def slot_peer(me, j, h):
        other = lax.rem(me + j, slots)
        return (lax.rem(other, sections), lax.div(other, sections), h)

    def query_rows(ref, m, c):
        block = ref[m * rows : (m + 1) * rows, :]
        base = c * group * head_width
        return jnp.concatenate(
            [block[:, base + r * head_width : base + (r + 1) * head_width] for r in range(group)], 0
        )

    def keys_of(all_ref, at, c, kind):
        block = all_ref[:, at * rows : (at + 1) * rows, :].reshape(block_tok, pair_width)
        base = kind * kv_local * head_width + c * head_width
        return block[:, base : base + head_width]

    def allowed_pairs(segq_ref, seg_ref, m, at, s, q):
        own_segments = segq_ref[m * rows : (m + 1) * rows, :]
        allowed = own_segments == seg_ref[at : at + 1, :].astype(FLOAT)
        if at == m:
            base = q * local_rows + s * rows
            order = base + lax.broadcasted_iota(jnp.int32, (rows, block_tok), 0)
            allowed = allowed & (lax.broadcasted_iota(jnp.int32, (rows, block_tok), 1) <= order)
        bias = jnp.where(allowed, 0.0, -1e30)
        return jnp.concatenate([bias] * group, 0)

    def probabilities(rows_in, keys, biases):
        scores = [back_product(rows_in, key) + bias for key, bias in zip(keys, biases)]
        summit = functools.reduce(jnp.maximum, [jnp.max(part, -1, keepdims=True) for part in scores])
        raised = [jnp.exp(part - summit) for part in scores]
        total = functools.reduce(jnp.add, [jnp.sum(part, -1, keepdims=True) for part in raised])
        return raised, 1.0 / total

    def gather_pairs(all_ref, me, where, send, recv, near_send, near_recv):
        s, q, h = where
        partner = (1 - s, q, h)
        far = []
        for k, peer in enumerate(seq_peers(where, seqs)):
            copy = remote(all_ref.at[me], all_ref.at[me], send.at[k], recv.at[k], peer)
            copy.start()
            far.append(copy)
        near = [remote(all_ref.at[me], all_ref.at[me], near_send.at[0], near_recv.at[0], partner)]
        near[0].start()

        def pass_on():
            for k in range(1, seqs):
                far[k - 1].wait()
                slot = lax.rem(q + seqs - k, seqs) * sections + s
                copy = remote(all_ref.at[slot], all_ref.at[slot], near_send.at[k], near_recv.at[k], partner)
                copy.start()
                near.append(copy)
            wait_all(near)

        return pass_on

    def attention_forward(
        n3_ref, wq_ref, wp_ref, cos_ref, sin_ref, qk_ref, segq_ref, seg_ref, wo_ref, m_ref, gain_ref,
        qr_ref, r_ref, q_ref, all_ref, o_ref, h2_ref, n4_ref,
        send, recv, near_send, near_recv, part, inbox, rs, rr, gs, gr, travel,
    ):
        where = place()
        s, q, h = where
        me = q * sections + s
        travel.ready(wp_ref, cos_ref, sin_ref)
        cos, sin = cos_ref[...], sin_ref[...]
        r_ref[...] = product(n3_ref[...], wp_ref[...])
        half_pair = pair_width // 2
        for start, size in chunks_of(half_pair):
            span = slice(start, start + size)
            all_ref[me, :, span] = rotary(r_ref[:, span], twice(qk_ref[1:2, :]), cos, sin).astype(HALF)
        all_ref[me, :, half_pair:] = r_ref[:, half_pair:].astype(HALF)
        pass_on = gather_pairs(all_ref, me, where, send, recv, near_send, near_recv)
        travel.ready(wq_ref)
        qr_ref[...] = product(n3_ref[...], wq_ref[...])
        for start, size in chunks_of(query_width):
            span = slice(start, start + size)
            q_ref[:, span] = rotary(qr_ref[:, span], twice(qk_ref[0:1, :]), cos, sin).astype(HALF)
        travel.leave(r_ref, qr_ref, q_ref)
        pass_on()
        travel.leave(all_ref)
        for m in range(micro):
            biases = [allowed_pairs(segq_ref, seg_ref, m, at, s, q) for at in range(m + 1)]
            results = []
            for c in range(kv_local):
                keys = [keys_of(all_ref, at, c, 0) for at in range(m + 1)]
                raised, inverse = probabilities(query_rows(q_ref, m, c) * HALF(score_scale), keys, biases)
                total = functools.reduce(
                    jnp.add,
                    [
                        product((raised[at] * inverse).astype(HALF), keys_of(all_ref, at, c, 1))
                        for at in range(m + 1)
                    ],
                )
                results += [total[r * rows : (r + 1) * rows] for r in range(group)]
            o_ref[m * rows : (m + 1) * rows, :] = jnp.concatenate(results, -1).astype(HALF)
        travel.leave(o_ref)
        travel.ready(wo_ref)
        part[...] = product(o_ref[...], wo_ref[...]).astype(HALF)

        def finish(flow, i, total):
            hidden = m_ref[kept_rows(i), :] + total
            h2_ref[kept_rows(i), :] = hidden
            return norm_apply(hidden, gain_ref[1:2, :]).astype(HALF)

        head_total(part, n4_ref, inbox, rs, rr, gs, gr, where, heads, finish)

    def forward(
        in_ref, gain_ref, win_ref, kernel_ref, wout_ref, attn_gain_ref, up_hbm, down_hbm, seg_ref,
        wq_ref, wp_ref, cos_ref, sin_ref, qk_ref, wo_ref,
        x_ref, g_ref, n1_ref, pc_ref, edge_ref, y_ref, h1_ref, n2_ref, f1_ref, a1_ref, m_ref, n3_ref, same_ref, segq_ref,
        qr_ref, r_ref, q_ref, all_ref, o_ref, h2_ref, n4_ref, *rest,
    ):
        travel, rest = rest[-1], rest[:-1]
        split = len(conv_scratch)
        conv_forward(
            in_ref, gain_ref, win_ref, kernel_ref, wout_ref, attn_gain_ref, up_hbm, down_hbm, seg_ref,
            x_ref, g_ref, n1_ref, pc_ref, edge_ref, y_ref, h1_ref, n2_ref, f1_ref, a1_ref, m_ref, n3_ref,
            same_ref, segq_ref, *rest[:split], travel,
        )
        part = rest[part_at]
        attention_forward(
            n3_ref, wq_ref, wp_ref, cos_ref, sin_ref, qk_ref, segq_ref, seg_ref, wo_ref, m_ref, attn_gain_ref,
            qr_ref, r_ref, q_ref, all_ref, o_ref, h2_ref, n4_ref, *rest[split : split + 4], part, *rest[split + 4 :], travel,
        )

    conv_scratch = (
            [
                pltpu.VMEM((micro, rows, width), HALF),
                pltpu.VMEM((2, micro, 16, width), HALF),
                pltpu.VMEM((micro * 16, width), HALF),
                pltpu.VMEM((micro, 8 + rows, channels), FLOAT),
                dma(1),
                dma(1),
                dma(2),
                dma(2),
            ]
            + weight_scratch
            + [pltpu.VMEM((tokens, width), FLOAT)]
            + part_scratch
            + total_scratch
            + total_scratch
    )
    part_at = len(conv_scratch) - 2 * len(total_scratch) - 1
    (
        x, g, n1, projected, edge_gated, mixed, h1, n2, f1, a1, middle, n3, same, local_segments,
        query_raw, pair_raw, queries, all_pairs, attended, h2, n4,
    ) = call(
        forward,
        "forward",
        0,
        [
            ((tokens, width), HALF, LATE),
            ((tokens, width), HALF, LATE),
            ((tokens, width), HALF, LATE),
            ((3, tokens, channels), FLOAT, LATE),
            ((micro, 8, channels), FLOAT, LATE),
            ((tokens, channels), HALF, LATE),
            ((half_tokens, width), FLOAT, LATE),
            ((tokens, width), HALF, LATE),
            ((2, tokens, hidden_units), FLOAT, LATE),
            ((tokens, hidden_units), HALF, LATE),
            ((half_tokens, width), FLOAT, LATE),
            ((tokens, width), HALF, LATE),
            ((tokens, 2), FLOAT, LATE),
            ((tokens, 1), FLOAT, LATE),
            ((tokens, query_width), FLOAT, LATE),
            ((tokens, pair_width), FLOAT, LATE),
            ((tokens, query_width), HALF, LATE),
            ((slots, tokens, pair_width), HALF, LATE),
            ((tokens, query_width), HALF, LATE),
            ((half_tokens, width), FLOAT),
            ((tokens, width), HALF),
        ],
        conv_scratch + [dma(seqs - 1), dma(seqs - 1), dma(seqs), dma(seqs)] + total_scratch,
        [
            (incoming, LAZY), conv_gains, (w_in, LAZY), conv_kernel, (conv_out, LAZY), attn_gains,
            (first_up, ANY), (conv_down, ANY), segment_ids,
            (w_query, LAZY), (w_pair, LAZY), (cosine, LAZY), (sine, LAZY), qk_gains, (attn_out, LAZY),
        ],
        flops=9 * 10**9,
        moved=350 << 20,
    )

    def slab_width(start, count):
        return min(-(-count // tile_width) * tile_width, padded_units - start)

    def clear_padding(latter):
        if padded_units > hidden_units:
            latter[:, :, hidden_units:] = jnp.zeros((3, 2 * tokens, padded_units - hidden_units), HALF)

    def second_ffn(
        n4_ref, g_ref, h2_ref, gain_ref, up_hbm, down_hbm,
        py_ref, gh2_ref, low_ref, gg_ref, partial_hbm, first_in,
        acc_y, up_ref, down_ref, weight_sems, acc, given, former, latter, stage, hs, hr, ls, lr, local_sems, ts, tr,
        part, inbox, rs, rr, gs, gr, travel,
    ):
        where = place()
        s, q, h = where
        weights = weight_loads(up_hbm, down_hbm, up_ref, down_ref, weight_sems)
        start_all(weights)
        clear_padding(latter)
        met = greet([(1 - s, q, h)] + seq_peers(where, seqs), where, heads)
        halves = half_swaps([g_ref, n4_ref], [given.at[0], given.at[1]], hs, hr, where)
        gg_ref[...] = jnp.zeros_like(gg_ref)
        swaps = []
        travel.ready(n4_ref, g_ref)
        for j, (start, count) in enumerate(slabs):
            wait_all(weights[3 * j : 3 * j + 3])
            span = slice(start, start + count)
            gate = back_product(n4_ref[...], up_ref[0, span, :])
            rise = back_product(n4_ref[...], up_ref[1, span, :])
            grad_active = back_product(g_ref[...], down_ref[span, :])
            chance = 1.0 / (1.0 + jnp.exp(-gate))
            silu = gate * chance
            active = (silu * rise).astype(HALF)
            grad_gate = (grad_active * rise * (chance * (1.0 + gate * (1.0 - chance)))).astype(HALF)
            grad_rise = (grad_active * silu).astype(HALF)
            latter[0, 0:tokens, span] = active
            latter[1, 0:tokens, span] = grad_gate
            latter[2, 0:tokens, span] = grad_rise
            if j == 0:
                met()
                start_all(halves)
            for kind in range(3):
                swap = latter_swap(
                    latter, kind, start, slab_width(start, count), ls.at[kind, j], lr.at[kind, j], where
                )
                swap.start()
                swaps.append(swap)
            term = product(grad_gate, up_ref[0, span, :]) + product(grad_rise, up_ref[1, span, :])
            term_y = product(active, down_ref[span, :])
            if j == 0:
                acc[...] = term
                acc_y[...] = term_y
            else:
                acc[...] += term
                acc_y[...] += term_y
        part[...] = acc[...].astype(HALF)

        travel.ready(h2_ref)
        for flow, holder in ((0, 0), (1, heads - 1)):

            @pl.when(h == holder)
            def _(flow=flow):
                acc_y[flow * half_tokens : (flow + 1) * half_tokens, :] += h2_ref[...]

        py_ref[...] = acc_y[...].astype(HALF)
        travel.leave(py_ref)
        tile, tiles_done = gradient_tiles(
            former, latter, stage, partial_hbm, first_in, local_sems, ts, tr, where, 2
        )

        def filler(t):
            for k, array_ref in enumerate((g_ref, n4_ref)):

                @pl.when(t == k)
                def _(k=k, array_ref=array_ref):
                    halves[k].wait()
                    if k:
                        wait_all(swaps)
                    former[k] = transposed(array_ref, given.at[k])

            @pl.when(t >= 2)
            def _():
                tile(t - 2)

        def finish(flow, i, total):
            grad_hidden, grad_gain = norm_back(h2_ref[kept_rows(i), :], gain_ref[1:2, :], total)
            grad = g_ref[own_rows(flow, i), :].astype(FLOAT) + grad_hidden
            gh2_ref[kept_rows(i), :] = grad
            gg_ref[...] += grad_gain
            return grad.astype(HALF)

        head_total(part, low_ref, inbox, rs, rr, gs, gr, where, heads, finish, filler, 3 * tiles + 2)
        tiles_done()

    (part_y, gh2, gh2_low, grad_gain_attn1, partial2, first2) = call(
        second_ffn,
        "second_ffn",
        4,
        [
            ((tokens, width), HALF, LATE),
            ((half_tokens, width), FLOAT),
            ((tokens, width), HALF),
            ((1, width), FLOAT),
        ]
        + partial_outs(2),
        [pltpu.VMEM((tokens, width), FLOAT)] + ffn_scratch + part_scratch + total_scratch,
        [(n4, LAZY), (g, LAZY), (h2, LAZY), attn_gains, (second_up, ANY), (attn_down, ANY)],
        flops=12 * 10**9,
        moved=150 << 20,
    )
    def attention_backward(
        glow_ref, wo_ref, q_ref, all_ref, segq_ref, seg_ref,
        qr_ref, r_ref, cos_ref, sin_ref, qk_ref, wq_ref, wp_ref, m_ref, gh2_ref, gain_ref, py_ref, n3_ref, o_ref, partial2_hbm, first2_hbm,
        low_ref, gg_ref, gqk_ref, yown_ref, stage0, stage1, in0, in1, second_in, first_in,
        bq_ref, br_ref, grads, totals, gq_ref, gp_ref, near_slots, pair_slots, ns, nr, ps, pr,
        passing, held, load_sems, vs, vr, fs, fr,
        ybox, ys, yr, given, former, latter0, latter1, hs, hr, ls, lr, ms, mr,
        part, inbox, rs, rr, gs, gr, travel,
    ):
        where = place()
        s, q, h = where
        partner = (1 - s, q, h)
        peers = seq_peers(where, seqs)
        loads = pass_loads(partial2_hbm, (0, 1), first2_hbm, passing, held, load_sems, where)
        loads += load_passing(partial2_hbm.at[2], passing.at[2], load_sems.at[2], where)
        start_all(loads)
        others = head_others(where)
        latters = [latter0, latter1]
        met = greet([partner] + peers + others, where, heads)
        travel.ready(glow_ref, wo_ref, q_ref, all_ref)
        grads[...] = back_product(glow_ref[...], wo_ref[...]).astype(HALF)
        met()
        later = first_stage(
            lambda dest, side: partial2_hbm.at[2, dest, half_rows(side)], lambda i: first_in.at[0, i], fs, fr, where
        )
        start_all(later)
        travel.ready(py_ref, n3_ref, o_ref)
        latter0[0:tokens, :] = o_ref[...]
        ysends = [
            remote(py_ref.at[rows_of(peer[2], small_rows)], ybox.at[n], ys.at[n], yr.at[n], peer)
            for n, peer in enumerate(others)
        ]
        start_all(ysends)
        halves = half_swaps([glow_ref, n3_ref], [given.at[0], given.at[1]], hs, hr, where)
        start_all(halves)
        swaps = latter_swaps(latters, ls, lr, partner)
        swaps[0].start()
        gg_ref[...] = jnp.zeros_like(gg_ref)
        gqk_ref[...] = jnp.zeros_like(gqk_ref)
        for m in range(micro):
            biases = [allowed_pairs(segq_ref, seg_ref, m, at, s, q) for at in range(m + 1)]
            results = []
            for c in range(kv_local):
                keys = [keys_of(all_ref, at, c, 0) for at in range(m + 1)]
                values = [keys_of(all_ref, at, c, 1) for at in range(m + 1)]
                rows_in = query_rows(q_ref, m, c) * HALF(score_scale)
                grad_rows = query_rows(grads, m, c)
                raised, inverse = probabilities(rows_in, keys, biases)
                chances = [part * inverse for part in raised]
                grad_chances = [back_product(grad_rows, value) for value in values]
                inner = functools.reduce(
                    jnp.add,
                    [jnp.sum(a * b, -1, keepdims=True) for a, b in zip(grad_chances, chances)],
                )
                total = None
                for at in range(m + 1):
                    grad_scores = (chances[at] * (grad_chances[at] - inner)).astype(HALF)
                    term = product(grad_scores, keys[at])
                    total = term if total is None else total + term
                    grad_key = outer_sum(grad_scores, rows_in)
                    grad_value = outer_sum(chances[at].astype(HALF), grad_rows)
                    if at == m:
                        totals[at, c] = grad_key
                        totals[at, kv_local + c] = grad_value
                    else:
                        totals[at, c] += grad_key
                        totals[at, kv_local + c] += grad_value
                total = total * score_scale
                results += [total[r * rows : (r + 1) * rows] for r in range(group)]
            gq_ref[m * rows : (m + 1) * rows, :] = jnp.concatenate(results, -1)
        for at in range(micro):
            joined = jnp.concatenate([totals[at, k] for k in range(2 * kv_local)], -1).astype(HALF)
            gp_ref[:, at * rows : (at + 1) * rows, :] = joined.reshape(slots, rows, pair_width)
        near = []
        for other in range(seqs):
            copy = remote(gp_ref.at[other * sections + 1 - s], near_slots.at[other], ns.at[other], nr.at[other], partner)
            copy.start()
            near.append(copy)
        copies = []
        wait_all(near)
        travel.ready(qr_ref, r_ref, cos_ref, sin_ref, wq_ref, wp_ref, m_ref, gh2_ref)
        for other in range(seqs):
            mine = gp_ref[other * sections + s].astype(FLOAT)
            near_slots[other] = (mine + near_slots[other].astype(FLOAT)).astype(HALF)
        for k, peer in enumerate(peers):
            copy = remote(near_slots.at[peer[1]], pair_slots.at[k], ps.at[k], pr.at[k], peer)
            copy.start()
            copies.append(copy)
        cos, sin = cos_ref[...], sin_ref[...]
        for start, size in chunks_of(query_width):
            span = slice(start, start + size)
            grad_raw, grad_gain = rotary_back(qr_ref[:, span], twice(qk_ref[0:1, :]), cos, sin, gq_ref[:, span])
            bq_ref[:, span] = grad_raw.astype(HALF)
            gqk_ref[0:1, :size] += grad_gain
        partial = back_product(bq_ref[...], wq_ref[...])
        wait_all(loads)
        travelling = pass_sends(2, passing, held, second_in, vs, vr, where)
        wait_all(copies)
        grad_pair = near_slots[q].astype(FLOAT)
        for j in range(seqs - 1):
            grad_pair = grad_pair + pair_slots[j].astype(FLOAT)
        half_pair = pair_width // 2
        for start, size in chunks_of(half_pair):
            span = slice(start, start + size)
            grad_raw, grad_gain = rotary_back(r_ref[:, span], twice(qk_ref[1:2, :]), cos, sin, grad_pair[:, span])
            br_ref[:, span] = grad_raw.astype(HALF)
            gqk_ref[1:2, :size] += grad_gain
        br_ref[:, half_pair:] = grad_pair[:, half_pair:].astype(HALF)
        wait_all(later)
        combine(lambda i: passing.at[2, i], first_in.at[0], where)
        turning = second_stage(lambda i: passing.at[2, i], second_in.at[2], vs.at[2], vr.at[2], where)
        start_all(turning)
        travelling += turning
        travel.leave(first_in)
        latter1[0:tokens, 0:query_width] = bq_ref[...]
        latter1[0:tokens, query_width:] = br_ref[...]
        swaps[1].start()
        part[...] = (partial + back_product(br_ref[...], wp_ref[...])).astype(HALF)
        wait_all(ysends)
        produced = py_ref[rows_of(h, small_rows), :].astype(FLOAT)
        for n in range(heads - 1):
            produced = produced + ybox[n].astype(FLOAT)
        yown_ref[...] = produced.astype(HALF)
        sends = mixer_sends([stage0, stage1], [in0, in1], ms, mr, where)
        mixer_step = mixer_steps([glow_ref, n3_ref], latters, [stage0, stage1], given, former, halves, swaps, sends)

        def finish(flow, i, total):
            grad_entry, grad_gain = norm_back(m_ref[kept_rows(i), :], gain_ref[0:1, :], total)
            gg_ref[...] += grad_gain
            return (gh2_ref[kept_rows(i), :] + grad_entry).astype(HALF)

        head_total(part, low_ref, inbox, rs, rr, gs, gr, where, heads, finish, mixer_step, 4)
        for copies in sends:
            wait_all(copies)
        wait_all(travelling)

    (gm_low, grad_gain_attn0, grad_qk, y_own, stage0, stage1, in0, in1, second2, first2_last) = call(
        attention_backward,
        "attention_backward",
        5,
        [
            ((tokens, width), HALF),
            ((1, width), FLOAT),
            ((8, 128), FLOAT),
            ((small_rows, width), HALF),
            ((seqs, share, widths[0]), HALF),
            ((seqs, share, widths[1]), HALF),
            *first_sums(widths[:2]),
            second_shape(3),
            ((1, first_blocks, half_share, padded_units), HALF, LATE),
        ],
        [
            pltpu.VMEM((tokens, query_width), HALF),
            pltpu.VMEM((tokens, pair_width), HALF),
            pltpu.VMEM((tokens, query_width), HALF),
            pltpu.VMEM((micro, 2 * kv_local, block_tok, head_width), FLOAT),
            pltpu.VMEM((tokens, query_width), FLOAT),
            pltpu.VMEM((slots, tokens, pair_width), HALF),
            pltpu.VMEM((seqs, tokens, pair_width), HALF),
            pltpu.VMEM((seqs - 1, tokens, pair_width), HALF),
            dma(seqs),
            dma(seqs),
            dma(seqs - 1),
            dma(seqs - 1),
        ]
        + passing_scratch(3)
        + [dma(first_blocks), dma(first_blocks)]
        + [
            pltpu.VMEM((heads - 1, small_rows, width), HALF),
            dma(heads - 1),
            dma(heads - 1),
            pltpu.VMEM((2, tokens, half_model), HALF),
            pltpu.VMEM((half_model, 2 * tokens), HALF),
            pltpu.VMEM((2 * tokens, widths[0]), HALF),
            pltpu.VMEM((2 * tokens, widths[1]), HALF),
            dma(2),
            dma(2),
            dma(2),
            dma(2),
            dma_grid(2, first_blocks),
            dma_grid(2, first_blocks),
        ]
        + part_scratch
        + total_scratch,
        [
            (gh2_low, LAZY), (attn_out, LAZY), (queries, LAZY), (all_pairs, LAZY), local_segments, segment_ids,
            (query_raw, LAZY), (pair_raw, LAZY), (cosine, LAZY), (sine, LAZY), qk_gains,
            (w_query, LAZY), (w_pair, LAZY), (middle, LAZY), (gh2, LAZY), attn_gains,
            (part_y, LAZY), (n3, LAZY), (attended, LAZY), (partial2, ANY), (first2, ANY),
        ],
        flops=6 * 10**9,
        moved=130 << 20,
    )

    def first_ffn_back(
        gm_ref, n2_ref, f1_ref, a1_ref, h1_ref, gain_ref, yown_ref, stage0, stage1, in0, in1, up_hbm, down_hbm,
        gh1_ref, low_ref, gg_ref, yout_ref, turn0, turn1, partial_hbm, first_in,
        up_ref, down_ref, weight_sems, acc, given, former, latter, stage, hs, hr, ls, lr, local_sems, ts, tr,
        ys, yr, pass0, pass1, us, ur,
        part, inbox, rs, rr, gs, gr, travel,
    ):
        where = place()
        s, q, h = where
        weights = weight_loads(up_hbm, down_hbm, up_ref, down_ref, weight_sems)
        start_all(weights)
        clear_padding(latter)
        others = head_others(where)
        own_y = rows_of(h, small_rows)
        met = greet([(1 - s, q, h)] + seq_peers(where, seqs) + others, where, heads)
        travel.ready(gm_ref, yown_ref, n2_ref, a1_ref)
        yout_ref[own_y, :] = yown_ref[...]
        latter[0, 0:tokens, 0:hidden_units] = a1_ref[...]
        travel.ready(stage0, stage1, in0, in1)
        turning = mixer_second([stage0, stage1], [in0, in1], [pass0, pass1], [turn0, turn1], us, ur, where)
        met()
        for copies in turning:
            start_all(copies)
        ysends = [
            remote(yout_ref.at[own_y], yout_ref.at[own_y], ys.at[n], yr.at[n], peer) for n, peer in enumerate(others)
        ]
        start_all(ysends)
        halves = half_swaps([gm_ref, n2_ref], [given.at[0], given.at[1]], hs, hr, where)
        start_all(halves)
        gg_ref[...] = jnp.zeros_like(gg_ref)
        tile, tiles_done = gradient_tiles(
            former, latter, stage, partial_hbm, first_in, local_sems, ts, tr, where, 3
        )
        active_swaps = [
            latter_swap(latter, 0, start, slab_width(start, count), ls.at[0, j], lr.at[0, j], where)
            for j, (start, count) in enumerate(slabs)
        ]
        start_all(active_swaps)
        halves[0].wait()
        former[0] = transposed(gm_ref, given.at[0])
        wait_all(active_swaps)
        loop(tiles, tile)
        swaps = []
        travel.ready(f1_ref, h1_ref)
        for j, (start, count) in enumerate(slabs):
            wait_all(weights[3 * j : 3 * j + 3])
            span = slice(start, start + count)
            gate = f1_ref[0, :, span]
            rise = f1_ref[1, :, span]
            grad_active = back_product(gm_ref[...], down_ref[span, :])
            chance = 1.0 / (1.0 + jnp.exp(-gate))
            grad_gate = (grad_active * rise * (chance * (1.0 + gate * (1.0 - chance)))).astype(HALF)
            grad_rise = (grad_active * (gate * chance)).astype(HALF)
            latter[1, 0:tokens, span] = grad_gate
            latter[2, 0:tokens, span] = grad_rise
            for kind in range(1, 3):
                swap = latter_swap(
                    latter, kind, start, slab_width(start, count), ls.at[kind, j], lr.at[kind, j], where
                )
                swap.start()
                swaps.append(swap)
            term = product(grad_gate, up_ref[0, span, :]) + product(grad_rise, up_ref[1, span, :])
            if j == 0:
                acc[...] = term
            else:
                acc[...] += term
        part[...] = acc[...].astype(HALF)
        def filler(t):
            @pl.when(t == 0)
            def _():
                halves[1].wait()
                wait_all(swaps)
                former[1] = transposed(n2_ref, given.at[1])

            @pl.when(t >= 1)
            def _():
                tile(tiles + t - 1)

        def finish(flow, i, total):
            grad_hidden, grad_gain = norm_back(h1_ref[kept_rows(i), :], gain_ref[1:2, :], total)
            gg_ref[...] += grad_gain
            grad = gm_ref[own_rows(flow, i), :].astype(FLOAT) + grad_hidden
            gh1_ref[kept_rows(i), :] = grad
            return grad.astype(HALF)

        head_total(part, low_ref, inbox, rs, rr, gs, gr, where, heads, finish, filler, 2 * tiles + 1)
        tiles_done()
        wait_all(ysends)
        for copies in turning:
            wait_all(copies)

    (gh1, gh1_low, grad_gain_conv1, yout, turn0, turn1, partial1, first1) = call(
        first_ffn_back,
        "first_ffn_back",
        6,
        [((half_tokens, width), FLOAT), ((tokens, width), HALF), ((1, width), FLOAT), ((tokens, width), HALF)]
        + [((grid_rows, half_share, size), HALF) for size in widths[:2]]
        + partial_outs(3),
        ffn_scratch + [dma(heads - 1), dma(heads - 1)]
        + [pltpu.VMEM((grid_rows, half_share, size), HALF) for size in widths[:2]]
        + [dma_grid(2, grid_rows), dma_grid(2, grid_rows)]
        + part_scratch + total_scratch,
        [(gm_low, LAZY), (n2, LAZY), (f1, LAZY), (a1, LAZY), (h1, LAZY), conv_gains, (y_own, LAZY),
         (stage0, LAZY), (stage1, LAZY), (in0, LAZY), (in1, LAZY), (first_up, ANY), (conv_down, ANY)],
        flops=9 * 10**9,
        moved=150 << 20,
    )
    small_width = max(share, channels, 2 * head_width)

    def conv_backward(
        low_ref, gh1_ref, pc_ref, edge_ref, same_ref, kernel_ref, wout_ref, win_ref, x_ref, gain_ref, yout_ref,
        n1_ref, mixed_ref, stage0, stage1, in0, in1, turn0, turn1, gain1_ref, gain2_ref, gain3_ref, gqk_ref,
        partial1, partial2, first1, first2, first2_last, second2,
        edges_ref, sums_ref, gout2_ref, gmix_ref, gout1_ref, gin_ref, gdown2, gup2, gdown1, gup1,
        bp_ref, ext, spread, gz_ext, outgoing, arrived, full, gg_ref, edge_send, edge_recv, swap_send, swap_recv,
        given, former, latter2, latter3, stage2, stage3, in2, in3, turn2, turn3, hs, hr, ls, lr, ms, mr, us, ur,
        own_buf, first_buf, second_buf, passing, item_sems, vs, vr, down_stage, up_stage, out_sems,
        packed, boxes, summed, final, zs, zr, ss, sr,
        part, inbox, rs, rr, gs, gr, travel,
    ):
        where = place()
        s, q, h = where
        first = s == 0
        partner = (1 - s, q, h)
        preceding = (1 - s, jnp.where(first, lax.rem(q + seqs - 1, seqs), q), h)
        following = (1 - s, jnp.where(first, q, lax.rem(q + 1, seqs)), h)
        others = head_others(where)
        me = q * sections + s
        slot_peers = [slot_peer(me, j, h) for j in range(1, slots)]
        peers = seq_peers(where, seqs)
        latters, stages = [latter2, latter3], [stage0, stage1, stage2, stage3]
        incomes, turns = [in0, in1, in2, in3], [turn0, turn1, turn2, turn3]
        loads = []
        sources = [
            (partial2.at[0], first2.at[0], second2.at[0]),
            (partial2.at[1], first2.at[1], second2.at[1]),
            (partial2.at[2], first2_last.at[0], second2.at[2]),
            (partial1.at[0], first1.at[0], None),
            (partial1.at[1], first1.at[1], None),
            (partial1.at[2], first1.at[2], None),
        ]
        for n, (partial, arrived_hbm, passed_hbm) in enumerate(sources):
            copies = [pltpu.make_async_copy(partial.at[q], own_buf.at[n], item_sems.at[n, 0])]
            if arrived_hbm is not None:
                copies.append(pltpu.make_async_copy(arrived_hbm, first_buf.at[n], item_sems.at[n, 1]))
            if passed_hbm is not None:
                copies.append(pltpu.make_async_copy(passed_hbm, second_buf.at[n], item_sems.at[n, 2]))
            else:
                copies += load_passing(partial, passing.at[n - 3], item_sems.at[n, pl.ds(3, grid_rows)], where)
            loads.append(copies)
        travel.begin(low_ref, wout_ref, pc_ref)
        for copies in loads[3:]:
            start_all(copies)
        travel.begin()
        for copies in loads[:3]:
            start_all(copies)
        met = greet([partner, preceding, following] + others + slot_peers, where, heads)
        bulk = []

        def pass_item(n):
            wait_all(loads[n])
            combine(lambda i: passing.at[n - 3, i], first_buf.at[n], where)
            sends = second_stage(
                lambda i: passing.at[n - 3, i], second_buf.at[n], vs.at[n - 3], vr.at[n - 3], where
            )
            start_all(sends)
            bulk.append(sends)

        gg_ref[...] = jnp.zeros_like(gg_ref)
        travel.ready(low_ref, wout_ref, pc_ref)
        gated = pc_ref[0] * pc_ref[2]
        grad_y = back_product(low_ref[...], wout_ref[...])
        gz = grad_y * pc_ref[1]
        zero = jnp.zeros((8, channels), FLOAT)
        for m in range(micro):
            span = slice(m * rows, (m + 1) * rows)
            one = jnp.where(same_ref[span, 0:1] > 0, gz[span], 0.0) * kernel_ref[1:2, :]
            two = jnp.where(same_ref[span, 1:2] > 0, gz[span], 0.0) * kernel_ref[0:1, :]
            gz_ext[0, m, 0:rows, :] = one
            gz_ext[0, m, rows : rows + 8, :] = zero
            gz_ext[1, m, 0:rows, :] = two
            gz_ext[1, m, rows : rows + 8, :] = zero
            outgoing[m] = zero
            outgoing[m, 0:1, :] = two[0:1]
            outgoing[m, 1:2, :] = one[0:1] + two[1:2]
        met()
        edge = remote(outgoing, arrived, edge_send.at[0], edge_recv.at[0], preceding)
        edge.start()
        for n in (3, 4, 5):
            pass_item(n)
        travel.ready(n1_ref, mixed_ref)
        latter2[0:tokens, :] = mixed_ref[...]
        halves = half_swaps([low_ref, n1_ref], [given.at[0], given.at[1]], hs, hr, where)
        start_all(halves)
        swaps = latter_swaps(latters, ls, lr, partner)
        swaps[0].start()
        taps = [None, None, None]
        for m in range(micro):
            span = slice(m * rows, (m + 1) * rows)
            ext[m, 0:8, :] = edge_ref[m]
            ext[m, 8 : 8 + rows, :] = gated[span]
            back_one = jnp.where(same_ref[span, 0:1] > 0, shifted_rows(ext, m, 1), 0.0)
            back_two = jnp.where(same_ref[span, 1:2] > 0, shifted_rows(ext, m, 2), 0.0)
            mixed = (
                kernel_ref[2:3, :] * gated[span]
                + kernel_ref[1:2, :] * back_one
                + kernel_ref[0:1, :] * back_two
            )
            bp_ref[span, channels : 2 * channels] = (grad_y[span] * mixed).astype(HALF)
            for k, value in enumerate((back_two, back_one, gated[span])):
                term = jnp.sum(value * gz[span], 0, keepdims=True)
                taps[k] = term if taps[k] is None else taps[k] + term
        for m in range(micro):
            span = slice(m * rows, (m + 1) * rows)
            spread[m] = (
                kernel_ref[2:3, :] * gz[span]
                + gz_ext[0, m, 1 : rows + 1, :]
                + gz_ext[1, m, 2 : rows + 2, :]
            )
        edge.wait()
        wrap = (s == sections - 1) & (q == seqs - 1)
        for m in range(micro):
            follow = arrived[m + 1, 0:2, :] if m + 1 < micro else jnp.zeros((2, channels), FLOAT)
            spread[m, rows - 2 : rows, :] += jnp.where(wrap, follow, arrived[m, 0:2, :])
        for m in range(micro):
            span = slice(m * rows, (m + 1) * rows)
            bp_ref[span, 0:channels] = (spread[m] * pc_ref[2, span, :]).astype(HALF)
            bp_ref[span, 2 * channels :] = (spread[m] * pc_ref[0, span, :]).astype(HALF)
        latter3[0:tokens, :] = bp_ref[...]
        swaps[1].start()
        travel.ready(win_ref, x_ref, gh1_ref, yout_ref)
        total = back_product(bp_ref[:, 0:channels], win_ref[0])
        total = total + back_product(bp_ref[:, channels : 2 * channels], win_ref[1])
        total = total + back_product(bp_ref[:, 2 * channels :], win_ref[2])
        part[...] = total.astype(HALF)

        def finish(flow, i, total):
            start = x_ref[own_rows(flow, i), :].astype(FLOAT)
            grad_start, grad_gain = norm_back(start, gain_ref[0:1, :], total)
            gg_ref[...] += grad_gain
            return (gh1_ref[kept_rows(i), :] + grad_start).astype(HALF)

        sent = mixer_sends(stages[2:], incomes[2:], ms, mr, where)
        mixer_step = mixer_steps([low_ref, n1_ref], latters, stages[2:], given, former, halves, swaps, sent)
        head_total(part, full, inbox, rs, rr, gs, gr, where, heads, finish, mixer_step, 4)
        keep = pl.ds(pl.multiple_of(s * rows, rows), rows)
        edges_ref[0, :, keep, :] = jnp.where(first, full[...], yout_ref[...]).reshape(micro, rows, width)
        part[...] = jnp.where(first, yout_ref[...], full[...])
        edge_swaps = []
        for m in range(micro):
            copy = remote(
                part.at[m * rows : (m + 1) * rows], edges_ref.at[0, m, keep], swap_send.at[m], swap_recv.at[m], partner
            )
            copy.start()
            edge_swaps.append(copy)
        packed[...] = jnp.zeros_like(packed)
        folded = [gqk_ref[n : n + 1, 0:head_width] + gqk_ref[n : n + 1, head_width : 2 * head_width] for n in range(2)]
        folded = jnp.concatenate(folded, -1)
        packed[:, 5:8, 0:channels] = jnp.broadcast_to(jnp.concatenate(taps, 0)[None], (slots, 3, channels))
        for d in range(slots):
            for n, rows_in in enumerate((gg_ref, gain1_ref, gain2_ref, gain3_ref)):
                packed[d, n : n + 1, 0:share] = rows_in[:, d * share : (d + 1) * share]
            packed[d, 4:5, 0 : 2 * head_width] = folded
        over = []
        for k, peer in enumerate(others):
            copy = remote(packed, boxes.at[k], zs.at[k], zr.at[k], peer)
            copy.start()
            over.append(copy)
        wait_all(over)
        over_heads = boxes[0]
        for j in range(1, heads - 1):
            over_heads = over_heads + boxes[j]
        row = lax.broadcasted_iota(jnp.int32, over_heads.shape, 1)
        summed[...] = packed[...] + jnp.where(row < 5, over_heads, 0.0)
        across = []
        for j, peer in enumerate(slot_peers):
            copy = remote(summed.at[peer[0] * seqs + peer[1]], final.at[j], ss.at[j], sr.at[j], peer)
            copy.start()
            across.append(copy)
        outs = []

        def leave(source, target, at):
            copy = pltpu.make_async_copy(source, target, out_sems.at[at])
            copy.start()
            outs.append(copy)

        def fill_stage(n, target):
            upper, lower = two_halves(own_buf.at[n], first_buf.at[n], second_buf.at[n], where)
            target[half_rows(0), :] = upper[:, :hidden_units].astype(HALF)
            target[half_rows(1), :] = lower[:, :hidden_units].astype(HALF)

        def second_half_items():
            for n in range(3):
                wait_all(loads[n])
            fill_stage(0, down_stage.at[0])
            leave(down_stage.at[0], gdown2, 0)
            for kind in range(2):
                fill_stage(1 + kind, up_stage.at[0, kind])
            leave(up_stage.at[0], gup2, 1)

        for copies in sent:
            wait_all(copies)
        mixer_turns = mixer_second(stages[2:], incomes[2:], [None, None], turns[2:], us, ur, where)
        for copies in mixer_turns:
            start_all(copies)
        travel.ready(stage0, stage1, in0, in1, turn0, turn1)
        second_half_items()
        for n in (3, 4, 5):
            wait_all(bulk[n - 3])
            if n == 3:
                fill_stage(3, down_stage.at[1])
                leave(down_stage.at[1], gdown1, 2)
            else:
                fill_stage(n, up_stage.at[1, n - 4])
        leave(up_stage.at[1], gup1, 3)
        wait_all(edge_swaps)
        wait_all(across)
        total = summed[s * seqs + q]
        for j in range(slots - 1):
            total = total + final[j]
        sums_ref[...] = total
        for k, target in enumerate((gout2_ref, gmix_ref, gout1_ref, None)):
            if k >= 2:
                wait_all(mixer_turns[k - 2])
            for side, value in enumerate(two_halves(stages[k].at[q], incomes[k], turns[k], where)):
                value = value.astype(HALF)
                if target is None:
                    for c in range(3):
                        gin_ref[c, half_rows(side), :] = value[:, c * channels : (c + 1) * channels]
                else:
                    target[half_rows(side), :] = value
        wait_all(outs)

    (section_edges, sums, gout2, gmix, gout1, gin, gdown2, gup2, gdown1, gup1) = call(
        conv_backward,
        "conv_backward",
        7,
        [
            ((1, micro, local_rows, width), HALF),
            ((8, small_width), FLOAT),
            ((share, widths[0]), HALF),
            ((share, widths[1]), HALF),
            ((share, widths[2]), HALF),
            ((3, share, channels), HALF),
            ((share, hidden_units), HALF, ANY),
            ((2, share, hidden_units), HALF, ANY),
            ((share, hidden_units), HALF, ANY),
            ((2, share, hidden_units), HALF, ANY),
        ],
        [
            pltpu.VMEM((tokens, 3 * channels), HALF),
            pltpu.VMEM((micro, 8 + rows, channels), FLOAT),
            pltpu.VMEM((micro, rows, channels), FLOAT),
            pltpu.VMEM((2, micro, rows + 8, channels), FLOAT),
            pltpu.VMEM((micro, 8, channels), FLOAT),
            pltpu.VMEM((micro, 8, channels), FLOAT),
            pltpu.VMEM((tokens, width), HALF),
            pltpu.VMEM((1, width), FLOAT),
            dma(1),
            dma(1),
            dma(micro),
            dma(micro),
            pltpu.VMEM((2, tokens, half_model), HALF),
            pltpu.VMEM((half_model, 2 * tokens), HALF),
        ]
        + [pltpu.VMEM((2 * tokens, size), HALF) for size in widths[2:]]
        + [pltpu.VMEM((seqs, share, size), HALF) for size in widths[2:]]
        + [pltpu.VMEM((first_blocks, half_share, size), HALF) for size in widths[2:]]
        + [pltpu.VMEM((grid_rows, half_share, size), HALF) for size in widths[2:]]
        + [
            dma(2),
            dma(2),
            dma(2),
            dma(2),
            dma_grid(2, first_blocks),
            dma_grid(2, first_blocks),
            dma_grid(2, grid_rows),
            dma_grid(2, grid_rows),
            pltpu.VMEM((6, share, padded_units), HALF),
            pltpu.VMEM((6, first_blocks, half_share, padded_units), HALF),
            pltpu.VMEM((6, grid_rows, half_share, padded_units), HALF),
            pltpu.VMEM((3, grid_rows, half_share, padded_units), HALF),
            dma_grid(6, 3 + grid_rows),
            dma_grid(3, grid_rows),
            dma_grid(3, grid_rows),
            pltpu.VMEM((2, share, hidden_units), HALF),
            pltpu.VMEM((2, 2, share, hidden_units), HALF),
            dma(4),
            pltpu.VMEM((slots, 8, small_width), FLOAT),
            pltpu.VMEM((heads - 1, slots, 8, small_width), FLOAT),
            pltpu.VMEM((slots, 8, small_width), FLOAT),
            pltpu.VMEM((slots - 1, 8, small_width), FLOAT),
            dma(heads - 1),
            dma(heads - 1),
            dma(slots - 1),
            dma(slots - 1),
        ]
        + part_scratch
        + total_scratch,
        [
            (gh1_low, LAZY), (gh1, LAZY), (projected, LAZY), edge_gated, same, conv_kernel, (conv_out, LAZY), (w_in, LAZY), (x, LAZY), conv_gains,
            (yout, LAZY), (n1, LAZY), (mixed, LAZY), (stage0, LAZY), (stage1, LAZY), (in0, LAZY), (in1, LAZY), (turn0, LAZY), (turn1, LAZY),
            grad_gain_conv1, grad_gain_attn0, grad_gain_attn1, grad_qk,
        ]
        + [(array, ANY) for array in (partial1, partial2, first1, first2, first2_last, second2)],
        flops=5 * 10**9,
        moved=300 << 20,
        begin=False,
    )
    def results(
        edges_in, sums_in, gout2_in, gmix_in, gout1_in, gin_in, gdown2_in, gup2_in, gdown1_in, gup1_in,
        edges_out, cgain_out, gin_out, taps_out, gout1_out, gup1_out, gdown1_out,
        again_out, gq_out, gkv_out, gqk_out, gout2_out, gup2_out, gdown2_out,
        down_in, up_in, down_stage, up_stage, edges_held, in_sems, out_sems, edge_sem, travel,
    ):
        edges_load = pltpu.make_async_copy(edges_in, edges_held, edge_sem.at[0])
        edges_load.start()
        loads = [
            pltpu.make_async_copy(source, target, in_sems.at[k])
            for k, (source, target) in enumerate(
                [(gdown1_in, down_in.at[0]), (gup1_in, up_in.at[0]), (gdown2_in, down_in.at[1]), (gup2_in, up_in.at[1])]
            )
        ]
        start_all(loads)
        cgain_out[...] = sums_in[0:2, 0:share]
        again_out[...] = sums_in[2:4, 0:share]
        taps_out[...] = sums_in[5:8, 0:channels]
        travel.ready(gmix_in, gout1_in, gout2_in, gin_in)
        for kind in range(2):
            gqk_out[kind : kind + 1, :] = sums_in[4:5, kind * head_width : (kind + 1) * head_width]
            start = query_width + kind * (pair_width // 2)
            gkv_out[:, kind, :] = gmix_in[:, start : start + pair_width // 2].astype(FLOAT)
        gq_out[...] = gmix_in[:, 0:query_width].astype(FLOAT)
        gout1_out[...] = gout1_in[...].astype(FLOAT)
        gout2_out[...] = gout2_in[...].astype(FLOAT)
        gin_out[...] = gin_in[...].astype(FLOAT)
        travel.leave(gq_out, gkv_out, gout1_out, gout2_out, gin_out)
        stores = []
        for k, (down_out, up_out) in enumerate(((gdown1_out, gup1_out), (gdown2_out, gup2_out))):
            loads[2 * k].wait()
            down_stage[k] = down_in[k].astype(FLOAT)
            stores.append(pltpu.make_async_copy(down_stage.at[k], down_out, out_sems.at[2 * k]))
            stores[-1].start()
            loads[2 * k + 1].wait()
            for kind in range(2):
                up_stage[k, :, kind, :] = up_in[k, kind].astype(FLOAT)
            stores.append(pltpu.make_async_copy(up_stage.at[k], up_out, out_sems.at[2 * k + 1]))
            stores[-1].start()
        edges_load.wait()
        stores.append(pltpu.make_async_copy(edges_held, edges_out, edge_sem.at[1]))
        stores[-1].start()
        wait_all(stores)

    (
        section_edges, cgain, gin, taps, gout1, gup1, gdown1, again, gq, gkv, gqk, gout2, gup2, gdown2,
    ) = call(
        results,
        "results",
        None,
        [
            ((1, micro, local_rows, width), HALF, ANY),
            ((2, share), FLOAT),
            ((3, share, channels), FLOAT, LATE),
            ((3, channels), FLOAT),
            ((share, channels), FLOAT, LATE),
            ((share, 2, hidden_units), FLOAT, ANY),
            ((share, hidden_units), FLOAT, ANY),
            ((2, share), FLOAT),
            ((share, query_width), FLOAT, LATE),
            ((share, 2, pair_width // 2), FLOAT, LATE),
            ((2, head_width), FLOAT),
            ((share, query_width), FLOAT, LATE),
            ((share, 2, hidden_units), FLOAT, ANY),
            ((share, hidden_units), FLOAT, ANY),
        ],
        [
            pltpu.VMEM((2, share, hidden_units), HALF),
            pltpu.VMEM((2, 2, share, hidden_units), HALF),
            pltpu.VMEM((2, share, hidden_units), FLOAT),
            pltpu.VMEM((2, share, 2, hidden_units), FLOAT),
            pltpu.VMEM((1, micro, local_rows, width), HALF),
            dma(4),
            dma(4),
            dma(2),
        ],
        [(section_edges, ANY), sums, (gout2, LAZY), (gmix, LAZY), (gout1, LAZY), (gin, LAZY)]
        + [(array, ANY) for array in (gdown2, gup2, gdown1, gup1)],
        moved=25 << 20,
    )
    return (
        section_edges,
        cgain,
        gin.transpose(1, 0, 2),
        taps,
        gout1.T,
        gup1,
        gdown1.T,
        again,
        gq,
        gkv,
        gqk,
        gout2.T,
        gup2,
        gdown2.T,
    )


def solution(mesh):
    return jax.shard_map(
        per_device,
        mesh=mesh,
        in_specs=(
            P("section", None, "seq", None),
            P(),
            P(None, "seq"),
            P(),
            P(None, None, "head"),
            P(None, "head"),
            P("head", None),
            P(None, None, "head"),
            P("head", None),
            P(),
            P(None, "head"),
            P(None, None, "head"),
            P(),
            P("head", None),
            P(None, None, "head"),
            P("head", None),
        ),
        out_specs=(
            P("section", None, "seq", None),
            P(None, ("section", "seq")),
            P(("section", "seq"), None, "head"),
            P(None, "head"),
            P("head", ("section", "seq")),
            P(("section", "seq"), None, "head"),
            P("head", ("section", "seq")),
            P(None, ("section", "seq")),
            P(("section", "seq"), "head"),
            P(("section", "seq"), None, "head"),
            P(),
            P("head", ("section", "seq")),
            P(("section", "seq"), None, "head"),
            P("head", ("section", "seq")),
        ),
        check_vma=False,
    )
```
